32 devices in a mesh: slab: 16 (over z, y, x), grp: 2 (over core).
Axes of the slice: x: 2, y: 2, z: 4, core: 2. Of those that a mesh axis runs over, the one named last changes fastest.
Arguments:
- photon_table: float32 [32, 10, 3200], P('slab', 'grp'), may hold values from -30 to 30
- bin_weights: float32 [32, 10, 3200], P('slab', 'grp'), may hold values from 0.005 to 0.03
- first_start: int32 [32], replicated, may hold values from 0 to 60, as said below
- first_band: float32 [32, 4], replicated, may hold values from 0.2 to 1
- second_start: int32 [10], replicated, may hold values from 0 to 60, as said below
- second_band: float32 [10, 4], replicated, may hold values from 0.2 to 1
- third_start: int32 [64], replicated, may hold values from 0 to 28, as said below
- third_band: float32 [64, 4], replicated, may hold values from 0.2 to 1
- fourth_start: int32 [50], replicated, may hold values from 0 to 28, as said below
- fourth_band: float32 [50, 4], replicated, may hold values from 0.2 to 1
Outputs:
- solution: float32 [64, 64, 1024], P('slab', 'grp')
- residual: float32 [64, 64, 1024], P('slab', 'grp')
The draws below stay inside these ranges and needn't reach their ends.
Inputs may be any that keep to these rules, and one draw needn't show every extreme that they name: Bin i of the first dimension uses coefficients first_start[i] to first_start[i] + 3; the starts never fall from one bin to the next, the first bin starts at 0 and the last at 60. Bin i of the second dimension uses coefficients second_start[i] to second_start[i] + 3; the starts never fall, the first is 0 and the last 60. Bin i of the third dimension uses coefficients third_start[i] to third_start[i] + 3; the starts never fall, the first is 0 and the last 28. Bin i of the fourth dimension uses coefficients fourth_start[i] to fourth_start[i] + 3; the starts never fall, the first is 0 and the last 28.
All inputs are finite; a program needn't handle non-finite values.
Results may differ from the reference program's by a relative error of at most 0.0003.
Values sent between devices are 32-bit elements; how exact they have to be, the bound alone decides.
No kernel may reach another device: no remote copies, remote signals or barrier semaphores. Data moves between devices by JAX's collectives and lax.ppermute only.
A program may use at most 64 MiB of HBM per device.

```python
import math
import jax
import jax.numpy as jnp
from jax import lax

K0 = 64
K1 = 64
K2 = 32
K3 = 32
R1 = 5
N2 = 64
N3 = 50
ITERS = 2
N0 = 32
N1 = 10


def start_table(key, bin_count, coef_count):
    positions = jnp.arange(bin_count, dtype=jnp.int32)
    levels = jax.random.randint(key, (8,), 0, 2, dtype=jnp.int32)
    levels = jnp.where(jnp.arange(8, dtype=jnp.int32) == 0, 1 - levels[1], levels)
    segment = positions * 8 // bin_count
    picked = jnp.sum(jnp.where(segment[:, None] == jnp.arange(8, dtype=jnp.int32)[None, :], levels[None, :], 0), axis=1)
    spacing = 1 + 4 * picked
    running = jnp.concatenate([jnp.zeros((1,), jnp.int32), jnp.cumsum(spacing[:-1]).astype(jnp.int32)])
    total = running[bin_count - 1]
    starts = running * (coef_count - 4) // total
    return starts.astype(jnp.int32)


def draw_first_start(key, part):
    return start_table(key, N0, K0)


def draw_second_start(key, part):
    offset_key = jax.random.fold_in(key, 11)
    spacing_key = jax.random.fold_in(key, 12)
    group_count = N1 // R1
    block_width = K1 // group_count
    lead_bin = N1 - R1
    target = (group_count // 2 - 1) * block_width + jax.random.randint(offset_key, (), 0, block_width, dtype=jnp.int32)
    spacing = jax.random.randint(spacing_key, (N1,), 1, 6, dtype=jnp.int32)
    running = jnp.concatenate([jnp.zeros((1,), jnp.int32), jnp.cumsum(spacing[:-1]).astype(jnp.int32)])
    total = jnp.maximum(running[lead_bin], 1)
    early = running * target // total
    positions = jnp.arange(N1, dtype=jnp.int32)
    late = target + (positions - lead_bin) * (K1 - 4 - target) // max(R1 - 1, 1)
    return jnp.where(positions <= lead_bin, early, late).astype(jnp.int32)


def draw_third_start(key, part):
    return start_table(key, N2, K2)


def draw_fourth_start(key, part):
    return start_table(key, N3, K3)


def block_levels(rng, dims, pieces, least, top_value):
    loudness = 1.0
    for dim, shards_of in pieces:
        draws = jax.random.uniform(jax.random.fold_in(jax.random.fold_in(rng, 6), dim), (shards_of,), jnp.float32, least / len(pieces), top_value / len(pieces))
        loudness = loudness * jnp.repeat(jnp.exp(draws), dims[dim] // shards_of).reshape((-1,) + (1,) * (len(dims) - 1 - dim))
    return loudness


def noise(rng, shape, spread, reach, split=(), held_as=jnp.bfloat16):
    values = spread * jax.random.normal(rng, shape, jnp.float32)
    if split:
        values = values * block_levels(rng, shape, split, -0.22, 0.18)
    return jnp.clip(values, -reach, reach).astype(held_as)


def setup_inputs(seed: int = 0) -> dict:
    streams_of = jax.random.split(jax.random.key(seed), 11)
    return {
        "photon_table": noise(streams_of[0], (N0, N1, N2 * N3), 5.0, 30.0, ((0, 16), (1, 2)), jnp.float32),
        "bin_weights": jnp.clip(jnp.exp(math.log(0.03) - 1.7917595 * jax.random.uniform(streams_of[1], (N0, N1, N2 * N3), jnp.float32) ** block_levels(streams_of[1], (N0, N1, N2 * N3), ((0, 16), (1, 2)), -0.2, 0.2)), 0.005, 0.03),
        "first_start": draw_first_start(jax.random.fold_in(streams_of[10], 71), 0),
        "first_band": jnp.clip(jax.random.uniform(streams_of[3], (N0, 4), jnp.float32, 0.2, 1.0), 0.2, 1.0),
        "second_start": draw_second_start(jax.random.fold_in(streams_of[10], 71), 0),
        "second_band": jnp.clip(jax.random.uniform(streams_of[5], (N1, 4), jnp.float32, 0.2, 1.0), 0.2, 1.0),
        "third_start": draw_third_start(jax.random.fold_in(streams_of[10], 71), 0),
        "third_band": jnp.clip(jax.random.uniform(streams_of[7], (N2, 4), jnp.float32, 0.2, 1.0), 0.2, 1.0),
        "fourth_start": draw_fourth_start(jax.random.fold_in(streams_of[10], 71), 0),
        "fourth_band": jnp.clip(jax.random.uniform(streams_of[9], (N3, 4), jnp.float32, 0.2, 1.0), 0.2, 1.0),
    }


highest = lax.Precision.HIGHEST
smoothing = 0.1
stencil_weights = (1.0, -4.0, 6.0, -4.0, 1.0)


def dense_basis(starts, values, coef_count):
    relative = jnp.arange(coef_count, dtype=jnp.int32)[None, :] - starts[:, None]
    matrix = jnp.zeros((starts.shape[0], coef_count), jnp.float32)
    for offset in range(4):
        matrix = matrix + jnp.where(relative == offset, values[:, offset:offset + 1], 0.0)
    return matrix


def five_point(source, along, extent):
    running = stencil_weights[0] * lax.slice_in_dim(source, 0, extent, axis=along)
    for offset in range(1, 5):
        running = running + stencil_weights[offset] * lax.slice_in_dim(source, offset, offset + extent, axis=along)
    return running


def local_stencil(tensor, along):
    widths = [(0, 0)] * tensor.ndim
    widths[along] = (2, 2)
    return five_point(jnp.pad(tensor, widths), along, tensor.shape[along])


def forward(coeffs, basis_set):
    first_basis, second_basis, third_basis, fourth_basis = basis_set
    blocked = coeffs.reshape(K0, K1, K2, K3)
    blocked = jnp.einsum('abcd,nd->abcn', blocked, fourth_basis, precision=highest)
    blocked = jnp.einsum('abcn,mc->abmn', blocked, third_basis, precision=highest)
    blocked = jnp.einsum('abmn,lb->almn', blocked, second_basis, precision=highest)
    blocked = jnp.einsum('almn,ka->klmn', blocked, first_basis, precision=highest)
    return blocked.reshape(N0, N1, N2 * N3)


def adjoint(table, basis_set):
    first_basis, second_basis, third_basis, fourth_basis = basis_set
    blocked = table.reshape(N0, N1, N2, N3)
    blocked = jnp.einsum('klmn,ka->almn', blocked, first_basis, precision=highest)
    blocked = jnp.einsum('almn,lb->abmn', blocked, second_basis, precision=highest)
    blocked = jnp.einsum('abmn,mc->abcn', blocked, third_basis, precision=highest)
    blocked = jnp.einsum('abcn,nd->abcd', blocked, fourth_basis, precision=highest)
    return blocked.reshape(K0, K1, K2 * K3)


def penalty(coeffs):
    blocked = coeffs.reshape(K0, K1, K2, K3)
    running = local_stencil(blocked, 0) + local_stencil(blocked, 1)
    running = running + local_stencil(blocked, 2) + local_stencil(blocked, 3)
    return running.reshape(K0, K1, K2 * K3)


def reference(photon_table, bin_weights, first_start, first_band, second_start, second_band, third_start, third_band, fourth_start, fourth_band):
    basis_set = (dense_basis(first_start, first_band, K0), dense_basis(second_start, second_band, K1),
                 dense_basis(third_start, third_band, K2), dense_basis(fourth_start, fourth_band, K3))

    def apply_normal(coeffs):
        return adjoint(bin_weights * forward(coeffs, basis_set), basis_set) + smoothing * penalty(coeffs)

    right_side = adjoint(bin_weights * photon_table, basis_set)
    solution = jnp.zeros_like(right_side)
    residual = right_side
    direction = right_side
    norm_now = jnp.sum(residual * residual)
    for sweep in range(ITERS):
        mapped = apply_normal(direction)
        step_size = norm_now / jnp.sum(direction * mapped)
        solution = solution + step_size * direction
        residual = residual - step_size * mapped
        norm_next = jnp.sum(residual * residual)
        direction = residual + (norm_next / norm_now) * direction
        norm_now = norm_next
    return solution, residual
```

```python
import jax
import jax.numpy as jnp
from jax import lax
from jax.experimental import pallas as pl
from jax.experimental.pallas import tpu as pltpu
from jax.sharding import PartitionSpec as P

K0 = 64
K1 = 64
K2 = 32
K3 = 32
ITERS = 2


highest = lax.Precision.HIGHEST
smoothing = 0.1
stencil_weights = (1.0, -4.0, 6.0, -4.0, 1.0)


def with_halo(value, sides, width):
    for axis, dim in sides:
        count, length = (lax.axis_size(axis), value.shape[dim])
        up = [(i, (i + 1) % count) for i in range(count - 1)]
        down = [(j, i) for i, j in up]
        last = lax.slice_in_dim(value, length - width, length, axis=dim)
        initial = lax.slice_in_dim(value, 0, width, axis=dim)
        before = lax.ppermute(last, axis, up)
        after = lax.ppermute(initial, axis, down)
        value = jnp.concatenate([before, value, after], axis=dim)
    return value


def dense_basis(starts, values, coef_count):
    relative = jnp.arange(coef_count, dtype=jnp.int32)[None, :] - starts[:, None]
    matrix = jnp.zeros((starts.shape[0], coef_count), jnp.float32)
    for offset in range(4):
        matrix = matrix + jnp.where(relative == offset, values[:, offset : offset + 1], 0.0)
    return matrix


def five_point(source, along, extent):
    running = stencil_weights[0] * lax.slice_in_dim(source, 0, extent, axis=along)
    for offset in range(1, 5):
        running = running + stencil_weights[offset] * lax.slice_in_dim(
            source, offset, offset + extent, axis=along
        )
    return running


def local_stencil(tensor, along):
    widths = [(0, 0)] * tensor.ndim
    widths[along] = (2, 2)
    return five_point(jnp.pad(tensor, widths), along, tensor.shape[along])


def inner_forward(tensor, third_basis, fourth_basis):
    leading, middle = (tensor.shape[0], tensor.shape[1])
    blocked = tensor.reshape(leading, middle, third_basis.shape[1], fourth_basis.shape[1])
    blocked = jnp.einsum("abcd,nd->abcn", blocked, fourth_basis, precision=highest)
    blocked = jnp.einsum("abcn,mc->abmn", blocked, third_basis, precision=highest)
    return blocked.reshape(leading, middle, third_basis.shape[0] * fourth_basis.shape[0])


def inner_adjoint(tensor, third_basis, fourth_basis):
    leading, middle = (tensor.shape[0], tensor.shape[1])
    blocked = tensor.reshape(leading, middle, third_basis.shape[0], fourth_basis.shape[0])
    blocked = jnp.einsum("abmn,mc->abcn", blocked, third_basis, precision=highest)
    blocked = jnp.einsum("abcn,nd->abcd", blocked, fourth_basis, precision=highest)
    return blocked.reshape(leading, middle, third_basis.shape[1] * fourth_basis.shape[1])


def lead_product(tensor, matrix):
    combined = jnp.einsum(
        "ka,ain->kin",
        matrix,
        lax.all_to_all(tensor, "slab", split_axis=2, concat_axis=0, tiled=True),
        precision=highest,
    )
    return lax.all_to_all(combined, "slab", split_axis=0, concat_axis=2, tiled=True)


def second_product(tensor, matrix):
    return jnp.einsum(
        "lp,apn->aln", matrix, lax.all_gather(tensor, "grp", axis=1, tiled=True), precision=highest
    )


def penalty(coeffs):
    leading, middle = (coeffs.shape[0], coeffs.shape[1])
    padded = with_halo(coeffs, (("slab", 0), ("grp", 1)), 2)
    along_lead = five_point(padded[:, 2 : 2 + middle], 0, leading)
    along_rows = five_point(padded[2 : 2 + leading, :], 1, middle)
    blocked = coeffs.reshape(leading, middle, K2, K3)
    inner_part = local_stencil(blocked, 2) + local_stencil(blocked, 3)
    return along_lead + along_rows + inner_part.reshape(leading, middle, K2 * K3)


def squared_total(vector):
    return lax.psum(jnp.sum(vector * vector), ("slab", "grp"))


def per_device(
    photon_table,
    bin_weights,
    first_start,
    first_band,
    second_start,
    second_band,
    third_start,
    third_band,
    fourth_start,
    fourth_band,
):
    first_basis = dense_basis(first_start, first_band, K0)
    second_basis = dense_basis(second_start, second_band, K1)
    third_basis = dense_basis(third_start, third_band, K2)
    fourth_basis = dense_basis(fourth_start, fourth_band, K3)
    first_back = first_basis.T
    group_index = lax.axis_index("grp")
    row_count = photon_table.shape[1]
    coef_rows = K1 // lax.axis_size("grp")
    near_rows = lax.dynamic_slice_in_dim(second_basis, group_index * row_count, row_count, 0)
    back_rows = lax.dynamic_slice_in_dim(second_basis.T, group_index * coef_rows, coef_rows, 0)

    def adjoint(table):
        tensor = lead_product(table, first_back)
        tensor = second_product(tensor, back_rows)
        return inner_adjoint(tensor, third_basis, fourth_basis)

    right_side = adjoint(bin_weights * photon_table)
    solution = jnp.zeros_like(right_side)
    residual = right_side
    direction = right_side
    norm_now = squared_total(residual)
    for sweep in range(ITERS):
        forward_tensor = inner_forward(direction, third_basis, fourth_basis)
        forward_tensor = second_product(forward_tensor, near_rows)
        mapped = adjoint(
            bin_weights * lead_product(forward_tensor, first_basis)
        ) + smoothing * penalty(direction)
        curve_total = lax.psum(jnp.sum(direction * mapped), ("slab", "grp"))
        step_size = norm_now / curve_total
        solution = solution + step_size * direction
        residual = residual - step_size * mapped
        norm_next = squared_total(residual)
        direction = residual + norm_next / norm_now * direction
        norm_now = norm_next
    return (solution, residual)


SLABS, GRPS = 16, 2
DEVICES = SLABS * GRPS
L0, L1 = 2, 5
ROWS = L0 * L1
N2, N3 = 64, 50
N0, N1 = 32, 10
HI = lax.Precision.HIGHEST
f32 = jnp.float32


def iota(shape, dim):
    return lax.broadcasted_iota(jnp.int32, shape, dim)


def mm(a, b):
    return jnp.dot(a, b, precision=HI, preferred_element_type=f32)


def mm_t(a, b):
    return lax.dot_general(
        a, b, (((1,), (1,)), ((), ())), precision=HI, preferred_element_type=f32
    )


def move(block, source, target):
    shift = (target - source) * 32 % 128
    return pltpu.roll(block, shift, 1) if shift else block


def merge(parts):
    lane = iota(parts[0].shape, 1)
    out = parts[-1]
    for q in range(len(parts) - 2, -1, -1):
        out = jnp.where(lane < 32 * (q + 1), parts[q], out)
    return out


def slot(r):
    return 8 * (r // L1) + r % L1


def banded(start_ref, band_ref, width, wrap):
    n = start_ref.shape[0]
    row = start_ref[...].reshape(1, n)
    eye = iota((n, n), 0) == iota((n, n), 1)
    start = jnp.sum(jnp.where(eye, row.astype(f32), 0.0), axis=1, keepdims=True)
    relative = (iota((n, width), 1) % wrap) - start.astype(jnp.int32)
    band = band_ref[...]
    out = jnp.zeros((n, width), f32)
    for offset in range(4):
        out = out + jnp.where(relative == offset, band[:, offset : offset + 1], 0.0)
    return out


def expand(ref, a, p):
    first = 200 * p
    tile, off = first // 128, first % 128
    lane = iota((L1, 128), 1)

    def window(t):
        low = ref[a, :, t * 128 : (t + 1) * 128]
        if off == 0:
            return low
        t1 = min(t + 1, 24)
        high = ref[a, :, t1 * 128 : (t1 + 1) * 128]
        return jnp.where(
            lane < 128 - off, pltpu.roll(low, 128 - off, 1), pltpu.roll(high, 128 - off, 1)
        )

    return window(tile), window(min(tile + 1, 24))


def table_to_mixed(field, kron_third, second_t, rows_ref, stack_ref):
    rows_ref[...] = mm(field, kron_third)
    for c in range(4):
        for j in range(3):
            parts = []
            for q in range(4):
                r = 4 * j + q
                if r < ROWS:
                    part = rows_ref[pl.ds(slot(r), 16, stride=16), :]
                    parts.append(move(part, c, q))
                else:
                    parts.append(jnp.zeros((16, 128), f32))
            stack_ref[16 * c : 16 * c + 16, 128 * j : 128 * j + 128] = merge(parts)
    return mm(second_t, stack_ref[...])


def mixed_to_table(value, kron_third, second, rows_ref, stack_ref):
    stack_ref[...] = mm(second, value)
    rows_ref[...] = jnp.zeros((256, 128), f32)
    for r in range(ROWS):
        j, q = r // 4, r % 4
        parts = [
            move(stack_ref[16 * c : 16 * c + 16, 128 * j : 128 * j + 128], q, c) for c in range(4)
        ]
        rows_ref[pl.ds(slot(r), 16, stride=16), :] = merge(parts)
    return mm_t(rows_ref[...], kron_third)


def inner_penalty(value):
    out = 12.0 * value
    row = iota((32, 128), 0)
    inside = iota((32, 128), 1) % 32
    tiles = []
    for j in range(3):
        tile = value[:, 128 * j : 128 * j + 128]
        total = 12.0 * tile
        for d, weight in ((1, -4.0), (2, 1.0)):
            total = total + weight * (
                jnp.where(row >= d, pltpu.roll(tile, d, 0), 0.0)
                + jnp.where(row < 32 - d, pltpu.roll(tile, 32 - d, 0), 0.0)
                + jnp.where(inside >= d, pltpu.roll(tile, d, 1), 0.0)
                + jnp.where(inside < 32 - d, pltpu.roll(tile, 128 - d, 1), 0.0)
            )
        tiles.append(total)
    return jnp.concatenate(tiles, axis=1)


def tile_of(value, j):
    return value[:, 128 * j : 128 * j + 128]


def put(ref, row, count, value):
    ref[pl.ds(row, 32, stride=count), :] = value


def lanes(values):
    lane = iota((8, 128), 1)
    out = jnp.zeros((8, 128), f32)
    for k, value in enumerate(values):
        out = jnp.where(lane == k, value, out)
    return out


def spread(ref, row, count, values):
    one = lanes(values)
    put(ref, row, count, jnp.concatenate([one] * 4, axis=0))


def totals(ref, row, count, number):
    summed = jnp.sum(ref[pl.ds(row, 32, stride=count), :], axis=0, keepdims=True)
    lane = iota((1, 128), 1)
    return [jnp.sum(jnp.where(lane == k, summed, 0.0)) for k in range(number)]


def pick(ref, k):
    lane = iota((1, 128), 1)
    return jnp.sum(jnp.where(lane == k, ref[0:1, :], 0.0))


def start_kernel(
    table_ref, weight_ref, start2_ref, band2_ref, start3_ref, band3_ref,
    send_ref, wide_ref, kron_ref, second_ref, second_t_ref, field_ref, rows_ref, stack_ref,
):
    fourth = banded(start3_ref, band3_ref, 128, 32)
    pick_bin = (iota((256, N3), 0) % N3 == iota((256, N3), 1)) & (iota((256, N3), 0) < 4 * N3)
    kron = mm(jnp.where(pick_bin, 1.0, 0.0), fourth)
    same = iota((256, 128), 0) // N3 == iota((256, 128), 1) // 32
    kron = jnp.where(same, kron, 0.0)
    kron_ref[...] = kron
    third = banded(start2_ref, band2_ref, 32, 32)
    order = iota((N2, N2), 0)
    permute = (order % 16) * 4 + order // 16 == iota((N2, N2), 1)
    second = mm(jnp.where(permute, 1.0, 0.0), third)
    second_ref[...] = second
    second_t = second.T
    second_t_ref[...] = second_t
    wide_ref[...] = jnp.zeros((256, 256), f32)
    field_ref[...] = jnp.zeros((256, 256), f32)
    for p in range(16):
        for a in range(L0):
            base = 16 * p + 8 * a
            low, high = expand(weight_ref, a, p)
            wide_ref[base : base + L1, 0:128] = low
            wide_ref[base : base + L1, 128:256] = high
            t_low, t_high = expand(table_ref, a, p)
            field_ref[base : base + L1, 0:128] = t_low * low
            field_ref[base : base + L1, 128:256] = t_high * high
    mixed = table_to_mixed(field_ref[...], kron, second_t, rows_ref, stack_ref)
    once = inner_penalty(mixed)
    twice = inner_penalty(once)
    for base, value in ((0, mixed), (3, once), (5, twice)):
        put(send_ref, base, 8, tile_of(value, 0))
        put(send_ref, base + 1, 8, tile_of(value, 1))
    lane = iota((32, 128), 1)
    put(send_ref, 2, 8, jnp.where(lane < 64, tile_of(mixed, 2), pltpu.roll(tile_of(once, 2), 64, 1)))
    put(send_ref, 7, 8, tile_of(twice, 2))


def pentadiagonal(n):
    gap = jnp.abs(iota((n, n), 0) - iota((n, n), 1))
    return jnp.where(gap == 0, 6.0, jnp.where(gap == 1, -4.0, jnp.where(gap == 2, 1.0, 0.0)))


def three_terms(value):
    high = value.astype(jnp.bfloat16)
    rest = value - high.astype(f32)
    middle = rest.astype(jnp.bfloat16)
    low = (rest - middle.astype(f32)).astype(jnp.bfloat16)
    return high, middle, low


def choose(pieces, selector):
    out = None
    for piece in pieces:
        term = jnp.dot(piece, selector, preferred_element_type=f32)
        out = term if out is None else out + term
    return out


def matrix_kernel(
    group_ref, start0_ref, band0_ref, start1_ref, band1_ref,
    gram_ref, high_ref, lift_ref, side_ref, rows0_ref, rows1_ref,
):
    first = banded(start0_ref, band0_ref, K0, K0)
    second = banded(start1_ref, band1_ref, K1, K1)
    penalty_matrix = pentadiagonal(K0)

    def powers(basis):
        out = [basis]
        for _ in range(3):
            out.append(mm(out[-1], penalty_matrix))
        return out

    total = DEVICES * ROWS
    row0 = iota((total, N0), 0)
    pick0 = 2 * (row0 % 32 // 2) + row0 // 32 // L1 == iota((total, N0), 1)
    row1 = iota((total, N1), 0)
    pick1 = L1 * (row1 % 2) + row1 // 32 % L1 == iota((total, N1), 1)
    powers0, powers1 = powers(first), powers(second)
    wide0 = mm(jnp.where(pick0, 1.0, 0.0), first)
    wide1 = mm(jnp.where(pick1, 1.0, 0.0), second)
    for k in range(4):
        rows0_ref[:, 32 * k : 32 * k + 32] = mm_t(wide0, powers0[k])
        rows1_ref[:, 16 * k : 16 * k + N1] = mm_t(wide1, powers1[k])
    col0 = iota((N0, total), 1)
    select0 = jnp.where(
        2 * (col0 % 32 // 2) + col0 // 32 // L1 == iota((N0, total), 0), 1.0, 0.0
    ).astype(jnp.bfloat16)
    col1 = iota((N1, total), 1)
    select1 = jnp.where(
        L1 * (col1 % 2) + col1 // 32 % L1 == iota((N1, total), 0), 1.0, 0.0
    ).astype(jnp.bfloat16)

    @pl.loop(0, ROWS)
    def _(step):
        base = pl.multiple_of(step * 32, 32)
        block0 = rows0_ref[pl.ds(base, 32), :]
        block1 = rows1_ref[pl.ds(base, 32), :]
        g = [choose(three_terms(block0[:, 32 * k : 32 * k + 32]), select0) for k in range(4)]
        h = [choose(three_terms(block1[:, 16 * k : 16 * k + N1]), select1) for k in range(4)]
        gram_ref[pl.ds(base, 32), :] = g[0] * h[0]
        gram_ref[pl.ds(base + total, 32), :] = g[1] * h[0] + g[0] * h[1]
        high_ref[pl.ds(base, 32), :] = g[2] * h[0] + 2.0 * g[1] * h[1] + g[0] * h[2]
        high_ref[pl.ds(base + total, 32), :] = (
            g[3] * h[0] + 3.0 * (g[2] * h[1] + g[1] * h[2]) + g[0] * h[3]
        )

    lifted = choose(three_terms(first.T), select0)
    column = iota((K0, total), 1)
    owner = L1 * (column % 2) + column // 32 % L1
    for n in range(N1):
        lift_ref[K0 * n : K0 * n + K0, :] = jnp.where(owner == n, lifted, 0.0)

    coef = iota((128, K1), 0) % 32 + 32 * group_ref[0]
    pick_coef = jnp.where(coef == iota((128, K1), 1), 1.0, 0.0)
    side_ref[...] = jnp.zeros((128, 128), f32)
    spot = iota((N1, 128), 1)
    for k in range(3):
        own = mm_t(pick_coef, powers1[k])
        for alpha in range(4):
            rows = slice(32 * alpha, 32 * alpha + 32)
            side_ref[rows, 40 * k + 10 * alpha : 40 * k + 10 * alpha + 10] = own[rows, :]


def unpack(ref, row, count, r, source, target):
    return move(ref[pl.ds(row, 32, stride=count), :], source, target)


def first_column_kernel(recv_ref, gram_ref, send_ref, fields_ref, images_ref):
    total = DEVICES * ROWS
    zero = jnp.zeros((32, 128), f32)
    for r in range(ROWS):
        j, q = r // 4, r % 4
        where0 = (j, q) if j < 2 else (2, q)
        where1 = (3 + j, q) if j < 2 else (2, q + 2)
        where2 = (5 + j, q) if j < 2 else (7, q)
        parts = [
            unpack(recv_ref, place[0], 8, r, place[1], k)
            for k, place in enumerate((where0, where1, where2))
        ]
        fields_ref[32 * r : 32 * r + 32, :] = merge(parts + [zero])
    fields = fields_ref[...]
    product = mm(gram_ref[...], fields)
    lane = iota((total, 128), 1)
    images = product[:total] + jnp.where(
        (lane >= 32) & (lane < 64), pltpu.roll(product[total:], 32, 1), 0.0
    )
    images_ref[...] = images
    norm = jnp.sum(jnp.where(lane < 32, fields * images, 0.0))
    bend = jnp.sum(jnp.where(lane < 32, fields * pltpu.roll(images, 96, 1), 0.0))
    send_rows(send_ref, images_ref)
    spread(send_ref, 3, 4, (norm, bend))


def send_rows(send_ref, value_ref):
    for j in range(3):
        parts = []
        for q in range(4):
            r = 4 * j + q
            if r < ROWS:
                parts.append(move(value_ref[32 * r : 32 * r + 32, :], 0, q))
            else:
                parts.append(jnp.zeros((32, 128), f32))
        put(send_ref, j, 4, merge(parts))


def received_rows(recv_ref):
    return jnp.concatenate([recv_ref[pl.ds(j, 32, stride=4), :] for j in range(3)], axis=1)


def first_row_kernel(
    recv_ref, wide_ref, kron_ref, second_ref, second_t_ref,
    send_ref, scalar_ref, rows_ref, stack_ref,
):
    norm, bend = totals(recv_ref, 3, 4, 2)
    scalar_ref[...] = lanes((norm, bend))
    kron = kron_ref[...]
    field = mixed_to_table(received_rows(recv_ref), kron, second_ref[...], rows_ref, stack_ref)
    weighted = wide_ref[...] * field
    energy = jnp.sum(field * weighted)
    mixed = table_to_mixed(weighted, kron, second_t_ref[...], rows_ref, stack_ref)
    once = inner_penalty(mixed)
    for base, value in ((0, mixed), (3, once)):
        put(send_ref, base, 8, tile_of(value, 0))
        put(send_ref, base + 1, 8, tile_of(value, 1))
    lane = iota((32, 128), 1)
    put(send_ref, 2, 8, jnp.where(lane < 64, tile_of(mixed, 2), pltpu.roll(tile_of(once, 2), 64, 1)))
    spread(send_ref, 5, 8, (energy,))
    for row in (6, 7):
        put(send_ref, row, 8, jnp.zeros((32, 128), f32))


def second_column_kernel(
    recv_ref, gram_ref, fields_ref, images_ref, scalar_ref,
    send_ref, blend_ref, out_scalar_ref, next_ref, image_ref,
):
    zero = jnp.zeros((32, 128), f32)
    for r in range(ROWS):
        j, q = r // 4, r % 4
        where0 = (j, q) if j < 2 else (2, q)
        where1 = (3 + j, q) if j < 2 else (2, q + 2)
        parts = [
            unpack(recv_ref, place[0], 8, r, place[1], k) for k, place in enumerate((where0, where1))
        ]
        next_ref[32 * r : 32 * r + 32, :] = merge(parts + [zero])
    (energy,) = totals(recv_ref, 5, 8, 1)
    norm, bend = pick(scalar_ref, 0), pick(scalar_ref, 1)
    step = norm / (energy + 0.1 * bend)
    out_scalar_ref[...] = lanes((norm, step))
    fields, images, following = fields_ref[...], images_ref[...], next_ref[...]
    image = mm(gram_ref[0 : DEVICES * ROWS, :], following)
    image_ref[...] = images - step * (image + 0.1 * pltpu.roll(images, 96, 1))
    send_rows(send_ref, image_ref)
    put(send_ref, 3, 4, zero)
    lane = iota(fields.shape, 1)
    reduced = fields - step * (following + 0.1 * pltpu.roll(fields, 96, 1))
    blend_ref[...] = jnp.where(lane < 64, reduced, pltpu.roll(fields, 64, 1))


def coefficient_penalty(value):
    k = iota(value.shape, 0) % K0
    count = value.shape[0]
    total = 6.0 * value
    for d, weight in ((1, -4.0), (2, 1.0)):
        total = total + weight * (
            jnp.where(k >= d, pltpu.roll(value, d, 0), 0.0)
            + jnp.where(k < K0 - d, pltpu.roll(value, count - d, 0), 0.0)
        )
    return total


def send_blocks(send_ref, count, base, value_ref, block):
    for j in range(10):
        parts = []
        for q in range(4):
            m = 4 * j + q
            alpha, n = m // 10, m % 10
            parts.append(move(value_ref[pl.ds(K0 * n + alpha, 16, stride=4), :], block, q))
        merged = merge(parts)
        for g in range(GRPS):
            send_ref[pl.ds(g * count + base + j, 16, stride=2 * count), :] = merged


def middle_kernel(blend_ref, gram_ref, high_ref, lift_ref, scalar_ref, send_ref, keep_ref, sums_ref):
    total = DEVICES * ROWS
    step = pick(scalar_ref, 1)
    small = 0.1 * step
    blend = blend_ref[...]
    lane = iota(blend.shape, 1)
    product, higher = mm(gram_ref[...], blend), mm(high_ref[...], blend)
    g0, g1, g2, g3 = product[:total], product[total:], higher[:total], higher[total:]
    head = g0 - small * pltpu.roll(g1, 64, 1)
    tail = g1 - small * pltpu.roll(g2, 64, 1)
    end = g2 - small * pltpu.roll(g3, 64, 1)
    scaled = pltpu.roll(blend, 64, 1)
    low = lane < 32
    norm = jnp.sum(jnp.where(low, blend * head - small * scaled * tail, 0.0))
    head_p = tail + pltpu.roll(head, 96, 1)
    tail_p = end + pltpu.roll(tail, 96, 1)
    bend = jnp.sum(jnp.where(low, blend * head_p - small * scaled * tail_p, 0.0))
    sums_ref[...] = lanes((norm, bend))
    lifted = mm(lift_ref[...], blend)
    once = coefficient_penalty(lifted)
    twice = coefficient_penalty(once)
    h_a = lifted - small * pltpu.roll(once, 64, 1)
    y_1 = once + pltpu.roll(lifted, 96, 1)
    x_a = once + pltpu.roll(lifted, 96, 1) - small * (
        pltpu.roll(twice, 64, 1) + pltpu.roll(once, 32, 1)
    )
    h_0 = pltpu.roll(lifted, 64, 1)
    wide = iota(lifted.shape, 1)
    keep = jnp.where(
        wide < 32, h_0, jnp.where(wide < 64, pltpu.roll(h_a, 32, 1), jnp.where(wide < 96, y_1, pltpu.roll(x_a, 96, 1)))
    )
    keep_ref[...] = keep
    for block in range(3):
        send_blocks(send_ref, 30, 10 * block, keep_ref, block)


def second_row_kernel(
    recv_ref, sums_ref, wide_ref, kron_ref, second_ref, second_t_ref,
    send_ref, rows_ref, stack_ref,
):
    kron = kron_ref[...]
    field = mixed_to_table(received_rows(recv_ref), kron, second_ref[...], rows_ref, stack_ref)
    weighted = wide_ref[...] * field
    energy = jnp.sum(field * weighted)
    mixed = table_to_mixed(weighted, kron, second_t_ref[...], rows_ref, stack_ref)
    for j in range(3):
        put(send_ref, j, 4, tile_of(mixed, j))
    spread(send_ref, 3, 4, (energy, pick(sums_ref, 0), pick(sums_ref, 1)))


def third_column_kernel(
    recv_ref, lift_ref, keep_ref, scalar_ref, send_ref, out_scalar_ref, last_ref, mixed_ref
):
    zero = jnp.zeros((32, 128), f32)
    for r in range(ROWS):
        j, q = r // 4, r % 4
        last_ref[32 * r : 32 * r + 32, :] = unpack(recv_ref, j, 4, r, q, 0)
    energy, norm_next, bend = totals(recv_ref, 3, 4, 3)
    norm, step = pick(scalar_ref, 0), pick(scalar_ref, 1)
    ratio = norm_next / norm
    curve = energy + 0.1 * bend - ratio * norm_next / step
    step_next = norm_next / curve
    out_scalar_ref[...] = lanes((norm, step, ratio, step_next))
    lifted = mm(lift_ref[...], last_ref[...])
    keep = keep_ref[...]
    h_a, x_a = pltpu.roll(keep, 96, 1), pltpu.roll(keep, 32, 1)
    mixed_ref[...] = (
        h_a - step_next * (lifted + 0.1 * x_a) - (step_next * ratio / step) * (keep - h_a)
    )
    send_blocks(send_ref, 10, 0, mixed_ref, 0)


def gather_blocks(ref, count, base, out_ref, row):
    for j in range(10):
        rows = [ref[pl.ds(rho * count + base + j, 8, stride=4 * count), :] for rho in range(4)]
        for q in range(4):
            m = row + 4 * j + q
            merged = merge([move(rows[rho], q, rho) for rho in range(4)])
            out_ref[pl.ds(m // 8 * 64 + m % 8, 8, stride=8), :] = merged


def final_kernel(early_ref, late_ref, side_ref, scalar_ref, solution_ref, residual_ref, early, late):
    for block in range(3):
        gather_blocks(early_ref, 30, 10 * block, early, 40 * block)
    gather_blocks(late_ref, 10, 0, late, 0)
    step, ratio, step_next = pick(scalar_ref, 1), pick(scalar_ref, 2), pick(scalar_ref, 3)
    small = 0.1 * step
    side = side_ref[...]
    for tile in range(8):
        def take(ref, block):
            return jnp.concatenate(
                [ref[pl.ds((5 * block + t) * 64 + 8 * tile, 8), :] for t in range(5)], axis=0
            )
        h_0, h_a, y_1, h_r = take(early, 0), take(early, 1), take(early, 2), take(late, 0)
        right = jnp.concatenate(
            [(step + step_next * ratio) * h_0 + step_next * h_a, (-step_next * small) * h_0], axis=0
        )
        columns = slice(128 * tile, 128 * tile + 128)
        solution_ref[:, :, columns] = mm(side[:, 0:80], right).reshape(4, 32, 128)
        right = jnp.concatenate(
            [
                h_r,
                (-small * (1.0 + step_next * ratio / step)) * h_0
                - (0.1 * step_next) * (h_a - small * y_1),
                (0.1 * step_next * small) * h_0,
            ],
            axis=0,
        )
        residual_ref[:, :, columns] = mm(side[:, 0:120], right).reshape(4, 32, 128)


def call(kernel, outputs, scratch, *operands):
    smem = [pl.BlockSpec(memory_space=pltpu.VMEM)] * len(operands)
    if kernel is matrix_kernel:
        smem[0] = pl.BlockSpec(memory_space=pltpu.SMEM)
    return pl.pallas_call(
        kernel,
        out_shape=[jax.ShapeDtypeStruct(shape, f32) for shape in outputs],
        in_specs=smem,
        out_specs=[pl.BlockSpec(memory_space=pltpu.VMEM)] * len(outputs),
        scratch_shapes=[pltpu.VMEM(shape, f32) for shape in scratch],
        compiler_params=pltpu.CompilerParams(vmem_limit_bytes=32 * 2**20),
    )(*operands)


def exchange(buffer):
    count = buffer.shape[0] // DEVICES
    shaped = buffer.reshape(DEVICES, count, 128) if count % 4 == 0 else buffer.reshape(DEVICES, 1, count * 128)
    moved = lax.all_to_all(shaped, ("slab", "grp"), 0, 0, tiled=True)
    return moved.reshape(buffer.shape)


def fast_program(
    photon_table,
    bin_weights,
    first_start,
    first_band,
    second_start,
    second_band,
    third_start,
    third_band,
    fourth_start,
    fourth_band,
):
    total = DEVICES * ROWS
    work = [(256, 128), (64, 384)]
    send, wide, kron, second, second_t = call(
        start_kernel,
        [(256, 128), (256, 256), (256, 128), (64, 32), (32, 64)],
        [(256, 256)] + work,
        photon_table, bin_weights, third_start, third_band, fourth_start, fourth_band,
    )
    recv = exchange(send)
    group = lax.axis_index("grp").reshape(1)
    gram, high, lift, side = call(
        matrix_kernel,
        [(2 * total, total), (2 * total, total), (K0 * N1, total), (128, 128)],
        [(total, 128), (total, 64)],
        group, first_start, first_band, second_start, second_band,
    )
    send, fields, images = call(
        first_column_kernel,
        [(128, 128), (total, 128), (total, 128)],
        [],
        recv, gram,
    )
    recv = exchange(send)
    send, scalars = call(
        first_row_kernel, [(256, 128), (8, 128)], work, recv, wide, kron, second, second_t
    )
    recv = exchange(send)
    send, blend, scalars = call(
        second_column_kernel,
        [(128, 128), (total, 128), (8, 128)],
        [(total, 128), (total, 128)],
        recv, gram, fields, images, scalars,
    )
    recv = exchange(send)
    early_send, keep, sums = call(
        middle_kernel,
        [(DEVICES * 30, 128), (K0 * N1, 128), (8, 128)],
        [],
        blend, gram, high, lift, scalars,
    )
    (send,) = call(
        second_row_kernel, [(128, 128)], work, recv, sums, wide, kron, second, second_t
    )
    early = exchange(early_send)
    recv = exchange(send)
    send, scalars = call(
        third_column_kernel,
        [(DEVICES * 10, 128), (8, 128)],
        [(total, 128), (K0 * N1, 128)],
        recv, lift, keep, scalars,
    )
    late = exchange(send)
    return call(
        final_kernel,
        [(4, 32, 1024), (4, 32, 1024)],
        [(960, 128), (320, 128)],
        early, late, side, scalars,
    )


def fits(mesh):
    return (mesh.shape["slab"], mesh.shape["grp"]) == (SLABS, GRPS)


def solution(mesh):
    placed = (
        P("slab", "grp", None),
        P("slab", "grp", None),
        P(),
        P(),
        P(),
        P(),
        P(),
        P(),
        P(),
        P(),
    )
    return jax.shard_map(
        fast_program if fits(mesh) else per_device,
        mesh=mesh,
        in_specs=placed,
        out_specs=(P("slab", "grp", None), P("slab", "grp", None)),
        check_vma=False,
    )
```

```python
import jax
import jax.numpy as jnp
from jax import lax
from jax.experimental import pallas as pl
from jax.experimental.pallas import tpu as pltpu
from jax.sharding import PartitionSpec as P

K0 = 64
K1 = 64
K2 = 32
K3 = 32
ITERS = 2


highest = lax.Precision.HIGHEST
smoothing = 0.1
stencil_weights = (1.0, -4.0, 6.0, -4.0, 1.0)


def with_halo(value, sides, width):
    for axis, dim in sides:
        count, length = (lax.axis_size(axis), value.shape[dim])
        up = [(i, (i + 1) % count) for i in range(count - 1)]
        down = [(j, i) for i, j in up]
        last = lax.slice_in_dim(value, length - width, length, axis=dim)
        initial = lax.slice_in_dim(value, 0, width, axis=dim)
        before = lax.ppermute(last, axis, up)
        after = lax.ppermute(initial, axis, down)
        value = jnp.concatenate([before, value, after], axis=dim)
    return value


def dense_basis(starts, values, coef_count):
    relative = jnp.arange(coef_count, dtype=jnp.int32)[None, :] - starts[:, None]
    matrix = jnp.zeros((starts.shape[0], coef_count), jnp.float32)
    for offset in range(4):
        matrix = matrix + jnp.where(relative == offset, values[:, offset : offset + 1], 0.0)
    return matrix


def five_point(source, along, extent):
    running = stencil_weights[0] * lax.slice_in_dim(source, 0, extent, axis=along)
    for offset in range(1, 5):
        running = running + stencil_weights[offset] * lax.slice_in_dim(
            source, offset, offset + extent, axis=along
        )
    return running


def local_stencil(tensor, along):
    widths = [(0, 0)] * tensor.ndim
    widths[along] = (2, 2)
    return five_point(jnp.pad(tensor, widths), along, tensor.shape[along])


def inner_forward(tensor, third_basis, fourth_basis):
    leading, middle = (tensor.shape[0], tensor.shape[1])
    blocked = tensor.reshape(leading, middle, third_basis.shape[1], fourth_basis.shape[1])
    blocked = jnp.einsum("abcd,nd->abcn", blocked, fourth_basis, precision=highest)
    blocked = jnp.einsum("abcn,mc->abmn", blocked, third_basis, precision=highest)
    return blocked.reshape(leading, middle, third_basis.shape[0] * fourth_basis.shape[0])


def inner_adjoint(tensor, third_basis, fourth_basis):
    leading, middle = (tensor.shape[0], tensor.shape[1])
    blocked = tensor.reshape(leading, middle, third_basis.shape[0], fourth_basis.shape[0])
    blocked = jnp.einsum("abmn,mc->abcn", blocked, third_basis, precision=highest)
    blocked = jnp.einsum("abcn,nd->abcd", blocked, fourth_basis, precision=highest)
    return blocked.reshape(leading, middle, third_basis.shape[1] * fourth_basis.shape[1])


def lead_product(tensor, matrix):
    combined = jnp.einsum(
        "ka,ain->kin",
        matrix,
        lax.all_to_all(tensor, "slab", split_axis=2, concat_axis=0, tiled=True),
        precision=highest,
    )
    return lax.all_to_all(combined, "slab", split_axis=0, concat_axis=2, tiled=True)


def second_product(tensor, matrix):
    return jnp.einsum(
        "lp,apn->aln", matrix, lax.all_gather(tensor, "grp", axis=1, tiled=True), precision=highest
    )


def penalty(coeffs):
    leading, middle = (coeffs.shape[0], coeffs.shape[1])
    padded = with_halo(coeffs, (("slab", 0), ("grp", 1)), 2)
    along_lead = five_point(padded[:, 2 : 2 + middle], 0, leading)
    along_rows = five_point(padded[2 : 2 + leading, :], 1, middle)
    blocked = coeffs.reshape(leading, middle, K2, K3)
    inner_part = local_stencil(blocked, 2) + local_stencil(blocked, 3)
    return along_lead + along_rows + inner_part.reshape(leading, middle, K2 * K3)


def squared_total(vector):
    return lax.psum(jnp.sum(vector * vector), ("slab", "grp"))


def per_device(
    photon_table,
    bin_weights,
    first_start,
    first_band,
    second_start,
    second_band,
    third_start,
    third_band,
    fourth_start,
    fourth_band,
):
    first_basis = dense_basis(first_start, first_band, K0)
    second_basis = dense_basis(second_start, second_band, K1)
    third_basis = dense_basis(third_start, third_band, K2)
    fourth_basis = dense_basis(fourth_start, fourth_band, K3)
    first_back = first_basis.T
    group_index = lax.axis_index("grp")
    row_count = photon_table.shape[1]
    coef_rows = K1 // lax.axis_size("grp")
    near_rows = lax.dynamic_slice_in_dim(second_basis, group_index * row_count, row_count, 0)
    back_rows = lax.dynamic_slice_in_dim(second_basis.T, group_index * coef_rows, coef_rows, 0)

    def adjoint(table):
        tensor = lead_product(table, first_back)
        tensor = second_product(tensor, back_rows)
        return inner_adjoint(tensor, third_basis, fourth_basis)

    right_side = adjoint(bin_weights * photon_table)
    solution = jnp.zeros_like(right_side)
    residual = right_side
    direction = right_side
    norm_now = squared_total(residual)
    for sweep in range(ITERS):
        forward_tensor = inner_forward(direction, third_basis, fourth_basis)
        forward_tensor = second_product(forward_tensor, near_rows)
        mapped = adjoint(
            bin_weights * lead_product(forward_tensor, first_basis)
        ) + smoothing * penalty(direction)
        curve_total = lax.psum(jnp.sum(direction * mapped), ("slab", "grp"))
        step_size = norm_now / curve_total
        solution = solution + step_size * direction
        residual = residual - step_size * mapped
        norm_next = squared_total(residual)
        direction = residual + norm_next / norm_now * direction
        norm_now = norm_next
    return (solution, residual)


SLABS, GRPS = 16, 2
DEVICES = SLABS * GRPS
L0, L1 = 2, 5
ROWS = L0 * L1
N2, N3 = 64, 50
N0, N1 = 32, 10
HI = lax.Precision.HIGHEST
f32 = jnp.float32
JOINT = 19


def iota(shape, dim):
    return lax.broadcasted_iota(jnp.int32, shape, dim)


def mm(a, b):
    return jnp.dot(a, b, precision=HI, preferred_element_type=f32)


def mm_t(a, b):
    return lax.dot_general(
        a, b, (((1,), (1,)), ((), ())), precision=HI, preferred_element_type=f32
    )


def move(block, source, target):
    shift = (target - source) * 32 % 128
    return pltpu.roll(block, shift, 1) if shift else block


def merge(parts):
    lane = iota(parts[0].shape, 1)
    out = parts[-1]
    for q in range(len(parts) - 2, -1, -1):
        out = jnp.where(lane < 32 * (q + 1), parts[q], out)
    return out


def slot(r):
    return L0 * (r % L1) + r // L1


def banded_t(start_ref, band_ref, width, wrap):
    n = start_ref.shape[0]
    relative = (iota((width, n), 0) % wrap) - start_ref[...].reshape(1, n)
    out = jnp.zeros((width, n), f32)
    for offset in range(4):
        out = out + jnp.where(relative == offset, band_ref[offset : offset + 1, :], 0.0)
    return out


def expand(ref, p):
    first = 200 * p
    tile, off = first // 128, first % 128
    lane = iota((16, 128), 1)

    def window(t):
        low = ref[:, t * 128 : (t + 1) * 128]
        if off == 0:
            return low
        t1 = min(t + 1, 24)
        high = ref[:, t1 * 128 : (t1 + 1) * 128]
        return jnp.where(
            lane < 128 - off, pltpu.roll(low, 128 - off, 1), pltpu.roll(high, 128 - off, 1)
        )

    return window(tile), window(min(tile + 1, 24))


def table_to_mixed(field, kron_third, second_t, rows_ref, stack_ref):
    rows_ref[...] = mm(field, kron_third)
    for c in range(4):
        for j in range(3):
            parts = []
            for q in range(4):
                r = 4 * j + q
                if r < ROWS:
                    part = rows_ref[pl.ds(slot(r), 16, stride=16), :]
                    parts.append(move(part, c, q))
                else:
                    parts.append(jnp.zeros((16, 128), f32))
            stack_ref[16 * c : 16 * c + 16, 128 * j : 128 * j + 128] = merge(parts)
    return mm(second_t, stack_ref[...])


def mixed_to_table(value, kron_third, second, rows_ref, stack_ref):
    stack_ref[...] = mm(second, value)
    rows_ref[...] = jnp.zeros((256, 128), f32)
    for r in range(ROWS):
        j, q = r // 4, r % 4
        parts = [
            move(stack_ref[16 * c : 16 * c + 16, 128 * j : 128 * j + 128], q, c) for c in range(4)
        ]
        rows_ref[pl.ds(slot(r), 16, stride=16), :] = merge(parts)
    return mm_t(rows_ref[...], kron_third)


def inner_penalty(value):
    out = 12.0 * value
    row = iota((32, 128), 0)
    inside = iota((32, 128), 1) % 32
    tiles = []
    for j in range(3):
        tile = value[:, 128 * j : 128 * j + 128]
        total = 12.0 * tile
        for d, weight in ((1, -4.0), (2, 1.0)):
            total = total + weight * (
                jnp.where(row >= d, pltpu.roll(tile, d, 0), 0.0)
                + jnp.where(row < 32 - d, pltpu.roll(tile, 32 - d, 0), 0.0)
                + jnp.where(inside >= d, pltpu.roll(tile, d, 1), 0.0)
                + jnp.where(inside < 32 - d, pltpu.roll(tile, 128 - d, 1), 0.0)
            )
        tiles.append(total)
    return jnp.concatenate(tiles, axis=1)


def tile_of(value, j):
    return value[:, 128 * j : 128 * j + 128]


def put(ref, row, count, value):
    ref[pl.ds(row, 32, stride=count), :] = value


def lanes(values):
    lane = iota((8, 128), 1)
    out = jnp.zeros((8, 128), f32)
    for k, value in enumerate(values):
        out = jnp.where(lane == k, value, out)
    return out


def spread(ref, row, count, values):
    one = lanes(values)
    put(ref, row, count, jnp.concatenate([one] * 4, axis=0))


def totals(ref, row, count, number):
    summed = jnp.sum(ref[pl.ds(row, 32, stride=count), :], axis=0, keepdims=True)
    lane = iota((1, 128), 1)
    return [jnp.sum(jnp.where(lane == k, summed, 0.0)) for k in range(number)]


def pick(ref, k):
    lane = iota((1, 128), 1)
    return jnp.sum(jnp.where(lane == k, ref[0:1, :], 0.0))


def start_kernel(
    table_ref, weight_ref, start2_ref, band2_ref, start3_ref, band3_ref,
    send_ref, wide_ref, kron_ref, second_ref, second_t_ref,
    product_ref, packed_ref, field_ref, rows_ref, stack_ref,
):
    fourth_t = banded_t(start3_ref, band3_ref, 128, 32)
    pick_bin = (iota((256, N3), 0) % N3 == iota((256, N3), 1)) & (iota((256, N3), 0) < 4 * N3)
    kron = mm_t(jnp.where(pick_bin, 1.0, 0.0), fourth_t)
    same = iota((256, 128), 0) // N3 == iota((256, 128), 1) // 32
    kron = jnp.where(same, kron, 0.0)
    kron_ref[...] = kron
    third_t = banded_t(start2_ref, band2_ref, 32, 32)
    order = iota((N2, N2), 1)
    permute = (order % 16) * 4 + order // 16 == iota((N2, N2), 0)
    second_t = mm(third_t, jnp.where(permute, 1.0, 0.0))
    second_t_ref[...] = second_t
    second_ref[...] = second_t.T
    packed_ref[8:16, :] = jnp.zeros((8, N2 * N3), f32)
    product_ref[8:16, :] = jnp.zeros((8, N2 * N3), f32)
    for b in range(L1):
        weight = weight_ref[b]
        packed_ref[L0 * b : L0 * b + L0, :] = weight
        product_ref[L0 * b : L0 * b + L0, :] = weight * table_ref[b]
    for p in range(16):
        for source, target in ((packed_ref, wide_ref), (product_ref, field_ref)):
            low, high = expand(source, p)
            target[16 * p : 16 * p + 16, 0:128] = low
            target[16 * p : 16 * p + 16, 128:256] = high
    mixed = table_to_mixed(field_ref[...], kron, second_t, rows_ref, stack_ref)
    once = inner_penalty(mixed)
    twice = inner_penalty(once)
    for base, value in ((0, mixed), (3, once), (5, twice)):
        put(send_ref, base, 8, tile_of(value, 0))
        put(send_ref, base + 1, 8, tile_of(value, 1))
    lane = iota((32, 128), 1)
    put(send_ref, 2, 8, jnp.where(lane < 64, tile_of(mixed, 2), pltpu.roll(tile_of(once, 2), 64, 1)))
    put(send_ref, 7, 8, tile_of(twice, 2))


def pentadiagonal(n):
    gap = jnp.abs(iota((n, n), 0) - iota((n, n), 1))
    return jnp.where(gap == 0, 6.0, jnp.where(gap == 1, -4.0, jnp.where(gap == 2, 1.0, 0.0)))


def three_terms(value):
    high = value.astype(jnp.bfloat16)
    rest = value - high.astype(f32)
    middle = rest.astype(jnp.bfloat16)
    low = (rest - middle.astype(f32)).astype(jnp.bfloat16)
    return high, middle, low


def choose(pieces, selector):
    out = None
    for piece in pieces:
        term = jnp.dot(piece, selector, preferred_element_type=f32)
        out = term if out is None else out + term
    return out


def powers(basis_t, count):
    penalty_matrix = pentadiagonal(basis_t.shape[0])
    out = [basis_t]
    for _ in range(count - 1):
        out.append(mm(penalty_matrix, out[-1]))
    return out


def select_first():
    column = iota((N0, DEVICES * ROWS), 1)
    chosen = L0 * (column % 32 // GRPS) + column // 32 // L1 == iota((N0, DEVICES * ROWS), 0)
    return jnp.where(chosen, 1.0, 0.0).astype(jnp.bfloat16)


def gram_rows(start0_ref, band0_ref, start1_ref, band1_ref, rows0_ref, rows1_ref, count):
    total = DEVICES * ROWS
    powers0 = powers(banded_t(start0_ref, band0_ref, K0, K0), count)
    powers1 = powers(banded_t(start1_ref, band1_ref, K1, K1), count)
    row0 = iota((total, N0), 0)
    pick0 = L0 * (row0 % 32 // GRPS) + row0 // 32 // L1 == iota((total, N0), 1)
    row1 = iota((total, N1), 0)
    pick1 = L1 * (row1 % GRPS) + row1 // 32 % L1 == iota((total, N1), 1)
    wide0 = mm_t(jnp.where(pick0, 1.0, 0.0), powers0[0])
    wide1 = mm_t(jnp.where(pick1, 1.0, 0.0), powers1[0])
    for k in range(count):
        rows0_ref[:, 32 * k : 32 * k + 32] = mm(wide0, powers0[k])
        rows1_ref[:, 16 * k : 16 * k + N1] = mm(wide1, powers1[k])
    column = iota((N1, total), 1)
    chosen = L1 * (column % GRPS) + column // 32 % L1 == iota((N1, total), 0)
    select0, select1 = select_first(), jnp.where(chosen, 1.0, 0.0).astype(jnp.bfloat16)

    def block(base):
        block0 = rows0_ref[pl.ds(base, 32), :]
        block1 = rows1_ref[pl.ds(base, 32), :]
        g = [choose(three_terms(block0[:, 32 * k : 32 * k + 32]), select0) for k in range(count)]
        h = [choose(three_terms(block1[:, 16 * k : 16 * k + N1]), select1) for k in range(count)]
        return g, h

    return block


def gram_kernel(start0_ref, band0_ref, start1_ref, band1_ref, gram_ref, rows0_ref, rows1_ref):
    total = DEVICES * ROWS
    block = gram_rows(start0_ref, band0_ref, start1_ref, band1_ref, rows0_ref, rows1_ref, 2)

    @pl.loop(0, ROWS)
    def _(step):
        base = pl.multiple_of(step * 32, 32)
        g, h = block(base)
        gram_ref[pl.ds(base, 32), :] = g[0] * h[0]
        gram_ref[pl.ds(base + total, 32), :] = g[1] * h[0] + g[0] * h[1]


def high_kernel(
    after_ref, start0_ref, band0_ref, start1_ref, band1_ref, high_ref, rows0_ref, rows1_ref
):
    total = DEVICES * ROWS
    block = gram_rows(start0_ref, band0_ref, start1_ref, band1_ref, rows0_ref, rows1_ref, 4)

    @pl.loop(0, ROWS)
    def _(step):
        base = pl.multiple_of(step * 32, 32)
        g, h = block(base)
        high_ref[pl.ds(base, 32), :] = g[2] * h[0] + 2.0 * g[1] * h[1] + g[0] * h[2]
        high_ref[pl.ds(base + total, 32), :] = (
            g[3] * h[0] + 3.0 * (g[2] * h[1] + g[1] * h[2]) + g[0] * h[3]
        )


def lift_kernel(
    after_ref, group_ref, start0_ref, band0_ref, start1_ref, band1_ref, lift_ref, side_ref
):
    total = DEVICES * ROWS
    lifted = choose(three_terms(banded_t(start0_ref, band0_ref, K0, K0)), select_first())
    column = iota((K0, total), 1)
    owner = L1 * (column % GRPS) + column // 32 % L1
    for n in range(N1):
        lift_ref[K0 * n : K0 * n + K0, :] = jnp.where(owner == n, lifted, 0.0)
    group = group_ref[0]
    coef = iota((128, K1), 0) % 32 + 32 * group
    pick_coef = jnp.where(coef == iota((128, K1), 1), 1.0, 0.0)
    half = iota((N1, N1), 1) // L1
    wanted = L1 * jnp.where(half == group, 0, 1) + iota((N1, N1), 1) % L1
    reorder = jnp.where(iota((N1, N1), 0) == wanted, 1.0, 0.0)
    side_ref[...] = jnp.zeros((128, 256), f32)
    for k, value in enumerate(powers(banded_t(start1_ref, band1_ref, K1, K1), 3)):
        own = mm(pick_coef, value)
        halves = mm(own, reorder)
        for alpha in range(4):
            rows = slice(32 * alpha, 32 * alpha + 32)
            if k == 0:
                side_ref[rows, 10 * alpha : 10 * alpha + 10] = own[rows, :]
            for h in range(2):
                piece = halves[rows, L1 * h : L1 * h + L1]
                place = 40 * k + 20 * h + L1 * alpha
                if k > 0:
                    side_ref[rows, place : place + L1] = piece
                if k < 2:
                    side_ref[rows, 128 + place : 128 + place + L1] = piece


def unpack(ref, row, count, r, source, target):
    return move(ref[pl.ds(row, 32, stride=count), :], source, target)


def first_column_kernel(recv_ref, gram_ref, send_ref, fields_ref, images_ref):
    total = DEVICES * ROWS
    zero = jnp.zeros((32, 128), f32)
    for r in range(ROWS):
        j, q = r // 4, r % 4
        where0 = (j, q) if j < 2 else (2, q)
        where1 = (3 + j, q) if j < 2 else (2, q + 2)
        where2 = (5 + j, q) if j < 2 else (7, q)
        parts = [
            unpack(recv_ref, place[0], 8, r, place[1], k)
            for k, place in enumerate((where0, where1, where2))
        ]
        fields_ref[32 * r : 32 * r + 32, :] = merge(parts + [zero])
    fields = fields_ref[...]
    product = mm(gram_ref[...], fields)
    lane = iota((total, 128), 1)
    images = product[:total] + jnp.where(
        (lane >= 32) & (lane < 64), pltpu.roll(product[total:], 32, 1), 0.0
    )
    images_ref[...] = images
    norm = jnp.sum(jnp.where(lane < 32, fields * images, 0.0))
    bend = jnp.sum(jnp.where(lane < 32, fields * pltpu.roll(images, 96, 1), 0.0))
    send_rows(send_ref, images_ref)
    spread(send_ref, 3, 4, (norm, bend))


def send_rows(send_ref, value_ref):
    for j in range(3):
        parts = []
        for q in range(4):
            r = 4 * j + q
            if r < ROWS:
                parts.append(move(value_ref[32 * r : 32 * r + 32, :], 0, q))
            else:
                parts.append(jnp.zeros((32, 128), f32))
        put(send_ref, j, 4, merge(parts))


def received_rows(recv_ref):
    return jnp.concatenate([recv_ref[pl.ds(j, 32, stride=4), :] for j in range(3)], axis=1)


def first_row_kernel(
    recv_ref, wide_ref, kron_ref, second_ref, second_t_ref,
    send_ref, scalar_ref, rows_ref, stack_ref,
):
    norm, bend = totals(recv_ref, 3, 4, 2)
    scalar_ref[...] = lanes((norm, bend))
    kron = kron_ref[...]
    field = mixed_to_table(received_rows(recv_ref), kron, second_ref[...], rows_ref, stack_ref)
    weighted = wide_ref[...] * field
    energy = jnp.sum(field * weighted)
    mixed = table_to_mixed(weighted, kron, second_t_ref[...], rows_ref, stack_ref)
    once = inner_penalty(mixed)
    for base, value in ((0, mixed), (3, once)):
        put(send_ref, base, 8, tile_of(value, 0))
        put(send_ref, base + 1, 8, tile_of(value, 1))
    lane = iota((32, 128), 1)
    put(send_ref, 2, 8, jnp.where(lane < 64, tile_of(mixed, 2), pltpu.roll(tile_of(once, 2), 64, 1)))
    spread(send_ref, 5, 8, (energy,))
    for row in (6, 7):
        put(send_ref, row, 8, jnp.zeros((32, 128), f32))


def second_column_kernel(
    recv_ref, gram_ref, fields_ref, images_ref, scalar_ref,
    send_ref, blend_ref, out_scalar_ref, next_ref, image_ref,
):
    zero = jnp.zeros((32, 128), f32)
    for r in range(ROWS):
        j, q = r // 4, r % 4
        where0 = (j, q) if j < 2 else (2, q)
        where1 = (3 + j, q) if j < 2 else (2, q + 2)
        parts = [
            unpack(recv_ref, place[0], 8, r, place[1], k) for k, place in enumerate((where0, where1))
        ]
        next_ref[32 * r : 32 * r + 32, :] = merge(parts + [zero])
    (energy,) = totals(recv_ref, 5, 8, 1)
    norm, bend = pick(scalar_ref, 0), pick(scalar_ref, 1)
    step = norm / (energy + 0.1 * bend)
    out_scalar_ref[...] = lanes((norm, step))
    fields, images, following = fields_ref[...], images_ref[...], next_ref[...]
    image = mm(gram_ref[0 : DEVICES * ROWS, :], following)
    image_ref[...] = images - step * (image + 0.1 * pltpu.roll(images, 96, 1))
    send_rows(send_ref, image_ref)
    put(send_ref, 3, 4, zero)
    lane = iota(fields.shape, 1)
    reduced = fields - step * (following + 0.1 * pltpu.roll(fields, 96, 1))
    blend_ref[...] = jnp.where(lane < 64, reduced, pltpu.roll(fields, 64, 1))


def coefficient_penalty(value):
    k = iota(value.shape, 0) % K0
    count = value.shape[0]
    total = 6.0 * value
    for d, weight in ((1, -4.0), (2, 1.0)):
        total = total + weight * (
            jnp.where(k >= d, pltpu.roll(value, d, 0), 0.0)
            + jnp.where(k < K0 - d, pltpu.roll(value, count - d, 0), 0.0)
        )
    return total


def send_blocks(send_ref, count, base, value_ref, block):
    for j in range(10):
        parts = []
        for q in range(4):
            m = 4 * j + q
            alpha, n = m // 10, m % 10
            parts.append(move(value_ref[pl.ds(K0 * n + alpha, 16, stride=4), :], block, q))
        merged = merge(parts)
        for g in range(GRPS):
            send_ref[pl.ds(g * count + base + j, 16, stride=2 * count), :] = merged


def send_halves(send_ref, count, base, value_ref, block):
    for g in range(GRPS):
        for j in range(5):
            parts = []
            for q in range(4):
                alpha, b = divmod(4 * j + q, L1)
                row = K0 * (L1 * g + b) + alpha
                parts.append(move(value_ref[pl.ds(row, 16, stride=4), :], block, q))
            send_ref[pl.ds(g * count + base + j, 16, stride=2 * count), :] = merge(parts)


def middle_kernel(blend_ref, gram_ref, high_ref, lift_ref, scalar_ref, send_ref, keep_ref, sums_ref):
    total = DEVICES * ROWS
    step = pick(scalar_ref, 1)
    small = 0.1 * step
    blend = blend_ref[...]
    lane = iota(blend.shape, 1)
    product, higher = mm(gram_ref[...], blend), mm(high_ref[...], blend)
    g0, g1, g2, g3 = product[:total], product[total:], higher[:total], higher[total:]
    head = g0 - small * pltpu.roll(g1, 64, 1)
    tail = g1 - small * pltpu.roll(g2, 64, 1)
    end = g2 - small * pltpu.roll(g3, 64, 1)
    scaled = pltpu.roll(blend, 64, 1)
    low = lane < 32
    norm = jnp.sum(jnp.where(low, blend * head - small * scaled * tail, 0.0))
    head_p = tail + pltpu.roll(head, 96, 1)
    tail_p = end + pltpu.roll(tail, 96, 1)
    bend = jnp.sum(jnp.where(low, blend * head_p - small * scaled * tail_p, 0.0))
    sums_ref[...] = lanes((norm, bend))
    lifted = mm(lift_ref[...], blend)
    once = coefficient_penalty(lifted)
    twice = coefficient_penalty(once)
    h_a = lifted - small * pltpu.roll(once, 64, 1)
    y_1 = once + pltpu.roll(lifted, 96, 1)
    x_a = once + pltpu.roll(lifted, 96, 1) - small * (
        pltpu.roll(twice, 64, 1) + pltpu.roll(once, 32, 1)
    )
    h_0 = pltpu.roll(lifted, 64, 1)
    wide = iota(lifted.shape, 1)
    keep = jnp.where(
        wide < 32, h_0, jnp.where(wide < 64, pltpu.roll(h_a, 32, 1), jnp.where(wide < 96, y_1, pltpu.roll(x_a, 96, 1)))
    )
    keep_ref[...] = keep
    for block in range(3):
        send_halves(send_ref, JOINT, 4 + 5 * block, keep_ref, block)


def second_row_kernel(
    early_ref, recv_ref, sums_ref, wide_ref, kron_ref, second_ref, second_t_ref,
    send_ref, rows_ref, stack_ref,
):
    kron = kron_ref[...]
    field = mixed_to_table(received_rows(recv_ref), kron, second_ref[...], rows_ref, stack_ref)
    weighted = wide_ref[...] * field
    energy = jnp.sum(field * weighted)
    mixed = table_to_mixed(weighted, kron, second_t_ref[...], rows_ref, stack_ref)
    for j in range(3):
        put(send_ref, j, JOINT, tile_of(mixed, j))
    spread(send_ref, 3, JOINT, (energy, pick(sums_ref, 0), pick(sums_ref, 1)))


def third_column_kernel(
    recv_ref, lift_ref, keep_ref, scalar_ref, send_ref, out_scalar_ref, last_ref, mixed_ref
):
    zero = jnp.zeros((32, 128), f32)
    for r in range(ROWS):
        j, q = r // 4, r % 4
        last_ref[32 * r : 32 * r + 32, :] = unpack(recv_ref, j, JOINT, r, q, 0)
    energy, norm_next, bend = totals(recv_ref, 3, JOINT, 3)
    norm, step = pick(scalar_ref, 0), pick(scalar_ref, 1)
    ratio = norm_next / norm
    curve = energy + 0.1 * bend - ratio * norm_next / step
    step_next = norm_next / curve
    out_scalar_ref[...] = lanes((norm, step, ratio, step_next))
    lifted = mm(lift_ref[...], last_ref[...])
    keep = keep_ref[...]
    h_a, x_a = pltpu.roll(keep, 96, 1), pltpu.roll(keep, 32, 1)
    mixed_ref[...] = (
        h_a - step_next * (lifted + 0.1 * x_a) - (step_next * ratio / step) * (keep - h_a)
    )
    send_blocks(send_ref, 10, 0, mixed_ref, 0)


def gather_blocks(ref, count, base, rows, out_ref, first):
    for j in range(rows):
        taken = [ref[pl.ds(rho * count + base + j, 8, stride=4 * count), :] for rho in range(4)]
        for q in range(4):
            m = first + 4 * j + q
            merged = merge([move(taken[rho], q, rho) for rho in range(4)])
            out_ref[pl.ds(m // 8 * 64 + m % 8, 8, stride=8), :] = merged


def final_kernel(
    own_ref, partner_ref, late_ref, side_ref, scalar_ref, solution_ref, residual_ref, early, late
):
    for block in range(3):
        for h, ref in enumerate((own_ref, partner_ref)):
            gather_blocks(ref, JOINT, 4 + 5 * block, 5, early, 40 * block + 20 * h)
    gather_blocks(late_ref, 10, 0, 10, late, 0)
    step, ratio, step_next = pick(scalar_ref, 1), pick(scalar_ref, 2), pick(scalar_ref, 3)
    small = 0.1 * step
    side = side_ref[...]
    for tile in range(8):
        def take(ref, block):
            return jnp.concatenate(
                [ref[pl.ds((5 * block + t) * 64 + 8 * tile, 8), :] for t in range(5)], axis=0
            )
        h_0, h_a, y_1, h_r = take(early, 0), take(early, 1), take(early, 2), take(late, 0)
        right = jnp.concatenate(
            [(step + step_next * ratio) * h_0 + step_next * h_a, (-step_next * small) * h_0], axis=0
        )
        columns = slice(128 * tile, 128 * tile + 128)
        solution_ref[:, :, columns] = mm(side[:, 128:208], right).reshape(4, 32, 128)
        right = jnp.concatenate(
            [
                h_r,
                (-small * (1.0 + step_next * ratio / step)) * h_0
                - (0.1 * step_next) * (h_a - small * y_1),
                (0.1 * step_next * small) * h_0,
            ],
            axis=0,
        )
        residual_ref[:, :, columns] = mm(side[:, 0:120], right).reshape(4, 32, 128)


def call(kernel, outputs, scratch, *operands, aliases={}):
    specs = [pl.BlockSpec(memory_space=pltpu.VMEM)] * len(operands)
    if kernel in (high_kernel, lift_kernel):
        specs[0] = pl.BlockSpec(memory_space=pl.ANY)
    if kernel is lift_kernel:
        specs[1] = pl.BlockSpec(memory_space=pltpu.SMEM)
    return pl.pallas_call(
        kernel,
        out_shape=[jax.ShapeDtypeStruct(shape, f32) for shape in outputs],
        in_specs=specs,
        out_specs=[pl.BlockSpec(memory_space=pltpu.VMEM)] * len(outputs),
        scratch_shapes=[pltpu.VMEM(shape, f32) for shape in scratch],
        input_output_aliases=aliases,
        compiler_params=pltpu.CompilerParams(vmem_limit_bytes=32 * 2**20),
    )(*operands)


def exchange(buffer):
    count = buffer.shape[0] // DEVICES
    tiled = count == 4 or count % 8 == 0
    shape = (DEVICES, count, 128) if tiled else (DEVICES, 1, count * 128)
    moved = lax.all_to_all(buffer.reshape(shape), ("slab", "grp"), 0, 0, tiled=True)
    return moved.reshape(buffer.shape)


def fast_program(
    photon_table,
    bin_weights,
    first_start,
    first_band,
    second_start,
    second_band,
    third_start,
    third_band,
    fourth_start,
    fourth_band,
):
    total = DEVICES * ROWS
    work = [(256, 128), (64, 384)]
    outer = (first_start, first_band.T, second_start, second_band.T)
    send, wide, kron, second, second_t = call(
        start_kernel,
        [(256, 128), (256, 256), (256, 128), (64, 32), (32, 64)],
        [(16, N2 * N3), (16, N2 * N3), (256, 256)] + work,
        photon_table.transpose(1, 0, 2),
        bin_weights.transpose(1, 0, 2),
        third_start, third_band.T, fourth_start, fourth_band.T,
    )
    recv = exchange(send)
    (gram,) = call(gram_kernel, [(2 * total, total)], [(total, 64), (total, 32)], *outer)
    send, fields, images = call(
        first_column_kernel, [(128, 128), (total, 128), (total, 128)], [], recv, gram
    )
    recv = exchange(send)
    (high,) = call(
        high_kernel, [(2 * total, total)], [(total, 128), (total, 64)], images, *outer
    )
    send, scalars = call(
        first_row_kernel, [(256, 128), (8, 128)], work, recv, wide, kron, second, second_t
    )
    recv = exchange(send)
    group = lax.axis_index("grp").reshape(1)
    lift, side = call(
        lift_kernel, [(K0 * N1, total), (128, 256)], [], scalars, group, *outer
    )
    send, blend, scalars = call(
        second_column_kernel,
        [(128, 128), (total, 128), (8, 128)],
        [(total, 128), (total, 128)],
        recv, gram, fields, images, scalars,
    )
    recv = exchange(send)
    send, keep, sums = call(
        middle_kernel,
        [(DEVICES * JOINT, 128), (K0 * N1, 128), (8, 128)],
        [],
        blend, gram, high, lift, scalars,
    )
    (send,) = call(
        second_row_kernel,
        [(DEVICES * JOINT, 128)],
        work,
        send, recv, sums, wide, kron, second, second_t,
        aliases={0: 0},
    )
    recv = exchange(send)
    partner = lax.ppermute(recv, "grp", [(0, 1), (1, 0)])
    send, scalars = call(
        third_column_kernel,
        [(DEVICES * 10, 128), (8, 128)],
        [(total, 128), (K0 * N1, 128)],
        recv, lift, keep, scalars,
    )
    late = exchange(send)
    return call(
        final_kernel,
        [(4, 32, 1024), (4, 32, 1024)],
        [(960, 128), (320, 128)],
        recv, partner, late, side, scalars,
    )


def fits(mesh):
    return (mesh.shape["slab"], mesh.shape["grp"]) == (SLABS, GRPS)


def solution(mesh):
    placed = (
        P("slab", "grp", None),
        P("slab", "grp", None),
        P(),
        P(),
        P(),
        P(),
        P(),
        P(),
        P(),
        P(),
    )
    return jax.shard_map(
        fast_program if fits(mesh) else per_device,
        mesh=mesh,
        in_specs=placed,
        out_specs=(P("slab", "grp", None), P("slab", "grp", None)),
        check_vma=False,
    )
```

```python
import jax
import jax.numpy as jnp
from jax import lax
from jax.experimental import pallas as pl
from jax.experimental.pallas import tpu as pltpu
from jax.sharding import PartitionSpec as P

K0 = 64
K1 = 64
K2 = 32
K3 = 32
ITERS = 2


highest = lax.Precision.HIGHEST
smoothing = 0.1
stencil_weights = (1.0, -4.0, 6.0, -4.0, 1.0)


def with_halo(value, sides, width):
    for axis, dim in sides:
        count, length = (lax.axis_size(axis), value.shape[dim])
        up = [(i, (i + 1) % count) for i in range(count - 1)]
        down = [(j, i) for i, j in up]
        last = lax.slice_in_dim(value, length - width, length, axis=dim)
        initial = lax.slice_in_dim(value, 0, width, axis=dim)
        before = lax.ppermute(last, axis, up)
        after = lax.ppermute(initial, axis, down)
        value = jnp.concatenate([before, value, after], axis=dim)
    return value


def dense_basis(starts, values, coef_count):
    relative = jnp.arange(coef_count, dtype=jnp.int32)[None, :] - starts[:, None]
    matrix = jnp.zeros((starts.shape[0], coef_count), jnp.float32)
    for offset in range(4):
        matrix = matrix + jnp.where(relative == offset, values[:, offset : offset + 1], 0.0)
    return matrix


def five_point(source, along, extent):
    running = stencil_weights[0] * lax.slice_in_dim(source, 0, extent, axis=along)
    for offset in range(1, 5):
        running = running + stencil_weights[offset] * lax.slice_in_dim(
            source, offset, offset + extent, axis=along
        )
    return running


def local_stencil(tensor, along):
    widths = [(0, 0)] * tensor.ndim
    widths[along] = (2, 2)
    return five_point(jnp.pad(tensor, widths), along, tensor.shape[along])


def inner_forward(tensor, third_basis, fourth_basis):
    leading, middle = (tensor.shape[0], tensor.shape[1])
    blocked = tensor.reshape(leading, middle, third_basis.shape[1], fourth_basis.shape[1])
    blocked = jnp.einsum("abcd,nd->abcn", blocked, fourth_basis, precision=highest)
    blocked = jnp.einsum("abcn,mc->abmn", blocked, third_basis, precision=highest)
    return blocked.reshape(leading, middle, third_basis.shape[0] * fourth_basis.shape[0])


def inner_adjoint(tensor, third_basis, fourth_basis):
    leading, middle = (tensor.shape[0], tensor.shape[1])
    blocked = tensor.reshape(leading, middle, third_basis.shape[0], fourth_basis.shape[0])
    blocked = jnp.einsum("abmn,mc->abcn", blocked, third_basis, precision=highest)
    blocked = jnp.einsum("abcn,nd->abcd", blocked, fourth_basis, precision=highest)
    return blocked.reshape(leading, middle, third_basis.shape[1] * fourth_basis.shape[1])


def lead_product(tensor, matrix):
    combined = jnp.einsum(
        "ka,ain->kin",
        matrix,
        lax.all_to_all(tensor, "slab", split_axis=2, concat_axis=0, tiled=True),
        precision=highest,
    )
    return lax.all_to_all(combined, "slab", split_axis=0, concat_axis=2, tiled=True)


def second_product(tensor, matrix):
    return jnp.einsum(
        "lp,apn->aln", matrix, lax.all_gather(tensor, "grp", axis=1, tiled=True), precision=highest
    )


def penalty(coeffs):
    leading, middle = (coeffs.shape[0], coeffs.shape[1])
    padded = with_halo(coeffs, (("slab", 0), ("grp", 1)), 2)
    along_lead = five_point(padded[:, 2 : 2 + middle], 0, leading)
    along_rows = five_point(padded[2 : 2 + leading, :], 1, middle)
    blocked = coeffs.reshape(leading, middle, K2, K3)
    inner_part = local_stencil(blocked, 2) + local_stencil(blocked, 3)
    return along_lead + along_rows + inner_part.reshape(leading, middle, K2 * K3)


def squared_total(vector):
    return lax.psum(jnp.sum(vector * vector), ("slab", "grp"))


def per_device(
    photon_table,
    bin_weights,
    first_start,
    first_band,
    second_start,
    second_band,
    third_start,
    third_band,
    fourth_start,
    fourth_band,
):
    first_basis = dense_basis(first_start, first_band, K0)
    second_basis = dense_basis(second_start, second_band, K1)
    third_basis = dense_basis(third_start, third_band, K2)
    fourth_basis = dense_basis(fourth_start, fourth_band, K3)
    first_back = first_basis.T
    group_index = lax.axis_index("grp")
    row_count = photon_table.shape[1]
    coef_rows = K1 // lax.axis_size("grp")
    near_rows = lax.dynamic_slice_in_dim(second_basis, group_index * row_count, row_count, 0)
    back_rows = lax.dynamic_slice_in_dim(second_basis.T, group_index * coef_rows, coef_rows, 0)

    def adjoint(table):
        tensor = lead_product(table, first_back)
        tensor = second_product(tensor, back_rows)
        return inner_adjoint(tensor, third_basis, fourth_basis)

    right_side = adjoint(bin_weights * photon_table)
    solution = jnp.zeros_like(right_side)
    residual = right_side
    direction = right_side
    norm_now = squared_total(residual)
    for sweep in range(ITERS):
        forward_tensor = inner_forward(direction, third_basis, fourth_basis)
        forward_tensor = second_product(forward_tensor, near_rows)
        mapped = adjoint(
            bin_weights * lead_product(forward_tensor, first_basis)
        ) + smoothing * penalty(direction)
        curve_total = lax.psum(jnp.sum(direction * mapped), ("slab", "grp"))
        step_size = norm_now / curve_total
        solution = solution + step_size * direction
        residual = residual - step_size * mapped
        norm_next = squared_total(residual)
        direction = residual + norm_next / norm_now * direction
        norm_now = norm_next
    return (solution, residual)


SLABS, GRPS = 16, 2
DEVICES = SLABS * GRPS
L0, L1 = 2, 5
ROWS = L0 * L1
N2, N3 = 64, 50
N0, N1 = 32, 10
HI = lax.Precision.HIGHEST
f32 = jnp.float32
JOINT = 19
LARGE = 60


def iota(shape, dim):
    return lax.broadcasted_iota(jnp.int32, shape, dim)


def mm(a, b):
    return jnp.dot(a, b, precision=HI, preferred_element_type=f32)


def mm_t(a, b):
    return lax.dot_general(
        a, b, (((1,), (1,)), ((), ())), precision=HI, preferred_element_type=f32
    )


def split(value):
    high = value.astype(jnp.bfloat16)
    return high, (value - high.astype(f32)).astype(jnp.bfloat16)


def product(a, b, transposed=False):
    dims = (((1,), (1 if transposed else 0,)), ((), ()))

    def one(x, y):
        return lax.dot_general(x, y, dims, preferred_element_type=f32)

    return one(a[0], b[0]) + (one(a[0], b[1]) + one(a[1], b[0]))


def load(pair):
    return pair[0][...], pair[1][...]


def move(block, source, target):
    shift = (target - source) * 32 % 128
    return pltpu.roll(block, shift, 1) if shift else block


def merge(parts):
    lane = iota(parts[0].shape, 1)
    out = parts[-1]
    for q in range(len(parts) - 2, -1, -1):
        out = jnp.where(lane < 32 * (q + 1), parts[q], out)
    return out


def slot(r):
    return L0 * (r % L1) + r // L1


def banded_t(start_ref, band_ref, width, wrap):
    n = start_ref.shape[0]
    relative = (iota((width, n), 0) % wrap) - start_ref[...].reshape(1, n)
    out = jnp.zeros((width, n), f32)
    for offset in range(4):
        out = out + jnp.where(relative == offset, band_ref[offset : offset + 1, :], 0.0)
    return out


def expand(ref, p):
    first = 200 * p
    tile, off = first // 128, first % 128
    lane = iota((16, 128), 1)

    def window(t):
        low = ref[:, t * 128 : (t + 1) * 128]
        if off == 0:
            return low
        t1 = min(t + 1, 24)
        high = ref[:, t1 * 128 : (t1 + 1) * 128]
        return jnp.where(
            lane < 128 - off, pltpu.roll(low, 128 - off, 1), pltpu.roll(high, 128 - off, 1)
        )

    return window(tile), window(min(tile + 1, 24))


def table_to_mixed(field, kron_third, second_t, rows_ref, stack_ref):
    rows_ref[...] = product(split(field), kron_third)
    for c in range(4):
        for j in range(3):
            parts = []
            for q in range(4):
                r = 4 * j + q
                if r < ROWS:
                    part = rows_ref[pl.ds(slot(r), 16, stride=16), :]
                    parts.append(move(part, c, q))
                else:
                    parts.append(jnp.zeros((16, 128), f32))
            stack_ref[16 * c : 16 * c + 16, 128 * j : 128 * j + 128] = merge(parts)
    return product(second_t, split(stack_ref[...]))


def mixed_to_table(value, kron_third, second, rows_ref, stack_ref):
    stack_ref[...] = product(second, split(value))
    rows_ref[...] = jnp.zeros((256, 128), f32)
    for r in range(ROWS):
        j, q = r // 4, r % 4
        parts = [
            move(stack_ref[16 * c : 16 * c + 16, 128 * j : 128 * j + 128], q, c) for c in range(4)
        ]
        rows_ref[pl.ds(slot(r), 16, stride=16), :] = merge(parts)
    return product(split(rows_ref[...]), kron_third, True)


def inner_penalty(value):
    out = 12.0 * value
    row = iota((32, 128), 0)
    inside = iota((32, 128), 1) % 32
    tiles = []
    for j in range(3):
        tile = value[:, 128 * j : 128 * j + 128]
        total = 12.0 * tile
        for d, weight in ((1, -4.0), (2, 1.0)):
            total = total + weight * (
                jnp.where(row >= d, pltpu.roll(tile, d, 0), 0.0)
                + jnp.where(row < 32 - d, pltpu.roll(tile, 32 - d, 0), 0.0)
                + jnp.where(inside >= d, pltpu.roll(tile, d, 1), 0.0)
                + jnp.where(inside < 32 - d, pltpu.roll(tile, 128 - d, 1), 0.0)
            )
        tiles.append(total)
    return jnp.concatenate(tiles, axis=1)


def tile_of(value, j):
    return value[:, 128 * j : 128 * j + 128]


def put(ref, row, count, value):
    ref[pl.ds(row, 32, stride=count), :] = value


def lanes(values):
    lane = iota((8, 128), 1)
    out = jnp.zeros((8, 128), f32)
    for k, value in enumerate(values):
        out = jnp.where(lane == k, value, out)
    return out


def spread(ref, row, count, values):
    one = lanes(values)
    put(ref, row, count, jnp.concatenate([one] * 4, axis=0))


def totals(ref, row, count, number):
    summed = jnp.sum(ref[pl.ds(row, 32, stride=count), :], axis=0, keepdims=True)
    lane = iota((1, 128), 1)
    return [jnp.sum(jnp.where(lane == k, summed, 0.0)) for k in range(number)]


def pick(ref, k):
    lane = iota((1, 128), 1)
    return jnp.sum(jnp.where(lane == k, ref[0:1, :], 0.0))


def constants(ref):
    kron = ref[0:256, :], ref[256:512, :]
    second = ref[512:576, 0:32], ref[576:640, 0:32]
    return kron, second, (ref[640:672, 0:64], ref[672:704, 0:64])


def start_kernel(
    table_hbm, weight_hbm, start2_hbm, band2_hbm, start3_hbm, band3_hbm,
    send_ref, wide_ref, inner_ref,
    table_ref, weight_ref, start2_ref, band2_ref, start3_ref, band3_ref, sems,
    product_ref, packed_ref, field_ref, rows_ref, stack_ref,
):
    copies = [
        pltpu.make_async_copy(source, target, sems.at[k])
        for k, (source, target) in enumerate(
            (
                (start3_hbm, start3_ref),
                (band3_hbm, band3_ref),
                (start2_hbm, start2_ref),
                (band2_hbm, band2_ref),
                (weight_hbm, weight_ref),
                (table_hbm, table_ref),
            )
        )
    ]
    for copy in copies:
        copy.start()
    copies[0].wait()
    copies[1].wait()
    pick_bin = (iota((256, N3), 0) % N3 == iota((256, N3), 1)) & (iota((256, N3), 0) < 4 * N3)
    same = iota((256, 128), 0) // N3 == iota((256, 128), 1) // 32
    picker = jnp.where(pick_bin, 1.0, 0.0).astype(jnp.bfloat16)
    for k, term in enumerate(split(banded_t(start3_ref, band3_ref, 128, 32))):
        spread_out = lax.dot_general(
            picker, term, (((1,), (1,)), ((), ())), preferred_element_type=f32
        )
        inner_ref[256 * k : 256 * k + 256, :] = jnp.where(same, spread_out, 0.0).astype(jnp.bfloat16)
    copies[2].wait()
    copies[3].wait()
    order, other = iota((N2, N2), 1), iota((N2, N2), 0)
    permute = jnp.where((order % 16) * 4 + order // 16 == other, 1.0, 0.0).astype(jnp.bfloat16)
    back = jnp.where((other % 16) * 4 + other // 16 == order, 1.0, 0.0).astype(jnp.bfloat16)
    for k, term in enumerate(split(banded_t(start2_ref, band2_ref, 32, 32))):
        value = jnp.dot(term, permute, preferred_element_type=f32)
        inner_ref[640 + 32 * k : 672 + 32 * k, 0:64] = value.astype(jnp.bfloat16)
        value = lax.dot_general(back, term, (((1,), (1,)), ((), ())), preferred_element_type=f32)
        inner_ref[512 + 64 * k : 576 + 64 * k, 0:32] = value.astype(jnp.bfloat16)
    kron, _, turned = constants(inner_ref)
    copies[4].wait()
    copies[5].wait()
    packed_ref[8:16, :] = jnp.zeros((8, N2 * N3), f32)
    product_ref[8:16, :] = jnp.zeros((8, N2 * N3), f32)
    for b in range(L1):
        weight = weight_ref[b]
        packed_ref[L0 * b : L0 * b + L0, :] = weight
        product_ref[L0 * b : L0 * b + L0, :] = weight * table_ref[b]
    for p in range(16):
        for source, target in ((packed_ref, wide_ref), (product_ref, field_ref)):
            low, high = expand(source, p)
            target[16 * p : 16 * p + 16, 0:128] = low
            target[16 * p : 16 * p + 16, 128:256] = high
    mixed = table_to_mixed(field_ref[...], kron, turned, rows_ref, stack_ref)
    once = inner_penalty(mixed)
    twice = inner_penalty(once)
    for base, value in ((0, mixed), (3, once), (5, twice)):
        put(send_ref, base, 8, tile_of(value, 0))
        put(send_ref, base + 1, 8, tile_of(value, 1))
    lane = iota((32, 128), 1)
    put(send_ref, 2, 8, jnp.where(lane < 64, tile_of(mixed, 2), pltpu.roll(tile_of(once, 2), 64, 1)))
    put(send_ref, 7, 8, tile_of(twice, 2))


def pentadiagonal(n):
    gap = jnp.abs(iota((n, n), 0) - iota((n, n), 1))
    return jnp.where(gap == 0, 6.0, jnp.where(gap == 1, -4.0, jnp.where(gap == 2, 1.0, 0.0)))


def three_terms(value):
    high = value.astype(jnp.bfloat16)
    rest = value - high.astype(f32)
    middle = rest.astype(jnp.bfloat16)
    low = (rest - middle.astype(f32)).astype(jnp.bfloat16)
    return high, middle, low


def choose(pieces, selector):
    out = None
    for piece in pieces:
        term = jnp.dot(piece, selector, preferred_element_type=f32)
        out = term if out is None else out + term
    return out


def powers(basis_t, count):
    penalty_matrix = pentadiagonal(basis_t.shape[0])
    out = [basis_t]
    for _ in range(count - 1):
        out.append(mm(penalty_matrix, out[-1]))
    return out


def select_first():
    column = iota((N0, DEVICES * ROWS), 1)
    chosen = L0 * (column % 32 // GRPS) + column // 32 // L1 == iota((N0, DEVICES * ROWS), 0)
    return jnp.where(chosen, 1.0, 0.0).astype(jnp.bfloat16)


def gram_rows(start0_ref, band0_ref, start1_ref, band1_ref, rows0_ref, rows1_ref, count):
    total = DEVICES * ROWS
    powers0 = powers(banded_t(start0_ref, band0_ref, K0, K0), count)
    powers1 = powers(banded_t(start1_ref, band1_ref, K1, K1), count)
    row0 = iota((total, N0), 0)
    pick0 = L0 * (row0 % 32 // GRPS) + row0 // 32 // L1 == iota((total, N0), 1)
    row1 = iota((total, N1), 0)
    pick1 = L1 * (row1 % GRPS) + row1 // 32 % L1 == iota((total, N1), 1)
    wide0 = mm_t(jnp.where(pick0, 1.0, 0.0), powers0[0])
    wide1 = mm_t(jnp.where(pick1, 1.0, 0.0), powers1[0])
    for k in range(count):
        rows0_ref[:, 32 * k : 32 * k + 32] = mm(wide0, powers0[k])
        rows1_ref[:, 16 * k : 16 * k + N1] = mm(wide1, powers1[k])
    column = iota((N1, total), 1)
    chosen = L1 * (column % GRPS) + column // 32 % L1 == iota((N1, total), 0)
    select0, select1 = select_first(), jnp.where(chosen, 1.0, 0.0).astype(jnp.bfloat16)

    def block(base):
        block0 = rows0_ref[pl.ds(base, 32), :]
        block1 = rows1_ref[pl.ds(base, 32), :]
        g = [choose(three_terms(block0[:, 32 * k : 32 * k + 32]), select0) for k in range(count)]
        h = [choose(three_terms(block1[:, 16 * k : 16 * k + N1]), select1) for k in range(count)]
        return g, h

    return block


def store_split(high_ref, low_ref, rows, value):
    high, low = split(value)
    high_ref[rows, :] = high
    low_ref[rows, :] = low


def gram_kernel(
    start0_ref, band0_ref, start1_ref, band1_ref, gram_h_ref, gram_l_ref, rows0_ref, rows1_ref
):
    total = DEVICES * ROWS
    block = gram_rows(start0_ref, band0_ref, start1_ref, band1_ref, rows0_ref, rows1_ref, 2)

    @pl.loop(0, ROWS)
    def _(step):
        base = pl.multiple_of(step * 32, 32)
        g, h = block(base)
        store_split(gram_h_ref, gram_l_ref, pl.ds(base, 32), g[0] * h[0])
        store_split(
            gram_h_ref, gram_l_ref, pl.ds(base + total, 32), g[1] * h[0] + g[0] * h[1]
        )


def high_kernel(
    after_ref, start0_ref, band0_ref, start1_ref, band1_ref, high_h_ref, high_l_ref, token_ref,
    rows0_ref, rows1_ref,
):
    token_ref[...] = after_ref[...]
    total = DEVICES * ROWS
    block = gram_rows(start0_ref, band0_ref, start1_ref, band1_ref, rows0_ref, rows1_ref, 4)

    @pl.loop(0, ROWS)
    def _(step):
        base = pl.multiple_of(step * 32, 32)
        g, h = block(base)
        squared = g[2] * h[0] + 2.0 * g[1] * h[1] + g[0] * h[2]
        cubed = g[3] * h[0] + 3.0 * (g[2] * h[1] + g[1] * h[2]) + g[0] * h[3]
        store_split(high_h_ref, high_l_ref, pl.ds(base, 32), squared)
        store_split(high_h_ref, high_l_ref, pl.ds(base + total, 32), cubed)


def lift_kernel(
    after_ref, group_ref, start0_ref, band0_ref, start1_ref, band1_ref,
    lift_h_ref, lift_l_ref, side_ref, token_ref,
):
    token_ref[...] = after_ref[...]
    total = DEVICES * ROWS
    lifted = choose(three_terms(banded_t(start0_ref, band0_ref, K0, K0)), select_first())
    column = iota((K0, total), 1)
    owner = L1 * (column % GRPS) + column // 32 % L1
    for n in range(N1):
        rows = slice(K0 * n, K0 * n + K0)
        store_split(lift_h_ref, lift_l_ref, rows, jnp.where(owner == n, lifted, 0.0))
    group = group_ref[0]
    coef = iota((128, K1), 0) % 32 + 32 * group
    pick_coef = jnp.where(coef == iota((128, K1), 1), 1.0, 0.0)
    half = iota((N1, N1), 1) // L1
    wanted = L1 * jnp.where(half == group, 0, 1) + iota((N1, N1), 1) % L1
    reorder = jnp.where(iota((N1, N1), 0) == wanted, 1.0, 0.0)
    side_ref[...] = jnp.zeros((128, 256), f32)
    for k, value in enumerate(powers(banded_t(start1_ref, band1_ref, K1, K1), 3)):
        own = mm(pick_coef, value)
        halves = mm(own, reorder)
        for alpha in range(4):
            rows = slice(32 * alpha, 32 * alpha + 32)
            if k == 0:
                side_ref[rows, 10 * alpha : 10 * alpha + 10] = own[rows, :]
            for h in range(2):
                piece = halves[rows, L1 * h : L1 * h + L1]
                place = 40 * k + 20 * h + L1 * alpha
                if k > 0:
                    side_ref[rows, place : place + L1] = piece
                if k < 2:
                    side_ref[rows, 128 + place : 128 + place + L1] = piece


def unpack(ref, row, count, r, source, target):
    return move(ref[pl.ds(row, 32, stride=count), :], source, target)


def first_column_kernel(recv_ref, gram_h_ref, gram_l_ref, send_ref, fields_ref, images_ref, token_ref):
    total = DEVICES * ROWS
    zero = jnp.zeros((32, 128), f32)
    for r in range(ROWS):
        j, q = r // 4, r % 4
        where0 = (j, q) if j < 2 else (2, q)
        where1 = (3 + j, q) if j < 2 else (2, q + 2)
        where2 = (5 + j, q) if j < 2 else (7, q)
        parts = [
            unpack(recv_ref, place[0], 8, r, place[1], k)
            for k, place in enumerate((where0, where1, where2))
        ]
        fields_ref[32 * r : 32 * r + 32, :] = merge(parts + [zero])
    fields = fields_ref[...]
    applied = product(load((gram_h_ref, gram_l_ref)), split(fields))
    lane = iota((total, 128), 1)
    images = applied[:total] + jnp.where(
        (lane >= 32) & (lane < 64), pltpu.roll(applied[total:], 32, 1), 0.0
    )
    images_ref[...] = images
    norm = jnp.sum(jnp.where(lane < 32, fields * images, 0.0))
    bend = jnp.sum(jnp.where(lane < 32, fields * pltpu.roll(images, 96, 1), 0.0))
    send_rows(send_ref, images_ref)
    spread(send_ref, 3, 4, (norm, bend))
    token_ref[...] = lanes((norm, bend))


def send_rows(send_ref, value_ref):
    for j in range(3):
        parts = []
        for q in range(4):
            r = 4 * j + q
            if r < ROWS:
                parts.append(move(value_ref[32 * r : 32 * r + 32, :], 0, q))
            else:
                parts.append(jnp.zeros((32, 128), f32))
        put(send_ref, j, 4, merge(parts))


def received_rows(recv_ref):
    return jnp.concatenate([recv_ref[pl.ds(j, 32, stride=4), :] for j in range(3)], axis=1)


def first_row_kernel(
    recv_ref, wide_ref, inner_ref, after_ref, send_ref, scalar_ref, rows_ref, stack_ref,
):
    norm, bend = totals(recv_ref, 3, 4, 2)
    scalar_ref[...] = lanes((norm, bend))
    kron, second, turned = constants(inner_ref)
    field = mixed_to_table(received_rows(recv_ref), kron, second, rows_ref, stack_ref)
    weighted = wide_ref[...] * field
    energy = jnp.sum(field * weighted)
    mixed = table_to_mixed(weighted, kron, turned, rows_ref, stack_ref)
    once = inner_penalty(mixed)
    for base, value in ((0, mixed), (3, once)):
        put(send_ref, base, 8, tile_of(value, 0))
        put(send_ref, base + 1, 8, tile_of(value, 1))
    lane = iota((32, 128), 1)
    put(send_ref, 2, 8, jnp.where(lane < 64, tile_of(mixed, 2), pltpu.roll(tile_of(once, 2), 64, 1)))
    spread(send_ref, 5, 8, (energy,))
    for row in (6, 7):
        put(send_ref, row, 8, jnp.zeros((32, 128), f32))


def second_column_kernel(
    recv_ref, gram_h_ref, gram_l_ref, fields_ref, images_ref, scalar_ref, after_ref,
    send_ref, blend_ref, out_scalar_ref, next_ref, image_ref,
):
    zero = jnp.zeros((32, 128), f32)
    for r in range(ROWS):
        j, q = r // 4, r % 4
        where0 = (j, q) if j < 2 else (2, q)
        where1 = (3 + j, q) if j < 2 else (2, q + 2)
        parts = [
            unpack(recv_ref, place[0], 8, r, place[1], k) for k, place in enumerate((where0, where1))
        ]
        next_ref[32 * r : 32 * r + 32, :] = merge(parts + [zero])
    (energy,) = totals(recv_ref, 5, 8, 1)
    norm, bend = pick(scalar_ref, 0), pick(scalar_ref, 1)
    step = norm / (energy + 0.1 * bend)
    out_scalar_ref[...] = lanes((norm, step))
    fields, images, following = fields_ref[...], images_ref[...], next_ref[...]
    gram = gram_h_ref[0 : DEVICES * ROWS, :], gram_l_ref[0 : DEVICES * ROWS, :]
    image = product(gram, split(following))
    image_ref[...] = images - step * (image + 0.1 * pltpu.roll(images, 96, 1))
    send_rows(send_ref, image_ref)
    put(send_ref, 3, 4, zero)
    lane = iota(fields.shape, 1)
    reduced = fields - step * (following + 0.1 * pltpu.roll(fields, 96, 1))
    blend_ref[...] = jnp.where(lane < 64, reduced, pltpu.roll(fields, 64, 1))


def coefficient_penalty(value):
    k = iota(value.shape, 0) % K0
    count = value.shape[0]
    total = 6.0 * value
    for d, weight in ((1, -4.0), (2, 1.0)):
        total = total + weight * (
            jnp.where(k >= d, pltpu.roll(value, d, 0), 0.0)
            + jnp.where(k < K0 - d, pltpu.roll(value, count - d, 0), 0.0)
        )
    return total


def send_blocks(send_ref, count, base, value_ref, block):
    for j in range(10):
        parts = []
        for q in range(4):
            m = 4 * j + q
            alpha, n = m // 10, m % 10
            parts.append(move(value_ref[pl.ds(K0 * n + alpha, 16, stride=4), :], block, q))
        merged = merge(parts)
        for g in range(GRPS):
            send_ref[pl.ds(g * count + base + j, 16, stride=2 * count), :] = merged


def send_halves(send_ref, count, base, value_ref, block):
    for g in range(GRPS):
        for j in range(5):
            parts = []
            for q in range(4):
                alpha, b = divmod(4 * j + q, L1)
                row = K0 * (L1 * g + b) + alpha
                parts.append(move(value_ref[pl.ds(row, 16, stride=4), :], block, q))
            send_ref[pl.ds(g * count + base + j, 16, stride=2 * count), :] = merge(parts)


def middle_kernel(
    blend_ref, gram_h_ref, gram_l_ref, high_h_ref, high_l_ref, lift_h_ref, lift_l_ref, scalar_ref,
    send_ref, keep_ref, sums_ref,
):
    total = DEVICES * ROWS
    step = pick(scalar_ref, 1)
    small = 0.1 * step
    blend = blend_ref[...]
    lane = iota(blend.shape, 1)
    pair = split(blend)
    lower = product(load((gram_h_ref, gram_l_ref)), pair)
    higher = product(load((high_h_ref, high_l_ref)), pair)
    g0, g1, g2, g3 = lower[:total], lower[total:], higher[:total], higher[total:]
    head = g0 - small * pltpu.roll(g1, 64, 1)
    tail = g1 - small * pltpu.roll(g2, 64, 1)
    end = g2 - small * pltpu.roll(g3, 64, 1)
    scaled = pltpu.roll(blend, 64, 1)
    low = lane < 32
    norm = jnp.sum(jnp.where(low, blend * head - small * scaled * tail, 0.0))
    head_p = tail + pltpu.roll(head, 96, 1)
    tail_p = end + pltpu.roll(tail, 96, 1)
    bend = jnp.sum(jnp.where(low, blend * head_p - small * scaled * tail_p, 0.0))
    sums_ref[...] = lanes((norm, bend))
    lifted = product(load((lift_h_ref, lift_l_ref)), pair)
    once = coefficient_penalty(lifted)
    twice = coefficient_penalty(once)
    h_a = lifted - small * pltpu.roll(once, 64, 1)
    y_1 = once + pltpu.roll(lifted, 96, 1)
    x_a = once + pltpu.roll(lifted, 96, 1) - small * (
        pltpu.roll(twice, 64, 1) + pltpu.roll(once, 32, 1)
    )
    h_0 = pltpu.roll(lifted, 64, 1)
    wide = iota(lifted.shape, 1)
    keep = jnp.where(
        wide < 32, h_0, jnp.where(wide < 64, pltpu.roll(h_a, 32, 1), jnp.where(wide < 96, y_1, pltpu.roll(x_a, 96, 1)))
    )
    keep_ref[...] = keep
    for block in range(3):
        send_halves(send_ref, JOINT, 4 + 5 * block, keep_ref, block)


def second_row_kernel(
    early_ref, recv_ref, sums_ref, wide_ref, inner_ref,
    send_ref, rows_ref, stack_ref,
):
    kron, second, turned = constants(inner_ref)
    field = mixed_to_table(received_rows(recv_ref), kron, second, rows_ref, stack_ref)
    weighted = wide_ref[...] * field
    energy = jnp.sum(field * weighted)
    mixed = table_to_mixed(weighted, kron, turned, rows_ref, stack_ref)
    for j in range(3):
        put(send_ref, j, JOINT, tile_of(mixed, j))
    spread(send_ref, 3, JOINT, (energy, pick(sums_ref, 0), pick(sums_ref, 1)))


def third_column_kernel(
    recv_ref, lift_h_ref, lift_l_ref, keep_ref, scalar_ref, send_ref, out_scalar_ref, last_ref, mixed_ref
):
    zero = jnp.zeros((32, 128), f32)
    for r in range(ROWS):
        j, q = r // 4, r % 4
        last_ref[32 * r : 32 * r + 32, :] = unpack(recv_ref, j, JOINT, r, q, 0)
    energy, norm_next, bend = totals(recv_ref, 3, JOINT, 3)
    norm, step = pick(scalar_ref, 0), pick(scalar_ref, 1)
    ratio = norm_next / norm
    curve = energy + 0.1 * bend - ratio * norm_next / step
    step_next = norm_next / curve
    out_scalar_ref[...] = lanes((norm, step, ratio, step_next))
    lifted = product(load((lift_h_ref, lift_l_ref)), split(last_ref[...]))
    keep = keep_ref[...]
    h_a, x_a = pltpu.roll(keep, 96, 1), pltpu.roll(keep, 32, 1)
    mixed_ref[...] = (
        h_a - step_next * (lifted + 0.1 * x_a) - (step_next * ratio / step) * (keep - h_a)
    )
    send_blocks(send_ref, 10, 0, mixed_ref, 0)


def gather_blocks(ref, count, base, rows, out_ref, first):
    for j in range(rows):
        taken = [ref[pl.ds(rho * count + base + j, 8, stride=4 * count), :] for rho in range(4)]
        for q in range(4):
            m = first + 4 * j + q
            merged = merge([move(taken[rho], q, rho) for rho in range(4)])
            out_ref[pl.ds(m // 8 * 64 + m % 8, 8, stride=8), :] = merged


def take(ref, block, tile):
    return jnp.concatenate(
        [ref[pl.ds((5 * block + t) * 64 + 8 * tile, 8), :] for t in range(5)], axis=0
    )


def settle_kernel(own_ref, partner_ref, side_ref, scalar_ref, solution_ref, part_ref, early):
    for block in range(3):
        for h, ref in enumerate((own_ref, partner_ref)):
            gather_blocks(ref, JOINT, 4 + 5 * block, 5, early, 40 * block + 20 * h)
    step, ratio, step_next = pick(scalar_ref, 1), pick(scalar_ref, 2), pick(scalar_ref, 3)
    small = 0.1 * step
    value = split(side_ref[:, 128:208])
    slope = split(side_ref[:, 40:120])
    for tile in range(8):
        h_0, h_a, y_1 = take(early, 0, tile), take(early, 1, tile), take(early, 2, tile)
        right = jnp.concatenate(
            [(step + step_next * ratio) * h_0 + step_next * h_a, (-step_next * small) * h_0], axis=0
        )
        columns = slice(128 * tile, 128 * tile + 128)
        solution_ref[:, :, columns] = product(value, split(right)).reshape(4, 32, 128)
        right = jnp.concatenate(
            [
                (-small * (1.0 + step_next * ratio / step)) * h_0
                - (0.1 * step_next) * (h_a - small * y_1),
                (0.1 * step_next * small) * h_0,
            ],
            axis=0,
        )
        part_ref[:, columns] = product(slope, split(right))


def final_kernel(late_ref, side_ref, part_ref, residual_ref, late):
    gather_blocks(late_ref, 10, 0, 10, late, 0)
    value = split(side_ref[:, 0:40])
    for tile in range(8):
        columns = slice(128 * tile, 128 * tile + 128)
        whole = part_ref[:, columns] + product(value, split(take(late, 0, tile)))
        residual_ref[:, :, columns] = whole.reshape(4, 32, 128)


def call(kernel, outputs, scratch, *operands, aliases={}, left=(), scalars=(), limit=16):
    vmem = pl.BlockSpec(memory_space=pltpu.VMEM)
    specs = [vmem] * len(operands)
    for k in left:
        specs[k] = pl.BlockSpec(memory_space=pltpu.HBM)
    for k in scalars:
        specs[k] = pl.BlockSpec(memory_space=pltpu.SMEM)
    return pl.pallas_call(
        kernel,
        out_shape=[
            shape if isinstance(shape, jax.ShapeDtypeStruct) else jax.ShapeDtypeStruct(shape, f32)
            for shape in outputs
        ],
        in_specs=specs,
        out_specs=[vmem] * len(outputs),
        scratch_shapes=[
            pltpu.VMEM(shape, f32) if isinstance(shape, tuple) else shape for shape in scratch
        ],
        input_output_aliases=aliases,
        compiler_params=pltpu.CompilerParams(vmem_limit_bytes=limit * 2**20),
    )(*operands)


def pair_of(*shape):
    return [jax.ShapeDtypeStruct(shape, jnp.bfloat16)] * 2


def exchange(buffer):
    count = buffer.shape[0] // DEVICES
    tiled = count == 4 or count % 8 == 0
    shape = (DEVICES, count, 128) if tiled else (DEVICES, 1, count * 128)
    moved = lax.all_to_all(buffer.reshape(shape), ("slab", "grp"), 0, 0, tiled=True)
    return moved.reshape(buffer.shape)


def fast_program(
    photon_table,
    bin_weights,
    first_start,
    first_band,
    second_start,
    second_band,
    third_start,
    third_band,
    fourth_start,
    fourth_band,
):
    total = DEVICES * ROWS
    work = [(256, 128), (64, 384)]
    outer = (first_start, first_band.T, second_start, second_band.T)
    inputs = (
        photon_table.transpose(1, 0, 2),
        bin_weights.transpose(1, 0, 2),
        third_start,
        third_band.T,
        fourth_start,
        fourth_band.T,
    )
    send, wide, inner = call(
        start_kernel,
        [(256, 128), (256, 256), jax.ShapeDtypeStruct((704, 128), jnp.bfloat16)],
        [pltpu.VMEM(value.shape, value.dtype) for value in inputs]
        + [pltpu.SemaphoreType.DMA((len(inputs),))]
        + [(16, N2 * N3), (16, N2 * N3), (256, 256)]
        + work,
        *inputs,
        left=range(len(inputs)),
        limit=LARGE,
    )
    recv = exchange(send)
    gram = call(gram_kernel, pair_of(2 * total, total), [(total, 64), (total, 32)], *outer)
    send, fields, images, token = call(
        first_column_kernel, [(128, 128), (total, 128), (total, 128), (8, 128)], [], recv, *gram
    )
    recv = exchange(send)
    *high, token = call(
        high_kernel,
        pair_of(2 * total, total) + [(8, 128)],
        [(total, 128), (total, 64)],
        token, *outer,
    )
    send, scalars = call(
        first_row_kernel, [(256, 128), (8, 128)], work, recv, wide, inner, token
    )
    recv = exchange(send)
    group = lax.axis_index("grp").reshape(1)
    *lift, side, token = call(
        lift_kernel,
        pair_of(K0 * N1, total) + [(128, 256), (8, 128)],
        [],
        scalars, group, *outer,
        scalars=(1,),
    )
    send, blend, scalars = call(
        second_column_kernel,
        [(128, 128), (total, 128), (8, 128)],
        [(total, 128), (total, 128)],
        recv, *gram, fields, images, scalars, token,
    )
    recv = exchange(send)
    send, keep, sums = call(
        middle_kernel,
        [(DEVICES * JOINT, 128), (K0 * N1, 128), (8, 128)],
        [],
        blend, *gram, *high, *lift, scalars,
    )
    (send,) = call(
        second_row_kernel,
        [(DEVICES * JOINT, 128)],
        work,
        send, recv, sums, wide, inner,
        aliases={0: 0},
    )
    recv = exchange(send)
    partner = lax.ppermute(recv, "grp", [(0, 1), (1, 0)])
    send, scalars = call(
        third_column_kernel,
        [(DEVICES * 10, 128), (8, 128)],
        [(total, 128), (K0 * N1, 128)],
        recv, *lift, keep, scalars,
    )
    late = exchange(send)
    solution_part, part = call(
        settle_kernel,
        [(4, 32, 1024), (128, 1024)],
        [(960, 128)],
        recv, partner, side, scalars,
    )
    (residual,) = call(final_kernel, [(4, 32, 1024)], [(320, 128)], late, side, part)
    return solution_part, residual


def fits(mesh):
    return (mesh.shape["slab"], mesh.shape["grp"]) == (SLABS, GRPS)


def solution(mesh):
    placed = (
        P("slab", "grp", None),
        P("slab", "grp", None),
        P(),
        P(),
        P(),
        P(),
        P(),
        P(),
        P(),
        P(),
    )
    return jax.shard_map(
        fast_program if fits(mesh) else per_device,
        mesh=mesh,
        in_specs=placed,
        out_specs=(P("slab", "grp", None), P("slab", "grp", None)),
        check_vma=False,
    )
```

```python
import jax
import jax.numpy as jnp
from jax import lax
from jax.experimental import pallas as pl
from jax.experimental.pallas import tpu as pltpu
from jax.sharding import PartitionSpec as P

K0 = 64
K1 = 64
K2 = 32
K3 = 32
ITERS = 2


highest = lax.Precision.HIGHEST
smoothing = 0.1
stencil_weights = (1.0, -4.0, 6.0, -4.0, 1.0)


def with_halo(value, sides, width):
    for axis, dim in sides:
        count, length = (lax.axis_size(axis), value.shape[dim])
        up = [(i, (i + 1) % count) for i in range(count - 1)]
        down = [(j, i) for i, j in up]
        last = lax.slice_in_dim(value, length - width, length, axis=dim)
        initial = lax.slice_in_dim(value, 0, width, axis=dim)
        before = lax.ppermute(last, axis, up)
        after = lax.ppermute(initial, axis, down)
        value = jnp.concatenate([before, value, after], axis=dim)
    return value


def dense_basis(starts, values, coef_count):
    relative = jnp.arange(coef_count, dtype=jnp.int32)[None, :] - starts[:, None]
    matrix = jnp.zeros((starts.shape[0], coef_count), jnp.float32)
    for offset in range(4):
        matrix = matrix + jnp.where(relative == offset, values[:, offset : offset + 1], 0.0)
    return matrix


def five_point(source, along, extent):
    running = stencil_weights[0] * lax.slice_in_dim(source, 0, extent, axis=along)
    for offset in range(1, 5):
        running = running + stencil_weights[offset] * lax.slice_in_dim(
            source, offset, offset + extent, axis=along
        )
    return running


def local_stencil(tensor, along):
    widths = [(0, 0)] * tensor.ndim
    widths[along] = (2, 2)
    return five_point(jnp.pad(tensor, widths), along, tensor.shape[along])


def inner_forward(tensor, third_basis, fourth_basis):
    leading, middle = (tensor.shape[0], tensor.shape[1])
    blocked = tensor.reshape(leading, middle, third_basis.shape[1], fourth_basis.shape[1])
    blocked = jnp.einsum("abcd,nd->abcn", blocked, fourth_basis, precision=highest)
    blocked = jnp.einsum("abcn,mc->abmn", blocked, third_basis, precision=highest)
    return blocked.reshape(leading, middle, third_basis.shape[0] * fourth_basis.shape[0])


def inner_adjoint(tensor, third_basis, fourth_basis):
    leading, middle = (tensor.shape[0], tensor.shape[1])
    blocked = tensor.reshape(leading, middle, third_basis.shape[0], fourth_basis.shape[0])
    blocked = jnp.einsum("abmn,mc->abcn", blocked, third_basis, precision=highest)
    blocked = jnp.einsum("abcn,nd->abcd", blocked, fourth_basis, precision=highest)
    return blocked.reshape(leading, middle, third_basis.shape[1] * fourth_basis.shape[1])


def lead_product(tensor, matrix):
    combined = jnp.einsum(
        "ka,ain->kin",
        matrix,
        lax.all_to_all(tensor, "slab", split_axis=2, concat_axis=0, tiled=True),
        precision=highest,
    )
    return lax.all_to_all(combined, "slab", split_axis=0, concat_axis=2, tiled=True)


def second_product(tensor, matrix):
    return jnp.einsum(
        "lp,apn->aln", matrix, lax.all_gather(tensor, "grp", axis=1, tiled=True), precision=highest
    )


def penalty(coeffs):
    leading, middle = (coeffs.shape[0], coeffs.shape[1])
    padded = with_halo(coeffs, (("slab", 0), ("grp", 1)), 2)
    along_lead = five_point(padded[:, 2 : 2 + middle], 0, leading)
    along_rows = five_point(padded[2 : 2 + leading, :], 1, middle)
    blocked = coeffs.reshape(leading, middle, K2, K3)
    inner_part = local_stencil(blocked, 2) + local_stencil(blocked, 3)
    return along_lead + along_rows + inner_part.reshape(leading, middle, K2 * K3)


def squared_total(vector):
    return lax.psum(jnp.sum(vector * vector), ("slab", "grp"))


def per_device(
    photon_table,
    bin_weights,
    first_start,
    first_band,
    second_start,
    second_band,
    third_start,
    third_band,
    fourth_start,
    fourth_band,
):
    first_basis = dense_basis(first_start, first_band, K0)
    second_basis = dense_basis(second_start, second_band, K1)
    third_basis = dense_basis(third_start, third_band, K2)
    fourth_basis = dense_basis(fourth_start, fourth_band, K3)
    first_back = first_basis.T
    group_index = lax.axis_index("grp")
    row_count = photon_table.shape[1]
    coef_rows = K1 // lax.axis_size("grp")
    near_rows = lax.dynamic_slice_in_dim(second_basis, group_index * row_count, row_count, 0)
    back_rows = lax.dynamic_slice_in_dim(second_basis.T, group_index * coef_rows, coef_rows, 0)

    def adjoint(table):
        tensor = lead_product(table, first_back)
        tensor = second_product(tensor, back_rows)
        return inner_adjoint(tensor, third_basis, fourth_basis)

    right_side = adjoint(bin_weights * photon_table)
    solution = jnp.zeros_like(right_side)
    residual = right_side
    direction = right_side
    norm_now = squared_total(residual)
    for sweep in range(ITERS):
        forward_tensor = inner_forward(direction, third_basis, fourth_basis)
        forward_tensor = second_product(forward_tensor, near_rows)
        mapped = adjoint(
            bin_weights * lead_product(forward_tensor, first_basis)
        ) + smoothing * penalty(direction)
        curve_total = lax.psum(jnp.sum(direction * mapped), ("slab", "grp"))
        step_size = norm_now / curve_total
        solution = solution + step_size * direction
        residual = residual - step_size * mapped
        norm_next = squared_total(residual)
        direction = residual + norm_next / norm_now * direction
        norm_now = norm_next
    return (solution, residual)


SLABS, GRPS = 16, 2
DEVICES = SLABS * GRPS
L0, L1 = 2, 5
ROWS = L0 * L1
N2, N3 = 64, 50
N0, N1 = 32, 10
HI = lax.Precision.HIGHEST
f32 = jnp.float32
JOINT = 19
LARGE = 60


def iota(shape, dim):
    return lax.broadcasted_iota(jnp.int32, shape, dim)


def mm(a, b):
    return jnp.dot(a, b, precision=HI, preferred_element_type=f32)


def mm_t(a, b):
    return lax.dot_general(
        a, b, (((1,), (1,)), ((), ())), precision=HI, preferred_element_type=f32
    )


def split(value):
    high = value.astype(jnp.bfloat16)
    return high, (value - high.astype(f32)).astype(jnp.bfloat16)


def product(a, b, transposed=False):
    dims = (((1,), (1 if transposed else 0,)), ((), ()))

    def one(x, y):
        return lax.dot_general(x, y, dims, preferred_element_type=f32)

    return one(a[0], b[0]) + (one(a[0], b[1]) + one(a[1], b[0]))


def load(pair):
    return pair[0][...], pair[1][...]


def move(block, source, target):
    shift = (target - source) * 32 % 128
    return pltpu.roll(block, shift, 1) if shift else block


def merge(parts):
    lane = iota(parts[0].shape, 1)
    out = parts[-1]
    for q in range(len(parts) - 2, -1, -1):
        out = jnp.where(lane < 32 * (q + 1), parts[q], out)
    return out


def slot(r):
    return L0 * (r % L1) + r // L1


def banded_t(start_ref, band_ref, width, wrap):
    n = start_ref.shape[0]
    relative = (iota((width, n), 0) % wrap) - start_ref[...].reshape(1, n)
    out = jnp.zeros((width, n), f32)
    for offset in range(4):
        out = out + jnp.where(relative == offset, band_ref[offset : offset + 1, :], 0.0)
    return out


def expand(ref, p):
    first = 200 * p
    tile, off = first // 128, first % 128
    lane = iota((16, 128), 1)

    def window(t):
        low = ref[:, t * 128 : (t + 1) * 128]
        if off == 0:
            return low
        t1 = min(t + 1, 24)
        high = ref[:, t1 * 128 : (t1 + 1) * 128]
        return jnp.where(
            lane < 128 - off, pltpu.roll(low, 128 - off, 1), pltpu.roll(high, 128 - off, 1)
        )

    return window(tile), window(min(tile + 1, 24))


def table_to_mixed(field, kron_third, second_t, rows_ref, stack_ref):
    rows_ref[...] = product(split(field), kron_third)
    for c in range(4):
        for j in range(3):
            parts = []
            for q in range(4):
                r = 4 * j + q
                if r < ROWS:
                    part = rows_ref[pl.ds(slot(r), 16, stride=16), :]
                    parts.append(move(part, c, q))
                else:
                    parts.append(jnp.zeros((16, 128), f32))
            stack_ref[16 * c : 16 * c + 16, 128 * j : 128 * j + 128] = merge(parts)
    return product(second_t, split(stack_ref[...]))


def mixed_to_table(value, kron_third, second, rows_ref, stack_ref):
    stack_ref[...] = product(second, split(value))
    rows_ref[...] = jnp.zeros((256, 128), f32)
    for r in range(ROWS):
        j, q = r // 4, r % 4
        parts = [
            move(stack_ref[16 * c : 16 * c + 16, 128 * j : 128 * j + 128], q, c) for c in range(4)
        ]
        rows_ref[pl.ds(slot(r), 16, stride=16), :] = merge(parts)
    return product(split(rows_ref[...]), kron_third, True)


def inner_penalty(value):
    out = 12.0 * value
    row = iota((32, 128), 0)
    inside = iota((32, 128), 1) % 32
    tiles = []
    for j in range(3):
        tile = value[:, 128 * j : 128 * j + 128]
        total = 12.0 * tile
        for d, weight in ((1, -4.0), (2, 1.0)):
            total = total + weight * (
                jnp.where(row >= d, pltpu.roll(tile, d, 0), 0.0)
                + jnp.where(row < 32 - d, pltpu.roll(tile, 32 - d, 0), 0.0)
                + jnp.where(inside >= d, pltpu.roll(tile, d, 1), 0.0)
                + jnp.where(inside < 32 - d, pltpu.roll(tile, 128 - d, 1), 0.0)
            )
        tiles.append(total)
    return jnp.concatenate(tiles, axis=1)


def tile_of(value, j):
    return value[:, 128 * j : 128 * j + 128]


def put(ref, row, count, value):
    ref[pl.ds(row, 32, stride=count), :] = value


def lanes(values):
    lane = iota((8, 128), 1)
    out = jnp.zeros((8, 128), f32)
    for k, value in enumerate(values):
        out = jnp.where(lane == k, value, out)
    return out


def spread(ref, row, count, values):
    one = lanes(values)
    put(ref, row, count, jnp.concatenate([one] * 4, axis=0))


def totals(ref, row, count, number):
    summed = jnp.sum(ref[pl.ds(row, 32, stride=count), :], axis=0, keepdims=True)
    lane = iota((1, 128), 1)
    return [jnp.sum(jnp.where(lane == k, summed, 0.0)) for k in range(number)]


def pick(ref, k):
    lane = iota((1, 128), 1)
    return jnp.sum(jnp.where(lane == k, ref[0:1, :], 0.0))


def constants(ref):
    kron = ref[0:256, :], ref[256:512, :]
    second = ref[512:576, 0:32], ref[576:640, 0:32]
    return kron, second, (ref[640:672, 0:64], ref[672:704, 0:64])


def start_kernel(
    table_hbm, weight_hbm, start2_hbm, band2_hbm, start3_hbm, band3_hbm,
    send_ref, wide_ref, inner_ref,
    table_ref, weight_ref, start2_ref, band2_ref, start3_ref, band3_ref, sems,
    product_ref, packed_ref, field_ref, rows_ref, stack_ref,
):
    copies = [
        pltpu.make_async_copy(source, target, sems.at[k])
        for k, (source, target) in enumerate(
            (
                (start3_hbm, start3_ref),
                (band3_hbm, band3_ref),
                (start2_hbm, start2_ref),
                (band2_hbm, band2_ref),
                (weight_hbm, weight_ref),
                (table_hbm, table_ref),
            )
        )
    ]
    for copy in copies:
        copy.start()
    copies[0].wait()
    copies[1].wait()
    pick_bin = (iota((256, N3), 0) % N3 == iota((256, N3), 1)) & (iota((256, N3), 0) < 4 * N3)
    same = iota((256, 128), 0) // N3 == iota((256, 128), 1) // 32
    picker = jnp.where(pick_bin, 1.0, 0.0).astype(jnp.bfloat16)
    for k, term in enumerate(split(banded_t(start3_ref, band3_ref, 128, 32))):
        spread_out = lax.dot_general(
            picker, term, (((1,), (1,)), ((), ())), preferred_element_type=f32
        )
        inner_ref[256 * k : 256 * k + 256, :] = jnp.where(same, spread_out, 0.0).astype(jnp.bfloat16)
    copies[2].wait()
    copies[3].wait()
    order, other = iota((N2, N2), 1), iota((N2, N2), 0)
    permute = jnp.where((order % 16) * 4 + order // 16 == other, 1.0, 0.0).astype(jnp.bfloat16)
    back = jnp.where((other % 16) * 4 + other // 16 == order, 1.0, 0.0).astype(jnp.bfloat16)
    for k, term in enumerate(split(banded_t(start2_ref, band2_ref, 32, 32))):
        value = jnp.dot(term, permute, preferred_element_type=f32)
        inner_ref[640 + 32 * k : 672 + 32 * k, 0:64] = value.astype(jnp.bfloat16)
        value = lax.dot_general(back, term, (((1,), (1,)), ((), ())), preferred_element_type=f32)
        inner_ref[512 + 64 * k : 576 + 64 * k, 0:32] = value.astype(jnp.bfloat16)
    kron, _, turned = constants(inner_ref)
    copies[4].wait()
    copies[5].wait()
    packed_ref[8:16, :] = jnp.zeros((8, N2 * N3), f32)
    product_ref[8:16, :] = jnp.zeros((8, N2 * N3), f32)
    for b in range(L1):
        weight = weight_ref[b]
        packed_ref[L0 * b : L0 * b + L0, :] = weight
        product_ref[L0 * b : L0 * b + L0, :] = weight * table_ref[b]
    for p in range(16):
        for source, target in ((packed_ref, wide_ref), (product_ref, field_ref)):
            low, high = expand(source, p)
            target[16 * p : 16 * p + 16, 0:128] = low
            target[16 * p : 16 * p + 16, 128:256] = high
    mixed = table_to_mixed(field_ref[...], kron, turned, rows_ref, stack_ref)
    once = inner_penalty(mixed)
    twice = inner_penalty(once)
    for base, value in ((0, mixed), (3, once), (5, twice)):
        put(send_ref, base, 8, tile_of(value, 0))
        put(send_ref, base + 1, 8, tile_of(value, 1))
    lane = iota((32, 128), 1)
    put(send_ref, 2, 8, jnp.where(lane < 64, tile_of(mixed, 2), pltpu.roll(tile_of(once, 2), 64, 1)))
    put(send_ref, 7, 8, tile_of(twice, 2))


def pentadiagonal(n):
    gap = jnp.abs(iota((n, n), 0) - iota((n, n), 1))
    return jnp.where(gap == 0, 6.0, jnp.where(gap == 1, -4.0, jnp.where(gap == 2, 1.0, 0.0)))


def choose(pieces, selector):
    out = None
    for piece in pieces:
        term = jnp.dot(piece, selector, preferred_element_type=f32)
        out = term if out is None else out + term
    return out


def powers(basis_t, count):
    penalty_matrix = pentadiagonal(basis_t.shape[0])
    out = [basis_t]
    for _ in range(count - 1):
        out.append(mm(penalty_matrix, out[-1]))
    return out


def store_split(high_ref, low_ref, rows, value):
    high, low = split(value)
    high_ref[rows, :] = high
    low_ref[rows, :] = low


def matrix_kernel(
    group_ref, start0_ref, band0_ref, start1_ref, band1_ref,
    gram_h_ref, gram_l_ref, high_h_ref, high_l_ref, lift_h_ref, lift_l_ref, side_ref,
    small_ref, rows0_h, rows0_l, rows1_h, rows1_l,
):
    total = DEVICES * ROWS
    powers0 = powers(banded_t(start0_ref, band0_ref, K0, K0), 4)
    powers1 = powers(banded_t(start1_ref, band1_ref, K1, K1), 4)
    small_ref[...] = jnp.zeros((48, 128), f32)
    first, second = powers0[0].T, powers1[0].T
    for k in range(4):
        small_ref[0:N0, 32 * k : 32 * k + N0] = mm(first, powers0[k])
        small_ref[N0 : N0 + N1, 32 * k : 32 * k + N1] = mm(second, powers1[k])
    row0 = iota((total, N0), 0)
    pick0 = L0 * (row0 % 32 // GRPS) + row0 // 32 // L1 == iota((total, N0), 1)
    row1 = iota((total, 16), 0)
    pick1 = L1 * (row1 % GRPS) + row1 // 32 % L1 == iota((total, 16), 1)
    for pick, rows, targets in (
        (pick0, slice(0, N0), (rows0_h, rows0_l)),
        (pick1, slice(N0, N0 + 16), (rows1_h, rows1_l)),
    ):
        chooser = jnp.where(pick, 1.0, 0.0).astype(jnp.bfloat16)
        for term, target in zip(split(small_ref[rows, :]), targets):
            spread_out = jnp.dot(chooser, term, preferred_element_type=f32)
            target[...] = spread_out.astype(jnp.bfloat16)
    line, column = iota((128, total), 0), iota((128, total), 1)
    match0 = line % 32 == L0 * (column % 32 // GRPS) + column // 32 // L1
    match1 = line % 32 == L1 * (column % GRPS) + column // 32 % L1
    select0 = [
        jnp.where(match0 & (line // 32 == k), 1.0, 0.0).astype(jnp.bfloat16) for k in range(4)
    ]
    select1 = [
        jnp.where(match1 & (line // 32 == k), 1.0, 0.0).astype(jnp.bfloat16) for k in range(4)
    ]

    @pl.loop(0, 5)
    def _(step):
        base = pl.multiple_of(step * 64, 64)
        block0 = rows0_h[pl.ds(base, 64), :], rows0_l[pl.ds(base, 64), :]
        block1 = rows1_h[pl.ds(base, 64), :], rows1_l[pl.ds(base, 64), :]
        g = [choose(block0, selector) for selector in select0]
        h = [choose(block1, selector) for selector in select1]
        first_power = g[1] * h[0] + g[0] * h[1]
        squared = g[2] * h[0] + 2.0 * g[1] * h[1] + g[0] * h[2]
        cubed = g[3] * h[0] + 3.0 * (g[2] * h[1] + g[1] * h[2]) + g[0] * h[3]
        store_split(gram_h_ref, gram_l_ref, pl.ds(base, 64), g[0] * h[0])
        store_split(gram_h_ref, gram_l_ref, pl.ds(base + total, 64), first_power)
        store_split(high_h_ref, high_l_ref, pl.ds(base, 64), squared)
        store_split(high_h_ref, high_l_ref, pl.ds(base + total, 64), cubed)

    lifted = [
        jnp.dot(term, select0[0][0:N0, :], preferred_element_type=f32)
        for term in split(powers0[0])
    ]
    owner = L1 * (iota((K0, total), 1) % GRPS) + iota((K0, total), 1) // 32 % L1
    for n in range(N1):
        rows = slice(K0 * n, K0 * n + K0)
        for term, target in zip(lifted, (lift_h_ref, lift_l_ref)):
            target[rows, :] = jnp.where(owner == n, term, 0.0).astype(jnp.bfloat16)
    group = group_ref[0]
    coef = iota((128, K1), 0) % 32 + 32 * group
    pick_coef = jnp.where(coef == iota((128, K1), 1), 1.0, 0.0)
    half = iota((N1, N1), 1) // L1
    wanted = L1 * jnp.where(half == group, 0, 1) + iota((N1, N1), 1) % L1
    reorder = jnp.where(iota((N1, N1), 0) == wanted, 1.0, 0.0)
    side_ref[...] = jnp.zeros((128, 256), f32)
    for k in range(3):
        own = mm(pick_coef, powers1[k])
        halves = mm(own, reorder)
        for alpha in range(4):
            rows = slice(32 * alpha, 32 * alpha + 32)
            if k == 0:
                side_ref[rows, 10 * alpha : 10 * alpha + 10] = own[rows, :]
            for h in range(2):
                piece = halves[rows, L1 * h : L1 * h + L1]
                place = 40 * k + 20 * h + L1 * alpha
                if k > 0:
                    side_ref[rows, place : place + L1] = piece
                if k < 2:
                    side_ref[rows, 128 + place : 128 + place + L1] = piece


def unpack(ref, row, count, r, source, target):
    return move(ref[pl.ds(row, 32, stride=count), :], source, target)


def first_column_kernel(recv_ref, gram_h_ref, gram_l_ref, send_ref, fields_ref, images_ref):
    total = DEVICES * ROWS
    zero = jnp.zeros((32, 128), f32)
    for r in range(ROWS):
        j, q = r // 4, r % 4
        where0 = (j, q) if j < 2 else (2, q)
        where1 = (3 + j, q) if j < 2 else (2, q + 2)
        where2 = (5 + j, q) if j < 2 else (7, q)
        parts = [
            unpack(recv_ref, place[0], 8, r, place[1], k)
            for k, place in enumerate((where0, where1, where2))
        ]
        fields_ref[32 * r : 32 * r + 32, :] = merge(parts + [zero])
    fields = fields_ref[...]
    applied = product(load((gram_h_ref, gram_l_ref)), split(fields))
    lane = iota((total, 128), 1)
    images = applied[:total] + jnp.where(
        (lane >= 32) & (lane < 64), pltpu.roll(applied[total:], 32, 1), 0.0
    )
    images_ref[...] = images
    norm = jnp.sum(jnp.where(lane < 32, fields * images, 0.0))
    bend = jnp.sum(jnp.where(lane < 32, fields * pltpu.roll(images, 96, 1), 0.0))
    send_rows(send_ref, images_ref)
    spread(send_ref, 3, 4, (norm, bend))


def send_rows(send_ref, value_ref):
    for j in range(3):
        parts = []
        for q in range(4):
            r = 4 * j + q
            if r < ROWS:
                parts.append(move(value_ref[32 * r : 32 * r + 32, :], 0, q))
            else:
                parts.append(jnp.zeros((32, 128), f32))
        put(send_ref, j, 4, merge(parts))


def received_rows(recv_ref):
    return jnp.concatenate([recv_ref[pl.ds(j, 32, stride=4), :] for j in range(3)], axis=1)


def first_row_kernel(
    recv_ref, wide_ref, inner_ref, send_ref, scalar_ref, rows_ref, stack_ref,
):
    norm, bend = totals(recv_ref, 3, 4, 2)
    scalar_ref[...] = lanes((norm, bend))
    kron, second, turned = constants(inner_ref)
    field = mixed_to_table(received_rows(recv_ref), kron, second, rows_ref, stack_ref)
    weighted = wide_ref[...] * field
    energy = jnp.sum(field * weighted)
    mixed = table_to_mixed(weighted, kron, turned, rows_ref, stack_ref)
    once = inner_penalty(mixed)
    for base, value in ((0, mixed), (3, once)):
        put(send_ref, base, 8, tile_of(value, 0))
        put(send_ref, base + 1, 8, tile_of(value, 1))
    lane = iota((32, 128), 1)
    put(send_ref, 2, 8, jnp.where(lane < 64, tile_of(mixed, 2), pltpu.roll(tile_of(once, 2), 64, 1)))
    spread(send_ref, 5, 8, (energy,))
    for row in (6, 7):
        put(send_ref, row, 8, jnp.zeros((32, 128), f32))


def second_column_kernel(
    recv_ref, gram_h_ref, gram_l_ref, fields_ref, images_ref, scalar_ref,
    send_ref, blend_ref, out_scalar_ref, next_ref, image_ref,
):
    zero = jnp.zeros((32, 128), f32)
    for r in range(ROWS):
        j, q = r // 4, r % 4
        where0 = (j, q) if j < 2 else (2, q)
        where1 = (3 + j, q) if j < 2 else (2, q + 2)
        parts = [
            unpack(recv_ref, place[0], 8, r, place[1], k) for k, place in enumerate((where0, where1))
        ]
        next_ref[32 * r : 32 * r + 32, :] = merge(parts + [zero])
    (energy,) = totals(recv_ref, 5, 8, 1)
    norm, bend = pick(scalar_ref, 0), pick(scalar_ref, 1)
    step = norm / (energy + 0.1 * bend)
    out_scalar_ref[...] = lanes((norm, step))
    fields, images, following = fields_ref[...], images_ref[...], next_ref[...]
    gram = gram_h_ref[0 : DEVICES * ROWS, :], gram_l_ref[0 : DEVICES * ROWS, :]
    image = product(gram, split(following))
    image_ref[...] = images - step * (image + 0.1 * pltpu.roll(images, 96, 1))
    send_rows(send_ref, image_ref)
    put(send_ref, 3, 4, zero)
    lane = iota(fields.shape, 1)
    reduced = fields - step * (following + 0.1 * pltpu.roll(fields, 96, 1))
    blend_ref[...] = jnp.where(lane < 64, reduced, pltpu.roll(fields, 64, 1))


def coefficient_penalty(value):
    k = iota(value.shape, 0) % K0
    count = value.shape[0]
    total = 6.0 * value
    for d, weight in ((1, -4.0), (2, 1.0)):
        total = total + weight * (
            jnp.where(k >= d, pltpu.roll(value, d, 0), 0.0)
            + jnp.where(k < K0 - d, pltpu.roll(value, count - d, 0), 0.0)
        )
    return total


def send_blocks(send_ref, count, base, value_ref, block):
    for j in range(10):
        parts = []
        for q in range(4):
            m = 4 * j + q
            alpha, n = m // 10, m % 10
            parts.append(move(value_ref[pl.ds(K0 * n + alpha, 16, stride=4), :], block, q))
        merged = merge(parts)
        for g in range(GRPS):
            send_ref[pl.ds(g * count + base + j, 16, stride=2 * count), :] = merged


def send_halves(send_ref, count, base, value_ref, block):
    for g in range(GRPS):
        for j in range(5):
            parts = []
            for q in range(4):
                alpha, b = divmod(4 * j + q, L1)
                row = K0 * (L1 * g + b) + alpha
                parts.append(move(value_ref[pl.ds(row, 16, stride=4), :], block, q))
            send_ref[pl.ds(g * count + base + j, 16, stride=2 * count), :] = merge(parts)


def middle_kernel(
    blend_ref, gram_h_ref, gram_l_ref, high_h_ref, high_l_ref, lift_h_ref, lift_l_ref, scalar_ref,
    send_ref, keep_ref, sums_ref,
):
    total = DEVICES * ROWS
    step = pick(scalar_ref, 1)
    small = 0.1 * step
    blend = blend_ref[...]
    lane = iota(blend.shape, 1)
    pair = split(blend)
    lower = product(load((gram_h_ref, gram_l_ref)), pair)
    higher = product(load((high_h_ref, high_l_ref)), pair)
    g0, g1, g2, g3 = lower[:total], lower[total:], higher[:total], higher[total:]
    head = g0 - small * pltpu.roll(g1, 64, 1)
    tail = g1 - small * pltpu.roll(g2, 64, 1)
    end = g2 - small * pltpu.roll(g3, 64, 1)
    scaled = pltpu.roll(blend, 64, 1)
    low = lane < 32
    norm = jnp.sum(jnp.where(low, blend * head - small * scaled * tail, 0.0))
    head_p = tail + pltpu.roll(head, 96, 1)
    tail_p = end + pltpu.roll(tail, 96, 1)
    bend = jnp.sum(jnp.where(low, blend * head_p - small * scaled * tail_p, 0.0))
    sums_ref[...] = lanes((norm, bend))
    lifted = product(load((lift_h_ref, lift_l_ref)), pair)
    once = coefficient_penalty(lifted)
    twice = coefficient_penalty(once)
    h_a = lifted - small * pltpu.roll(once, 64, 1)
    y_1 = once + pltpu.roll(lifted, 96, 1)
    x_a = once + pltpu.roll(lifted, 96, 1) - small * (
        pltpu.roll(twice, 64, 1) + pltpu.roll(once, 32, 1)
    )
    h_0 = pltpu.roll(lifted, 64, 1)
    wide = iota(lifted.shape, 1)
    keep = jnp.where(
        wide < 32, h_0, jnp.where(wide < 64, pltpu.roll(h_a, 32, 1), jnp.where(wide < 96, y_1, pltpu.roll(x_a, 96, 1)))
    )
    keep_ref[...] = keep
    for block in range(3):
        send_halves(send_ref, JOINT, 4 + 5 * block, keep_ref, block)


def second_row_kernel(
    early_ref, recv_ref, sums_ref, wide_ref, inner_ref,
    send_ref, rows_ref, stack_ref,
):
    kron, second, turned = constants(inner_ref)
    field = mixed_to_table(received_rows(recv_ref), kron, second, rows_ref, stack_ref)
    weighted = wide_ref[...] * field
    energy = jnp.sum(field * weighted)
    mixed = table_to_mixed(weighted, kron, turned, rows_ref, stack_ref)
    for j in range(3):
        put(send_ref, j, JOINT, tile_of(mixed, j))
    spread(send_ref, 3, JOINT, (energy, pick(sums_ref, 0), pick(sums_ref, 1)))


def third_column_kernel(
    recv_ref, lift_h_ref, lift_l_ref, keep_ref, scalar_ref, send_ref, out_scalar_ref, last_ref, mixed_ref
):
    zero = jnp.zeros((32, 128), f32)
    for r in range(ROWS):
        j, q = r // 4, r % 4
        last_ref[32 * r : 32 * r + 32, :] = unpack(recv_ref, j, JOINT, r, q, 0)
    energy, norm_next, bend = totals(recv_ref, 3, JOINT, 3)
    norm, step = pick(scalar_ref, 0), pick(scalar_ref, 1)
    ratio = norm_next / norm
    curve = energy + 0.1 * bend - ratio * norm_next / step
    step_next = norm_next / curve
    out_scalar_ref[...] = lanes((norm, step, ratio, step_next))
    lifted = product(load((lift_h_ref, lift_l_ref)), split(last_ref[...]))
    keep = keep_ref[...]
    h_a, x_a = pltpu.roll(keep, 96, 1), pltpu.roll(keep, 32, 1)
    mixed_ref[...] = (
        h_a - step_next * (lifted + 0.1 * x_a) - (step_next * ratio / step) * (keep - h_a)
    )
    send_blocks(send_ref, 10, 0, mixed_ref, 0)


def gather_blocks(ref, count, base, rows, out_ref, first):
    for j in range(rows):
        taken = [ref[pl.ds(rho * count + base + j, 8, stride=4 * count), :] for rho in range(4)]
        for q in range(4):
            m = first + 4 * j + q
            merged = merge([move(taken[rho], q, rho) for rho in range(4)])
            out_ref[pl.ds(m // 8 * 64 + m % 8, 8, stride=8), :] = merged


def take(ref, block, tile):
    return jnp.concatenate(
        [ref[pl.ds((5 * block + t) * 64 + 8 * tile, 8), :] for t in range(5)], axis=0
    )


def settle_kernel(own_ref, partner_ref, side_ref, scalar_ref, solution_ref, part_ref, early):
    for block in range(3):
        for h, ref in enumerate((own_ref, partner_ref)):
            gather_blocks(ref, JOINT, 4 + 5 * block, 5, early, 40 * block + 20 * h)
    step, ratio, step_next = pick(scalar_ref, 1), pick(scalar_ref, 2), pick(scalar_ref, 3)
    small = 0.1 * step
    value = split(side_ref[:, 128:208])
    slope = split(side_ref[:, 40:120])
    for tile in range(8):
        h_0, h_a, y_1 = take(early, 0, tile), take(early, 1, tile), take(early, 2, tile)
        right = jnp.concatenate(
            [(step + step_next * ratio) * h_0 + step_next * h_a, (-step_next * small) * h_0], axis=0
        )
        columns = slice(128 * tile, 128 * tile + 128)
        solution_ref[:, :, columns] = product(value, split(right)).reshape(4, 32, 128)
        right = jnp.concatenate(
            [
                (-small * (1.0 + step_next * ratio / step)) * h_0
                - (0.1 * step_next) * (h_a - small * y_1),
                (0.1 * step_next * small) * h_0,
            ],
            axis=0,
        )
        part_ref[:, columns] = product(slope, split(right))


def final_kernel(late_ref, side_ref, part_ref, residual_ref, late):
    gather_blocks(late_ref, 10, 0, 10, late, 0)
    value = split(side_ref[:, 0:40])
    for tile in range(8):
        columns = slice(128 * tile, 128 * tile + 128)
        whole = part_ref[:, columns] + product(value, split(take(late, 0, tile)))
        residual_ref[:, :, columns] = whole.reshape(4, 32, 128)


def call(kernel, outputs, scratch, *operands, aliases={}, left=(), scalars=(), limit=16):
    vmem = pl.BlockSpec(memory_space=pltpu.VMEM)
    specs = [vmem] * len(operands)
    for k in left:
        specs[k] = pl.BlockSpec(memory_space=pltpu.HBM)
    for k in scalars:
        specs[k] = pl.BlockSpec(memory_space=pltpu.SMEM)
    return pl.pallas_call(
        kernel,
        out_shape=[
            shape if isinstance(shape, jax.ShapeDtypeStruct) else jax.ShapeDtypeStruct(shape, f32)
            for shape in outputs
        ],
        in_specs=specs,
        out_specs=[vmem] * len(outputs),
        scratch_shapes=[
            pltpu.VMEM(shape, f32) if isinstance(shape, tuple) else shape for shape in scratch
        ],
        input_output_aliases=aliases,
        compiler_params=pltpu.CompilerParams(vmem_limit_bytes=limit * 2**20),
    )(*operands)


def pair_of(*shape):
    return [jax.ShapeDtypeStruct(shape, jnp.bfloat16)] * 2


def exchange(buffer):
    count = buffer.shape[0] // DEVICES
    tiled = count == 4 or count % 8 == 0
    shape = (DEVICES, count, 128) if tiled else (DEVICES, 1, count * 128)
    moved = lax.all_to_all(buffer.reshape(shape), ("slab", "grp"), 0, 0, tiled=True)
    return moved.reshape(buffer.shape)


def fast_program(
    photon_table,
    bin_weights,
    first_start,
    first_band,
    second_start,
    second_band,
    third_start,
    third_band,
    fourth_start,
    fourth_band,
):
    total = DEVICES * ROWS
    work = [(256, 128), (64, 384)]
    outer = (first_start, first_band.T, second_start, second_band.T)
    inputs = (
        photon_table.transpose(1, 0, 2),
        bin_weights.transpose(1, 0, 2),
        third_start,
        third_band.T,
        fourth_start,
        fourth_band.T,
    )
    send, wide, inner = call(
        start_kernel,
        [(256, 128), (256, 256), jax.ShapeDtypeStruct((704, 128), jnp.bfloat16)],
        [pltpu.VMEM(value.shape, value.dtype) for value in inputs]
        + [pltpu.SemaphoreType.DMA((len(inputs),))]
        + [(16, N2 * N3), (16, N2 * N3), (256, 256)]
        + work,
        *inputs,
        left=range(len(inputs)),
        limit=LARGE,
    )
    recv = exchange(send)
    group = lax.axis_index("grp").reshape(1)
    *matrices, side = call(
        matrix_kernel,
        pair_of(2 * total, total) * 2 + pair_of(K0 * N1, total) + [(128, 256)],
        [(48, 128)] + [pltpu.VMEM((total, 128), jnp.bfloat16)] * 4,
        group, *outer,
        scalars=(0,),
    )
    gram, high, lift = matrices[0:2], matrices[2:4], matrices[4:6]
    send, fields, images = call(
        first_column_kernel, [(128, 128), (total, 128), (total, 128)], [], recv, *gram
    )
    recv = exchange(send)
    send, scalars = call(
        first_row_kernel, [(256, 128), (8, 128)], work, recv, wide, inner
    )
    recv = exchange(send)
    send, blend, scalars = call(
        second_column_kernel,
        [(128, 128), (total, 128), (8, 128)],
        [(total, 128), (total, 128)],
        recv, *gram, fields, images, scalars,
    )
    recv = exchange(send)
    send, keep, sums = call(
        middle_kernel,
        [(DEVICES * JOINT, 128), (K0 * N1, 128), (8, 128)],
        [],
        blend, *gram, *high, *lift, scalars,
    )
    (send,) = call(
        second_row_kernel,
        [(DEVICES * JOINT, 128)],
        work,
        send, recv, sums, wide, inner,
        aliases={0: 0},
    )
    recv = exchange(send)
    partner = lax.ppermute(recv, "grp", [(0, 1), (1, 0)])
    send, scalars = call(
        third_column_kernel,
        [(DEVICES * 10, 128), (8, 128)],
        [(total, 128), (K0 * N1, 128)],
        recv, *lift, keep, scalars,
    )
    late = exchange(send)
    solution_part, part = call(
        settle_kernel,
        [(4, 32, 1024), (128, 1024)],
        [(960, 128)],
        recv, partner, side, scalars,
    )
    (residual,) = call(final_kernel, [(4, 32, 1024)], [(320, 128)], late, side, part)
    return solution_part, residual


def fits(mesh):
    return (mesh.shape["slab"], mesh.shape["grp"]) == (SLABS, GRPS)


def solution(mesh):
    placed = (
        P("slab", "grp", None),
        P("slab", "grp", None),
        P(),
        P(),
        P(),
        P(),
        P(),
        P(),
        P(),
        P(),
    )
    return jax.shard_map(
        fast_program if fits(mesh) else per_device,
        mesh=mesh,
        in_specs=placed,
        out_specs=(P("slab", "grp", None), P("slab", "grp", None)),
        check_vma=False,
    )
```

```python
import jax
import jax.numpy as jnp
from jax import lax
from jax.experimental import pallas as pl
from jax.experimental.pallas import tpu as pltpu
from jax.sharding import PartitionSpec as P

K0 = 64
K1 = 64
K2 = 32
K3 = 32
ITERS = 2


highest = lax.Precision.HIGHEST
smoothing = 0.1
stencil_weights = (1.0, -4.0, 6.0, -4.0, 1.0)


def with_halo(value, sides, width):
    for axis, dim in sides:
        count, length = (lax.axis_size(axis), value.shape[dim])
        up = [(i, (i + 1) % count) for i in range(count - 1)]
        down = [(j, i) for i, j in up]
        last = lax.slice_in_dim(value, length - width, length, axis=dim)
        initial = lax.slice_in_dim(value, 0, width, axis=dim)
        before = lax.ppermute(last, axis, up)
        after = lax.ppermute(initial, axis, down)
        value = jnp.concatenate([before, value, after], axis=dim)
    return value


def dense_basis(starts, values, coef_count):
    relative = jnp.arange(coef_count, dtype=jnp.int32)[None, :] - starts[:, None]
    matrix = jnp.zeros((starts.shape[0], coef_count), jnp.float32)
    for offset in range(4):
        matrix = matrix + jnp.where(relative == offset, values[:, offset : offset + 1], 0.0)
    return matrix


def five_point(source, along, extent):
    running = stencil_weights[0] * lax.slice_in_dim(source, 0, extent, axis=along)
    for offset in range(1, 5):
        running = running + stencil_weights[offset] * lax.slice_in_dim(
            source, offset, offset + extent, axis=along
        )
    return running


def local_stencil(tensor, along):
    widths = [(0, 0)] * tensor.ndim
    widths[along] = (2, 2)
    return five_point(jnp.pad(tensor, widths), along, tensor.shape[along])


def inner_forward(tensor, third_basis, fourth_basis):
    leading, middle = (tensor.shape[0], tensor.shape[1])
    blocked = tensor.reshape(leading, middle, third_basis.shape[1], fourth_basis.shape[1])
    blocked = jnp.einsum("abcd,nd->abcn", blocked, fourth_basis, precision=highest)
    blocked = jnp.einsum("abcn,mc->abmn", blocked, third_basis, precision=highest)
    return blocked.reshape(leading, middle, third_basis.shape[0] * fourth_basis.shape[0])


def inner_adjoint(tensor, third_basis, fourth_basis):
    leading, middle = (tensor.shape[0], tensor.shape[1])
    blocked = tensor.reshape(leading, middle, third_basis.shape[0], fourth_basis.shape[0])
    blocked = jnp.einsum("abmn,mc->abcn", blocked, third_basis, precision=highest)
    blocked = jnp.einsum("abcn,nd->abcd", blocked, fourth_basis, precision=highest)
    return blocked.reshape(leading, middle, third_basis.shape[1] * fourth_basis.shape[1])


def lead_product(tensor, matrix):
    combined = jnp.einsum(
        "ka,ain->kin",
        matrix,
        lax.all_to_all(tensor, "slab", split_axis=2, concat_axis=0, tiled=True),
        precision=highest,
    )
    return lax.all_to_all(combined, "slab", split_axis=0, concat_axis=2, tiled=True)


def second_product(tensor, matrix):
    return jnp.einsum(
        "lp,apn->aln", matrix, lax.all_gather(tensor, "grp", axis=1, tiled=True), precision=highest
    )


def penalty(coeffs):
    leading, middle = (coeffs.shape[0], coeffs.shape[1])
    padded = with_halo(coeffs, (("slab", 0), ("grp", 1)), 2)
    along_lead = five_point(padded[:, 2 : 2 + middle], 0, leading)
    along_rows = five_point(padded[2 : 2 + leading, :], 1, middle)
    blocked = coeffs.reshape(leading, middle, K2, K3)
    inner_part = local_stencil(blocked, 2) + local_stencil(blocked, 3)
    return along_lead + along_rows + inner_part.reshape(leading, middle, K2 * K3)


def squared_total(vector):
    return lax.psum(jnp.sum(vector * vector), ("slab", "grp"))


def per_device(
    photon_table,
    bin_weights,
    first_start,
    first_band,
    second_start,
    second_band,
    third_start,
    third_band,
    fourth_start,
    fourth_band,
):
    first_basis = dense_basis(first_start, first_band, K0)
    second_basis = dense_basis(second_start, second_band, K1)
    third_basis = dense_basis(third_start, third_band, K2)
    fourth_basis = dense_basis(fourth_start, fourth_band, K3)
    first_back = first_basis.T
    group_index = lax.axis_index("grp")
    row_count = photon_table.shape[1]
    coef_rows = K1 // lax.axis_size("grp")
    near_rows = lax.dynamic_slice_in_dim(second_basis, group_index * row_count, row_count, 0)
    back_rows = lax.dynamic_slice_in_dim(second_basis.T, group_index * coef_rows, coef_rows, 0)

    def adjoint(table):
        tensor = lead_product(table, first_back)
        tensor = second_product(tensor, back_rows)
        return inner_adjoint(tensor, third_basis, fourth_basis)

    right_side = adjoint(bin_weights * photon_table)
    solution = jnp.zeros_like(right_side)
    residual = right_side
    direction = right_side
    norm_now = squared_total(residual)
    for sweep in range(ITERS):
        forward_tensor = inner_forward(direction, third_basis, fourth_basis)
        forward_tensor = second_product(forward_tensor, near_rows)
        mapped = adjoint(
            bin_weights * lead_product(forward_tensor, first_basis)
        ) + smoothing * penalty(direction)
        curve_total = lax.psum(jnp.sum(direction * mapped), ("slab", "grp"))
        step_size = norm_now / curve_total
        solution = solution + step_size * direction
        residual = residual - step_size * mapped
        norm_next = squared_total(residual)
        direction = residual + norm_next / norm_now * direction
        norm_now = norm_next
    return (solution, residual)


SLABS, GRPS = 16, 2
DEVICES = SLABS * GRPS
L0, L1 = 2, 5
ROWS = L0 * L1
N2, N3 = 64, 50
N0, N1 = 32, 10
HI = lax.Precision.HIGHEST
f32 = jnp.float32
JOINT = 19
LARGE = 60


def iota(shape, dim):
    return lax.broadcasted_iota(jnp.int32, shape, dim)


def mm(a, b):
    return jnp.dot(a, b, precision=HI, preferred_element_type=f32)


def mm_t(a, b):
    return lax.dot_general(
        a, b, (((1,), (1,)), ((), ())), precision=HI, preferred_element_type=f32
    )


def split(value):
    high = value.astype(jnp.bfloat16)
    return high, (value - high.astype(f32)).astype(jnp.bfloat16)


def product(a, b, transposed=False):
    dims = (((1,), (1 if transposed else 0,)), ((), ()))

    def one(x, y):
        return lax.dot_general(x, y, dims, preferred_element_type=f32)

    return one(a[0], b[0]) + (one(a[0], b[1]) + one(a[1], b[0]))


def load(pair):
    return pair[0][...], pair[1][...]


def move(block, source, target):
    shift = (target - source) * 32 % 128
    return pltpu.roll(block, shift, 1) if shift else block


def merge(parts):
    lane = iota(parts[0].shape, 1)
    out = parts[-1]
    for q in range(len(parts) - 2, -1, -1):
        out = jnp.where(lane < 32 * (q + 1), parts[q], out)
    return out


def slot(r):
    return L0 * (r % L1) + r // L1


def banded_t(start_ref, band_ref, width, wrap):
    n = start_ref.shape[0]
    relative = (iota((width, n), 0) % wrap) - start_ref[...].reshape(1, n)
    out = jnp.zeros((width, n), f32)
    for offset in range(4):
        out = out + jnp.where(relative == offset, band_ref[offset : offset + 1, :], 0.0)
    return out


def expand(ref, p):
    first = 200 * p
    tile, off = first // 128, first % 128
    lane = iota((16, 128), 1)

    def window(t):
        low = ref[:, t * 128 : (t + 1) * 128]
        if off == 0:
            return low
        t1 = min(t + 1, 24)
        high = ref[:, t1 * 128 : (t1 + 1) * 128]
        return jnp.where(
            lane < 128 - off, pltpu.roll(low, 128 - off, 1), pltpu.roll(high, 128 - off, 1)
        )

    return window(tile), window(min(tile + 1, 24))


def table_to_mixed(field, kron_third, second_t, rows_ref, stack_ref):
    rows_ref[...] = product(split(field), kron_third)
    for c in range(4):
        for j in range(3):
            parts = []
            for q in range(4):
                r = 4 * j + q
                if r < ROWS:
                    part = rows_ref[pl.ds(slot(r), 16, stride=16), :]
                    parts.append(move(part, c, q))
                else:
                    parts.append(jnp.zeros((16, 128), f32))
            stack_ref[16 * c : 16 * c + 16, 128 * j : 128 * j + 128] = merge(parts)
    return product(second_t, split(stack_ref[...]))


def mixed_to_table(value, kron_third, second, rows_ref, stack_ref):
    stack_ref[...] = product(second, split(value))
    rows_ref[...] = jnp.zeros((256, 128), f32)
    for r in range(ROWS):
        j, q = r // 4, r % 4
        parts = [
            move(stack_ref[16 * c : 16 * c + 16, 128 * j : 128 * j + 128], q, c) for c in range(4)
        ]
        rows_ref[pl.ds(slot(r), 16, stride=16), :] = merge(parts)
    return product(split(rows_ref[...]), kron_third, True)


def inner_penalty(value):
    out = 12.0 * value
    row = iota((32, 128), 0)
    inside = iota((32, 128), 1) % 32
    tiles = []
    for j in range(3):
        tile = value[:, 128 * j : 128 * j + 128]
        total = 12.0 * tile
        for d, weight in ((1, -4.0), (2, 1.0)):
            total = total + weight * (
                jnp.where(row >= d, pltpu.roll(tile, d, 0), 0.0)
                + jnp.where(row < 32 - d, pltpu.roll(tile, 32 - d, 0), 0.0)
                + jnp.where(inside >= d, pltpu.roll(tile, d, 1), 0.0)
                + jnp.where(inside < 32 - d, pltpu.roll(tile, 128 - d, 1), 0.0)
            )
        tiles.append(total)
    return jnp.concatenate(tiles, axis=1)


def tile_of(value, j):
    return value[:, 128 * j : 128 * j + 128]


def put(ref, row, count, value):
    ref[pl.ds(row, 32, stride=count), :] = value


def lanes(values):
    lane = iota((8, 128), 1)
    out = jnp.zeros((8, 128), f32)
    for k, value in enumerate(values):
        out = jnp.where(lane == k, value, out)
    return out


def spread(ref, row, count, values):
    one = lanes(values)
    put(ref, row, count, jnp.concatenate([one] * 4, axis=0))


def totals(ref, row, count, number):
    summed = jnp.sum(ref[pl.ds(row, 32, stride=count), :], axis=0, keepdims=True)
    lane = iota((1, 128), 1)
    return [jnp.sum(jnp.where(lane == k, summed, 0.0)) for k in range(number)]


def pick(ref, k):
    lane = iota((1, 128), 1)
    return jnp.sum(jnp.where(lane == k, ref[0:1, :], 0.0))


def constants(ref):
    kron = ref[0:256, :], ref[256:512, :]
    second = ref[512:576, 0:32], ref[576:640, 0:32]
    return kron, second, (ref[640:672, 0:64], ref[672:704, 0:64])


def start_kernel(
    table_hbm, weight_hbm, start2_hbm, band2_hbm, start3_hbm, band3_hbm,
    send_ref, wide_ref, inner_ref, mixed_ref,
    table_ref, weight_ref, start2_ref, band2_ref, start3_ref, band3_ref, sems,
    product_ref, packed_ref, field_ref, rows_ref, stack_ref,
):
    copies = [
        pltpu.make_async_copy(source, target, sems.at[k])
        for k, (source, target) in enumerate(
            (
                (start3_hbm, start3_ref),
                (band3_hbm, band3_ref),
                (start2_hbm, start2_ref),
                (band2_hbm, band2_ref),
                (weight_hbm, weight_ref),
                (table_hbm, table_ref),
            )
        )
    ]
    for copy in copies:
        copy.start()
    copies[0].wait()
    copies[1].wait()
    pick_bin = (iota((256, N3), 0) % N3 == iota((256, N3), 1)) & (iota((256, N3), 0) < 4 * N3)
    same = iota((256, 128), 0) // N3 == iota((256, 128), 1) // 32
    picker = jnp.where(pick_bin, 1.0, 0.0).astype(jnp.bfloat16)
    for k, term in enumerate(split(banded_t(start3_ref, band3_ref, 128, 32))):
        spread_out = lax.dot_general(
            picker, term, (((1,), (1,)), ((), ())), preferred_element_type=f32
        )
        inner_ref[256 * k : 256 * k + 256, :] = jnp.where(same, spread_out, 0.0).astype(jnp.bfloat16)
    copies[2].wait()
    copies[3].wait()
    order, other = iota((N2, N2), 1), iota((N2, N2), 0)
    permute = jnp.where((order % 16) * 4 + order // 16 == other, 1.0, 0.0).astype(jnp.bfloat16)
    back = jnp.where((other % 16) * 4 + other // 16 == order, 1.0, 0.0).astype(jnp.bfloat16)
    for k, term in enumerate(split(banded_t(start2_ref, band2_ref, 32, 32))):
        value = jnp.dot(term, permute, preferred_element_type=f32)
        inner_ref[640 + 32 * k : 672 + 32 * k, 0:64] = value.astype(jnp.bfloat16)
        value = lax.dot_general(back, term, (((1,), (1,)), ((), ())), preferred_element_type=f32)
        inner_ref[512 + 64 * k : 576 + 64 * k, 0:32] = value.astype(jnp.bfloat16)
    kron, _, turned = constants(inner_ref)
    copies[4].wait()
    copies[5].wait()
    packed_ref[8:16, :] = jnp.zeros((8, N2 * N3), f32)
    product_ref[8:16, :] = jnp.zeros((8, N2 * N3), f32)
    for b in range(L1):
        weight = weight_ref[b]
        packed_ref[L0 * b : L0 * b + L0, :] = weight
        product_ref[L0 * b : L0 * b + L0, :] = weight * table_ref[b]
    for p in range(16):
        for source, target in ((packed_ref, wide_ref), (product_ref, field_ref)):
            low, high = expand(source, p)
            target[16 * p : 16 * p + 16, 0:128] = low
            target[16 * p : 16 * p + 16, 128:256] = high
    mixed = table_to_mixed(field_ref[...], kron, turned, rows_ref, stack_ref)
    once = inner_penalty(mixed)
    mixed_ref[0:32, :] = mixed
    mixed_ref[32:64, :] = once
    for base, value in ((0, mixed), (3, once)):
        put(send_ref, base, 5, tile_of(value, 0))
        put(send_ref, base + 1, 5, tile_of(value, 1))
    lane = iota((32, 128), 1)
    put(send_ref, 2, 5, jnp.where(lane < 64, tile_of(mixed, 2), pltpu.roll(tile_of(once, 2), 64, 1)))


def pentadiagonal(n):
    gap = jnp.abs(iota((n, n), 0) - iota((n, n), 1))
    return jnp.where(gap == 0, 6.0, jnp.where(gap == 1, -4.0, jnp.where(gap == 2, 1.0, 0.0)))


def choose(pieces, selector):
    out = None
    for piece in pieces:
        term = jnp.dot(piece, selector, preferred_element_type=f32)
        out = term if out is None else out + term
    return out


def powers(basis_t, count):
    penalty_matrix = pentadiagonal(basis_t.shape[0])
    out = [basis_t]
    for _ in range(count - 1):
        out.append(mm(penalty_matrix, out[-1]))
    return out


def store_split(high_ref, low_ref, rows, value):
    high, low = split(value)
    high_ref[rows, :] = high
    low_ref[rows, :] = low


def matrix_kernel(
    group_ref, start0_ref, band0_ref, start1_ref, band1_ref,
    gram_h_ref, gram_l_ref, high_h_ref, high_l_ref, lift_h_ref, lift_l_ref, side_ref,
    small_ref, rows0_h, rows0_l, rows1_h, rows1_l,
):
    total = DEVICES * ROWS
    powers0 = powers(banded_t(start0_ref, band0_ref, K0, K0), 4)
    powers1 = powers(banded_t(start1_ref, band1_ref, K1, K1), 4)
    small_ref[...] = jnp.zeros((48, 128), f32)
    first, second = powers0[0].T, powers1[0].T
    for k in range(4):
        small_ref[0:N0, 32 * k : 32 * k + N0] = mm(first, powers0[k])
        small_ref[N0 : N0 + N1, 32 * k : 32 * k + N1] = mm(second, powers1[k])
    row0 = iota((total, N0), 0)
    pick0 = L0 * (row0 % 32 // GRPS) + row0 // 32 // L1 == iota((total, N0), 1)
    row1 = iota((total, 16), 0)
    pick1 = L1 * (row1 % GRPS) + row1 // 32 % L1 == iota((total, 16), 1)
    for pick, rows, targets in (
        (pick0, slice(0, N0), (rows0_h, rows0_l)),
        (pick1, slice(N0, N0 + 16), (rows1_h, rows1_l)),
    ):
        chooser = jnp.where(pick, 1.0, 0.0).astype(jnp.bfloat16)
        for term, target in zip(split(small_ref[rows, :]), targets):
            spread_out = jnp.dot(chooser, term, preferred_element_type=f32)
            target[...] = spread_out.astype(jnp.bfloat16)
    line, column = iota((128, total), 0), iota((128, total), 1)
    match0 = line % 32 == L0 * (column % 32 // GRPS) + column // 32 // L1
    match1 = line % 32 == L1 * (column % GRPS) + column // 32 % L1
    select0 = [
        jnp.where(match0 & (line // 32 == k), 1.0, 0.0).astype(jnp.bfloat16) for k in range(4)
    ]
    select1 = [
        jnp.where(match1 & (line // 32 == k), 1.0, 0.0).astype(jnp.bfloat16) for k in range(4)
    ]

    @pl.loop(0, 5)
    def _(step):
        base = pl.multiple_of(step * 64, 64)
        block0 = rows0_h[pl.ds(base, 64), :], rows0_l[pl.ds(base, 64), :]
        block1 = rows1_h[pl.ds(base, 64), :], rows1_l[pl.ds(base, 64), :]
        g = [choose(block0, selector) for selector in select0]
        h = [choose(block1, selector) for selector in select1]
        first_power = g[1] * h[0] + g[0] * h[1]
        squared = g[2] * h[0] + 2.0 * g[1] * h[1] + g[0] * h[2]
        cubed = g[3] * h[0] + 3.0 * (g[2] * h[1] + g[1] * h[2]) + g[0] * h[3]
        store_split(gram_h_ref, gram_l_ref, pl.ds(base, 64), g[0] * h[0])
        store_split(gram_h_ref, gram_l_ref, pl.ds(base + total, 64), first_power)
        store_split(high_h_ref, high_l_ref, pl.ds(base, 64), squared)
        store_split(high_h_ref, high_l_ref, pl.ds(base + total, 64), cubed)

    lifted = [
        jnp.dot(term, select0[0][0:N0, :], preferred_element_type=f32)
        for term in split(powers0[0])
    ]
    owner = L1 * (iota((K0, total), 1) % GRPS) + iota((K0, total), 1) // 32 % L1
    for n in range(N1):
        rows = slice(K0 * n, K0 * n + K0)
        for term, target in zip(lifted, (lift_h_ref, lift_l_ref)):
            target[rows, :] = jnp.where(owner == n, term, 0.0).astype(jnp.bfloat16)
    group = group_ref[0]
    coef = iota((128, K1), 0) % 32 + 32 * group
    pick_coef = jnp.where(coef == iota((128, K1), 1), 1.0, 0.0)
    half = iota((N1, N1), 1) // L1
    wanted = L1 * jnp.where(half == group, 0, 1) + iota((N1, N1), 1) % L1
    reorder = jnp.where(iota((N1, N1), 0) == wanted, 1.0, 0.0)
    side_ref[...] = jnp.zeros((128, 384), f32)
    for k in range(3):
        own = mm(pick_coef, powers1[k])
        halves = mm(own, reorder)
        for alpha in range(4):
            rows = slice(32 * alpha, 32 * alpha + 32)
            if k == 0:
                side_ref[rows, 10 * alpha : 10 * alpha + 10] = own[rows, :]
            for h in range(2):
                piece = halves[rows, L1 * h : L1 * h + L1]
                place = 40 * k + 20 * h + L1 * alpha
                side_ref[rows, 256 + place : 256 + place + L1] = piece
                if k < 2:
                    side_ref[rows, 128 + place : 128 + place + L1] = piece


def unpack(ref, row, count, r, source, target):
    return move(ref[pl.ds(row, 32, stride=count), :], source, target)


def first_column_kernel(recv_ref, gram_h_ref, gram_l_ref, send_ref, fields_ref, images_ref):
    total = DEVICES * ROWS
    zero = jnp.zeros((32, 128), f32)
    for r in range(ROWS):
        j, q = r // 4, r % 4
        where0 = (j, q) if j < 2 else (2, q)
        where1 = (3 + j, q) if j < 2 else (2, q + 2)
        parts = [
            unpack(recv_ref, place[0], 5, r, place[1], k) for k, place in enumerate((where0, where1))
        ]
        fields_ref[32 * r : 32 * r + 32, :] = merge(parts + [zero])
    fields = fields_ref[...]
    applied = product(load((gram_h_ref, gram_l_ref)), split(fields))
    lane = iota((total, 128), 1)
    images = applied[:total] + jnp.where(
        (lane >= 32) & (lane < 64), pltpu.roll(applied[total:], 32, 1), 0.0
    )
    images_ref[...] = images
    norm = jnp.sum(jnp.where(lane < 32, fields * images, 0.0))
    bend = jnp.sum(jnp.where(lane < 32, fields * pltpu.roll(images, 96, 1), 0.0))
    send_rows(send_ref, images_ref)
    spread(send_ref, 3, 4, (norm, bend))


def send_rows(send_ref, value_ref):
    for j in range(3):
        parts = []
        for q in range(4):
            r = 4 * j + q
            if r < ROWS:
                parts.append(move(value_ref[32 * r : 32 * r + 32, :], 0, q))
            else:
                parts.append(jnp.zeros((32, 128), f32))
        put(send_ref, j, 4, merge(parts))


def received_rows(recv_ref):
    return jnp.concatenate([recv_ref[pl.ds(j, 32, stride=4), :] for j in range(3)], axis=1)


def first_row_kernel(
    recv_ref, wide_ref, inner_ref, start_ref, send_ref, scalar_ref, mixed_ref, rows_ref, stack_ref,
):
    norm, bend = totals(recv_ref, 3, 4, 2)
    scalar_ref[...] = lanes((norm, bend))
    kron, second, turned = constants(inner_ref)
    field = mixed_to_table(received_rows(recv_ref), kron, second, rows_ref, stack_ref)
    weighted = wide_ref[...] * field
    energy = jnp.sum(field * weighted)
    mixed = table_to_mixed(weighted, kron, turned, rows_ref, stack_ref)
    mixed_ref[0:32, :] = mixed
    mixed_ref[32:96, :] = start_ref[...]
    for j in range(3):
        put(send_ref, j, 4, tile_of(mixed, j))
    spread(send_ref, 3, 4, (energy,))


def second_column_kernel(
    recv_ref, gram_h_ref, gram_l_ref, fields_ref, images_ref, scalar_ref,
    send_ref, blend_ref, out_scalar_ref, next_ref, image_ref,
):
    zero = jnp.zeros((32, 128), f32)
    for r in range(ROWS):
        part = unpack(recv_ref, r // 4, 4, r, r % 4, 0)
        next_ref[32 * r : 32 * r + 32, :] = merge([part, zero])
    (energy,) = totals(recv_ref, 3, 4, 1)
    norm, bend = pick(scalar_ref, 0), pick(scalar_ref, 1)
    step = norm / (energy + 0.1 * bend)
    out_scalar_ref[...] = lanes((norm, step))
    fields, images, following = fields_ref[...], images_ref[...], next_ref[...]
    gram = gram_h_ref[0 : DEVICES * ROWS, :], gram_l_ref[0 : DEVICES * ROWS, :]
    image = product(gram, split(following))
    image_ref[...] = images - step * (image + 0.1 * pltpu.roll(images, 96, 1))
    send_rows(send_ref, image_ref)
    put(send_ref, 3, 4, zero)
    lane = iota(fields.shape, 1)
    reduced = fields - step * (following + 0.1 * pltpu.roll(fields, 96, 1))
    kept = jnp.where(lane < 64, 0.0, pltpu.roll(fields, 64, 1))
    blend_ref[...] = jnp.where(lane < 32, reduced, kept)


def coefficient_penalty(value):
    k = iota(value.shape, 0) % K0
    count = value.shape[0]
    total = 6.0 * value
    for d, weight in ((1, -4.0), (2, 1.0)):
        total = total + weight * (
            jnp.where(k >= d, pltpu.roll(value, d, 0), 0.0)
            + jnp.where(k < K0 - d, pltpu.roll(value, count - d, 0), 0.0)
        )
    return total


def send_blocks(send_ref, count, base, value_ref, block):
    for j in range(10):
        parts = []
        for q in range(4):
            m = 4 * j + q
            alpha, n = m // 10, m % 10
            parts.append(move(value_ref[pl.ds(K0 * n + alpha, 16, stride=4), :], block, q))
        merged = merge(parts)
        for g in range(GRPS):
            send_ref[pl.ds(g * count + base + j, 16, stride=2 * count), :] = merged


def send_halves(send_ref, count, base, value_ref, block):
    for g in range(GRPS):
        for j in range(5):
            parts = []
            for q in range(4):
                alpha, b = divmod(4 * j + q, L1)
                row = K0 * (L1 * g + b) + alpha
                parts.append(move(value_ref[pl.ds(row, 16, stride=4), :], block, q))
            send_ref[pl.ds(g * count + base + j, 16, stride=2 * count), :] = merge(parts)


def middle_kernel(
    blend_ref, gram_h_ref, gram_l_ref, high_h_ref, high_l_ref, lift_h_ref, lift_l_ref, scalar_ref,
    send_ref, keep_ref, sums_ref,
):
    total = DEVICES * ROWS
    step = pick(scalar_ref, 1)
    small = 0.1 * step
    blend = blend_ref[...]
    lane = iota(blend.shape, 1)
    pair = split(blend)
    lower = product(load((gram_h_ref, gram_l_ref)), pair)
    higher = product(load((high_h_ref, high_l_ref)), pair)
    g0, g1, g2, g3 = lower[:total], lower[total:], higher[:total], higher[total:]
    head = g0 - small * pltpu.roll(g1, 64, 1)
    tail = g1 - small * pltpu.roll(g2, 64, 1)
    end = g2 - small * pltpu.roll(g3, 64, 1)
    scaled = pltpu.roll(blend, 64, 1)
    low = lane < 32
    norm = jnp.sum(jnp.where(low, blend * head - small * scaled * tail, 0.0))
    head_p = tail + pltpu.roll(head, 96, 1)
    tail_p = end + pltpu.roll(tail, 96, 1)
    bend = jnp.sum(jnp.where(low, blend * head_p - small * scaled * tail_p, 0.0))
    sums_ref[...] = lanes((norm, bend))
    lifted = product(load((lift_h_ref, lift_l_ref)), pair)
    once = coefficient_penalty(lifted)
    twice = coefficient_penalty(once)
    h_a = lifted - small * pltpu.roll(once, 64, 1)
    y_1 = once + pltpu.roll(lifted, 96, 1)
    x_a = once - small * pltpu.roll(twice, 64, 1)
    h_0 = pltpu.roll(lifted, 64, 1)
    wide = iota(lifted.shape, 1)
    keep = jnp.where(
        wide < 32, h_0, jnp.where(wide < 64, pltpu.roll(h_a, 32, 1), jnp.where(wide < 96, y_1, pltpu.roll(x_a, 96, 1)))
    )
    keep_ref[...] = keep
    for block in range(3):
        send_halves(send_ref, JOINT, 4 + 5 * block, keep_ref, block)


def second_row_kernel(
    early_ref, recv_ref, sums_ref, scalar_ref, mixed_ref, wide_ref, inner_ref,
    send_ref, rows_ref, stack_ref,
):
    kron, second, turned = constants(inner_ref)
    image = received_rows(recv_ref)
    step = pick(scalar_ref, 1)
    reduced = mixed_ref[32:64, :] - step * (mixed_ref[0:32, :] + 0.1 * mixed_ref[64:96, :])
    inner = jnp.sum(reduced * inner_penalty(image))
    field = mixed_to_table(image, kron, second, rows_ref, stack_ref)
    weighted = wide_ref[...] * field
    energy = jnp.sum(field * weighted)
    mixed = table_to_mixed(weighted, kron, turned, rows_ref, stack_ref)
    for j in range(3):
        put(send_ref, j, JOINT, tile_of(mixed, j))
    spread(send_ref, 3, JOINT, (energy, pick(sums_ref, 0), pick(sums_ref, 1) + inner))


def third_column_kernel(
    recv_ref, lift_h_ref, lift_l_ref, keep_ref, scalar_ref, send_ref, out_scalar_ref, last_ref, mixed_ref
):
    zero = jnp.zeros((32, 128), f32)
    for r in range(ROWS):
        j, q = r // 4, r % 4
        last_ref[32 * r : 32 * r + 32, :] = unpack(recv_ref, j, JOINT, r, q, 0)
    energy, norm_next, bend = totals(recv_ref, 3, JOINT, 3)
    norm, step = pick(scalar_ref, 0), pick(scalar_ref, 1)
    ratio = norm_next / norm
    curve = energy + 0.1 * bend - ratio * norm_next / step
    step_next = norm_next / curve
    out_scalar_ref[...] = lanes((norm, step, ratio, step_next))
    lifted = product(load((lift_h_ref, lift_l_ref)), split(last_ref[...]))
    keep = keep_ref[...]
    h_a, x_a = pltpu.roll(keep, 96, 1), pltpu.roll(keep, 32, 1)
    mixed_ref[...] = (
        h_a - step_next * (lifted + 0.1 * x_a) - (step_next * ratio / step) * (keep - h_a)
    )
    send_blocks(send_ref, 10, 0, mixed_ref, 0)


def gather_blocks(ref, count, base, rows, out_ref, first):
    for j in range(rows):
        taken = [ref[pl.ds(rho * count + base + j, 8, stride=4 * count), :] for rho in range(4)]
        for q in range(4):
            m = first + 4 * j + q
            merged = merge([move(taken[rho], q, rho) for rho in range(4)])
            out_ref[pl.ds(m // 8 * 64 + m % 8, 8, stride=8), :] = merged


def take(ref, block, tile):
    return jnp.concatenate(
        [ref[pl.ds((5 * block + t) * 64 + 8 * tile, 8), :] for t in range(5)], axis=0
    )


def bent_rows(value):
    lane = iota(value.shape, 1)
    inside = lane % 32
    total = 12.0 * value
    for d, weight in ((1, -4.0), (2, 1.0)):
        total = total + weight * (
            jnp.where(lane >= 32 * d, pltpu.roll(value, 32 * d, 1), 0.0)
            + jnp.where(lane < 1024 - 32 * d, pltpu.roll(value, 1024 - 32 * d, 1), 0.0)
            + jnp.where(inside >= d, pltpu.roll(value, d, 1), 0.0)
            + jnp.where(inside < 32 - d, pltpu.roll(value, 1024 - d, 1), 0.0)
        )
    return total


def settle_kernel(own_ref, partner_ref, side_ref, scalar_ref, solution_ref, part_ref, early):
    for block in range(3):
        for h, ref in enumerate((own_ref, partner_ref)):
            gather_blocks(ref, JOINT, 4 + 5 * block, 5, early, 40 * block + 20 * h)
    step, ratio, step_next = pick(scalar_ref, 1), pick(scalar_ref, 2), pick(scalar_ref, 3)
    small = 0.1 * step
    value = split(side_ref[:, 128:208])
    slope = split(side_ref[:, 256:376])
    bent = bent_rows(jnp.concatenate([take(early, 1, tile) for tile in range(8)], axis=1))
    for tile in range(8):
        h_0, h_a, y_1 = take(early, 0, tile), take(early, 1, tile), take(early, 2, tile)
        right = jnp.concatenate(
            [(step + step_next * ratio) * h_0 + step_next * h_a, (-step_next * small) * h_0], axis=0
        )
        columns = slice(128 * tile, 128 * tile + 128)
        solution_ref[:, :, columns] = product(value, split(right)).reshape(4, 32, 128)
        right = jnp.concatenate(
            [
                (-0.1 * step_next) * bent[:, columns],
                (-small * (1.0 + step_next * ratio / step)) * h_0
                - (0.1 * step_next) * (h_a - small * y_1),
                (0.1 * step_next * small) * h_0,
            ],
            axis=0,
        )
        part_ref[:, columns] = product(slope, split(right))


def final_kernel(late_ref, side_ref, part_ref, residual_ref, late):
    gather_blocks(late_ref, 10, 0, 10, late, 0)
    value = split(side_ref[:, 0:40])
    for tile in range(8):
        columns = slice(128 * tile, 128 * tile + 128)
        whole = part_ref[:, columns] + product(value, split(take(late, 0, tile)))
        residual_ref[:, :, columns] = whole.reshape(4, 32, 128)


def call(kernel, outputs, scratch, *operands, aliases={}, left=(), scalars=(), limit=16):
    vmem = pl.BlockSpec(memory_space=pltpu.VMEM)
    specs = [vmem] * len(operands)
    for k in left:
        specs[k] = pl.BlockSpec(memory_space=pltpu.HBM)
    for k in scalars:
        specs[k] = pl.BlockSpec(memory_space=pltpu.SMEM)
    return pl.pallas_call(
        kernel,
        out_shape=[
            shape if isinstance(shape, jax.ShapeDtypeStruct) else jax.ShapeDtypeStruct(shape, f32)
            for shape in outputs
        ],
        in_specs=specs,
        out_specs=[vmem] * len(outputs),
        scratch_shapes=[
            pltpu.VMEM(shape, f32) if isinstance(shape, tuple) else shape for shape in scratch
        ],
        input_output_aliases=aliases,
        compiler_params=pltpu.CompilerParams(vmem_limit_bytes=limit * 2**20),
    )(*operands)


def pair_of(*shape):
    return [jax.ShapeDtypeStruct(shape, jnp.bfloat16)] * 2


def exchange(buffer):
    count = buffer.shape[0] // DEVICES
    tiled = count == 4 or count % 8 == 0
    shape = (DEVICES, count, 128) if tiled else (DEVICES, 1, count * 128)
    moved = lax.all_to_all(buffer.reshape(shape), ("slab", "grp"), 0, 0, tiled=True)
    return moved.reshape(buffer.shape)


def fast_program(
    photon_table,
    bin_weights,
    first_start,
    first_band,
    second_start,
    second_band,
    third_start,
    third_band,
    fourth_start,
    fourth_band,
):
    total = DEVICES * ROWS
    work = [(256, 128), (64, 384)]
    outer = (first_start, first_band.T, second_start, second_band.T)
    inputs = (
        photon_table.transpose(1, 0, 2),
        bin_weights.transpose(1, 0, 2),
        third_start,
        third_band.T,
        fourth_start,
        fourth_band.T,
    )
    send, wide, inner, mixed0 = call(
        start_kernel,
        [(160, 128), (256, 256), jax.ShapeDtypeStruct((704, 128), jnp.bfloat16), (64, 384)],
        [pltpu.VMEM(value.shape, value.dtype) for value in inputs]
        + [pltpu.SemaphoreType.DMA((len(inputs),))]
        + [(16, N2 * N3), (16, N2 * N3), (256, 256)]
        + work,
        *inputs,
        left=range(len(inputs)),
        limit=LARGE,
    )
    recv = exchange(send)
    group = lax.axis_index("grp").reshape(1)
    *matrices, side = call(
        matrix_kernel,
        pair_of(2 * total, total) * 2 + pair_of(K0 * N1, total) + [(128, 384)],
        [(48, 128)] + [pltpu.VMEM((total, 128), jnp.bfloat16)] * 4,
        group, *outer,
        scalars=(0,),
    )
    gram, high, lift = matrices[0:2], matrices[2:4], matrices[4:6]
    send, fields, images = call(
        first_column_kernel, [(128, 128), (total, 128), (total, 128)], [], recv, *gram
    )
    recv = exchange(send)
    send, scalars, mixed1 = call(
        first_row_kernel, [(128, 128), (8, 128), (96, 384)], work, recv, wide, inner, mixed0
    )
    recv = exchange(send)
    send, blend, scalars = call(
        second_column_kernel,
        [(128, 128), (total, 128), (8, 128)],
        [(total, 128), (total, 128)],
        recv, *gram, fields, images, scalars,
        aliases={3: 1},
    )
    recv = exchange(send)
    send, keep, sums = call(
        middle_kernel,
        [(DEVICES * JOINT, 128), (K0 * N1, 128), (8, 128)],
        [],
        blend, *gram, *high, *lift, scalars,
    )
    (send,) = call(
        second_row_kernel,
        [(DEVICES * JOINT, 128)],
        work,
        send, recv, sums, scalars, mixed1, wide, inner,
        aliases={0: 0},
    )
    recv = exchange(send)
    partner = lax.ppermute(recv, "grp", [(0, 1), (1, 0)])
    send, scalars = call(
        third_column_kernel,
        [(DEVICES * 10, 128), (8, 128)],
        [(total, 128), (K0 * N1, 128)],
        recv, *lift, keep, scalars,
    )
    late = exchange(send)
    solution_part, part = call(
        settle_kernel,
        [(4, 32, 1024), (128, 1024)],
        [(960, 128)],
        recv, partner, side, scalars,
    )
    (residual,) = call(final_kernel, [(4, 32, 1024)], [(320, 128)], late, side, part)
    return solution_part, residual


def fits(mesh):
    return (mesh.shape["slab"], mesh.shape["grp"]) == (SLABS, GRPS)


def solution(mesh):
    placed = (
        P("slab", "grp", None),
        P("slab", "grp", None),
        P(),
        P(),
        P(),
        P(),
        P(),
        P(),
        P(),
        P(),
    )
    return jax.shard_map(
        fast_program if fits(mesh) else per_device,
        mesh=mesh,
        in_specs=placed,
        out_specs=(P("slab", "grp", None), P("slab", "grp", None)),
        check_vma=False,
    )
```

```python
import jax
import jax.numpy as jnp
from jax import lax
from jax.experimental import pallas as pl
from jax.experimental.pallas import tpu as pltpu
from jax.sharding import PartitionSpec as P

K0 = 64
K1 = 64
K2 = 32
K3 = 32
ITERS = 2


highest = lax.Precision.HIGHEST
smoothing = 0.1
stencil_weights = (1.0, -4.0, 6.0, -4.0, 1.0)


def with_halo(value, sides, width):
    for axis, dim in sides:
        count, length = (lax.axis_size(axis), value.shape[dim])
        up = [(i, (i + 1) % count) for i in range(count - 1)]
        down = [(j, i) for i, j in up]
        last = lax.slice_in_dim(value, length - width, length, axis=dim)
        initial = lax.slice_in_dim(value, 0, width, axis=dim)
        before = lax.ppermute(last, axis, up)
        after = lax.ppermute(initial, axis, down)
        value = jnp.concatenate([before, value, after], axis=dim)
    return value


def dense_basis(starts, values, coef_count):
    relative = jnp.arange(coef_count, dtype=jnp.int32)[None, :] - starts[:, None]
    matrix = jnp.zeros((starts.shape[0], coef_count), jnp.float32)
    for offset in range(4):
        matrix = matrix + jnp.where(relative == offset, values[:, offset : offset + 1], 0.0)
    return matrix


def five_point(source, along, extent):
    running = stencil_weights[0] * lax.slice_in_dim(source, 0, extent, axis=along)
    for offset in range(1, 5):
        running = running + stencil_weights[offset] * lax.slice_in_dim(
            source, offset, offset + extent, axis=along
        )
    return running


def local_stencil(tensor, along):
    widths = [(0, 0)] * tensor.ndim
    widths[along] = (2, 2)
    return five_point(jnp.pad(tensor, widths), along, tensor.shape[along])


def inner_forward(tensor, third_basis, fourth_basis):
    leading, middle = (tensor.shape[0], tensor.shape[1])
    blocked = tensor.reshape(leading, middle, third_basis.shape[1], fourth_basis.shape[1])
    blocked = jnp.einsum("abcd,nd->abcn", blocked, fourth_basis, precision=highest)
    blocked = jnp.einsum("abcn,mc->abmn", blocked, third_basis, precision=highest)
    return blocked.reshape(leading, middle, third_basis.shape[0] * fourth_basis.shape[0])


def inner_adjoint(tensor, third_basis, fourth_basis):
    leading, middle = (tensor.shape[0], tensor.shape[1])
    blocked = tensor.reshape(leading, middle, third_basis.shape[0], fourth_basis.shape[0])
    blocked = jnp.einsum("abmn,mc->abcn", blocked, third_basis, precision=highest)
    blocked = jnp.einsum("abcn,nd->abcd", blocked, fourth_basis, precision=highest)
    return blocked.reshape(leading, middle, third_basis.shape[1] * fourth_basis.shape[1])


def lead_product(tensor, matrix):
    combined = jnp.einsum(
        "ka,ain->kin",
        matrix,
        lax.all_to_all(tensor, "slab", split_axis=2, concat_axis=0, tiled=True),
        precision=highest,
    )
    return lax.all_to_all(combined, "slab", split_axis=0, concat_axis=2, tiled=True)


def second_product(tensor, matrix):
    return jnp.einsum(
        "lp,apn->aln", matrix, lax.all_gather(tensor, "grp", axis=1, tiled=True), precision=highest
    )


def penalty(coeffs):
    leading, middle = (coeffs.shape[0], coeffs.shape[1])
    padded = with_halo(coeffs, (("slab", 0), ("grp", 1)), 2)
    along_lead = five_point(padded[:, 2 : 2 + middle], 0, leading)
    along_rows = five_point(padded[2 : 2 + leading, :], 1, middle)
    blocked = coeffs.reshape(leading, middle, K2, K3)
    inner_part = local_stencil(blocked, 2) + local_stencil(blocked, 3)
    return along_lead + along_rows + inner_part.reshape(leading, middle, K2 * K3)


def squared_total(vector):
    return lax.psum(jnp.sum(vector * vector), ("slab", "grp"))


def per_device(
    photon_table,
    bin_weights,
    first_start,
    first_band,
    second_start,
    second_band,
    third_start,
    third_band,
    fourth_start,
    fourth_band,
):
    first_basis = dense_basis(first_start, first_band, K0)
    second_basis = dense_basis(second_start, second_band, K1)
    third_basis = dense_basis(third_start, third_band, K2)
    fourth_basis = dense_basis(fourth_start, fourth_band, K3)
    first_back = first_basis.T
    group_index = lax.axis_index("grp")
    row_count = photon_table.shape[1]
    coef_rows = K1 // lax.axis_size("grp")
    near_rows = lax.dynamic_slice_in_dim(second_basis, group_index * row_count, row_count, 0)
    back_rows = lax.dynamic_slice_in_dim(second_basis.T, group_index * coef_rows, coef_rows, 0)

    def adjoint(table):
        tensor = lead_product(table, first_back)
        tensor = second_product(tensor, back_rows)
        return inner_adjoint(tensor, third_basis, fourth_basis)

    right_side = adjoint(bin_weights * photon_table)
    solution = jnp.zeros_like(right_side)
    residual = right_side
    direction = right_side
    norm_now = squared_total(residual)
    for sweep in range(ITERS):
        forward_tensor = inner_forward(direction, third_basis, fourth_basis)
        forward_tensor = second_product(forward_tensor, near_rows)
        mapped = adjoint(
            bin_weights * lead_product(forward_tensor, first_basis)
        ) + smoothing * penalty(direction)
        curve_total = lax.psum(jnp.sum(direction * mapped), ("slab", "grp"))
        step_size = norm_now / curve_total
        solution = solution + step_size * direction
        residual = residual - step_size * mapped
        norm_next = squared_total(residual)
        direction = residual + norm_next / norm_now * direction
        norm_now = norm_next
    return (solution, residual)


SLABS, GRPS = 16, 2
DEVICES = SLABS * GRPS
L0, L1 = 2, 5
ROWS = L0 * L1
N2, N3 = 64, 50
N0, N1 = 32, 10
HI = lax.Precision.HIGHEST
f32 = jnp.float32
JOINT = 19
LARGE = 60


def iota(shape, dim):
    return lax.broadcasted_iota(jnp.int32, shape, dim)


def mm(a, b):
    return jnp.dot(a, b, precision=HI, preferred_element_type=f32)


def mm_t(a, b):
    return lax.dot_general(
        a, b, (((1,), (1,)), ((), ())), precision=HI, preferred_element_type=f32
    )


def split(value):
    high = value.astype(jnp.bfloat16)
    return high, (value - high.astype(f32)).astype(jnp.bfloat16)


def product(a, b, transposed=False):
    dims = (((1,), (1 if transposed else 0,)), ((), ()))

    def one(x, y):
        return lax.dot_general(x, y, dims, preferred_element_type=f32)

    return one(a[0], b[0]) + (one(a[0], b[1]) + one(a[1], b[0]))


def load(pair):
    return pair[0][...], pair[1][...]


def move(block, source, target):
    shift = (target - source) * 32 % 128
    return pltpu.roll(block, shift, 1) if shift else block


def merge(parts):
    lane = iota(parts[0].shape, 1)
    out = parts[-1]
    for q in range(len(parts) - 2, -1, -1):
        out = jnp.where(lane < 32 * (q + 1), parts[q], out)
    return out


def slot(r):
    return L0 * (r % L1) + r // L1


def banded_t(start_ref, band_ref, width, wrap):
    n = start_ref.shape[0]
    relative = (iota((width, n), 0) % wrap) - start_ref[...].reshape(1, n)
    out = jnp.zeros((width, n), f32)
    for offset in range(4):
        out = out + jnp.where(relative == offset, band_ref[offset : offset + 1, :], 0.0)
    return out


def expand(ref, p):
    first = 200 * p
    tile, off = first // 128, first % 128
    lane = iota((16, 128), 1)

    def window(t):
        low = ref[:, t * 128 : (t + 1) * 128]
        if off == 0:
            return low
        t1 = min(t + 1, 24)
        high = ref[:, t1 * 128 : (t1 + 1) * 128]
        return jnp.where(
            lane < 128 - off, pltpu.roll(low, 128 - off, 1), pltpu.roll(high, 128 - off, 1)
        )

    return window(tile), window(min(tile + 1, 24))


def table_to_mixed(field, kron_third, second_t, rows_ref, stack_ref):
    rows_ref[...] = product(split(field), kron_third)
    for c in range(4):
        for j in range(3):
            parts = []
            for q in range(4):
                r = 4 * j + q
                if r < ROWS:
                    part = rows_ref[pl.ds(slot(r), 16, stride=16), :]
                    parts.append(move(part, c, q))
                else:
                    parts.append(jnp.zeros((16, 128), f32))
            stack_ref[16 * c : 16 * c + 16, 128 * j : 128 * j + 128] = merge(parts)
    return product(second_t, split(stack_ref[...]))


def mixed_to_table(value, kron_third, second, rows_ref, stack_ref):
    stack_ref[...] = product(second, split(value))
    rows_ref[...] = jnp.zeros((256, 128), f32)
    for r in range(ROWS):
        j, q = r // 4, r % 4
        parts = [
            move(stack_ref[16 * c : 16 * c + 16, 128 * j : 128 * j + 128], q, c) for c in range(4)
        ]
        rows_ref[pl.ds(slot(r), 16, stride=16), :] = merge(parts)
    return product(split(rows_ref[...]), kron_third, True)


def inner_penalty(value):
    out = 12.0 * value
    row = iota((32, 128), 0)
    inside = iota((32, 128), 1) % 32
    tiles = []
    for j in range(3):
        tile = value[:, 128 * j : 128 * j + 128]
        total = 12.0 * tile
        for d, weight in ((1, -4.0), (2, 1.0)):
            total = total + weight * (
                jnp.where(row >= d, pltpu.roll(tile, d, 0), 0.0)
                + jnp.where(row < 32 - d, pltpu.roll(tile, 32 - d, 0), 0.0)
                + jnp.where(inside >= d, pltpu.roll(tile, d, 1), 0.0)
                + jnp.where(inside < 32 - d, pltpu.roll(tile, 128 - d, 1), 0.0)
            )
        tiles.append(total)
    return jnp.concatenate(tiles, axis=1)


def tile_of(value, j):
    return value[:, 128 * j : 128 * j + 128]


def put(ref, row, count, value):
    ref[pl.ds(row, 32, stride=count), :] = value


def lanes(values):
    lane = iota((8, 128), 1)
    out = jnp.zeros((8, 128), f32)
    for k, value in enumerate(values):
        out = jnp.where(lane == k, value, out)
    return out


def spread(ref, row, count, values):
    one = lanes(values)
    put(ref, row, count, jnp.concatenate([one] * 4, axis=0))


def totals(ref, row, count, number):
    summed = jnp.sum(ref[pl.ds(row, 32, stride=count), :], axis=0, keepdims=True)
    lane = iota((1, 128), 1)
    return [jnp.sum(jnp.where(lane == k, summed, 0.0)) for k in range(number)]


def pick(ref, k):
    lane = iota((1, 128), 1)
    return jnp.sum(jnp.where(lane == k, ref[0:1, :], 0.0))


def constants(ref):
    kron = ref[0:256, :], ref[256:512, :]
    second = ref[512:576, 0:32], ref[576:640, 0:32]
    return kron, second, (ref[640:672, 0:64], ref[672:704, 0:64])


def row_tile(piece, j):
    place = 3 * piece + j
    first = 256 + 32 * (place // 2)
    return slice(first, first + 32), slice(128 * (place % 2), 128 * (place % 2) + 128)


def keep_rows(ref, piece, value):
    for j in range(3):
        ref[row_tile(piece, j)] = tile_of(value, j)


def kept_rows(ref, piece):
    return jnp.concatenate([ref[row_tile(piece, j)] for j in range(3)], axis=1)


def start_kernel(
    table_hbm, weight_hbm, start2_hbm, band2_hbm, start3_hbm, band3_hbm,
    send_ref, wide_ref, inner_ref,
    table_ref, weight_ref, start2_ref, band2_ref, start3_ref, band3_ref, sems,
    product_ref, packed_ref, field_ref, rows_ref, stack_ref,
):
    copies = [
        pltpu.make_async_copy(source, target, sems.at[k])
        for k, (source, target) in enumerate(
            (
                (start3_hbm, start3_ref),
                (band3_hbm, band3_ref),
                (start2_hbm, start2_ref),
                (band2_hbm, band2_ref),
                (weight_hbm, weight_ref),
                (table_hbm, table_ref),
            )
        )
    ]
    for copy in copies:
        copy.start()
    copies[0].wait()
    copies[1].wait()
    pick_bin = (iota((256, N3), 0) % N3 == iota((256, N3), 1)) & (iota((256, N3), 0) < 4 * N3)
    same = iota((256, 128), 0) // N3 == iota((256, 128), 1) // 32
    picker = jnp.where(pick_bin, 1.0, 0.0).astype(jnp.bfloat16)
    for k, term in enumerate(split(banded_t(start3_ref, band3_ref, 128, 32))):
        spread_out = lax.dot_general(
            picker, term, (((1,), (1,)), ((), ())), preferred_element_type=f32
        )
        inner_ref[256 * k : 256 * k + 256, :] = jnp.where(same, spread_out, 0.0).astype(jnp.bfloat16)
    copies[2].wait()
    copies[3].wait()
    order, other = iota((N2, N2), 1), iota((N2, N2), 0)
    permute = jnp.where((order % 16) * 4 + order // 16 == other, 1.0, 0.0).astype(jnp.bfloat16)
    back = jnp.where((other % 16) * 4 + other // 16 == order, 1.0, 0.0).astype(jnp.bfloat16)
    for k, term in enumerate(split(banded_t(start2_ref, band2_ref, 32, 32))):
        value = jnp.dot(term, permute, preferred_element_type=f32)
        inner_ref[640 + 32 * k : 672 + 32 * k, 0:64] = value.astype(jnp.bfloat16)
        value = lax.dot_general(back, term, (((1,), (1,)), ((), ())), preferred_element_type=f32)
        inner_ref[512 + 64 * k : 576 + 64 * k, 0:32] = value.astype(jnp.bfloat16)
    kron, _, turned = constants(inner_ref)
    copies[4].wait()
    copies[5].wait()
    packed_ref[8:16, :] = jnp.zeros((8, N2 * N3), f32)
    product_ref[8:16, :] = jnp.zeros((8, N2 * N3), f32)
    for b in range(L1):
        weight = weight_ref[b]
        packed_ref[L0 * b : L0 * b + L0, :] = weight
        product_ref[L0 * b : L0 * b + L0, :] = weight * table_ref[b]
    for p in range(16):
        for source, target in ((packed_ref, wide_ref), (product_ref, field_ref)):
            low, high = expand(source, p)
            target[16 * p : 16 * p + 16, 0:128] = low
            target[16 * p : 16 * p + 16, 128:256] = high
    mixed = table_to_mixed(field_ref[...], kron, turned, rows_ref, stack_ref)
    once = inner_penalty(mixed)
    keep_rows(wide_ref, 1, mixed)
    keep_rows(wide_ref, 2, once)
    for base, value in ((0, mixed), (3, once)):
        put(send_ref, base, 5, tile_of(value, 0))
        put(send_ref, base + 1, 5, tile_of(value, 1))
    lane = iota((32, 128), 1)
    put(send_ref, 2, 5, jnp.where(lane < 64, tile_of(mixed, 2), pltpu.roll(tile_of(once, 2), 64, 1)))


def pentadiagonal(n):
    gap = jnp.abs(iota((n, n), 0) - iota((n, n), 1))
    return jnp.where(gap == 0, 6.0, jnp.where(gap == 1, -4.0, jnp.where(gap == 2, 1.0, 0.0)))


def choose(pieces, selector):
    out = None
    for piece in pieces:
        term = jnp.dot(piece, selector, preferred_element_type=f32)
        out = term if out is None else out + term
    return out


def powers(basis_t, count):
    penalty_matrix = pentadiagonal(basis_t.shape[0])
    out = [basis_t]
    for _ in range(count - 1):
        out.append(mm(penalty_matrix, out[-1]))
    return out


def store_split(high_ref, low_ref, rows, value):
    high, low = split(value)
    high_ref[rows, :] = high
    low_ref[rows, :] = low


def gram_blocks(refs, count, small_ref, rows0_h, rows0_l, rows1_h, rows1_l):
    start0_ref, band0_ref, start1_ref, band1_ref = refs
    total = DEVICES * ROWS
    powers0 = powers(banded_t(start0_ref, band0_ref, K0, K0), count)
    powers1 = powers(banded_t(start1_ref, band1_ref, K1, K1), max(count, 3))
    small_ref[...] = jnp.zeros((48, 128), f32)
    first, second = powers0[0].T, powers1[0].T
    for k in range(count):
        small_ref[0:N0, 32 * k : 32 * k + N0] = mm(first, powers0[k])
        small_ref[N0 : N0 + N1, 32 * k : 32 * k + N1] = mm(second, powers1[k])
    row0 = iota((total, N0), 0)
    pick0 = L0 * (row0 % 32 // GRPS) + row0 // 32 // L1 == iota((total, N0), 1)
    row1 = iota((total, 16), 0)
    pick1 = L1 * (row1 % GRPS) + row1 // 32 % L1 == iota((total, 16), 1)
    for pick, rows, targets in (
        (pick0, slice(0, N0), (rows0_h, rows0_l)),
        (pick1, slice(N0, N0 + 16), (rows1_h, rows1_l)),
    ):
        chooser = jnp.where(pick, 1.0, 0.0).astype(jnp.bfloat16)
        for term, target in zip(split(small_ref[rows, :]), targets):
            spread_out = jnp.dot(chooser, term, preferred_element_type=f32)
            target[...] = spread_out.astype(jnp.bfloat16)
    line, column = iota((128, total), 0), iota((128, total), 1)
    match0 = line % 32 == L0 * (column % 32 // GRPS) + column // 32 // L1
    match1 = line % 32 == L1 * (column % GRPS) + column // 32 % L1
    select0, select1 = [
        [
            jnp.where(match & (line // 32 == k), 1.0, 0.0).astype(jnp.bfloat16)
            for k in range(count)
        ]
        for match in (match0, match1)
    ]

    def block(base):
        block0 = rows0_h[pl.ds(base, 64), :], rows0_l[pl.ds(base, 64), :]
        block1 = rows1_h[pl.ds(base, 64), :], rows1_l[pl.ds(base, 64), :]
        g = [choose(block0, selector) for selector in select0]
        h = [choose(block1, selector) for selector in select1]
        return g, h

    return powers0, powers1, select0[0][0:N0, :], block


def matrix_kernel(
    group_ref, start0_ref, band0_ref, start1_ref, band1_ref,
    gram_h_ref, gram_l_ref, lift_h_ref, lift_l_ref, side_ref, *scratch,
):
    total = DEVICES * ROWS
    refs = (start0_ref, band0_ref, start1_ref, band1_ref)
    powers0, powers1, chosen, block = gram_blocks(refs, 2, *scratch)

    @pl.loop(0, 5)
    def _(step):
        base = pl.multiple_of(step * 64, 64)
        g, h = block(base)
        store_split(gram_h_ref, gram_l_ref, pl.ds(base, 64), g[0] * h[0])
        store_split(
            gram_h_ref, gram_l_ref, pl.ds(base + total, 64), g[1] * h[0] + g[0] * h[1]
        )

    lifted = [
        jnp.dot(term, chosen, preferred_element_type=f32)
        for term in split(powers0[0])
    ]
    owner = L1 * (iota((K0, total), 1) % GRPS) + iota((K0, total), 1) // 32 % L1
    for n in range(N1):
        rows = slice(K0 * n, K0 * n + K0)
        for term, target in zip(lifted, (lift_h_ref, lift_l_ref)):
            target[rows, :] = jnp.where(owner == n, term, 0.0).astype(jnp.bfloat16)
    group = group_ref[0]
    coef = iota((128, K1), 0) % 32 + 32 * group
    pick_coef = jnp.where(coef == iota((128, K1), 1), 1.0, 0.0)
    half = iota((N1, N1), 1) // L1
    wanted = L1 * jnp.where(half == group, 0, 1) + iota((N1, N1), 1) % L1
    reorder = jnp.where(iota((N1, N1), 0) == wanted, 1.0, 0.0)
    side_ref[...] = jnp.zeros((128, 384), f32)
    for k in range(3):
        own = mm(pick_coef, powers1[k])
        halves = mm(own, reorder)
        for alpha in range(4):
            rows = slice(32 * alpha, 32 * alpha + 32)
            if k == 0:
                side_ref[rows, 10 * alpha : 10 * alpha + 10] = own[rows, :]
            for h in range(2):
                piece = halves[rows, L1 * h : L1 * h + L1]
                place = 40 * k + 20 * h + L1 * alpha
                side_ref[rows, 256 + place : 256 + place + L1] = piece
                if k < 2:
                    side_ref[rows, 128 + place : 128 + place + L1] = piece


def unpack(ref, row, count, r, source, target):
    return move(ref[pl.ds(row, 32, stride=count), :], source, target)


def first_column_kernel(recv_ref, gram_h_ref, gram_l_ref, send_ref, fields_ref, images_ref):
    total = DEVICES * ROWS
    zero = jnp.zeros((32, 128), f32)
    for r in range(ROWS):
        j, q = r // 4, r % 4
        where0 = (j, q) if j < 2 else (2, q)
        where1 = (3 + j, q) if j < 2 else (2, q + 2)
        parts = [
            unpack(recv_ref, place[0], 5, r, place[1], k) for k, place in enumerate((where0, where1))
        ]
        fields_ref[32 * r : 32 * r + 32, :] = merge(parts + [zero])
    fields = fields_ref[...]
    applied = product(load((gram_h_ref, gram_l_ref)), split(fields))
    lane = iota((total, 128), 1)
    images = applied[:total] + jnp.where(
        (lane >= 32) & (lane < 64), pltpu.roll(applied[total:], 32, 1), 0.0
    )
    images_ref[...] = images
    norm = jnp.sum(jnp.where(lane < 32, fields * images, 0.0))
    bend = jnp.sum(jnp.where(lane < 32, fields * pltpu.roll(images, 96, 1), 0.0))
    send_rows(send_ref, images_ref)
    spread(send_ref, 3, 4, (norm, bend))


def send_rows(send_ref, value_ref):
    for j in range(3):
        parts = []
        for q in range(4):
            r = 4 * j + q
            if r < ROWS:
                parts.append(move(value_ref[32 * r : 32 * r + 32, :], 0, q))
            else:
                parts.append(jnp.zeros((32, 128), f32))
        put(send_ref, j, 4, merge(parts))


def received_rows(recv_ref):
    return jnp.concatenate([recv_ref[pl.ds(j, 32, stride=4), :] for j in range(3)], axis=1)


def first_row_kernel(
    recv_ref, wide_ref, inner_ref, send_ref, scalar_ref, carried_ref, rows_ref, stack_ref,
):
    norm, bend = totals(recv_ref, 3, 4, 2)
    scalar_ref[...] = lanes((norm, bend))
    kron, second, turned = constants(inner_ref)
    field = mixed_to_table(received_rows(recv_ref), kron, second, rows_ref, stack_ref)
    weighted = wide_ref[0:256, :] * field
    energy = jnp.sum(field * weighted)
    mixed = table_to_mixed(weighted, kron, turned, rows_ref, stack_ref)
    carried_ref[...] = wide_ref[...]
    keep_rows(carried_ref, 0, mixed)
    for j in range(3):
        put(send_ref, j, 4, tile_of(mixed, j))
    spread(send_ref, 3, 4, (energy,))


def second_column_kernel(
    recv_ref, gram_h_ref, gram_l_ref, fields_ref, images_ref, scalar_ref,
    send_ref, blend_ref, out_scalar_ref, next_ref, image_ref,
):
    zero = jnp.zeros((32, 128), f32)
    for r in range(ROWS):
        part = unpack(recv_ref, r // 4, 4, r, r % 4, 0)
        next_ref[32 * r : 32 * r + 32, :] = merge([part, zero])
    (energy,) = totals(recv_ref, 3, 4, 1)
    norm, bend = pick(scalar_ref, 0), pick(scalar_ref, 1)
    step = norm / (energy + 0.1 * bend)
    out_scalar_ref[...] = lanes((norm, step))
    fields, images, following = fields_ref[...], images_ref[...], next_ref[...]
    gram = gram_h_ref[0 : DEVICES * ROWS, :], gram_l_ref[0 : DEVICES * ROWS, :]
    image = product(gram, split(following))
    image_ref[...] = images - step * (image + 0.1 * pltpu.roll(images, 96, 1))
    send_rows(send_ref, image_ref)
    put(send_ref, 3, 4, zero)
    lane = iota(fields.shape, 1)
    reduced = fields - step * (following + 0.1 * pltpu.roll(fields, 96, 1))
    kept = jnp.where(lane < 64, 0.0, pltpu.roll(fields, 64, 1))
    blend_ref[...] = jnp.where(lane < 32, reduced, kept)


def coefficient_penalty(value):
    k = iota(value.shape, 0) % K0
    count = value.shape[0]
    total = 6.0 * value
    for d, weight in ((1, -4.0), (2, 1.0)):
        total = total + weight * (
            jnp.where(k >= d, pltpu.roll(value, d, 0), 0.0)
            + jnp.where(k < K0 - d, pltpu.roll(value, count - d, 0), 0.0)
        )
    return total


def send_blocks(send_ref, count, base, value_ref, block):
    for j in range(10):
        parts = []
        for q in range(4):
            m = 4 * j + q
            alpha, n = m // 10, m % 10
            parts.append(move(value_ref[pl.ds(K0 * n + alpha, 16, stride=4), :], block, q))
        merged = merge(parts)
        for g in range(GRPS):
            send_ref[pl.ds(g * count + base + j, 16, stride=2 * count), :] = merged


def send_halves(send_ref, count, base, value_ref, block):
    for g in range(GRPS):
        for j in range(5):
            parts = []
            for q in range(4):
                alpha, b = divmod(4 * j + q, L1)
                row = K0 * (L1 * g + b) + alpha
                parts.append(move(value_ref[pl.ds(row, 16, stride=4), :], block, q))
            send_ref[pl.ds(g * count + base + j, 16, stride=2 * count), :] = merge(parts)


def middle_kernel(
    blend_ref, gram_h_ref, gram_l_ref, lift_h_ref, lift_l_ref, scalar_ref,
    start0_ref, band0_ref, start1_ref, band1_ref,
    send_ref, keep_ref, sums_ref, higher_ref, *scratch,
):
    total = DEVICES * ROWS
    step = pick(scalar_ref, 1)
    small = 0.1 * step
    blend = blend_ref[...]
    lane = iota(blend.shape, 1)
    pair = split(blend)
    lower = product(load((gram_h_ref, gram_l_ref)), pair)
    *_, block = gram_blocks((start0_ref, band0_ref, start1_ref, band1_ref), 4, *scratch)

    @pl.loop(0, 5)
    def _(index):
        base = pl.multiple_of(index * 64, 64)
        g, h = block(base)
        squared = g[2] * h[0] + 2.0 * g[1] * h[1] + g[0] * h[2]
        cubed = g[3] * h[0] + 3.0 * (g[2] * h[1] + g[1] * h[2]) + g[0] * h[3]
        higher_ref[pl.ds(base, 64), :] = product(split(squared), pair)
        higher_ref[pl.ds(base + total, 64), :] = product(split(cubed), pair)

    g0, g1, g2, g3 = lower[:total], lower[total:], higher_ref[0:total, :], higher_ref[total:, :]
    head = g0 - small * pltpu.roll(g1, 64, 1)
    tail = g1 - small * pltpu.roll(g2, 64, 1)
    end = g2 - small * pltpu.roll(g3, 64, 1)
    scaled = pltpu.roll(blend, 64, 1)
    low = lane < 32
    norm = jnp.sum(jnp.where(low, blend * head - small * scaled * tail, 0.0))
    head_p = tail + pltpu.roll(head, 96, 1)
    tail_p = end + pltpu.roll(tail, 96, 1)
    bend = jnp.sum(jnp.where(low, blend * head_p - small * scaled * tail_p, 0.0))
    sums_ref[...] = lanes((norm, bend))
    lifted = product(load((lift_h_ref, lift_l_ref)), pair)
    once = coefficient_penalty(lifted)
    twice = coefficient_penalty(once)
    h_a = lifted - small * pltpu.roll(once, 64, 1)
    y_1 = once + pltpu.roll(lifted, 96, 1)
    x_a = once - small * pltpu.roll(twice, 64, 1)
    h_0 = pltpu.roll(lifted, 64, 1)
    wide = iota(lifted.shape, 1)
    keep = jnp.where(
        wide < 32, h_0, jnp.where(wide < 64, pltpu.roll(h_a, 32, 1), jnp.where(wide < 96, y_1, pltpu.roll(x_a, 96, 1)))
    )
    keep_ref[...] = keep
    for block in range(3):
        send_halves(send_ref, JOINT, 4 + 5 * block, keep_ref, block)


def second_row_kernel(
    early_ref, recv_ref, sums_ref, scalar_ref, wide_ref, inner_ref,
    send_ref, rows_ref, stack_ref,
):
    kron, second, turned = constants(inner_ref)
    send_ref[...] = early_ref[...]
    image = received_rows(recv_ref)
    step = pick(scalar_ref, 1)
    reduced = kept_rows(wide_ref, 1) - step * (
        kept_rows(wide_ref, 0) + 0.1 * kept_rows(wide_ref, 2)
    )
    inner = jnp.sum(reduced * inner_penalty(image))
    field = mixed_to_table(image, kron, second, rows_ref, stack_ref)
    weighted = wide_ref[0:256, :] * field
    energy = jnp.sum(field * weighted)
    mixed = table_to_mixed(weighted, kron, turned, rows_ref, stack_ref)
    for j in range(3):
        put(send_ref, j, JOINT, tile_of(mixed, j))
    spread(send_ref, 3, JOINT, (energy, pick(sums_ref, 0), pick(sums_ref, 1) + inner))


def third_column_kernel(
    recv_ref, lift_h_ref, lift_l_ref, keep_ref, scalar_ref, send_ref, out_scalar_ref, last_ref, mixed_ref
):
    zero = jnp.zeros((32, 128), f32)
    for r in range(ROWS):
        j, q = r // 4, r % 4
        last_ref[32 * r : 32 * r + 32, :] = unpack(recv_ref, j, JOINT, r, q, 0)
    energy, norm_next, bend = totals(recv_ref, 3, JOINT, 3)
    norm, step = pick(scalar_ref, 0), pick(scalar_ref, 1)
    ratio = norm_next / norm
    curve = energy + 0.1 * bend - ratio * norm_next / step
    step_next = norm_next / curve
    out_scalar_ref[...] = lanes((norm, step, ratio, step_next))
    lifted = product(load((lift_h_ref, lift_l_ref)), split(last_ref[...]))
    keep = keep_ref[...]
    h_a, x_a = pltpu.roll(keep, 96, 1), pltpu.roll(keep, 32, 1)
    mixed_ref[...] = (
        h_a - step_next * (lifted + 0.1 * x_a) - (step_next * ratio / step) * (keep - h_a)
    )
    send_blocks(send_ref, 10, 0, mixed_ref, 0)


def gather_blocks(ref, count, base, rows, out_ref, first):
    for j in range(rows):
        taken = [ref[pl.ds(rho * count + base + j, 8, stride=4 * count), :] for rho in range(4)]
        for q in range(4):
            m = first + 4 * j + q
            merged = merge([move(taken[rho], q, rho) for rho in range(4)])
            out_ref[pl.ds(m // 8 * 64 + m % 8, 8, stride=8), :] = merged


def take(ref, block, tile):
    return jnp.concatenate(
        [ref[pl.ds((5 * block + t) * 64 + 8 * tile, 8), :] for t in range(5)], axis=0
    )


def bent_rows(value):
    lane = iota(value.shape, 1)
    inside = lane % 32
    total = 12.0 * value
    for d, weight in ((1, -4.0), (2, 1.0)):
        total = total + weight * (
            jnp.where(lane >= 32 * d, pltpu.roll(value, 32 * d, 1), 0.0)
            + jnp.where(lane < 1024 - 32 * d, pltpu.roll(value, 1024 - 32 * d, 1), 0.0)
            + jnp.where(inside >= d, pltpu.roll(value, d, 1), 0.0)
            + jnp.where(inside < 32 - d, pltpu.roll(value, 1024 - d, 1), 0.0)
        )
    return total


def settle_kernel(own_ref, partner_ref, side_ref, scalar_ref, solution_ref, part_ref, early):
    for block in range(3):
        for h, ref in enumerate((own_ref, partner_ref)):
            gather_blocks(ref, JOINT, 4 + 5 * block, 5, early, 40 * block + 20 * h)
    step, ratio, step_next = pick(scalar_ref, 1), pick(scalar_ref, 2), pick(scalar_ref, 3)
    small = 0.1 * step
    value = split(side_ref[:, 128:208])
    slope = split(side_ref[:, 256:376])
    bent = bent_rows(jnp.concatenate([take(early, 1, tile) for tile in range(8)], axis=1))
    for tile in range(8):
        h_0, h_a, y_1 = take(early, 0, tile), take(early, 1, tile), take(early, 2, tile)
        right = jnp.concatenate(
            [(step + step_next * ratio) * h_0 + step_next * h_a, (-step_next * small) * h_0], axis=0
        )
        columns = slice(128 * tile, 128 * tile + 128)
        solution_ref[:, :, columns] = product(value, split(right)).reshape(4, 32, 128)
        right = jnp.concatenate(
            [
                (-0.1 * step_next) * bent[:, columns],
                (-small * (1.0 + step_next * ratio / step)) * h_0
                - (0.1 * step_next) * (h_a - small * y_1),
                (0.1 * step_next * small) * h_0,
            ],
            axis=0,
        )
        part_ref[:, columns] = product(slope, split(right))


def final_kernel(late_ref, side_ref, part_ref, residual_ref, late):
    gather_blocks(late_ref, 10, 0, 10, late, 0)
    value = split(side_ref[:, 0:40])
    for tile in range(8):
        columns = slice(128 * tile, 128 * tile + 128)
        whole = part_ref[:, columns] + product(value, split(take(late, 0, tile)))
        residual_ref[:, :, columns] = whole.reshape(4, 32, 128)


def call(kernel, outputs, scratch, *operands, aliases={}, left=(), scalars=(), limit=16):
    vmem = pl.BlockSpec(memory_space=pltpu.VMEM)
    specs = [vmem] * len(operands)
    for k in left:
        specs[k] = pl.BlockSpec(memory_space=pltpu.HBM)
    for k in scalars:
        specs[k] = pl.BlockSpec(memory_space=pltpu.SMEM)
    return pl.pallas_call(
        kernel,
        out_shape=[
            shape if isinstance(shape, jax.ShapeDtypeStruct) else jax.ShapeDtypeStruct(shape, f32)
            for shape in outputs
        ],
        in_specs=specs,
        out_specs=[vmem] * len(outputs),
        scratch_shapes=[
            pltpu.VMEM(shape, f32) if isinstance(shape, tuple) else shape for shape in scratch
        ],
        input_output_aliases=aliases,
        compiler_params=pltpu.CompilerParams(vmem_limit_bytes=limit * 2**20),
    )(*operands)


def pair_of(*shape):
    return [jax.ShapeDtypeStruct(shape, jnp.bfloat16)] * 2


def exchange(buffer):
    count = buffer.shape[0] // DEVICES
    tiled = count == 4 or count % 8 == 0
    shape = (DEVICES, count, 128) if tiled else (DEVICES, 1, count * 128)
    moved = lax.all_to_all(buffer.reshape(shape), ("slab", "grp"), 0, 0, tiled=True)
    return moved.reshape(buffer.shape)


def fast_program(
    photon_table,
    bin_weights,
    first_start,
    first_band,
    second_start,
    second_band,
    third_start,
    third_band,
    fourth_start,
    fourth_band,
):
    total = DEVICES * ROWS
    work = [(256, 128), (64, 384)]
    outer = (first_start, first_band.T, second_start, second_band.T)
    inputs = (
        photon_table.transpose(1, 0, 2),
        bin_weights.transpose(1, 0, 2),
        third_start,
        third_band.T,
        fourth_start,
        fourth_band.T,
    )
    send, wide, inner = call(
        start_kernel,
        [(160, 128), (416, 256), jax.ShapeDtypeStruct((704, 128), jnp.bfloat16)],
        [pltpu.VMEM(value.shape, value.dtype) for value in inputs]
        + [pltpu.SemaphoreType.DMA((len(inputs),))]
        + [(16, N2 * N3), (16, N2 * N3), (256, 256)]
        + work,
        *inputs,
        left=range(len(inputs)),
        limit=LARGE,
    )
    recv = exchange(send)
    grams = [(48, 128)] + [pltpu.VMEM((total, 128), jnp.bfloat16)] * 4
    group = lax.axis_index("grp").reshape(1)
    *matrices, side = call(
        matrix_kernel,
        pair_of(2 * total, total) + pair_of(K0 * N1, total) + [(128, 384)],
        grams,
        group, *outer,
        scalars=(0,),
    )
    gram, lift = matrices[0:2], matrices[2:4]
    send, fields, images = call(
        first_column_kernel, [(128, 128), (total, 128), (total, 128)], [], recv, *gram
    )
    recv = exchange(send)
    send, scalars, wide = call(
        first_row_kernel,
        [(128, 128), (8, 128), (416, 256)],
        work,
        recv, wide, inner,
        aliases={1: 2},
    )
    recv = exchange(send)
    send, blend, scalars = call(
        second_column_kernel,
        [(128, 128), (total, 128), (8, 128)],
        [(total, 128), (total, 128)],
        recv, *gram, fields, images, scalars,
        aliases={3: 1},
    )
    recv = exchange(send)
    send, keep, sums = call(
        middle_kernel,
        [(DEVICES * JOINT, 128), (K0 * N1, 128), (8, 128)],
        [(2 * total, 128)] + grams,
        blend, *gram, *lift, scalars, *outer,
    )
    (send,) = call(
        second_row_kernel,
        [(DEVICES * JOINT, 128)],
        work,
        send, recv, sums, scalars, wide, inner,
        aliases={0: 0},
    )
    recv = exchange(send)
    partner = lax.ppermute(recv, "grp", [(0, 1), (1, 0)])
    send, scalars = call(
        third_column_kernel,
        [(DEVICES * 10, 128), (8, 128)],
        [(total, 128), (K0 * N1, 128)],
        recv, *lift, keep, scalars,
    )
    late = exchange(send)
    solution_part, part = call(
        settle_kernel,
        [(4, 32, 1024), (128, 1024)],
        [(960, 128)],
        recv, partner, side, scalars,
    )
    (residual,) = call(final_kernel, [(4, 32, 1024)], [(320, 128)], late, side, part)
    return solution_part, residual


def fits(mesh):
    return (mesh.shape["slab"], mesh.shape["grp"]) == (SLABS, GRPS)


def solution(mesh):
    placed = (
        P("slab", "grp", None),
        P("slab", "grp", None),
        P(),
        P(),
        P(),
        P(),
        P(),
        P(),
        P(),
        P(),
    )
    return jax.shard_map(
        fast_program if fits(mesh) else per_device,
        mesh=mesh,
        in_specs=placed,
        out_specs=(P("slab", "grp", None), P("slab", "grp", None)),
        check_vma=False,
    )
```

```python
import jax
import jax.numpy as jnp
from jax import lax
from jax.experimental import pallas as pl
from jax.experimental.pallas import tpu as pltpu
from jax.sharding import PartitionSpec as P

K0 = 64
K1 = 64
K2 = 32
K3 = 32
ITERS = 2


highest = lax.Precision.HIGHEST
smoothing = 0.1
stencil_weights = (1.0, -4.0, 6.0, -4.0, 1.0)


def with_halo(value, sides, width):
    for axis, dim in sides:
        count, length = (lax.axis_size(axis), value.shape[dim])
        up = [(i, (i + 1) % count) for i in range(count - 1)]
        down = [(j, i) for i, j in up]
        last = lax.slice_in_dim(value, length - width, length, axis=dim)
        initial = lax.slice_in_dim(value, 0, width, axis=dim)
        before = lax.ppermute(last, axis, up)
        after = lax.ppermute(initial, axis, down)
        value = jnp.concatenate([before, value, after], axis=dim)
    return value


def dense_basis(starts, values, coef_count):
    relative = jnp.arange(coef_count, dtype=jnp.int32)[None, :] - starts[:, None]
    matrix = jnp.zeros((starts.shape[0], coef_count), jnp.float32)
    for offset in range(4):
        matrix = matrix + jnp.where(relative == offset, values[:, offset : offset + 1], 0.0)
    return matrix


def five_point(source, along, extent):
    running = stencil_weights[0] * lax.slice_in_dim(source, 0, extent, axis=along)
    for offset in range(1, 5):
        running = running + stencil_weights[offset] * lax.slice_in_dim(
            source, offset, offset + extent, axis=along
        )
    return running


def local_stencil(tensor, along):
    widths = [(0, 0)] * tensor.ndim
    widths[along] = (2, 2)
    return five_point(jnp.pad(tensor, widths), along, tensor.shape[along])


def inner_forward(tensor, third_basis, fourth_basis):
    leading, middle = (tensor.shape[0], tensor.shape[1])
    blocked = tensor.reshape(leading, middle, third_basis.shape[1], fourth_basis.shape[1])
    blocked = jnp.einsum("abcd,nd->abcn", blocked, fourth_basis, precision=highest)
    blocked = jnp.einsum("abcn,mc->abmn", blocked, third_basis, precision=highest)
    return blocked.reshape(leading, middle, third_basis.shape[0] * fourth_basis.shape[0])


def inner_adjoint(tensor, third_basis, fourth_basis):
    leading, middle = (tensor.shape[0], tensor.shape[1])
    blocked = tensor.reshape(leading, middle, third_basis.shape[0], fourth_basis.shape[0])
    blocked = jnp.einsum("abmn,mc->abcn", blocked, third_basis, precision=highest)
    blocked = jnp.einsum("abcn,nd->abcd", blocked, fourth_basis, precision=highest)
    return blocked.reshape(leading, middle, third_basis.shape[1] * fourth_basis.shape[1])


def lead_product(tensor, matrix):
    combined = jnp.einsum(
        "ka,ain->kin",
        matrix,
        lax.all_to_all(tensor, "slab", split_axis=2, concat_axis=0, tiled=True),
        precision=highest,
    )
    return lax.all_to_all(combined, "slab", split_axis=0, concat_axis=2, tiled=True)


def second_product(tensor, matrix):
    return jnp.einsum(
        "lp,apn->aln", matrix, lax.all_gather(tensor, "grp", axis=1, tiled=True), precision=highest
    )


def penalty(coeffs):
    leading, middle = (coeffs.shape[0], coeffs.shape[1])
    padded = with_halo(coeffs, (("slab", 0), ("grp", 1)), 2)
    along_lead = five_point(padded[:, 2 : 2 + middle], 0, leading)
    along_rows = five_point(padded[2 : 2 + leading, :], 1, middle)
    blocked = coeffs.reshape(leading, middle, K2, K3)
    inner_part = local_stencil(blocked, 2) + local_stencil(blocked, 3)
    return along_lead + along_rows + inner_part.reshape(leading, middle, K2 * K3)


def squared_total(vector):
    return lax.psum(jnp.sum(vector * vector), ("slab", "grp"))


def per_device(
    photon_table,
    bin_weights,
    first_start,
    first_band,
    second_start,
    second_band,
    third_start,
    third_band,
    fourth_start,
    fourth_band,
):
    first_basis = dense_basis(first_start, first_band, K0)
    second_basis = dense_basis(second_start, second_band, K1)
    third_basis = dense_basis(third_start, third_band, K2)
    fourth_basis = dense_basis(fourth_start, fourth_band, K3)
    first_back = first_basis.T
    group_index = lax.axis_index("grp")
    row_count = photon_table.shape[1]
    coef_rows = K1 // lax.axis_size("grp")
    near_rows = lax.dynamic_slice_in_dim(second_basis, group_index * row_count, row_count, 0)
    back_rows = lax.dynamic_slice_in_dim(second_basis.T, group_index * coef_rows, coef_rows, 0)

    def adjoint(table):
        tensor = lead_product(table, first_back)
        tensor = second_product(tensor, back_rows)
        return inner_adjoint(tensor, third_basis, fourth_basis)

    right_side = adjoint(bin_weights * photon_table)
    solution = jnp.zeros_like(right_side)
    residual = right_side
    direction = right_side
    norm_now = squared_total(residual)
    for sweep in range(ITERS):
        forward_tensor = inner_forward(direction, third_basis, fourth_basis)
        forward_tensor = second_product(forward_tensor, near_rows)
        mapped = adjoint(
            bin_weights * lead_product(forward_tensor, first_basis)
        ) + smoothing * penalty(direction)
        curve_total = lax.psum(jnp.sum(direction * mapped), ("slab", "grp"))
        step_size = norm_now / curve_total
        solution = solution + step_size * direction
        residual = residual - step_size * mapped
        norm_next = squared_total(residual)
        direction = residual + norm_next / norm_now * direction
        norm_now = norm_next
    return (solution, residual)


SLABS, GRPS = 16, 2
DEVICES = SLABS * GRPS
L0, L1 = 2, 5
ROWS = L0 * L1
N2, N3 = 64, 50
N0, N1 = 32, 10
HI = lax.Precision.HIGHEST
f32 = jnp.float32
JOINT = 19
LARGE = 60


def iota(shape, dim):
    return lax.broadcasted_iota(jnp.int32, shape, dim)


def mm(a, b):
    return jnp.dot(a, b, precision=HI, preferred_element_type=f32)


def mm_t(a, b):
    return lax.dot_general(
        a, b, (((1,), (1,)), ((), ())), precision=HI, preferred_element_type=f32
    )


def split(value):
    high = value.astype(jnp.bfloat16)
    return high, (value - high.astype(f32)).astype(jnp.bfloat16)


def product(a, b, transposed=False):
    dims = (((1,), (1 if transposed else 0,)), ((), ()))

    def one(x, y):
        return lax.dot_general(x, y, dims, preferred_element_type=f32)

    return one(a[0], b[0]) + (one(a[0], b[1]) + one(a[1], b[0]))


def load(pair):
    return pair[0][...], pair[1][...]


def move(block, source, target):
    shift = (target - source) * 32 % 128
    return pltpu.roll(block, shift, 1) if shift else block


def merge(parts):
    lane = iota(parts[0].shape, 1)
    out = parts[-1]
    for q in range(len(parts) - 2, -1, -1):
        out = jnp.where(lane < 32 * (q + 1), parts[q], out)
    return out


def slot(r):
    return L0 * (r % L1) + r // L1


def banded_t(start_ref, band_ref, width, wrap):
    n = start_ref.shape[0]
    relative = (iota((width, n), 0) % wrap) - start_ref[...].reshape(1, n)
    out = jnp.zeros((width, n), f32)
    for offset in range(4):
        out = out + jnp.where(relative == offset, band_ref[offset : offset + 1, :], 0.0)
    return out


def expand(ref, p):
    first = 200 * p
    tile, off = first // 128, first % 128
    lane = iota((16, 128), 1)

    def window(t):
        low = ref[:, t * 128 : (t + 1) * 128]
        if off == 0:
            return low
        t1 = min(t + 1, 24)
        high = ref[:, t1 * 128 : (t1 + 1) * 128]
        return jnp.where(
            lane < 128 - off, pltpu.roll(low, 128 - off, 1), pltpu.roll(high, 128 - off, 1)
        )

    return window(tile), window(min(tile + 1, 24))


def table_to_mixed(field, kron_third, second_t, rows_ref, stack_ref):
    rows_ref[...] = product(split(field), kron_third)
    for c in range(4):
        for j in range(3):
            parts = []
            for q in range(4):
                r = 4 * j + q
                if r < ROWS:
                    part = rows_ref[pl.ds(slot(r), 16, stride=16), :]
                    parts.append(move(part, c, q))
                else:
                    parts.append(jnp.zeros((16, 128), f32))
            stack_ref[16 * c : 16 * c + 16, 128 * j : 128 * j + 128] = merge(parts)
    return product(second_t, split(stack_ref[...]))


def mixed_to_table(value, kron_third, second, rows_ref, stack_ref):
    stack_ref[...] = product(second, split(value))
    rows_ref[...] = jnp.zeros((256, 128), f32)
    for r in range(ROWS):
        j, q = r // 4, r % 4
        parts = [
            move(stack_ref[16 * c : 16 * c + 16, 128 * j : 128 * j + 128], q, c) for c in range(4)
        ]
        rows_ref[pl.ds(slot(r), 16, stride=16), :] = merge(parts)
    return product(split(rows_ref[...]), kron_third, True)


def inner_penalty(value):
    out = 12.0 * value
    row = iota((32, 128), 0)
    inside = iota((32, 128), 1) % 32
    tiles = []
    for j in range(3):
        tile = value[:, 128 * j : 128 * j + 128]
        total = 12.0 * tile
        for d, weight in ((1, -4.0), (2, 1.0)):
            total = total + weight * (
                jnp.where(row >= d, pltpu.roll(tile, d, 0), 0.0)
                + jnp.where(row < 32 - d, pltpu.roll(tile, 32 - d, 0), 0.0)
                + jnp.where(inside >= d, pltpu.roll(tile, d, 1), 0.0)
                + jnp.where(inside < 32 - d, pltpu.roll(tile, 128 - d, 1), 0.0)
            )
        tiles.append(total)
    return jnp.concatenate(tiles, axis=1)


def tile_of(value, j):
    return value[:, 128 * j : 128 * j + 128]


def put(ref, row, count, value):
    ref[pl.ds(row, 32, stride=count), :] = value


def lanes(values):
    lane = iota((8, 128), 1)
    out = jnp.zeros((8, 128), f32)
    for k, value in enumerate(values):
        out = jnp.where(lane == k, value, out)
    return out


def spread(ref, row, count, values):
    one = lanes(values)
    put(ref, row, count, jnp.concatenate([one] * 4, axis=0))


def totals(ref, row, count, number):
    summed = jnp.sum(ref[pl.ds(row, 32, stride=count), :], axis=0, keepdims=True)
    lane = iota((1, 128), 1)
    return [jnp.sum(jnp.where(lane == k, summed, 0.0)) for k in range(number)]


def pick(ref, k):
    lane = iota((1, 128), 1)
    return jnp.sum(jnp.where(lane == k, ref[0:1, :], 0.0))


def constants(ref):
    kron = ref[0:256, :], ref[256:512, :]
    second = ref[512:576, 0:32], ref[576:640, 0:32]
    return kron, second, (ref[640:672, 0:64], ref[672:704, 0:64])


def row_tile(piece, j):
    place = 3 * piece + j
    first = 256 + 32 * (place // 2)
    return slice(first, first + 32), slice(128 * (place % 2), 128 * (place % 2) + 128)


def keep_rows(ref, piece, value):
    for j in range(3):
        ref[row_tile(piece, j)] = tile_of(value, j)


def kept_rows(ref, piece):
    return jnp.concatenate([ref[row_tile(piece, j)] for j in range(3)], axis=1)


def start_kernel(
    table_hbm, weight_hbm, start2_hbm, band2_hbm, start3_hbm, band3_hbm,
    send_ref, wide_ref, inner_ref,
    table_ref, weight_ref, start2_ref, band2_ref, start3_ref, band3_ref, sems,
    product_ref, packed_ref, field_ref, rows_ref, stack_ref,
):
    copies = [
        pltpu.make_async_copy(source, target, sems.at[k])
        for k, (source, target) in enumerate(
            (
                (start3_hbm, start3_ref),
                (band3_hbm, band3_ref),
                (start2_hbm, start2_ref),
                (band2_hbm, band2_ref),
                (weight_hbm, weight_ref),
                (table_hbm, table_ref),
            )
        )
    ]
    for copy in copies:
        copy.start()
    copies[0].wait()
    copies[1].wait()
    pick_bin = (iota((256, N3), 0) % N3 == iota((256, N3), 1)) & (iota((256, N3), 0) < 4 * N3)
    same = iota((256, 128), 0) // N3 == iota((256, 128), 1) // 32
    picker = jnp.where(pick_bin, 1.0, 0.0).astype(jnp.bfloat16)
    for k, term in enumerate(split(banded_t(start3_ref, band3_ref, 128, 32))):
        spread_out = lax.dot_general(
            picker, term, (((1,), (1,)), ((), ())), preferred_element_type=f32
        )
        inner_ref[256 * k : 256 * k + 256, :] = jnp.where(same, spread_out, 0.0).astype(jnp.bfloat16)
    copies[2].wait()
    copies[3].wait()
    order, other = iota((N2, N2), 1), iota((N2, N2), 0)
    permute = jnp.where((order % 16) * 4 + order // 16 == other, 1.0, 0.0).astype(jnp.bfloat16)
    back = jnp.where((other % 16) * 4 + other // 16 == order, 1.0, 0.0).astype(jnp.bfloat16)
    for k, term in enumerate(split(banded_t(start2_ref, band2_ref, 32, 32))):
        value = jnp.dot(term, permute, preferred_element_type=f32)
        inner_ref[640 + 32 * k : 672 + 32 * k, 0:64] = value.astype(jnp.bfloat16)
        value = lax.dot_general(back, term, (((1,), (1,)), ((), ())), preferred_element_type=f32)
        inner_ref[512 + 64 * k : 576 + 64 * k, 0:32] = value.astype(jnp.bfloat16)
    kron, _, turned = constants(inner_ref)
    copies[4].wait()
    copies[5].wait()
    packed_ref[8:16, :] = jnp.zeros((8, N2 * N3), f32)
    product_ref[8:16, :] = jnp.zeros((8, N2 * N3), f32)
    for b in range(L1):
        weight = weight_ref[b]
        packed_ref[L0 * b : L0 * b + L0, :] = weight
        product_ref[L0 * b : L0 * b + L0, :] = weight * table_ref[b]
    for p in range(16):
        for source, target in ((packed_ref, wide_ref), (product_ref, field_ref)):
            low, high = expand(source, p)
            target[16 * p : 16 * p + 16, 0:128] = low
            target[16 * p : 16 * p + 16, 128:256] = high
    mixed = table_to_mixed(field_ref[...], kron, turned, rows_ref, stack_ref)
    once = inner_penalty(mixed)
    keep_rows(wide_ref, 1, mixed)
    keep_rows(wide_ref, 2, once)
    for base, value in ((0, mixed), (3, once)):
        put(send_ref, base, 5, tile_of(value, 0))
        put(send_ref, base + 1, 5, tile_of(value, 1))
    lane = iota((32, 128), 1)
    put(send_ref, 2, 5, jnp.where(lane < 64, tile_of(mixed, 2), pltpu.roll(tile_of(once, 2), 64, 1)))


def pentadiagonal(n):
    gap = jnp.abs(iota((n, n), 0) - iota((n, n), 1))
    return jnp.where(gap == 0, 6.0, jnp.where(gap == 1, -4.0, jnp.where(gap == 2, 1.0, 0.0)))


def choose(pieces, selector):
    out = None
    for piece in pieces:
        term = jnp.dot(piece, selector, preferred_element_type=f32)
        out = term if out is None else out + term
    return out


def powers(basis_t, count):
    penalty_matrix = pentadiagonal(basis_t.shape[0])
    out = [basis_t]
    for _ in range(count - 1):
        out.append(mm(penalty_matrix, out[-1]))
    return out


def store_split(high_ref, low_ref, rows, value):
    high, low = split(value)
    high_ref[rows, :] = high
    low_ref[rows, :] = low


def gram_blocks(refs, count, small_ref, rows0_h, rows0_l, rows1_h, rows1_l):
    start0_ref, band0_ref, start1_ref, band1_ref = refs
    total = DEVICES * ROWS
    powers0 = powers(banded_t(start0_ref, band0_ref, K0, K0), count)
    powers1 = powers(banded_t(start1_ref, band1_ref, K1, K1), 4)
    small_ref[...] = jnp.zeros((48, 128), f32)
    first, second = powers0[0].T, powers1[0].T
    for k in range(count):
        small_ref[0:N0, 32 * k : 32 * k + N0] = mm(first, powers0[k])
        small_ref[N0 : N0 + N1, 32 * k : 32 * k + N1] = mm(second, powers1[k])
    row0 = iota((total, N0), 0)
    pick0 = L0 * (row0 % 32 // GRPS) + row0 // 32 // L1 == iota((total, N0), 1)
    row1 = iota((total, 16), 0)
    pick1 = L1 * (row1 % GRPS) + row1 // 32 % L1 == iota((total, 16), 1)
    for pick, rows, targets in (
        (pick0, slice(0, N0), (rows0_h, rows0_l)),
        (pick1, slice(N0, N0 + 16), (rows1_h, rows1_l)),
    ):
        chooser = jnp.where(pick, 1.0, 0.0).astype(jnp.bfloat16)
        for term, target in zip(split(small_ref[rows, :]), targets):
            spread_out = jnp.dot(chooser, term, preferred_element_type=f32)
            target[...] = spread_out.astype(jnp.bfloat16)
    line, column = iota((128, total), 0), iota((128, total), 1)
    match0 = line % 32 == L0 * (column % 32 // GRPS) + column // 32 // L1
    match1 = line % 32 == L1 * (column % GRPS) + column // 32 % L1
    select0, select1 = [
        [
            jnp.where(match & (line // 32 == k), 1.0, 0.0).astype(jnp.bfloat16)
            for k in range(count)
        ]
        for match in (match0, match1)
    ]

    def block(base):
        block0 = rows0_h[pl.ds(base, 64), :], rows0_l[pl.ds(base, 64), :]
        block1 = rows1_h[pl.ds(base, 64), :], rows1_l[pl.ds(base, 64), :]
        g = [choose(block0, selector) for selector in select0]
        h = [choose(block1, selector) for selector in select1]
        return g, h

    return powers0, powers1, select0[0][0:N0, :], block


def matrix_kernel(
    group_ref, start0_ref, band0_ref, start1_ref, band1_ref,
    gram_h_ref, gram_l_ref, lift_h_ref, lift_l_ref, side_ref, *scratch,
):
    total = DEVICES * ROWS
    refs = (start0_ref, band0_ref, start1_ref, band1_ref)
    powers0, powers1, chosen, block = gram_blocks(refs, 2, *scratch)

    @pl.loop(0, 5)
    def _(step):
        base = pl.multiple_of(step * 64, 64)
        g, h = block(base)
        store_split(gram_h_ref, gram_l_ref, pl.ds(base, 64), g[0] * h[0])
        store_split(
            gram_h_ref, gram_l_ref, pl.ds(base + total, 64), g[1] * h[0] + g[0] * h[1]
        )

    lifted = [
        jnp.dot(term, chosen, preferred_element_type=f32)
        for term in split(powers0[0])
    ]
    owner = L1 * (iota((K0, total), 1) % GRPS) + iota((K0, total), 1) // 32 % L1
    for n in range(N1):
        rows = slice(K0 * n, K0 * n + K0)
        for term, target in zip(lifted, (lift_h_ref, lift_l_ref)):
            target[rows, :] = jnp.where(owner == n, term, 0.0).astype(jnp.bfloat16)
    group = group_ref[0]
    coef = iota((128, K1), 0) % 32 + 32 * group
    pick_coef = jnp.where(coef == iota((128, K1), 1), 1.0, 0.0)
    half = iota((N1, N1), 1) // L1
    wanted = L1 * jnp.where(half == group, 0, 1) + iota((N1, N1), 1) % L1
    reorder = jnp.where(iota((N1, N1), 0) == wanted, 1.0, 0.0)
    side_ref[...] = jnp.zeros((192, 384), f32)
    across = powers1[0].T
    for k in range(4):
        side_ref[128 + 16 * k : 128 + 16 * k + N1, 0:N1] = mm(across, powers1[k])
    for k in range(3):
        own = mm(pick_coef, powers1[k])
        halves = mm(own, reorder)
        for alpha in range(4):
            rows = slice(32 * alpha, 32 * alpha + 32)
            if k == 0:
                side_ref[rows, 10 * alpha : 10 * alpha + 10] = own[rows, :]
            for h in range(2):
                piece = halves[rows, L1 * h : L1 * h + L1]
                place = 40 * k + 20 * h + L1 * alpha
                side_ref[rows, 256 + place : 256 + place + L1] = piece
                if k < 2:
                    side_ref[rows, 128 + place : 128 + place + L1] = piece


def unpack(ref, row, count, r, source, target):
    return move(ref[pl.ds(row, 32, stride=count), :], source, target)


def first_column_kernel(recv_ref, gram_h_ref, gram_l_ref, send_ref, fields_ref, images_ref):
    total = DEVICES * ROWS
    zero = jnp.zeros((32, 128), f32)
    for r in range(ROWS):
        j, q = r // 4, r % 4
        where0 = (j, q) if j < 2 else (2, q)
        where1 = (3 + j, q) if j < 2 else (2, q + 2)
        parts = [
            unpack(recv_ref, place[0], 5, r, place[1], k) for k, place in enumerate((where0, where1))
        ]
        fields_ref[32 * r : 32 * r + 32, :] = merge(parts + [zero])
    fields = fields_ref[...]
    applied = product(load((gram_h_ref, gram_l_ref)), split(fields))
    lane = iota((total, 128), 1)
    images = applied[:total] + jnp.where(
        (lane >= 32) & (lane < 64), pltpu.roll(applied[total:], 32, 1), 0.0
    )
    images_ref[...] = images
    norm = jnp.sum(jnp.where(lane < 32, fields * images, 0.0))
    bend = jnp.sum(jnp.where(lane < 32, fields * pltpu.roll(images, 96, 1), 0.0))
    send_rows(send_ref, images_ref)
    spread(send_ref, 3, 4, (norm, bend))


def send_rows(send_ref, value_ref):
    for j in range(3):
        parts = []
        for q in range(4):
            r = 4 * j + q
            if r < ROWS:
                parts.append(move(value_ref[32 * r : 32 * r + 32, :], 0, q))
            else:
                parts.append(jnp.zeros((32, 128), f32))
        put(send_ref, j, 4, merge(parts))


def received_rows(recv_ref):
    return jnp.concatenate([recv_ref[pl.ds(j, 32, stride=4), :] for j in range(3)], axis=1)


def first_row_kernel(
    recv_ref, wide_ref, inner_ref, send_ref, scalar_ref, carried_ref, rows_ref, stack_ref,
):
    norm, bend = totals(recv_ref, 3, 4, 2)
    scalar_ref[...] = lanes((norm, bend))
    kron, second, turned = constants(inner_ref)
    field = mixed_to_table(received_rows(recv_ref), kron, second, rows_ref, stack_ref)
    weighted = wide_ref[0:256, :] * field
    energy = jnp.sum(field * weighted)
    mixed = table_to_mixed(weighted, kron, turned, rows_ref, stack_ref)
    carried_ref[...] = wide_ref[...]
    keep_rows(carried_ref, 0, mixed)
    for j in range(3):
        put(send_ref, j, 4, tile_of(mixed, j))
    spread(send_ref, 3, 4, (energy,))


def second_column_kernel(
    recv_ref, gram_h_ref, gram_l_ref, fields_ref, images_ref, scalar_ref,
    send_ref, blend_ref, out_scalar_ref, next_ref, image_ref,
):
    zero = jnp.zeros((32, 128), f32)
    for r in range(ROWS):
        part = unpack(recv_ref, r // 4, 4, r, r % 4, 0)
        next_ref[32 * r : 32 * r + 32, :] = merge([part, zero])
    (energy,) = totals(recv_ref, 3, 4, 1)
    norm, bend = pick(scalar_ref, 0), pick(scalar_ref, 1)
    step = norm / (energy + 0.1 * bend)
    out_scalar_ref[...] = lanes((norm, step))
    fields, images, following = fields_ref[...], images_ref[...], next_ref[...]
    gram = gram_h_ref[0 : DEVICES * ROWS, :], gram_l_ref[0 : DEVICES * ROWS, :]
    image = product(gram, split(following))
    image_ref[...] = images - step * (image + 0.1 * pltpu.roll(images, 96, 1))
    send_rows(send_ref, image_ref)
    put(send_ref, 3, 4, zero)
    lane = iota(fields.shape, 1)
    reduced = fields - step * (following + 0.1 * pltpu.roll(fields, 96, 1))
    kept = jnp.where(lane < 64, 0.0, pltpu.roll(fields, 64, 1))
    blend_ref[...] = jnp.where(lane < 32, reduced, kept)


def coefficient_penalty(value):
    k = iota(value.shape, 0) % K0
    count = value.shape[0]
    total = 6.0 * value
    for d, weight in ((1, -4.0), (2, 1.0)):
        total = total + weight * (
            jnp.where(k >= d, pltpu.roll(value, d, 0), 0.0)
            + jnp.where(k < K0 - d, pltpu.roll(value, count - d, 0), 0.0)
        )
    return total


def send_blocks(send_ref, count, base, value_ref, block):
    for j in range(10):
        parts = []
        for q in range(4):
            m = 4 * j + q
            alpha, n = m // 10, m % 10
            parts.append(move(value_ref[pl.ds(K0 * n + alpha, 16, stride=4), :], block, q))
        merged = merge(parts)
        for g in range(GRPS):
            send_ref[pl.ds(g * count + base + j, 16, stride=2 * count), :] = merged


def send_halves(send_ref, count, base, value_ref, block):
    for g in range(GRPS):
        for j in range(5):
            parts = []
            for q in range(4):
                alpha, b = divmod(4 * j + q, L1)
                row = K0 * (L1 * g + b) + alpha
                parts.append(move(value_ref[pl.ds(row, 16, stride=4), :], block, q))
            send_ref[pl.ds(g * count + base + j, 16, stride=2 * count), :] = merge(parts)


def middle_kernel(
    blend_ref, lift_h_ref, lift_l_ref, scalar_ref, side_ref, send_ref, keep_ref, sums_ref, four_ref
):
    step = pick(scalar_ref, 1)
    small = 0.1 * step
    lifted = product(load((lift_h_ref, lift_l_ref)), split(blend_ref[...]))
    once = coefficient_penalty(lifted)
    twice = coefficient_penalty(once)
    h_a = lifted - small * pltpu.roll(once, 64, 1)
    y_1 = once + pltpu.roll(lifted, 96, 1)
    x_a = once - small * pltpu.roll(twice, 64, 1)
    h_0 = pltpu.roll(lifted, 64, 1)
    lane = iota(lifted.shape, 1)

    def blocks(first, second, third, fourth):
        return jnp.where(
            lane < 32, first, jnp.where(lane < 64, second, jnp.where(lane < 96, third, fourth))
        )

    keep_ref[...] = blocks(h_0, pltpu.roll(h_a, 32, 1), y_1, pltpu.roll(x_a, 96, 1))
    flat = x_a - small * pltpu.roll(once, 32, 1)
    slope = h_a - small * pltpu.roll(y_1, 64, 1)
    four_ref[...] = blocks(
        h_a, -small * pltpu.roll(h_0, 32, 1), pltpu.roll(flat, 64, 1), pltpu.roll(slope, 96, 1)
    )
    grams = split(side_ref[128:192, 0:N1])
    corner = iota((16, 128), 1) // 32
    norm, bend = jnp.zeros((16, 128), f32), jnp.zeros((16, 128), f32)
    filler = jnp.zeros((16 - N1, 128), f32)
    for chunk in range(8):
        tiles = [four_ref[pl.ds(8 * chunk + k, N1, stride=K0), :] for k in range(8)]
        applied = product(grams, split(jnp.concatenate(tiles, axis=1)))
        for k, tile in enumerate(tiles):
            x = jnp.concatenate([tile, filler], axis=0)
            r1, r2, r3 = [pltpu.roll(x, 32 * d, 1) for d in (1, 2, 3)]
            y0, y1, y2, y3 = [applied[16 * d : 16 * d + 16, 128 * k : 128 * k + 128] for d in range(4)]
            norm = norm + jnp.where(
                corner == 0, x * y0, jnp.where(corner == 1, 2.0 * r1 * y1 + x * y2, 0.0)
            )
            bend = bend + jnp.where(
                corner == 1,
                r1 * y2 + x * y3,
                jnp.where(
                    corner == 2, r2 * y0 + r1 * y1, jnp.where(corner == 3, r3 * y1 + r2 * y2, 0.0)
                ),
            )
    sums_ref[...] = lanes((jnp.sum(norm), jnp.sum(bend)))
    for block in range(3):
        send_halves(send_ref, JOINT, 4 + 5 * block, keep_ref, block)


def second_row_kernel(
    early_ref, recv_ref, sums_ref, scalar_ref, wide_ref, inner_ref,
    send_ref, rows_ref, stack_ref,
):
    kron, second, turned = constants(inner_ref)
    send_ref[...] = early_ref[...]
    image = received_rows(recv_ref)
    step = pick(scalar_ref, 1)
    reduced = kept_rows(wide_ref, 1) - step * (
        kept_rows(wide_ref, 0) + 0.1 * kept_rows(wide_ref, 2)
    )
    inner = jnp.sum(reduced * inner_penalty(image))
    field = mixed_to_table(image, kron, second, rows_ref, stack_ref)
    weighted = wide_ref[0:256, :] * field
    energy = jnp.sum(field * weighted)
    mixed = table_to_mixed(weighted, kron, turned, rows_ref, stack_ref)
    for j in range(3):
        put(send_ref, j, JOINT, tile_of(mixed, j))
    spread(send_ref, 3, JOINT, (energy, pick(sums_ref, 0), pick(sums_ref, 1) + inner))


def third_column_kernel(
    recv_ref, lift_h_ref, lift_l_ref, keep_ref, scalar_ref, send_ref, out_scalar_ref, last_ref, mixed_ref
):
    zero = jnp.zeros((32, 128), f32)
    for r in range(ROWS):
        j, q = r // 4, r % 4
        last_ref[32 * r : 32 * r + 32, :] = unpack(recv_ref, j, JOINT, r, q, 0)
    energy, norm_next, bend = totals(recv_ref, 3, JOINT, 3)
    norm, step = pick(scalar_ref, 0), pick(scalar_ref, 1)
    ratio = norm_next / norm
    curve = energy + 0.1 * bend - ratio * norm_next / step
    step_next = norm_next / curve
    out_scalar_ref[...] = lanes((norm, step, ratio, step_next))
    lifted = product(load((lift_h_ref, lift_l_ref)), split(last_ref[...]))
    keep = keep_ref[...]
    h_a, x_a = pltpu.roll(keep, 96, 1), pltpu.roll(keep, 32, 1)
    mixed_ref[...] = (
        h_a - step_next * (lifted + 0.1 * x_a) - (step_next * ratio / step) * (keep - h_a)
    )
    send_blocks(send_ref, 10, 0, mixed_ref, 0)


def gather_blocks(ref, count, base, rows, out_ref, first):
    for j in range(rows):
        taken = [ref[pl.ds(rho * count + base + j, 8, stride=4 * count), :] for rho in range(4)]
        for q in range(4):
            m = first + 4 * j + q
            merged = merge([move(taken[rho], q, rho) for rho in range(4)])
            out_ref[pl.ds(m // 8 * 64 + m % 8, 8, stride=8), :] = merged


def take(ref, block, tile):
    return jnp.concatenate(
        [ref[pl.ds((5 * block + t) * 64 + 8 * tile, 8), :] for t in range(5)], axis=0
    )


def bent_rows(value):
    lane = iota(value.shape, 1)
    inside = lane % 32
    total = 12.0 * value
    for d, weight in ((1, -4.0), (2, 1.0)):
        total = total + weight * (
            jnp.where(lane >= 32 * d, pltpu.roll(value, 32 * d, 1), 0.0)
            + jnp.where(lane < 1024 - 32 * d, pltpu.roll(value, 1024 - 32 * d, 1), 0.0)
            + jnp.where(inside >= d, pltpu.roll(value, d, 1), 0.0)
            + jnp.where(inside < 32 - d, pltpu.roll(value, 1024 - d, 1), 0.0)
        )
    return total


def settle_kernel(own_ref, partner_ref, side_ref, scalar_ref, solution_ref, part_ref, early):
    for block in range(3):
        for h, ref in enumerate((own_ref, partner_ref)):
            gather_blocks(ref, JOINT, 4 + 5 * block, 5, early, 40 * block + 20 * h)
    step, ratio, step_next = pick(scalar_ref, 1), pick(scalar_ref, 2), pick(scalar_ref, 3)
    small = 0.1 * step
    value = split(side_ref[0:128, 128:208])
    slope = split(side_ref[0:128, 256:376])
    bent = bent_rows(jnp.concatenate([take(early, 1, tile) for tile in range(8)], axis=1))
    for tile in range(8):
        h_0, h_a, y_1 = take(early, 0, tile), take(early, 1, tile), take(early, 2, tile)
        right = jnp.concatenate(
            [(step + step_next * ratio) * h_0 + step_next * h_a, (-step_next * small) * h_0], axis=0
        )
        columns = slice(128 * tile, 128 * tile + 128)
        solution_ref[:, :, columns] = product(value, split(right)).reshape(4, 32, 128)
        right = jnp.concatenate(
            [
                (-0.1 * step_next) * bent[:, columns],
                (-small * (1.0 + step_next * ratio / step)) * h_0
                - (0.1 * step_next) * (h_a - small * y_1),
                (0.1 * step_next * small) * h_0,
            ],
            axis=0,
        )
        part_ref[:, columns] = product(slope, split(right))


def final_kernel(late_ref, side_ref, part_ref, residual_ref, late):
    gather_blocks(late_ref, 10, 0, 10, late, 0)
    value = split(side_ref[0:128, 0:40])
    for tile in range(8):
        columns = slice(128 * tile, 128 * tile + 128)
        whole = part_ref[:, columns] + product(value, split(take(late, 0, tile)))
        residual_ref[:, :, columns] = whole.reshape(4, 32, 128)


def call(kernel, outputs, scratch, *operands, aliases={}, left=(), scalars=(), limit=16):
    vmem = pl.BlockSpec(memory_space=pltpu.VMEM)
    specs = [vmem] * len(operands)
    for k in left:
        specs[k] = pl.BlockSpec(memory_space=pltpu.HBM)
    for k in scalars:
        specs[k] = pl.BlockSpec(memory_space=pltpu.SMEM)
    return pl.pallas_call(
        kernel,
        out_shape=[
            shape if isinstance(shape, jax.ShapeDtypeStruct) else jax.ShapeDtypeStruct(shape, f32)
            for shape in outputs
        ],
        in_specs=specs,
        out_specs=[vmem] * len(outputs),
        scratch_shapes=[
            pltpu.VMEM(shape, f32) if isinstance(shape, tuple) else shape for shape in scratch
        ],
        input_output_aliases=aliases,
        compiler_params=pltpu.CompilerParams(vmem_limit_bytes=limit * 2**20),
    )(*operands)


def pair_of(*shape):
    return [jax.ShapeDtypeStruct(shape, jnp.bfloat16)] * 2


def exchange(buffer):
    count = buffer.shape[0] // DEVICES
    tiled = count == 4 or count % 8 == 0
    shape = (DEVICES, count, 128) if tiled else (DEVICES, 1, count * 128)
    moved = lax.all_to_all(buffer.reshape(shape), ("slab", "grp"), 0, 0, tiled=True)
    return moved.reshape(buffer.shape)


def fast_program(
    photon_table,
    bin_weights,
    first_start,
    first_band,
    second_start,
    second_band,
    third_start,
    third_band,
    fourth_start,
    fourth_band,
):
    total = DEVICES * ROWS
    work = [(256, 128), (64, 384)]
    outer = (first_start, first_band.T, second_start, second_band.T)
    inputs = (
        photon_table.transpose(1, 0, 2),
        bin_weights.transpose(1, 0, 2),
        third_start,
        third_band.T,
        fourth_start,
        fourth_band.T,
    )
    send, wide, inner = call(
        start_kernel,
        [(160, 128), (416, 256), jax.ShapeDtypeStruct((704, 128), jnp.bfloat16)],
        [pltpu.VMEM(value.shape, value.dtype) for value in inputs]
        + [pltpu.SemaphoreType.DMA((len(inputs),))]
        + [(16, N2 * N3), (16, N2 * N3), (256, 256)]
        + work,
        *inputs,
        left=range(len(inputs)),
        limit=LARGE,
    )
    recv = exchange(send)
    grams = [(48, 128)] + [pltpu.VMEM((total, 128), jnp.bfloat16)] * 4
    group = lax.axis_index("grp").reshape(1)
    *matrices, side = call(
        matrix_kernel,
        pair_of(2 * total, total) + pair_of(K0 * N1, total) + [(192, 384)],
        grams,
        group, *outer,
        scalars=(0,),
    )
    gram, lift = matrices[0:2], matrices[2:4]
    send, fields, images = call(
        first_column_kernel, [(128, 128), (total, 128), (total, 128)], [], recv, *gram
    )
    recv = exchange(send)
    send, scalars, wide = call(
        first_row_kernel,
        [(128, 128), (8, 128), (416, 256)],
        work,
        recv, wide, inner,
        aliases={1: 2},
    )
    recv = exchange(send)
    send, blend, scalars = call(
        second_column_kernel,
        [(128, 128), (total, 128), (8, 128)],
        [(total, 128), (total, 128)],
        recv, *gram, fields, images, scalars,
        aliases={3: 1},
    )
    recv = exchange(send)
    send, keep, sums = call(
        middle_kernel,
        [(DEVICES * JOINT, 128), (K0 * N1, 128), (8, 128)],
        [(K0 * N1, 128)],
        blend, *lift, scalars, side,
    )
    (send,) = call(
        second_row_kernel,
        [(DEVICES * JOINT, 128)],
        work,
        send, recv, sums, scalars, wide, inner,
        aliases={0: 0},
    )
    recv = exchange(send)
    partner = lax.ppermute(recv, "grp", [(0, 1), (1, 0)])
    send, scalars = call(
        third_column_kernel,
        [(DEVICES * 10, 128), (8, 128)],
        [(total, 128), (K0 * N1, 128)],
        recv, *lift, keep, scalars,
    )
    late = exchange(send)
    solution_part, part = call(
        settle_kernel,
        [(4, 32, 1024), (128, 1024)],
        [(960, 128)],
        recv, partner, side, scalars,
    )
    (residual,) = call(final_kernel, [(4, 32, 1024)], [(320, 128)], late, side, part)
    return solution_part, residual


def fits(mesh):
    return (mesh.shape["slab"], mesh.shape["grp"]) == (SLABS, GRPS)


def solution(mesh):
    placed = (
        P("slab", "grp", None),
        P("slab", "grp", None),
        P(),
        P(),
        P(),
        P(),
        P(),
        P(),
        P(),
        P(),
    )
    return jax.shard_map(
        fast_program if fits(mesh) else per_device,
        mesh=mesh,
        in_specs=placed,
        out_specs=(P("slab", "grp", None), P("slab", "grp", None)),
        check_vma=False,
    )
```

```python
import jax
import jax.numpy as jnp
from jax import lax
from jax.experimental import pallas as pl
from jax.experimental.pallas import tpu as pltpu
from jax.sharding import PartitionSpec as P

K0 = 64
K1 = 64
K2 = 32
K3 = 32
ITERS = 2


highest = lax.Precision.HIGHEST
smoothing = 0.1
stencil_weights = (1.0, -4.0, 6.0, -4.0, 1.0)


def with_halo(value, sides, width):
    for axis, dim in sides:
        count, length = (lax.axis_size(axis), value.shape[dim])
        up = [(i, (i + 1) % count) for i in range(count - 1)]
        down = [(j, i) for i, j in up]
        last = lax.slice_in_dim(value, length - width, length, axis=dim)
        initial = lax.slice_in_dim(value, 0, width, axis=dim)
        before = lax.ppermute(last, axis, up)
        after = lax.ppermute(initial, axis, down)
        value = jnp.concatenate([before, value, after], axis=dim)
    return value


def dense_basis(starts, values, coef_count):
    relative = jnp.arange(coef_count, dtype=jnp.int32)[None, :] - starts[:, None]
    matrix = jnp.zeros((starts.shape[0], coef_count), jnp.float32)
    for offset in range(4):
        matrix = matrix + jnp.where(relative == offset, values[:, offset : offset + 1], 0.0)
    return matrix


def five_point(source, along, extent):
    running = stencil_weights[0] * lax.slice_in_dim(source, 0, extent, axis=along)
    for offset in range(1, 5):
        running = running + stencil_weights[offset] * lax.slice_in_dim(
            source, offset, offset + extent, axis=along
        )
    return running


def local_stencil(tensor, along):
    widths = [(0, 0)] * tensor.ndim
    widths[along] = (2, 2)
    return five_point(jnp.pad(tensor, widths), along, tensor.shape[along])


def inner_forward(tensor, third_basis, fourth_basis):
    leading, middle = (tensor.shape[0], tensor.shape[1])
    blocked = tensor.reshape(leading, middle, third_basis.shape[1], fourth_basis.shape[1])
    blocked = jnp.einsum("abcd,nd->abcn", blocked, fourth_basis, precision=highest)
    blocked = jnp.einsum("abcn,mc->abmn", blocked, third_basis, precision=highest)
    return blocked.reshape(leading, middle, third_basis.shape[0] * fourth_basis.shape[0])


def inner_adjoint(tensor, third_basis, fourth_basis):
    leading, middle = (tensor.shape[0], tensor.shape[1])
    blocked = tensor.reshape(leading, middle, third_basis.shape[0], fourth_basis.shape[0])
    blocked = jnp.einsum("abmn,mc->abcn", blocked, third_basis, precision=highest)
    blocked = jnp.einsum("abcn,nd->abcd", blocked, fourth_basis, precision=highest)
    return blocked.reshape(leading, middle, third_basis.shape[1] * fourth_basis.shape[1])


def lead_product(tensor, matrix):
    combined = jnp.einsum(
        "ka,ain->kin",
        matrix,
        lax.all_to_all(tensor, "slab", split_axis=2, concat_axis=0, tiled=True),
        precision=highest,
    )
    return lax.all_to_all(combined, "slab", split_axis=0, concat_axis=2, tiled=True)


def second_product(tensor, matrix):
    return jnp.einsum(
        "lp,apn->aln", matrix, lax.all_gather(tensor, "grp", axis=1, tiled=True), precision=highest
    )


def penalty(coeffs):
    leading, middle = (coeffs.shape[0], coeffs.shape[1])
    padded = with_halo(coeffs, (("slab", 0), ("grp", 1)), 2)
    along_lead = five_point(padded[:, 2 : 2 + middle], 0, leading)
    along_rows = five_point(padded[2 : 2 + leading, :], 1, middle)
    blocked = coeffs.reshape(leading, middle, K2, K3)
    inner_part = local_stencil(blocked, 2) + local_stencil(blocked, 3)
    return along_lead + along_rows + inner_part.reshape(leading, middle, K2 * K3)


def squared_total(vector):
    return lax.psum(jnp.sum(vector * vector), ("slab", "grp"))


def per_device(
    photon_table,
    bin_weights,
    first_start,
    first_band,
    second_start,
    second_band,
    third_start,
    third_band,
    fourth_start,
    fourth_band,
):
    first_basis = dense_basis(first_start, first_band, K0)
    second_basis = dense_basis(second_start, second_band, K1)
    third_basis = dense_basis(third_start, third_band, K2)
    fourth_basis = dense_basis(fourth_start, fourth_band, K3)
    first_back = first_basis.T
    group_index = lax.axis_index("grp")
    row_count = photon_table.shape[1]
    coef_rows = K1 // lax.axis_size("grp")
    near_rows = lax.dynamic_slice_in_dim(second_basis, group_index * row_count, row_count, 0)
    back_rows = lax.dynamic_slice_in_dim(second_basis.T, group_index * coef_rows, coef_rows, 0)

    def adjoint(table):
        tensor = lead_product(table, first_back)
        tensor = second_product(tensor, back_rows)
        return inner_adjoint(tensor, third_basis, fourth_basis)

    right_side = adjoint(bin_weights * photon_table)
    solution = jnp.zeros_like(right_side)
    residual = right_side
    direction = right_side
    norm_now = squared_total(residual)
    for sweep in range(ITERS):
        forward_tensor = inner_forward(direction, third_basis, fourth_basis)
        forward_tensor = second_product(forward_tensor, near_rows)
        mapped = adjoint(
            bin_weights * lead_product(forward_tensor, first_basis)
        ) + smoothing * penalty(direction)
        curve_total = lax.psum(jnp.sum(direction * mapped), ("slab", "grp"))
        step_size = norm_now / curve_total
        solution = solution + step_size * direction
        residual = residual - step_size * mapped
        norm_next = squared_total(residual)
        direction = residual + norm_next / norm_now * direction
        norm_now = norm_next
    return (solution, residual)


SLABS, GRPS = 16, 2
DEVICES = SLABS * GRPS
L0, L1 = 2, 5
ROWS = L0 * L1
N2, N3 = 64, 50
N0, N1 = 32, 10
HI = lax.Precision.HIGHEST
f32 = jnp.float32
JOINT = 19
LARGE = 60


def iota(shape, dim):
    return lax.broadcasted_iota(jnp.int32, shape, dim)


def mm(a, b):
    return jnp.dot(a, b, precision=HI, preferred_element_type=f32)


def mm_t(a, b):
    return lax.dot_general(
        a, b, (((1,), (1,)), ((), ())), precision=HI, preferred_element_type=f32
    )


def split(value):
    high = value.astype(jnp.bfloat16)
    return high, (value - high.astype(f32)).astype(jnp.bfloat16)


def product(a, b, transposed=False):
    dims = (((1,), (1 if transposed else 0,)), ((), ()))

    def one(x, y):
        return lax.dot_general(x, y, dims, preferred_element_type=f32)

    return one(a[0], b[0]) + (one(a[0], b[1]) + one(a[1], b[0]))


def load(pair):
    return pair[0][...], pair[1][...]


def move(block, source, target):
    shift = (target - source) * 32 % 128
    return pltpu.roll(block, shift, 1) if shift else block


def merge(parts):
    lane = iota(parts[0].shape, 1)
    out = parts[-1]
    for q in range(len(parts) - 2, -1, -1):
        out = jnp.where(lane < 32 * (q + 1), parts[q], out)
    return out


def slot(r):
    return L0 * (r % L1) + r // L1


def banded_t(start_ref, band_ref, width, wrap):
    n = start_ref.shape[0]
    relative = (iota((width, n), 0) % wrap) - start_ref[...].reshape(1, n)
    out = jnp.zeros((width, n), f32)
    for offset in range(4):
        out = out + jnp.where(relative == offset, band_ref[offset : offset + 1, :], 0.0)
    return out


def expand(ref, p):
    first = 200 * p
    tile, off = first // 128, first % 128
    lane = iota((16, 128), 1)

    def window(t):
        low = ref[:, t * 128 : (t + 1) * 128]
        if off == 0:
            return low
        t1 = min(t + 1, 24)
        high = ref[:, t1 * 128 : (t1 + 1) * 128]
        return jnp.where(
            lane < 128 - off, pltpu.roll(low, 128 - off, 1), pltpu.roll(high, 128 - off, 1)
        )

    return window(tile), window(min(tile + 1, 24))


def table_to_mixed(field, kron_third, second_t, rows_ref, stack_ref):
    rows_ref[...] = product(split(field), kron_third)
    for c in range(4):
        for j in range(3):
            parts = []
            for q in range(4):
                r = 4 * j + q
                if r < ROWS:
                    part = rows_ref[pl.ds(slot(r), 16, stride=16), :]
                    parts.append(move(part, c, q))
                else:
                    parts.append(jnp.zeros((16, 128), f32))
            stack_ref[16 * c : 16 * c + 16, 128 * j : 128 * j + 128] = merge(parts)
    return product(second_t, split(stack_ref[...]))


def mixed_to_table(value, kron_third, second, rows_ref, stack_ref):
    stack_ref[...] = product(second, split(value))
    rows_ref[...] = jnp.zeros((256, 128), f32)
    for r in range(ROWS):
        j, q = r // 4, r % 4
        parts = [
            move(stack_ref[16 * c : 16 * c + 16, 128 * j : 128 * j + 128], q, c) for c in range(4)
        ]
        rows_ref[pl.ds(slot(r), 16, stride=16), :] = merge(parts)
    return product(split(rows_ref[...]), kron_third, True)


def inner_penalty(value):
    out = 12.0 * value
    row = iota((32, 128), 0)
    inside = iota((32, 128), 1) % 32
    tiles = []
    for j in range(3):
        tile = value[:, 128 * j : 128 * j + 128]
        total = 12.0 * tile
        for d, weight in ((1, -4.0), (2, 1.0)):
            total = total + weight * (
                jnp.where(row >= d, pltpu.roll(tile, d, 0), 0.0)
                + jnp.where(row < 32 - d, pltpu.roll(tile, 32 - d, 0), 0.0)
                + jnp.where(inside >= d, pltpu.roll(tile, d, 1), 0.0)
                + jnp.where(inside < 32 - d, pltpu.roll(tile, 128 - d, 1), 0.0)
            )
        tiles.append(total)
    return jnp.concatenate(tiles, axis=1)


def tile_of(value, j):
    return value[:, 128 * j : 128 * j + 128]


def put(ref, row, count, value):
    ref[pl.ds(row, 32, stride=count), :] = value


def lanes(values):
    lane = iota((8, 128), 1)
    out = jnp.zeros((8, 128), f32)
    for k, value in enumerate(values):
        out = jnp.where(lane == k, value, out)
    return out


def spread(ref, row, count, values):
    one = lanes(values)
    put(ref, row, count, jnp.concatenate([one] * 4, axis=0))


def totals(ref, row, count, number):
    summed = jnp.sum(ref[pl.ds(row, 32, stride=count), :], axis=0, keepdims=True)
    lane = iota((1, 128), 1)
    return [jnp.sum(jnp.where(lane == k, summed, 0.0)) for k in range(number)]


def pick(ref, k):
    lane = iota((1, 128), 1)
    return jnp.sum(jnp.where(lane == k, ref[0:1, :], 0.0))


def constants(ref):
    kron = ref[0:256, :], ref[256:512, :]
    second = ref[512:576, 0:32], ref[576:640, 0:32]
    return kron, second, (ref[640:672, 0:64], ref[672:704, 0:64])


def row_tile(piece, j):
    place = 3 * piece + j
    first = 256 + 32 * (place // 2)
    return slice(first, first + 32), slice(128 * (place % 2), 128 * (place % 2) + 128)


def keep_rows(ref, piece, value):
    for j in range(3):
        ref[row_tile(piece, j)] = tile_of(value, j)


def kept_rows(ref, piece):
    return jnp.concatenate([ref[row_tile(piece, j)] for j in range(3)], axis=1)


def start_kernel(
    table_hbm, weight_hbm, start2_hbm, band2_hbm, start3_hbm, band3_hbm,
    send_ref, wide_ref, inner_ref,
    table_ref, weight_ref, start2_ref, band2_ref, start3_ref, band3_ref, sems,
    product_ref, packed_ref, field_ref, rows_ref, stack_ref,
):
    copies = [
        pltpu.make_async_copy(source, target, sems.at[k])
        for k, (source, target) in enumerate(
            (
                (start3_hbm, start3_ref),
                (band3_hbm, band3_ref),
                (start2_hbm, start2_ref),
                (band2_hbm, band2_ref),
                (weight_hbm, weight_ref),
                (table_hbm, table_ref),
            )
        )
    ]
    for k in (4, 5, 1, 0, 3, 2):
        copies[k].start()
    copies[0].wait()
    copies[1].wait()
    pick_bin = (iota((256, N3), 0) % N3 == iota((256, N3), 1)) & (iota((256, N3), 0) < 4 * N3)
    same = iota((256, 128), 0) // N3 == iota((256, 128), 1) // 32
    picker = jnp.where(pick_bin, 1.0, 0.0).astype(jnp.bfloat16)
    for k, term in enumerate(split(banded_t(start3_ref, band3_ref, 128, 32))):
        spread_out = lax.dot_general(
            picker, term, (((1,), (1,)), ((), ())), preferred_element_type=f32
        )
        inner_ref[256 * k : 256 * k + 256, :] = jnp.where(same, spread_out, 0.0).astype(jnp.bfloat16)
    copies[2].wait()
    copies[3].wait()
    order, other = iota((N2, N2), 1), iota((N2, N2), 0)
    permute = jnp.where((order % 16) * 4 + order // 16 == other, 1.0, 0.0).astype(jnp.bfloat16)
    back = jnp.where((other % 16) * 4 + other // 16 == order, 1.0, 0.0).astype(jnp.bfloat16)
    for k, term in enumerate(split(banded_t(start2_ref, band2_ref, 32, 32))):
        value = jnp.dot(term, permute, preferred_element_type=f32)
        inner_ref[640 + 32 * k : 672 + 32 * k, 0:64] = value.astype(jnp.bfloat16)
        value = lax.dot_general(back, term, (((1,), (1,)), ((), ())), preferred_element_type=f32)
        inner_ref[512 + 64 * k : 576 + 64 * k, 0:32] = value.astype(jnp.bfloat16)
    kron, _, turned = constants(inner_ref)
    copies[4].wait()
    copies[5].wait()
    packed_ref[8:16, :] = jnp.zeros((8, N2 * N3), f32)
    product_ref[8:16, :] = jnp.zeros((8, N2 * N3), f32)
    for b in range(L1):
        weight = weight_ref[b]
        packed_ref[L0 * b : L0 * b + L0, :] = weight
        product_ref[L0 * b : L0 * b + L0, :] = weight * table_ref[b]
    for p in range(16):
        for source, target in ((packed_ref, wide_ref), (product_ref, field_ref)):
            low, high = expand(source, p)
            target[16 * p : 16 * p + 16, 0:128] = low
            target[16 * p : 16 * p + 16, 128:256] = high
    mixed = table_to_mixed(field_ref[...], kron, turned, rows_ref, stack_ref)
    once = inner_penalty(mixed)
    keep_rows(wide_ref, 1, mixed)
    keep_rows(wide_ref, 2, once)
    for base, value in ((0, mixed), (3, once)):
        put(send_ref, base, 5, tile_of(value, 0))
        put(send_ref, base + 1, 5, tile_of(value, 1))
    lane = iota((32, 128), 1)
    put(send_ref, 2, 5, jnp.where(lane < 64, tile_of(mixed, 2), pltpu.roll(tile_of(once, 2), 64, 1)))


def pentadiagonal(n):
    gap = jnp.abs(iota((n, n), 0) - iota((n, n), 1))
    return jnp.where(gap == 0, 6.0, jnp.where(gap == 1, -4.0, jnp.where(gap == 2, 1.0, 0.0)))


def choose(pieces, selector):
    out = None
    for piece in pieces:
        term = jnp.dot(piece, selector, preferred_element_type=f32)
        out = term if out is None else out + term
    return out


def powers(basis_t, count):
    penalty_matrix = pentadiagonal(basis_t.shape[0])
    out = [basis_t]
    for _ in range(count - 1):
        out.append(mm(penalty_matrix, out[-1]))
    return out


def store_split(high_ref, low_ref, rows, value):
    high, low = split(value)
    high_ref[rows, :] = high
    low_ref[rows, :] = low


def gram_blocks(refs, count, small_ref, rows0_h, rows0_l, rows1_h, rows1_l):
    start0_ref, band0_ref, start1_ref, band1_ref = refs
    total = DEVICES * ROWS
    powers0 = powers(banded_t(start0_ref, band0_ref, K0, K0), count)
    powers1 = powers(banded_t(start1_ref, band1_ref, K1, K1), 4)
    small_ref[...] = jnp.zeros((48, 128), f32)
    first, second = powers0[0].T, powers1[0].T
    for k in range(count):
        small_ref[0:N0, 32 * k : 32 * k + N0] = mm(first, powers0[k])
        small_ref[N0 : N0 + N1, 32 * k : 32 * k + N1] = mm(second, powers1[k])
    row0 = iota((total, N0), 0)
    pick0 = L0 * (row0 % 32 // GRPS) + row0 // 32 // L1 == iota((total, N0), 1)
    row1 = iota((total, 16), 0)
    pick1 = L1 * (row1 % GRPS) + row1 // 32 % L1 == iota((total, 16), 1)
    for pick, rows, targets in (
        (pick0, slice(0, N0), (rows0_h, rows0_l)),
        (pick1, slice(N0, N0 + 16), (rows1_h, rows1_l)),
    ):
        chooser = jnp.where(pick, 1.0, 0.0).astype(jnp.bfloat16)
        for term, target in zip(split(small_ref[rows, :]), targets):
            spread_out = jnp.dot(chooser, term, preferred_element_type=f32)
            target[...] = spread_out.astype(jnp.bfloat16)
    line, column = iota((128, total), 0), iota((128, total), 1)
    match0 = line % 32 == L0 * (column % 32 // GRPS) + column // 32 // L1
    match1 = line % 32 == L1 * (column % GRPS) + column // 32 % L1
    select0, select1 = [
        [
            jnp.where(match & (line // 32 == k), 1.0, 0.0).astype(jnp.bfloat16)
            for k in range(count)
        ]
        for match in (match0, match1)
    ]

    def block(base):
        block0 = rows0_h[pl.ds(base, 64), :], rows0_l[pl.ds(base, 64), :]
        block1 = rows1_h[pl.ds(base, 64), :], rows1_l[pl.ds(base, 64), :]
        g = [choose(block0, selector) for selector in select0]
        h = [choose(block1, selector) for selector in select1]
        return g, h

    return powers0, powers1, select0[0][0:N0, :], block


def matrix_kernel(
    group_ref, start0_ref, band0_ref, start1_ref, band1_ref,
    gram_h_ref, gram_l_ref, lift_h_ref, lift_l_ref, side_ref, small_h_ref, small_l_ref, *scratch,
):
    total = DEVICES * ROWS
    refs = (start0_ref, band0_ref, start1_ref, band1_ref)
    powers0, powers1, chosen, block = gram_blocks(refs, 2, *scratch)

    @pl.loop(0, 5)
    def _(step):
        base = pl.multiple_of(step * 64, 64)
        g, h = block(base)
        store_split(gram_h_ref, gram_l_ref, pl.ds(base, 64), g[0] * h[0])
        store_split(
            gram_h_ref, gram_l_ref, pl.ds(base + total, 64), g[1] * h[0] + g[0] * h[1]
        )

    lifted = [
        jnp.dot(term, chosen, preferred_element_type=f32)
        for term in split(powers0[0])
    ]
    spot = iota((N0, N0), 1)
    order = jnp.where(L0 * (spot % 16) + spot // 16 == iota((N0, N0), 0), 1.0, 0.0).astype(jnp.bfloat16)
    for term, target in zip(split(powers0[0]), (small_h_ref, small_l_ref)):
        target[...] = jnp.dot(term, order, preferred_element_type=f32).astype(jnp.bfloat16)
    owner = L1 * (iota((K0, total), 1) % GRPS) + iota((K0, total), 1) // 32 % L1
    for n in range(N1):
        rows = slice(K0 * n, K0 * n + K0)
        for term, target in zip(lifted, (lift_h_ref, lift_l_ref)):
            target[rows, :] = jnp.where(owner == n, term, 0.0).astype(jnp.bfloat16)
    group = group_ref[0]
    coef = iota((128, K1), 0) % 32 + 32 * group
    pick_coef = jnp.where(coef == iota((128, K1), 1), 1.0, 0.0)
    half = iota((N1, N1), 1) // L1
    wanted = L1 * jnp.where(half == group, 0, 1) + iota((N1, N1), 1) % L1
    reorder = jnp.where(iota((N1, N1), 0) == wanted, 1.0, 0.0)
    side_ref[...] = jnp.zeros((192, 384), f32)
    across = powers1[0].T
    for k in range(4):
        side_ref[128 + 16 * k : 128 + 16 * k + N1, 0:N1] = mm(across, powers1[k])
    for k in range(3):
        own = mm(pick_coef, powers1[k])
        halves = mm(own, reorder)
        for alpha in range(4):
            rows = slice(32 * alpha, 32 * alpha + 32)
            if k == 0:
                side_ref[rows, 10 * alpha : 10 * alpha + 10] = own[rows, :]
            for h in range(2):
                piece = halves[rows, L1 * h : L1 * h + L1]
                place = 40 * k + 20 * h + L1 * alpha
                side_ref[rows, 256 + place : 256 + place + L1] = piece
                if k < 2:
                    side_ref[rows, 128 + place : 128 + place + L1] = piece


def unpack(ref, row, count, r, source, target):
    return move(ref[pl.ds(row, 32, stride=count), :], source, target)


def first_column_kernel(recv_ref, gram_h_ref, gram_l_ref, send_ref, fields_ref, images_ref):
    total = DEVICES * ROWS
    zero = jnp.zeros((32, 128), f32)
    for r in range(ROWS):
        j, q = r // 4, r % 4
        where0 = (j, q) if j < 2 else (2, q)
        where1 = (3 + j, q) if j < 2 else (2, q + 2)
        parts = [
            unpack(recv_ref, place[0], 5, r, place[1], k) for k, place in enumerate((where0, where1))
        ]
        fields_ref[32 * r : 32 * r + 32, :] = merge(parts + [zero])
    fields = fields_ref[...]
    applied = product(load((gram_h_ref, gram_l_ref)), split(fields))
    lane = iota((total, 128), 1)
    images = applied[:total] + jnp.where(
        (lane >= 32) & (lane < 64), pltpu.roll(applied[total:], 32, 1), 0.0
    )
    images_ref[...] = images
    norm = jnp.sum(jnp.where(lane < 32, fields * images, 0.0))
    bend = jnp.sum(jnp.where(lane < 32, fields * pltpu.roll(images, 96, 1), 0.0))
    send_rows(send_ref, images_ref)
    spread(send_ref, 3, 4, (norm, bend))


def send_rows(send_ref, value_ref):
    for j in range(3):
        parts = []
        for q in range(4):
            r = 4 * j + q
            if r < ROWS:
                parts.append(move(value_ref[32 * r : 32 * r + 32, :], 0, q))
            else:
                parts.append(jnp.zeros((32, 128), f32))
        put(send_ref, j, 4, merge(parts))


def received_rows(recv_ref):
    return jnp.concatenate([recv_ref[pl.ds(j, 32, stride=4), :] for j in range(3)], axis=1)


def first_row_kernel(
    recv_ref, wide_ref, inner_ref, send_ref, scalar_ref, carried_ref, rows_ref, stack_ref,
):
    norm, bend = totals(recv_ref, 3, 4, 2)
    scalar_ref[...] = lanes((norm, bend))
    kron, second, turned = constants(inner_ref)
    field = mixed_to_table(received_rows(recv_ref), kron, second, rows_ref, stack_ref)
    weighted = wide_ref[0:256, :] * field
    energy = jnp.sum(field * weighted)
    mixed = table_to_mixed(weighted, kron, turned, rows_ref, stack_ref)
    carried_ref[...] = wide_ref[...]
    keep_rows(carried_ref, 0, mixed)
    for j in range(3):
        put(send_ref, j, 4, tile_of(mixed, j))
    spread(send_ref, 3, 4, (energy,))


def second_column_kernel(
    recv_ref, gram_h_ref, gram_l_ref, fields_ref, images_ref, scalar_ref,
    send_ref, blend_ref, out_scalar_ref, next_ref, image_ref,
):
    zero = jnp.zeros((32, 128), f32)
    for r in range(ROWS):
        part = unpack(recv_ref, r // 4, 4, r, r % 4, 0)
        next_ref[32 * r : 32 * r + 32, :] = merge([part, zero])
    (energy,) = totals(recv_ref, 3, 4, 1)
    norm, bend = pick(scalar_ref, 0), pick(scalar_ref, 1)
    step = norm / (energy + 0.1 * bend)
    out_scalar_ref[...] = lanes((norm, step))
    fields, images, following = fields_ref[...], images_ref[...], next_ref[...]
    gram = gram_h_ref[0 : DEVICES * ROWS, :], gram_l_ref[0 : DEVICES * ROWS, :]
    image = product(gram, split(following))
    image_ref[...] = images - step * (image + 0.1 * pltpu.roll(images, 96, 1))
    send_rows(send_ref, image_ref)
    put(send_ref, 3, 4, zero)
    lane = iota(fields.shape, 1)
    reduced = fields - step * (following + 0.1 * pltpu.roll(fields, 96, 1))
    kept = jnp.where(lane < 64, 0.0, pltpu.roll(fields, 64, 1))
    blend_ref[...] = jnp.where(lane < 32, reduced, kept)


def coefficient_penalty(value):
    k = iota(value.shape, 0) % K0
    count = value.shape[0]
    total = 6.0 * value
    for d, weight in ((1, -4.0), (2, 1.0)):
        total = total + weight * (
            jnp.where(k >= d, pltpu.roll(value, d, 0), 0.0)
            + jnp.where(k < K0 - d, pltpu.roll(value, count - d, 0), 0.0)
        )
    return total


def send_blocks(send_ref, count, base, value_ref, block):
    for j in range(10):
        parts = []
        for q in range(4):
            m = 4 * j + q
            alpha, n = m // 10, m % 10
            parts.append(move(value_ref[pl.ds(K0 * n + alpha, 16, stride=4), :], block, q))
        merged = merge(parts)
        for g in range(GRPS):
            send_ref[pl.ds(g * count + base + j, 16, stride=2 * count), :] = merged


def send_halves(send_ref, count, base, value_ref, block):
    for g in range(GRPS):
        for j in range(5):
            parts = []
            for q in range(4):
                alpha, b = divmod(4 * j + q, L1)
                row = K0 * (L1 * g + b) + alpha
                parts.append(move(value_ref[pl.ds(row, 16, stride=4), :], block, q))
            send_ref[pl.ds(g * count + base + j, 16, stride=2 * count), :] = merge(parts)


def middle_kernel(
    blend_ref, lift_h_ref, lift_l_ref, scalar_ref, side_ref, send_ref, keep_ref, sums_ref, four_ref
):
    step = pick(scalar_ref, 1)
    small = 0.1 * step
    lifted = product(load((lift_h_ref, lift_l_ref)), split(blend_ref[...]))
    once = coefficient_penalty(lifted)
    twice = coefficient_penalty(once)
    h_a = lifted - small * pltpu.roll(once, 64, 1)
    y_1 = once + pltpu.roll(lifted, 96, 1)
    x_a = once - small * pltpu.roll(twice, 64, 1)
    h_0 = pltpu.roll(lifted, 64, 1)
    lane = iota(lifted.shape, 1)

    def blocks(first, second, third, fourth):
        return jnp.where(
            lane < 32, first, jnp.where(lane < 64, second, jnp.where(lane < 96, third, fourth))
        )

    keep_ref[...] = blocks(h_0, pltpu.roll(h_a, 32, 1), y_1, pltpu.roll(x_a, 96, 1))
    flat = x_a - small * pltpu.roll(once, 32, 1)
    slope = h_a - small * pltpu.roll(y_1, 64, 1)
    four_ref[...] = blocks(
        h_a, -small * pltpu.roll(h_0, 32, 1), pltpu.roll(flat, 64, 1), pltpu.roll(slope, 96, 1)
    )
    grams = split(side_ref[128:192, 0:N1])
    corner = iota((16, 128), 1) // 32
    norm, bend = jnp.zeros((16, 128), f32), jnp.zeros((16, 128), f32)
    filler = jnp.zeros((16 - N1, 128), f32)
    for chunk in range(8):
        tiles = [four_ref[pl.ds(8 * chunk + k, N1, stride=K0), :] for k in range(8)]
        applied = product(grams, split(jnp.concatenate(tiles, axis=1)))
        for k, tile in enumerate(tiles):
            x = jnp.concatenate([tile, filler], axis=0)
            r1, r2, r3 = [pltpu.roll(x, 32 * d, 1) for d in (1, 2, 3)]
            y0, y1, y2, y3 = [applied[16 * d : 16 * d + 16, 128 * k : 128 * k + 128] for d in range(4)]
            norm = norm + jnp.where(
                corner == 0, x * y0, jnp.where(corner == 1, 2.0 * r1 * y1 + x * y2, 0.0)
            )
            bend = bend + jnp.where(
                corner == 1,
                r1 * y2 + x * y3,
                jnp.where(
                    corner == 2, r2 * y0 + r1 * y1, jnp.where(corner == 3, r3 * y1 + r2 * y2, 0.0)
                ),
            )
    sums_ref[...] = lanes((jnp.sum(norm), jnp.sum(bend)))
    for block in range(3):
        send_halves(send_ref, JOINT, 4 + 5 * block, keep_ref, block)


def second_row_kernel(
    early_ref, recv_ref, sums_ref, scalar_ref, wide_ref, inner_ref,
    send_ref, rows_ref, stack_ref,
):
    kron, second, turned = constants(inner_ref)
    send_ref[...] = early_ref[...]
    image = received_rows(recv_ref)
    step = pick(scalar_ref, 1)
    reduced = kept_rows(wide_ref, 1) - step * (
        kept_rows(wide_ref, 0) + 0.1 * kept_rows(wide_ref, 2)
    )
    inner = jnp.sum(reduced * inner_penalty(image))
    field = mixed_to_table(image, kron, second, rows_ref, stack_ref)
    weighted = wide_ref[0:256, :] * field
    energy = jnp.sum(field * weighted)
    mixed = table_to_mixed(weighted, kron, turned, rows_ref, stack_ref)
    for j in range(3):
        put(send_ref, j, JOINT, tile_of(mixed, j))
    spread(send_ref, 3, JOINT, (energy, pick(sums_ref, 0), pick(sums_ref, 1) + inner))


def third_column_kernel(
    recv_ref, small_h_ref, small_l_ref, keep_ref, scalar_ref,
    send_ref, out_scalar_ref, packed_ref, lifted_ref, mixed_ref,
):
    for a in range(L0):
        for t in range(3):
            parts = []
            for block in range(4):
                n = 4 * t + block
                if n < N1:
                    g, b = divmod(n, L1)
                    j, q = divmod(L1 * a + b, 4)
                    part = recv_ref[pl.ds(g * JOINT + j, 16, stride=2 * JOINT), :]
                    parts.append(move(part, q, block))
                else:
                    parts.append(jnp.zeros((16, 128), f32))
            packed_ref[16 * a : 16 * a + 16, 128 * t : 128 * t + 128] = merge(parts)
    packed = product(load((small_h_ref, small_l_ref)), split(packed_ref[...]))
    for n in range(N1):
        lifted_ref[K0 * n : K0 * n + K0, :] = move(tile_of(packed, n // 4), n % 4, 0)
    energy, norm_next, bend = totals(recv_ref, 3, JOINT, 3)
    norm, step = pick(scalar_ref, 0), pick(scalar_ref, 1)
    ratio = norm_next / norm
    curve = energy + 0.1 * bend - ratio * norm_next / step
    step_next = norm_next / curve
    out_scalar_ref[...] = lanes((norm, step, ratio, step_next))
    lifted = lifted_ref[...]
    keep = keep_ref[...]
    h_a, x_a = pltpu.roll(keep, 96, 1), pltpu.roll(keep, 32, 1)
    mixed_ref[...] = (
        h_a - step_next * (lifted + 0.1 * x_a) - (step_next * ratio / step) * (keep - h_a)
    )
    send_blocks(send_ref, 10, 0, mixed_ref, 0)


def gather_blocks(ref, count, base, rows, out_ref, first):
    for j in range(rows):
        taken = [ref[pl.ds(rho * count + base + j, 8, stride=4 * count), :] for rho in range(4)]
        for q in range(4):
            m = first + 4 * j + q
            merged = merge([move(taken[rho], q, rho) for rho in range(4)])
            out_ref[pl.ds(m // 8 * 64 + m % 8, 8, stride=8), :] = merged


def take(ref, block, tile):
    return jnp.concatenate(
        [ref[pl.ds((5 * block + t) * 64 + 8 * tile, 8), :] for t in range(5)], axis=0
    )


def bent_rows(value):
    lane = iota(value.shape, 1)
    inside = lane % 32
    total = 12.0 * value
    for d, weight in ((1, -4.0), (2, 1.0)):
        total = total + weight * (
            jnp.where(lane >= 32 * d, pltpu.roll(value, 32 * d, 1), 0.0)
            + jnp.where(lane < 1024 - 32 * d, pltpu.roll(value, 1024 - 32 * d, 1), 0.0)
            + jnp.where(inside >= d, pltpu.roll(value, d, 1), 0.0)
            + jnp.where(inside < 32 - d, pltpu.roll(value, 1024 - d, 1), 0.0)
        )
    return total


def settle_kernel(own_ref, partner_ref, side_ref, scalar_ref, solution_ref, part_ref, early):
    for block in range(3):
        for h, ref in enumerate((own_ref, partner_ref)):
            gather_blocks(ref, JOINT, 4 + 5 * block, 5, early, 40 * block + 20 * h)
    step, ratio, step_next = pick(scalar_ref, 1), pick(scalar_ref, 2), pick(scalar_ref, 3)
    small = 0.1 * step
    value = split(side_ref[0:128, 128:208])
    slope = split(side_ref[0:128, 256:376])
    bent = bent_rows(jnp.concatenate([take(early, 1, tile) for tile in range(8)], axis=1))
    for tile in range(8):
        h_0, h_a, y_1 = take(early, 0, tile), take(early, 1, tile), take(early, 2, tile)
        right = jnp.concatenate(
            [(step + step_next * ratio) * h_0 + step_next * h_a, (-step_next * small) * h_0], axis=0
        )
        columns = slice(128 * tile, 128 * tile + 128)
        solution_ref[:, :, columns] = product(value, split(right)).reshape(4, 32, 128)
        right = jnp.concatenate(
            [
                (-0.1 * step_next) * bent[:, columns],
                (-small * (1.0 + step_next * ratio / step)) * h_0
                - (0.1 * step_next) * (h_a - small * y_1),
                (0.1 * step_next * small) * h_0,
            ],
            axis=0,
        )
        part_ref[:, columns] = product(slope, split(right))


def final_kernel(late_ref, side_ref, part_ref, residual_ref, late):
    gather_blocks(late_ref, 10, 0, 10, late, 0)
    value = split(side_ref[0:128, 0:40])
    for tile in range(8):
        columns = slice(128 * tile, 128 * tile + 128)
        whole = part_ref[:, columns] + product(value, split(take(late, 0, tile)))
        residual_ref[:, :, columns] = whole.reshape(4, 32, 128)


def call(kernel, outputs, scratch, *operands, aliases={}, left=(), scalars=(), limit=16):
    vmem = pl.BlockSpec(memory_space=pltpu.VMEM)
    specs = [vmem] * len(operands)
    for k in left:
        specs[k] = pl.BlockSpec(memory_space=pltpu.HBM)
    for k in scalars:
        specs[k] = pl.BlockSpec(memory_space=pltpu.SMEM)
    return pl.pallas_call(
        kernel,
        out_shape=[
            shape if isinstance(shape, jax.ShapeDtypeStruct) else jax.ShapeDtypeStruct(shape, f32)
            for shape in outputs
        ],
        in_specs=specs,
        out_specs=[vmem] * len(outputs),
        scratch_shapes=[
            pltpu.VMEM(shape, f32) if isinstance(shape, tuple) else shape for shape in scratch
        ],
        input_output_aliases=aliases,
        compiler_params=pltpu.CompilerParams(vmem_limit_bytes=limit * 2**20),
    )(*operands)


def pair_of(*shape):
    return [jax.ShapeDtypeStruct(shape, jnp.bfloat16)] * 2


def exchange(buffer):
    count = buffer.shape[0] // DEVICES
    tiled = count == 4 or count % 8 == 0
    shape = (DEVICES, count, 128) if tiled else (DEVICES, 1, count * 128)
    moved = lax.all_to_all(buffer.reshape(shape), ("slab", "grp"), 0, 0, tiled=True)
    return moved.reshape(buffer.shape)


def fast_program(
    photon_table,
    bin_weights,
    first_start,
    first_band,
    second_start,
    second_band,
    third_start,
    third_band,
    fourth_start,
    fourth_band,
):
    total = DEVICES * ROWS
    work = [(256, 128), (64, 384)]
    outer = (first_start, first_band.T, second_start, second_band.T)
    inputs = (
        photon_table.transpose(1, 0, 2),
        bin_weights.transpose(1, 0, 2),
        third_start,
        third_band.T,
        fourth_start,
        fourth_band.T,
    )
    send, wide, inner = call(
        start_kernel,
        [(160, 128), (416, 256), jax.ShapeDtypeStruct((704, 128), jnp.bfloat16)],
        [pltpu.VMEM(value.shape, value.dtype) for value in inputs]
        + [pltpu.SemaphoreType.DMA((len(inputs),))]
        + [(16, N2 * N3), (16, N2 * N3), (256, 256)]
        + work,
        *inputs,
        left=range(len(inputs)),
        limit=LARGE,
    )
    recv = exchange(send)
    grams = [(48, 128)] + [pltpu.VMEM((total, 128), jnp.bfloat16)] * 4
    group = lax.axis_index("grp").reshape(1)
    *matrices, side, small_h, small_l = call(
        matrix_kernel,
        pair_of(2 * total, total) + pair_of(K0 * N1, total) + [(192, 384)] + pair_of(K0, N0),
        grams,
        group, *outer,
        scalars=(0,),
    )
    gram, lift = matrices[0:2], matrices[2:4]
    send, fields, images = call(
        first_column_kernel, [(128, 128), (total, 128), (total, 128)], [], recv, *gram
    )
    recv = exchange(send)
    send, scalars, wide = call(
        first_row_kernel,
        [(128, 128), (8, 128), (416, 256)],
        work,
        recv, wide, inner,
        aliases={1: 2},
    )
    recv = exchange(send)
    send, blend, scalars = call(
        second_column_kernel,
        [(128, 128), (total, 128), (8, 128)],
        [(total, 128), (total, 128)],
        recv, *gram, fields, images, scalars,
        aliases={3: 1},
    )
    recv = exchange(send)
    send, keep, sums = call(
        middle_kernel,
        [(DEVICES * JOINT, 128), (K0 * N1, 128), (8, 128)],
        [(K0 * N1, 128)],
        blend, *lift, scalars, side,
    )
    (send,) = call(
        second_row_kernel,
        [(DEVICES * JOINT, 128)],
        work,
        send, recv, sums, scalars, wide, inner,
        aliases={0: 0},
    )
    recv = exchange(send)
    partner = lax.ppermute(recv, "grp", [(0, 1), (1, 0)])
    send, scalars = call(
        third_column_kernel,
        [(DEVICES * 10, 128), (8, 128)],
        [(32, 384), (K0 * N1, 128), (K0 * N1, 128)],
        recv, small_h, small_l, keep, scalars,
    )
    late = exchange(send)
    solution_part, part = call(
        settle_kernel,
        [(4, 32, 1024), (128, 1024)],
        [(960, 128)],
        recv, partner, side, scalars,
    )
    (residual,) = call(final_kernel, [(4, 32, 1024)], [(320, 128)], late, side, part)
    return solution_part, residual


def fits(mesh):
    return (mesh.shape["slab"], mesh.shape["grp"]) == (SLABS, GRPS)


def solution(mesh):
    placed = (
        P("slab", "grp", None),
        P("slab", "grp", None),
        P(),
        P(),
        P(),
        P(),
        P(),
        P(),
        P(),
        P(),
    )
    return jax.shard_map(
        fast_program if fits(mesh) else per_device,
        mesh=mesh,
        in_specs=placed,
        out_specs=(P("slab", "grp", None), P("slab", "grp", None)),
        check_vma=False,
    )
```

```python
import jax
import jax.numpy as jnp
from jax import lax
from jax.experimental import pallas as pl
from jax.experimental.pallas import tpu as pltpu
from jax.sharding import PartitionSpec as P

K0 = 64
K1 = 64
K2 = 32
K3 = 32
ITERS = 2


highest = lax.Precision.HIGHEST
smoothing = 0.1
stencil_weights = (1.0, -4.0, 6.0, -4.0, 1.0)


def with_halo(value, sides, width):
    for axis, dim in sides:
        count, length = (lax.axis_size(axis), value.shape[dim])
        up = [(i, (i + 1) % count) for i in range(count - 1)]
        down = [(j, i) for i, j in up]
        last = lax.slice_in_dim(value, length - width, length, axis=dim)
        initial = lax.slice_in_dim(value, 0, width, axis=dim)
        before = lax.ppermute(last, axis, up)
        after = lax.ppermute(initial, axis, down)
        value = jnp.concatenate([before, value, after], axis=dim)
    return value


def dense_basis(starts, values, coef_count):
    relative = jnp.arange(coef_count, dtype=jnp.int32)[None, :] - starts[:, None]
    matrix = jnp.zeros((starts.shape[0], coef_count), jnp.float32)
    for offset in range(4):
        matrix = matrix + jnp.where(relative == offset, values[:, offset : offset + 1], 0.0)
    return matrix


def five_point(source, along, extent):
    running = stencil_weights[0] * lax.slice_in_dim(source, 0, extent, axis=along)
    for offset in range(1, 5):
        running = running + stencil_weights[offset] * lax.slice_in_dim(
            source, offset, offset + extent, axis=along
        )
    return running


def local_stencil(tensor, along):
    widths = [(0, 0)] * tensor.ndim
    widths[along] = (2, 2)
    return five_point(jnp.pad(tensor, widths), along, tensor.shape[along])


def inner_forward(tensor, third_basis, fourth_basis):
    leading, middle = (tensor.shape[0], tensor.shape[1])
    blocked = tensor.reshape(leading, middle, third_basis.shape[1], fourth_basis.shape[1])
    blocked = jnp.einsum("abcd,nd->abcn", blocked, fourth_basis, precision=highest)
    blocked = jnp.einsum("abcn,mc->abmn", blocked, third_basis, precision=highest)
    return blocked.reshape(leading, middle, third_basis.shape[0] * fourth_basis.shape[0])


def inner_adjoint(tensor, third_basis, fourth_basis):
    leading, middle = (tensor.shape[0], tensor.shape[1])
    blocked = tensor.reshape(leading, middle, third_basis.shape[0], fourth_basis.shape[0])
    blocked = jnp.einsum("abmn,mc->abcn", blocked, third_basis, precision=highest)
    blocked = jnp.einsum("abcn,nd->abcd", blocked, fourth_basis, precision=highest)
    return blocked.reshape(leading, middle, third_basis.shape[1] * fourth_basis.shape[1])


def lead_product(tensor, matrix):
    combined = jnp.einsum(
        "ka,ain->kin",
        matrix,
        lax.all_to_all(tensor, "slab", split_axis=2, concat_axis=0, tiled=True),
        precision=highest,
    )
    return lax.all_to_all(combined, "slab", split_axis=0, concat_axis=2, tiled=True)


def second_product(tensor, matrix):
    return jnp.einsum(
        "lp,apn->aln", matrix, lax.all_gather(tensor, "grp", axis=1, tiled=True), precision=highest
    )


def penalty(coeffs):
    leading, middle = (coeffs.shape[0], coeffs.shape[1])
    padded = with_halo(coeffs, (("slab", 0), ("grp", 1)), 2)
    along_lead = five_point(padded[:, 2 : 2 + middle], 0, leading)
    along_rows = five_point(padded[2 : 2 + leading, :], 1, middle)
    blocked = coeffs.reshape(leading, middle, K2, K3)
    inner_part = local_stencil(blocked, 2) + local_stencil(blocked, 3)
    return along_lead + along_rows + inner_part.reshape(leading, middle, K2 * K3)


def squared_total(vector):
    return lax.psum(jnp.sum(vector * vector), ("slab", "grp"))


def per_device(
    photon_table,
    bin_weights,
    first_start,
    first_band,
    second_start,
    second_band,
    third_start,
    third_band,
    fourth_start,
    fourth_band,
):
    first_basis = dense_basis(first_start, first_band, K0)
    second_basis = dense_basis(second_start, second_band, K1)
    third_basis = dense_basis(third_start, third_band, K2)
    fourth_basis = dense_basis(fourth_start, fourth_band, K3)
    first_back = first_basis.T
    group_index = lax.axis_index("grp")
    row_count = photon_table.shape[1]
    coef_rows = K1 // lax.axis_size("grp")
    near_rows = lax.dynamic_slice_in_dim(second_basis, group_index * row_count, row_count, 0)
    back_rows = lax.dynamic_slice_in_dim(second_basis.T, group_index * coef_rows, coef_rows, 0)

    def adjoint(table):
        tensor = lead_product(table, first_back)
        tensor = second_product(tensor, back_rows)
        return inner_adjoint(tensor, third_basis, fourth_basis)

    right_side = adjoint(bin_weights * photon_table)
    solution = jnp.zeros_like(right_side)
    residual = right_side
    direction = right_side
    norm_now = squared_total(residual)
    for sweep in range(ITERS):
        forward_tensor = inner_forward(direction, third_basis, fourth_basis)
        forward_tensor = second_product(forward_tensor, near_rows)
        mapped = adjoint(
            bin_weights * lead_product(forward_tensor, first_basis)
        ) + smoothing * penalty(direction)
        curve_total = lax.psum(jnp.sum(direction * mapped), ("slab", "grp"))
        step_size = norm_now / curve_total
        solution = solution + step_size * direction
        residual = residual - step_size * mapped
        norm_next = squared_total(residual)
        direction = residual + norm_next / norm_now * direction
        norm_now = norm_next
    return (solution, residual)


SLABS, GRPS = 16, 2
DEVICES = SLABS * GRPS
L0, L1 = 2, 5
ROWS = L0 * L1
N2, N3 = 64, 50
N0, N1 = 32, 10
HI = lax.Precision.HIGHEST
f32 = jnp.float32
JOINT = 18
PLAIN = 3
LARGE = 60


def iota(shape, dim):
    return lax.broadcasted_iota(jnp.int32, shape, dim)


def mm(a, b):
    return jnp.dot(a, b, precision=HI, preferred_element_type=f32)


def mm_t(a, b):
    return lax.dot_general(
        a, b, (((1,), (1,)), ((), ())), precision=HI, preferred_element_type=f32
    )


def split(value):
    high = value.astype(jnp.bfloat16)
    return high, (value - high.astype(f32)).astype(jnp.bfloat16)


def product(a, b, transposed=False):
    dims = (((1,), (1 if transposed else 0,)), ((), ()))

    def one(x, y):
        return lax.dot_general(x, y, dims, preferred_element_type=f32)

    return one(a[0], b[0]) + (one(a[0], b[1]) + one(a[1], b[0]))


def load(pair):
    return pair[0][...], pair[1][...]


def move(block, source, target):
    shift = (target - source) * 32 % 128
    return pltpu.roll(block, shift, 1) if shift else block


def merge(parts):
    lane = iota(parts[0].shape, 1)
    out = parts[-1]
    for q in range(len(parts) - 2, -1, -1):
        out = jnp.where(lane < 32 * (q + 1), parts[q], out)
    return out


def slot(r):
    return L0 * (r % L1) + r // L1


def banded_t(start_ref, band_ref, width, wrap):
    n = start_ref.shape[0]
    relative = (iota((width, n), 0) % wrap) - start_ref[...].reshape(1, n)
    out = jnp.zeros((width, n), f32)
    for offset in range(4):
        out = out + jnp.where(relative == offset, band_ref[offset : offset + 1, :], 0.0)
    return out


def expand(ref, p):
    first = 200 * p
    tile, off = first // 128, first % 128
    lane = iota((16, 128), 1)

    def window(t):
        low = ref[:, t * 128 : (t + 1) * 128]
        if off == 0:
            return low
        t1 = min(t + 1, 24)
        high = ref[:, t1 * 128 : (t1 + 1) * 128]
        return jnp.where(
            lane < 128 - off, pltpu.roll(low, 128 - off, 1), pltpu.roll(high, 128 - off, 1)
        )

    return window(tile), window(min(tile + 1, 24))


def table_to_mixed(field, kron_third, second_t, rows_ref, stack_ref):
    rows_ref[...] = product(split(field), kron_third)
    for c in range(4):
        for j in range(3):
            parts = []
            for q in range(4):
                r = 4 * j + q
                if r < ROWS:
                    part = rows_ref[pl.ds(slot(r), 16, stride=16), :]
                    parts.append(move(part, c, q))
                else:
                    parts.append(jnp.zeros((16, 128), f32))
            stack_ref[16 * c : 16 * c + 16, 128 * j : 128 * j + 128] = merge(parts)
    return product(second_t, split(stack_ref[...]))


def mixed_to_table(value, kron_third, second, rows_ref, stack_ref):
    stack_ref[...] = product(second, split(value))
    rows_ref[...] = jnp.zeros((256, 128), f32)
    for r in range(ROWS):
        j, q = r // 4, r % 4
        parts = [
            move(stack_ref[16 * c : 16 * c + 16, 128 * j : 128 * j + 128], q, c) for c in range(4)
        ]
        rows_ref[pl.ds(slot(r), 16, stride=16), :] = merge(parts)
    return product(split(rows_ref[...]), kron_third, True)


def inner_penalty(value):
    out = 12.0 * value
    row = iota((32, 128), 0)
    inside = iota((32, 128), 1) % 32
    tiles = []
    for j in range(3):
        tile = value[:, 128 * j : 128 * j + 128]
        total = 12.0 * tile
        for d, weight in ((1, -4.0), (2, 1.0)):
            total = total + weight * (
                jnp.where(row >= d, pltpu.roll(tile, d, 0), 0.0)
                + jnp.where(row < 32 - d, pltpu.roll(tile, 32 - d, 0), 0.0)
                + jnp.where(inside >= d, pltpu.roll(tile, d, 1), 0.0)
                + jnp.where(inside < 32 - d, pltpu.roll(tile, 128 - d, 1), 0.0)
            )
        tiles.append(total)
    return jnp.concatenate(tiles, axis=1)


def tile_of(value, j):
    return value[:, 128 * j : 128 * j + 128]


def put(ref, row, count, value):
    ref[pl.ds(row, 32, stride=count), :] = value


def lanes(values):
    lane = iota((8, 128), 1)
    out = jnp.zeros((8, 128), f32)
    for k, value in enumerate(values):
        out = jnp.where(lane == k, value, out)
    return out


def with_scalars(tile, values):
    one = pltpu.roll(lanes(values), 64, 1)
    return jnp.where(iota((32, 128), 1) < 64, tile, jnp.concatenate([one] * 4, axis=0))


def totals(ref, count, number):
    summed = jnp.sum(ref[pl.ds(2, 32, stride=count), :], axis=0, keepdims=True)
    lane = iota((1, 128), 1)
    return [jnp.sum(jnp.where(lane == 64 + k, summed, 0.0)) for k in range(number)]


def pick(ref, k):
    lane = iota((1, 128), 1)
    return jnp.sum(jnp.where(lane == k, ref[0:1, :], 0.0))


def constants(ref):
    kron = ref[0:256, :], ref[256:512, :]
    second = ref[512:576, 0:32], ref[576:640, 0:32]
    return kron, second, (ref[640:672, 0:64], ref[672:704, 0:64])


def row_tile(piece, j):
    place = 3 * piece + j
    first = 256 + 32 * (place // 2)
    return slice(first, first + 32), slice(128 * (place % 2), 128 * (place % 2) + 128)


def keep_rows(ref, piece, value):
    for j in range(3):
        ref[row_tile(piece, j)] = tile_of(value, j)


def kept_rows(ref, piece):
    return jnp.concatenate([ref[row_tile(piece, j)] for j in range(3)], axis=1)


def start_kernel(
    table_hbm, weight_hbm, start2_hbm, band2_hbm, start3_hbm, band3_hbm,
    send_ref, wide_ref, inner_ref,
    table_ref, weight_ref, start2_ref, band2_ref, start3_ref, band3_ref, sems,
    product_ref, packed_ref, field_ref, rows_ref, stack_ref,
):
    copies = [
        pltpu.make_async_copy(source, target, sems.at[k])
        for k, (source, target) in enumerate(
            (
                (start3_hbm, start3_ref),
                (band3_hbm, band3_ref),
                (start2_hbm, start2_ref),
                (band2_hbm, band2_ref),
                (weight_hbm, weight_ref),
                (table_hbm, table_ref),
            )
        )
    ]
    for copy in copies:
        copy.start()
    copies[0].wait()
    copies[1].wait()
    pick_bin = (iota((256, N3), 0) % N3 == iota((256, N3), 1)) & (iota((256, N3), 0) < 4 * N3)
    same = iota((256, 128), 0) // N3 == iota((256, 128), 1) // 32
    picker = jnp.where(pick_bin, 1.0, 0.0).astype(jnp.bfloat16)
    for k, term in enumerate(split(banded_t(start3_ref, band3_ref, 128, 32))):
        spread_out = lax.dot_general(
            picker, term, (((1,), (1,)), ((), ())), preferred_element_type=f32
        )
        inner_ref[256 * k : 256 * k + 256, :] = jnp.where(same, spread_out, 0.0).astype(jnp.bfloat16)
    copies[2].wait()
    copies[3].wait()
    order, other = iota((N2, N2), 1), iota((N2, N2), 0)
    permute = jnp.where((order % 16) * 4 + order // 16 == other, 1.0, 0.0).astype(jnp.bfloat16)
    back = jnp.where((other % 16) * 4 + other // 16 == order, 1.0, 0.0).astype(jnp.bfloat16)
    for k, term in enumerate(split(banded_t(start2_ref, band2_ref, 32, 32))):
        value = jnp.dot(term, permute, preferred_element_type=f32)
        inner_ref[640 + 32 * k : 672 + 32 * k, 0:64] = value.astype(jnp.bfloat16)
        value = lax.dot_general(back, term, (((1,), (1,)), ((), ())), preferred_element_type=f32)
        inner_ref[512 + 64 * k : 576 + 64 * k, 0:32] = value.astype(jnp.bfloat16)
    kron, _, turned = constants(inner_ref)
    copies[4].wait()
    copies[5].wait()
    packed_ref[8:16, :] = jnp.zeros((8, N2 * N3), f32)
    product_ref[8:16, :] = jnp.zeros((8, N2 * N3), f32)
    for b in range(L1):
        weight = weight_ref[b]
        packed_ref[L0 * b : L0 * b + L0, :] = weight
        product_ref[L0 * b : L0 * b + L0, :] = weight * table_ref[b]
    for p in range(16):
        for source, target in ((packed_ref, wide_ref), (product_ref, field_ref)):
            low, high = expand(source, p)
            target[16 * p : 16 * p + 16, 0:128] = low
            target[16 * p : 16 * p + 16, 128:256] = high
    mixed = table_to_mixed(field_ref[...], kron, turned, rows_ref, stack_ref)
    once = inner_penalty(mixed)
    keep_rows(wide_ref, 1, mixed)
    keep_rows(wide_ref, 2, once)
    for base, value in ((0, mixed), (3, once)):
        put(send_ref, base, 5, tile_of(value, 0))
        put(send_ref, base + 1, 5, tile_of(value, 1))
    lane = iota((32, 128), 1)
    put(send_ref, 2, 5, jnp.where(lane < 64, tile_of(mixed, 2), pltpu.roll(tile_of(once, 2), 64, 1)))


def pentadiagonal(n):
    gap = jnp.abs(iota((n, n), 0) - iota((n, n), 1))
    return jnp.where(gap == 0, 6.0, jnp.where(gap == 1, -4.0, jnp.where(gap == 2, 1.0, 0.0)))


def choose(pieces, selector):
    out = None
    for piece in pieces:
        term = jnp.dot(piece, selector, preferred_element_type=f32)
        out = term if out is None else out + term
    return out


def powers(basis_t, count):
    penalty_matrix = pentadiagonal(basis_t.shape[0])
    out = [basis_t]
    for _ in range(count - 1):
        out.append(mm(penalty_matrix, out[-1]))
    return out


def store_split(high_ref, low_ref, rows, value):
    high, low = split(value)
    high_ref[rows, :] = high
    low_ref[rows, :] = low


def gram_blocks(refs, count, small_ref, rows0_h, rows0_l, rows1_h, rows1_l):
    start0_ref, band0_ref, start1_ref, band1_ref = refs
    total = DEVICES * ROWS
    powers0 = powers(banded_t(start0_ref, band0_ref, K0, K0), count)
    powers1 = powers(banded_t(start1_ref, band1_ref, K1, K1), 4)
    small_ref[...] = jnp.zeros((48, 128), f32)
    first, second = powers0[0].T, powers1[0].T
    for k in range(count):
        small_ref[0:N0, 32 * k : 32 * k + N0] = mm(first, powers0[k])
        small_ref[N0 : N0 + N1, 32 * k : 32 * k + N1] = mm(second, powers1[k])
    row0 = iota((total, N0), 0)
    pick0 = L0 * (row0 % 32 // GRPS) + row0 // 32 // L1 == iota((total, N0), 1)
    row1 = iota((total, 16), 0)
    pick1 = L1 * (row1 % GRPS) + row1 // 32 % L1 == iota((total, 16), 1)
    for pick, rows, targets in (
        (pick0, slice(0, N0), (rows0_h, rows0_l)),
        (pick1, slice(N0, N0 + 16), (rows1_h, rows1_l)),
    ):
        chooser = jnp.where(pick, 1.0, 0.0).astype(jnp.bfloat16)
        for term, target in zip(split(small_ref[rows, :]), targets):
            spread_out = jnp.dot(chooser, term, preferred_element_type=f32)
            target[...] = spread_out.astype(jnp.bfloat16)
    line, column = iota((128, total), 0), iota((128, total), 1)
    match0 = line % 32 == L0 * (column % 32 // GRPS) + column // 32 // L1
    match1 = line % 32 == L1 * (column % GRPS) + column // 32 % L1
    select0, select1 = [
        [
            jnp.where(match & (line // 32 == k), 1.0, 0.0).astype(jnp.bfloat16)
            for k in range(count)
        ]
        for match in (match0, match1)
    ]

    def block(base):
        block0 = rows0_h[pl.ds(base, 64), :], rows0_l[pl.ds(base, 64), :]
        block1 = rows1_h[pl.ds(base, 64), :], rows1_l[pl.ds(base, 64), :]
        g = [choose(block0, selector) for selector in select0]
        h = [choose(block1, selector) for selector in select1]
        return g, h

    return powers0, powers1, select0[0][0:N0, :], block


def matrix_kernel(
    group_ref, start0_ref, band0_ref, start1_ref, band1_ref,
    gram_h_ref, gram_l_ref, lift_h_ref, lift_l_ref, side_ref, small_h_ref, small_l_ref, *scratch,
):
    total = DEVICES * ROWS
    refs = (start0_ref, band0_ref, start1_ref, band1_ref)
    powers0, powers1, chosen, block = gram_blocks(refs, 2, *scratch)

    @pl.loop(0, 5)
    def _(step):
        base = pl.multiple_of(step * 64, 64)
        g, h = block(base)
        store_split(gram_h_ref, gram_l_ref, pl.ds(base, 64), g[0] * h[0])
        store_split(
            gram_h_ref, gram_l_ref, pl.ds(base + total, 64), g[1] * h[0] + g[0] * h[1]
        )

    lifted = [
        jnp.dot(term, chosen, preferred_element_type=f32)
        for term in split(powers0[0])
    ]
    spot = iota((N0, N0), 1)
    order = jnp.where(L0 * (spot % 16) + spot // 16 == iota((N0, N0), 0), 1.0, 0.0).astype(jnp.bfloat16)
    for term, target in zip(split(powers0[0]), (small_h_ref, small_l_ref)):
        target[...] = jnp.dot(term, order, preferred_element_type=f32).astype(jnp.bfloat16)
    owner = L1 * (iota((K0, total), 1) % GRPS) + iota((K0, total), 1) // 32 % L1
    for n in range(N1):
        rows = slice(K0 * n, K0 * n + K0)
        for term, target in zip(lifted, (lift_h_ref, lift_l_ref)):
            target[rows, :] = jnp.where(owner == n, term, 0.0).astype(jnp.bfloat16)
    group = group_ref[0]
    coef = iota((128, K1), 0) % 32 + 32 * group
    pick_coef = jnp.where(coef == iota((128, K1), 1), 1.0, 0.0)
    half = iota((N1, N1), 1) // L1
    wanted = L1 * jnp.where(half == group, 0, 1) + iota((N1, N1), 1) % L1
    reorder = jnp.where(iota((N1, N1), 0) == wanted, 1.0, 0.0)
    side_ref[...] = jnp.zeros((192, 384), f32)
    across = powers1[0].T
    for k in range(4):
        side_ref[128 + 16 * k : 128 + 16 * k + N1, 0:N1] = mm(across, powers1[k])
    for k in range(3):
        own = mm(pick_coef, powers1[k])
        halves = mm(own, reorder)
        for alpha in range(4):
            rows = slice(32 * alpha, 32 * alpha + 32)
            if k == 0:
                side_ref[rows, 10 * alpha : 10 * alpha + 10] = own[rows, :]
            for h in range(2):
                piece = halves[rows, L1 * h : L1 * h + L1]
                place = 40 * k + 20 * h + L1 * alpha
                side_ref[rows, 256 + place : 256 + place + L1] = piece
                if k < 2:
                    side_ref[rows, 128 + place : 128 + place + L1] = piece


def unpack(ref, row, count, r, source, target):
    return move(ref[pl.ds(row, 32, stride=count), :], source, target)


def first_column_kernel(recv_ref, gram_h_ref, gram_l_ref, send_ref, fields_ref, images_ref):
    total = DEVICES * ROWS
    zero = jnp.zeros((32, 128), f32)
    for r in range(ROWS):
        j, q = r // 4, r % 4
        where0 = (j, q) if j < 2 else (2, q)
        where1 = (3 + j, q) if j < 2 else (2, q + 2)
        parts = [
            unpack(recv_ref, place[0], 5, r, place[1], k) for k, place in enumerate((where0, where1))
        ]
        fields_ref[32 * r : 32 * r + 32, :] = merge(parts + [zero])
    fields = fields_ref[...]
    applied = product(load((gram_h_ref, gram_l_ref)), split(fields))
    lane = iota((total, 128), 1)
    images = applied[:total] + jnp.where(
        (lane >= 32) & (lane < 64), pltpu.roll(applied[total:], 32, 1), 0.0
    )
    images_ref[...] = images
    norm = jnp.sum(jnp.where(lane < 32, fields * images, 0.0))
    bend = jnp.sum(jnp.where(lane < 32, fields * pltpu.roll(images, 96, 1), 0.0))
    send_rows(send_ref, images_ref, (norm, bend))


def send_rows(send_ref, value_ref, values=()):
    for j in range(3):
        parts = []
        for q in range(4):
            r = 4 * j + q
            if r < ROWS:
                parts.append(move(value_ref[32 * r : 32 * r + 32, :], 0, q))
            else:
                parts.append(jnp.zeros((32, 128), f32))
        tile = merge(parts)
        put(send_ref, j, PLAIN, with_scalars(tile, values) if j == 2 else tile)


def received_rows(recv_ref):
    tiles = [recv_ref[pl.ds(j, 32, stride=PLAIN), :] for j in range(3)]
    tiles[2] = jnp.where(iota((32, 128), 1) < 64, tiles[2], 0.0)
    return jnp.concatenate(tiles, axis=1)


def first_row_kernel(
    recv_ref, wide_ref, inner_ref, send_ref, scalar_ref, carried_ref, rows_ref, stack_ref,
):
    norm, bend = totals(recv_ref, PLAIN, 2)
    scalar_ref[...] = lanes((norm, bend))
    kron, second, turned = constants(inner_ref)
    field = mixed_to_table(received_rows(recv_ref), kron, second, rows_ref, stack_ref)
    weighted = wide_ref[0:256, :] * field
    energy = jnp.sum(field * weighted)
    mixed = table_to_mixed(weighted, kron, turned, rows_ref, stack_ref)
    carried_ref[...] = wide_ref[...]
    keep_rows(carried_ref, 0, mixed)
    for j in range(2):
        put(send_ref, j, PLAIN, tile_of(mixed, j))
    put(send_ref, 2, PLAIN, with_scalars(tile_of(mixed, 2), (energy,)))


def second_column_kernel(
    recv_ref, gram_h_ref, gram_l_ref, fields_ref, images_ref, scalar_ref,
    send_ref, blend_ref, out_scalar_ref, next_ref, image_ref,
):
    zero = jnp.zeros((32, 128), f32)
    for r in range(ROWS):
        part = unpack(recv_ref, r // 4, PLAIN, r, r % 4, 0)
        next_ref[32 * r : 32 * r + 32, :] = merge([part, zero])
    (energy,) = totals(recv_ref, PLAIN, 1)
    norm, bend = pick(scalar_ref, 0), pick(scalar_ref, 1)
    step = norm / (energy + 0.1 * bend)
    out_scalar_ref[...] = lanes((norm, step))
    fields, images, following = fields_ref[...], images_ref[...], next_ref[...]
    gram = gram_h_ref[0 : DEVICES * ROWS, :], gram_l_ref[0 : DEVICES * ROWS, :]
    image = product(gram, split(following))
    image_ref[...] = images - step * (image + 0.1 * pltpu.roll(images, 96, 1))
    send_rows(send_ref, image_ref)
    lane = iota(fields.shape, 1)
    reduced = fields - step * (following + 0.1 * pltpu.roll(fields, 96, 1))
    kept = jnp.where(lane < 64, 0.0, pltpu.roll(fields, 64, 1))
    blend_ref[...] = jnp.where(lane < 32, reduced, kept)


def coefficient_penalty(value):
    k = iota(value.shape, 0) % K0
    count = value.shape[0]
    total = 6.0 * value
    for d, weight in ((1, -4.0), (2, 1.0)):
        total = total + weight * (
            jnp.where(k >= d, pltpu.roll(value, d, 0), 0.0)
            + jnp.where(k < K0 - d, pltpu.roll(value, count - d, 0), 0.0)
        )
    return total


def send_blocks(send_ref, count, base, value_ref, block):
    for j in range(10):
        parts = []
        for q in range(4):
            m = 4 * j + q
            alpha, n = m // 10, m % 10
            parts.append(move(value_ref[pl.ds(K0 * n + alpha, 16, stride=4), :], block, q))
        merged = merge(parts)
        for g in range(GRPS):
            send_ref[pl.ds(g * count + base + j, 16, stride=2 * count), :] = merged


def send_halves(send_ref, count, base, value_ref, block):
    for g in range(GRPS):
        for j in range(5):
            parts = []
            for q in range(4):
                alpha, b = divmod(4 * j + q, L1)
                row = K0 * (L1 * g + b) + alpha
                parts.append(move(value_ref[pl.ds(row, 16, stride=4), :], block, q))
            send_ref[pl.ds(g * count + base + j, 16, stride=2 * count), :] = merge(parts)


def middle_kernel(
    blend_ref, lift_h_ref, lift_l_ref, scalar_ref, side_ref, send_ref, keep_ref, sums_ref, four_ref
):
    step = pick(scalar_ref, 1)
    small = 0.1 * step
    lifted = product(load((lift_h_ref, lift_l_ref)), split(blend_ref[...]))
    once = coefficient_penalty(lifted)
    twice = coefficient_penalty(once)
    h_a = lifted - small * pltpu.roll(once, 64, 1)
    y_1 = once + pltpu.roll(lifted, 96, 1)
    x_a = once - small * pltpu.roll(twice, 64, 1)
    h_0 = pltpu.roll(lifted, 64, 1)
    lane = iota(lifted.shape, 1)

    def blocks(first, second, third, fourth):
        return jnp.where(
            lane < 32, first, jnp.where(lane < 64, second, jnp.where(lane < 96, third, fourth))
        )

    keep_ref[...] = blocks(h_0, pltpu.roll(h_a, 32, 1), y_1, pltpu.roll(x_a, 96, 1))
    flat = x_a - small * pltpu.roll(once, 32, 1)
    slope = h_a - small * pltpu.roll(y_1, 64, 1)
    four_ref[...] = blocks(
        h_a, -small * pltpu.roll(h_0, 32, 1), pltpu.roll(flat, 64, 1), pltpu.roll(slope, 96, 1)
    )
    grams = split(side_ref[128:192, 0:N1])
    corner = iota((16, 128), 1) // 32
    norm, bend = jnp.zeros((16, 128), f32), jnp.zeros((16, 128), f32)
    filler = jnp.zeros((16 - N1, 128), f32)
    for chunk in range(8):
        tiles = [four_ref[pl.ds(8 * chunk + k, N1, stride=K0), :] for k in range(8)]
        applied = product(grams, split(jnp.concatenate(tiles, axis=1)))
        for k, tile in enumerate(tiles):
            x = jnp.concatenate([tile, filler], axis=0)
            r1, r2, r3 = [pltpu.roll(x, 32 * d, 1) for d in (1, 2, 3)]
            y0, y1, y2, y3 = [applied[16 * d : 16 * d + 16, 128 * k : 128 * k + 128] for d in range(4)]
            norm = norm + jnp.where(
                corner == 0, x * y0, jnp.where(corner == 1, 2.0 * r1 * y1 + x * y2, 0.0)
            )
            bend = bend + jnp.where(
                corner == 1,
                r1 * y2 + x * y3,
                jnp.where(
                    corner == 2, r2 * y0 + r1 * y1, jnp.where(corner == 3, r3 * y1 + r2 * y2, 0.0)
                ),
            )
    sums_ref[...] = lanes((jnp.sum(norm), jnp.sum(bend)))
    for block in range(3):
        send_halves(send_ref, JOINT, PLAIN + 5 * block, keep_ref, block)


def second_row_kernel(
    early_ref, recv_ref, sums_ref, scalar_ref, wide_ref, inner_ref,
    send_ref, rows_ref, stack_ref,
):
    kron, second, turned = constants(inner_ref)
    send_ref[...] = early_ref[...]
    image = received_rows(recv_ref)
    step = pick(scalar_ref, 1)
    reduced = kept_rows(wide_ref, 1) - step * (
        kept_rows(wide_ref, 0) + 0.1 * kept_rows(wide_ref, 2)
    )
    inner = jnp.sum(reduced * inner_penalty(image))
    field = mixed_to_table(image, kron, second, rows_ref, stack_ref)
    weighted = wide_ref[0:256, :] * field
    energy = jnp.sum(field * weighted)
    mixed = table_to_mixed(weighted, kron, turned, rows_ref, stack_ref)
    for j in range(2):
        put(send_ref, j, JOINT, tile_of(mixed, j))
    values = (energy, pick(sums_ref, 0), pick(sums_ref, 1) + inner)
    put(send_ref, 2, JOINT, with_scalars(tile_of(mixed, 2), values))


def third_column_kernel(
    recv_ref, small_h_ref, small_l_ref, keep_ref, scalar_ref,
    send_ref, out_scalar_ref, packed_ref, lifted_ref, mixed_ref,
):
    for a in range(L0):
        for t in range(3):
            parts = []
            for block in range(4):
                n = 4 * t + block
                if n < N1:
                    g, b = divmod(n, L1)
                    j, q = divmod(L1 * a + b, 4)
                    part = recv_ref[pl.ds(g * JOINT + j, 16, stride=2 * JOINT), :]
                    parts.append(move(part, q, block))
                else:
                    parts.append(jnp.zeros((16, 128), f32))
            packed_ref[16 * a : 16 * a + 16, 128 * t : 128 * t + 128] = merge(parts)
    packed = product(load((small_h_ref, small_l_ref)), split(packed_ref[...]))
    for n in range(N1):
        lifted_ref[K0 * n : K0 * n + K0, :] = move(tile_of(packed, n // 4), n % 4, 0)
    energy, norm_next, bend = totals(recv_ref, JOINT, 3)
    norm, step = pick(scalar_ref, 0), pick(scalar_ref, 1)
    ratio = norm_next / norm
    curve = energy + 0.1 * bend - ratio * norm_next / step
    step_next = norm_next / curve
    out_scalar_ref[...] = lanes((norm, step, ratio, step_next))
    lifted = lifted_ref[...]
    keep = keep_ref[...]
    h_a, x_a = pltpu.roll(keep, 96, 1), pltpu.roll(keep, 32, 1)
    mixed_ref[...] = (
        h_a - step_next * (lifted + 0.1 * x_a) - (step_next * ratio / step) * (keep - h_a)
    )
    send_blocks(send_ref, 10, 0, mixed_ref, 0)


def gather_blocks(ref, count, base, rows, out_ref, first):
    for j in range(rows):
        taken = [ref[pl.ds(rho * count + base + j, 8, stride=4 * count), :] for rho in range(4)]
        for q in range(4):
            m = first + 4 * j + q
            merged = merge([move(taken[rho], q, rho) for rho in range(4)])
            out_ref[pl.ds(m // 8 * 64 + m % 8, 8, stride=8), :] = merged


def take(ref, block, tile):
    return jnp.concatenate(
        [ref[pl.ds((5 * block + t) * 64 + 8 * tile, 8), :] for t in range(5)], axis=0
    )


def bent_rows(value):
    lane = iota(value.shape, 1)
    inside = lane % 32
    total = 12.0 * value
    for d, weight in ((1, -4.0), (2, 1.0)):
        total = total + weight * (
            jnp.where(lane >= 32 * d, pltpu.roll(value, 32 * d, 1), 0.0)
            + jnp.where(lane < 1024 - 32 * d, pltpu.roll(value, 1024 - 32 * d, 1), 0.0)
            + jnp.where(inside >= d, pltpu.roll(value, d, 1), 0.0)
            + jnp.where(inside < 32 - d, pltpu.roll(value, 1024 - d, 1), 0.0)
        )
    return total


def settle_kernel(own_ref, partner_ref, side_ref, scalar_ref, solution_ref, part_ref, early):
    for block in range(3):
        for h, ref in enumerate((own_ref, partner_ref)):
            gather_blocks(ref, JOINT, PLAIN + 5 * block, 5, early, 40 * block + 20 * h)
    step, ratio, step_next = pick(scalar_ref, 1), pick(scalar_ref, 2), pick(scalar_ref, 3)
    small = 0.1 * step
    value = split(side_ref[0:128, 128:208])
    slope = split(side_ref[0:128, 256:376])
    bent = bent_rows(jnp.concatenate([take(early, 1, tile) for tile in range(8)], axis=1))
    for tile in range(8):
        h_0, h_a, y_1 = take(early, 0, tile), take(early, 1, tile), take(early, 2, tile)
        right = jnp.concatenate(
            [(step + step_next * ratio) * h_0 + step_next * h_a, (-step_next * small) * h_0], axis=0
        )
        columns = slice(128 * tile, 128 * tile + 128)
        solution_ref[:, :, columns] = product(value, split(right)).reshape(4, 32, 128)
        right = jnp.concatenate(
            [
                (-0.1 * step_next) * bent[:, columns],
                (-small * (1.0 + step_next * ratio / step)) * h_0
                - (0.1 * step_next) * (h_a - small * y_1),
                (0.1 * step_next * small) * h_0,
            ],
            axis=0,
        )
        part_ref[:, columns] = product(slope, split(right))


def final_kernel(late_ref, side_ref, part_ref, residual_ref, late):
    gather_blocks(late_ref, 10, 0, 10, late, 0)
    value = split(side_ref[0:128, 0:40])
    for tile in range(8):
        columns = slice(128 * tile, 128 * tile + 128)
        whole = part_ref[:, columns] + product(value, split(take(late, 0, tile)))
        residual_ref[:, :, columns] = whole.reshape(4, 32, 128)


def call(kernel, outputs, scratch, *operands, aliases={}, left=(), scalars=(), limit=16):
    vmem = pl.BlockSpec(memory_space=pltpu.VMEM)
    specs = [vmem] * len(operands)
    for k in left:
        specs[k] = pl.BlockSpec(memory_space=pltpu.HBM)
    for k in scalars:
        specs[k] = pl.BlockSpec(memory_space=pltpu.SMEM)
    return pl.pallas_call(
        kernel,
        out_shape=[
            shape if isinstance(shape, jax.ShapeDtypeStruct) else jax.ShapeDtypeStruct(shape, f32)
            for shape in outputs
        ],
        in_specs=specs,
        out_specs=[vmem] * len(outputs),
        scratch_shapes=[
            pltpu.VMEM(shape, f32) if isinstance(shape, tuple) else shape for shape in scratch
        ],
        input_output_aliases=aliases,
        compiler_params=pltpu.CompilerParams(vmem_limit_bytes=limit * 2**20),
    )(*operands)


def pair_of(*shape):
    return [jax.ShapeDtypeStruct(shape, jnp.bfloat16)] * 2


def exchange(buffer):
    count = buffer.shape[0] // DEVICES
    tiled = count == 4 or count % 8 == 0
    shape = (DEVICES, count, 128) if tiled else (DEVICES, 1, count * 128)
    moved = lax.all_to_all(buffer.reshape(shape), ("slab", "grp"), 0, 0, tiled=True)
    return moved.reshape(buffer.shape)


def fast_program(
    photon_table,
    bin_weights,
    first_start,
    first_band,
    second_start,
    second_band,
    third_start,
    third_band,
    fourth_start,
    fourth_band,
):
    total = DEVICES * ROWS
    work = [(256, 128), (64, 384)]
    outer = (first_start, first_band.T, second_start, second_band.T)
    inputs = (
        photon_table.transpose(1, 0, 2),
        bin_weights.transpose(1, 0, 2),
        third_start,
        third_band.T,
        fourth_start,
        fourth_band.T,
    )
    send, wide, inner = call(
        start_kernel,
        [(160, 128), (416, 256), jax.ShapeDtypeStruct((704, 128), jnp.bfloat16)],
        [pltpu.VMEM(value.shape, value.dtype) for value in inputs]
        + [pltpu.SemaphoreType.DMA((len(inputs),))]
        + [(16, N2 * N3), (16, N2 * N3), (256, 256)]
        + work,
        *inputs,
        left=range(len(inputs)),
        limit=LARGE,
    )
    recv = exchange(send)
    grams = [(48, 128)] + [pltpu.VMEM((total, 128), jnp.bfloat16)] * 4
    group = lax.axis_index("grp").reshape(1)
    *matrices, side, small_h, small_l = call(
        matrix_kernel,
        pair_of(2 * total, total) + pair_of(K0 * N1, total) + [(192, 384)] + pair_of(K0, N0),
        grams,
        group, *outer,
        scalars=(0,),
    )
    gram, lift = matrices[0:2], matrices[2:4]
    send, fields, images = call(
        first_column_kernel, [(32 * PLAIN, 128), (total, 128), (total, 128)], [], recv, *gram
    )
    recv = exchange(send)
    send, scalars, wide = call(
        first_row_kernel,
        [(32 * PLAIN, 128), (8, 128), (416, 256)],
        work,
        recv, wide, inner,
        aliases={1: 2},
    )
    recv = exchange(send)
    send, blend, scalars = call(
        second_column_kernel,
        [(32 * PLAIN, 128), (total, 128), (8, 128)],
        [(total, 128), (total, 128)],
        recv, *gram, fields, images, scalars,
        aliases={3: 1},
    )
    recv = exchange(send)
    send, keep, sums = call(
        middle_kernel,
        [(DEVICES * JOINT, 128), (K0 * N1, 128), (8, 128)],
        [(K0 * N1, 128)],
        blend, *lift, scalars, side,
    )
    (send,) = call(
        second_row_kernel,
        [(DEVICES * JOINT, 128)],
        work,
        send, recv, sums, scalars, wide, inner,
        aliases={0: 0},
    )
    recv = exchange(send)
    partner = lax.ppermute(recv, "grp", [(0, 1), (1, 0)])
    send, scalars = call(
        third_column_kernel,
        [(DEVICES * 10, 128), (8, 128)],
        [(32, 384), (K0 * N1, 128), (K0 * N1, 128)],
        recv, small_h, small_l, keep, scalars,
    )
    late = exchange(send)
    solution_part, part = call(
        settle_kernel,
        [(4, 32, 1024), (128, 1024)],
        [(960, 128)],
        recv, partner, side, scalars,
    )
    (residual,) = call(final_kernel, [(4, 32, 1024)], [(320, 128)], late, side, part)
    return solution_part, residual


def fits(mesh):
    return (mesh.shape["slab"], mesh.shape["grp"]) == (SLABS, GRPS)


def solution(mesh):
    placed = (
        P("slab", "grp", None),
        P("slab", "grp", None),
        P(),
        P(),
        P(),
        P(),
        P(),
        P(),
        P(),
        P(),
    )
    return jax.shard_map(
        fast_program if fits(mesh) else per_device,
        mesh=mesh,
        in_specs=placed,
        out_specs=(P("slab", "grp", None), P("slab", "grp", None)),
        check_vma=False,
    )
```

```python
import jax
import jax.numpy as jnp
from jax import lax
from jax.experimental import pallas as pl
from jax.experimental.pallas import tpu as pltpu
from jax.sharding import PartitionSpec as P

K0 = 64
K1 = 64
K2 = 32
K3 = 32
ITERS = 2


highest = lax.Precision.HIGHEST
smoothing = 0.1
stencil_weights = (1.0, -4.0, 6.0, -4.0, 1.0)


def with_halo(value, sides, width):
    for axis, dim in sides:
        count, length = (lax.axis_size(axis), value.shape[dim])
        up = [(i, (i + 1) % count) for i in range(count - 1)]
        down = [(j, i) for i, j in up]
        last = lax.slice_in_dim(value, length - width, length, axis=dim)
        initial = lax.slice_in_dim(value, 0, width, axis=dim)
        before = lax.ppermute(last, axis, up)
        after = lax.ppermute(initial, axis, down)
        value = jnp.concatenate([before, value, after], axis=dim)
    return value


def dense_basis(starts, values, coef_count):
    relative = jnp.arange(coef_count, dtype=jnp.int32)[None, :] - starts[:, None]
    matrix = jnp.zeros((starts.shape[0], coef_count), jnp.float32)
    for offset in range(4):
        matrix = matrix + jnp.where(relative == offset, values[:, offset : offset + 1], 0.0)
    return matrix


def five_point(source, along, extent):
    running = stencil_weights[0] * lax.slice_in_dim(source, 0, extent, axis=along)
    for offset in range(1, 5):
        running = running + stencil_weights[offset] * lax.slice_in_dim(
            source, offset, offset + extent, axis=along
        )
    return running


def local_stencil(tensor, along):
    widths = [(0, 0)] * tensor.ndim
    widths[along] = (2, 2)
    return five_point(jnp.pad(tensor, widths), along, tensor.shape[along])


def inner_forward(tensor, third_basis, fourth_basis):
    leading, middle = (tensor.shape[0], tensor.shape[1])
    blocked = tensor.reshape(leading, middle, third_basis.shape[1], fourth_basis.shape[1])
    blocked = jnp.einsum("abcd,nd->abcn", blocked, fourth_basis, precision=highest)
    blocked = jnp.einsum("abcn,mc->abmn", blocked, third_basis, precision=highest)
    return blocked.reshape(leading, middle, third_basis.shape[0] * fourth_basis.shape[0])


def inner_adjoint(tensor, third_basis, fourth_basis):
    leading, middle = (tensor.shape[0], tensor.shape[1])
    blocked = tensor.reshape(leading, middle, third_basis.shape[0], fourth_basis.shape[0])
    blocked = jnp.einsum("abmn,mc->abcn", blocked, third_basis, precision=highest)
    blocked = jnp.einsum("abcn,nd->abcd", blocked, fourth_basis, precision=highest)
    return blocked.reshape(leading, middle, third_basis.shape[1] * fourth_basis.shape[1])


def lead_product(tensor, matrix):
    combined = jnp.einsum(
        "ka,ain->kin",
        matrix,
        lax.all_to_all(tensor, "slab", split_axis=2, concat_axis=0, tiled=True),
        precision=highest,
    )
    return lax.all_to_all(combined, "slab", split_axis=0, concat_axis=2, tiled=True)


def second_product(tensor, matrix):
    return jnp.einsum(
        "lp,apn->aln", matrix, lax.all_gather(tensor, "grp", axis=1, tiled=True), precision=highest
    )


def penalty(coeffs):
    leading, middle = (coeffs.shape[0], coeffs.shape[1])
    padded = with_halo(coeffs, (("slab", 0), ("grp", 1)), 2)
    along_lead = five_point(padded[:, 2 : 2 + middle], 0, leading)
    along_rows = five_point(padded[2 : 2 + leading, :], 1, middle)
    blocked = coeffs.reshape(leading, middle, K2, K3)
    inner_part = local_stencil(blocked, 2) + local_stencil(blocked, 3)
    return along_lead + along_rows + inner_part.reshape(leading, middle, K2 * K3)


def squared_total(vector):
    return lax.psum(jnp.sum(vector * vector), ("slab", "grp"))


def per_device(
    photon_table,
    bin_weights,
    first_start,
    first_band,
    second_start,
    second_band,
    third_start,
    third_band,
    fourth_start,
    fourth_band,
):
    first_basis = dense_basis(first_start, first_band, K0)
    second_basis = dense_basis(second_start, second_band, K1)
    third_basis = dense_basis(third_start, third_band, K2)
    fourth_basis = dense_basis(fourth_start, fourth_band, K3)
    first_back = first_basis.T
    group_index = lax.axis_index("grp")
    row_count = photon_table.shape[1]
    coef_rows = K1 // lax.axis_size("grp")
    near_rows = lax.dynamic_slice_in_dim(second_basis, group_index * row_count, row_count, 0)
    back_rows = lax.dynamic_slice_in_dim(second_basis.T, group_index * coef_rows, coef_rows, 0)

    def adjoint(table):
        tensor = lead_product(table, first_back)
        tensor = second_product(tensor, back_rows)
        return inner_adjoint(tensor, third_basis, fourth_basis)

    right_side = adjoint(bin_weights * photon_table)
    solution = jnp.zeros_like(right_side)
    residual = right_side
    direction = right_side
    norm_now = squared_total(residual)
    for sweep in range(ITERS):
        forward_tensor = inner_forward(direction, third_basis, fourth_basis)
        forward_tensor = second_product(forward_tensor, near_rows)
        mapped = adjoint(
            bin_weights * lead_product(forward_tensor, first_basis)
        ) + smoothing * penalty(direction)
        curve_total = lax.psum(jnp.sum(direction * mapped), ("slab", "grp"))
        step_size = norm_now / curve_total
        solution = solution + step_size * direction
        residual = residual - step_size * mapped
        norm_next = squared_total(residual)
        direction = residual + norm_next / norm_now * direction
        norm_now = norm_next
    return (solution, residual)


SLABS, GRPS = 16, 2
DEVICES = SLABS * GRPS
L0, L1 = 2, 5
ROWS = L0 * L1
N2, N3 = 64, 50
N0, N1 = 32, 10
HI = lax.Precision.HIGHEST
f32 = jnp.float32
JOINT = 18
PLAIN = 3
LARGE = 60


def iota(shape, dim):
    return lax.broadcasted_iota(jnp.int32, shape, dim)


def mm(a, b):
    return jnp.dot(a, b, precision=HI, preferred_element_type=f32)


def mm_t(a, b):
    return lax.dot_general(
        a, b, (((1,), (1,)), ((), ())), precision=HI, preferred_element_type=f32
    )


def split(value):
    high = value.astype(jnp.bfloat16)
    return high, (value - high.astype(f32)).astype(jnp.bfloat16)


def product(a, b, transposed=False):
    dims = (((1,), (1 if transposed else 0,)), ((), ()))

    def one(x, y):
        return lax.dot_general(x, y, dims, preferred_element_type=f32)

    if b[0].shape[1] == 128 and not transposed:
        both = one(a[0], jnp.concatenate(b, axis=1))
        return both[:, 0:128] + (both[:, 128:256] + one(a[1], b[0]))
    return one(a[0], b[0]) + (one(a[0], b[1]) + one(a[1], b[0]))


def load(pair):
    return pair[0][...], pair[1][...]


def move(block, source, target):
    shift = (target - source) * 32 % 128
    return pltpu.roll(block, shift, 1) if shift else block


def merge(parts):
    lane = iota(parts[0].shape, 1)
    out = parts[-1]
    for q in range(len(parts) - 2, -1, -1):
        out = jnp.where(lane < 32 * (q + 1), parts[q], out)
    return out


def slot(r):
    return L0 * (r % L1) + r // L1


def banded_t(start_ref, band_ref, width, wrap):
    n = start_ref.shape[0]
    relative = (iota((width, n), 0) % wrap) - start_ref[...].reshape(1, n)
    out = jnp.zeros((width, n), f32)
    for offset in range(4):
        out = out + jnp.where(relative == offset, band_ref[offset : offset + 1, :], 0.0)
    return out


def expand(ref, p):
    first = 200 * p
    tile, off = first // 128, first % 128
    lane = iota((16, 128), 1)

    def window(t):
        low = ref[:, t * 128 : (t + 1) * 128]
        if off == 0:
            return low
        t1 = min(t + 1, 24)
        high = ref[:, t1 * 128 : (t1 + 1) * 128]
        return jnp.where(
            lane < 128 - off, pltpu.roll(low, 128 - off, 1), pltpu.roll(high, 128 - off, 1)
        )

    return window(tile), window(min(tile + 1, 24))


def table_to_mixed(field, kron_third, second_t, rows_ref, stack_ref):
    rows_ref[...] = product(split(field), kron_third)
    for c in range(4):
        for j in range(3):
            parts = []
            for q in range(4):
                r = 4 * j + q
                if r < ROWS:
                    part = rows_ref[pl.ds(slot(r), 16, stride=16), :]
                    parts.append(move(part, c, q))
                else:
                    parts.append(jnp.zeros((16, 128), f32))
            stack_ref[16 * c : 16 * c + 16, 128 * j : 128 * j + 128] = merge(parts)
    return product(second_t, split(stack_ref[...]))


def mixed_to_table(value, kron_third, second, rows_ref, stack_ref):
    stack_ref[...] = product(second, split(value))
    rows_ref[...] = jnp.zeros((256, 128), f32)
    for r in range(ROWS):
        j, q = r // 4, r % 4
        parts = [
            move(stack_ref[16 * c : 16 * c + 16, 128 * j : 128 * j + 128], q, c) for c in range(4)
        ]
        rows_ref[pl.ds(slot(r), 16, stride=16), :] = merge(parts)
    return product(split(rows_ref[...]), kron_third, True)


def inner_penalty(value):
    out = 12.0 * value
    row = iota((32, 128), 0)
    inside = iota((32, 128), 1) % 32
    tiles = []
    for j in range(3):
        tile = value[:, 128 * j : 128 * j + 128]
        total = 12.0 * tile
        for d, weight in ((1, -4.0), (2, 1.0)):
            total = total + weight * (
                jnp.where(row >= d, pltpu.roll(tile, d, 0), 0.0)
                + jnp.where(row < 32 - d, pltpu.roll(tile, 32 - d, 0), 0.0)
                + jnp.where(inside >= d, pltpu.roll(tile, d, 1), 0.0)
                + jnp.where(inside < 32 - d, pltpu.roll(tile, 128 - d, 1), 0.0)
            )
        tiles.append(total)
    return jnp.concatenate(tiles, axis=1)


def tile_of(value, j):
    return value[:, 128 * j : 128 * j + 128]


def put(ref, row, count, value):
    ref[pl.ds(row, 32, stride=count), :] = value


def lanes(values):
    lane = iota((8, 128), 1)
    out = jnp.zeros((8, 128), f32)
    for k, value in enumerate(values):
        out = jnp.where(lane == k, value, out)
    return out


def with_scalars(tile, values):
    one = pltpu.roll(lanes(values), 64, 1)
    return jnp.where(iota((32, 128), 1) < 64, tile, jnp.concatenate([one] * 4, axis=0))


def totals(ref, count, number):
    summed = jnp.sum(ref[pl.ds(2, 32, stride=count), :], axis=0, keepdims=True)
    lane = iota((1, 128), 1)
    return [jnp.sum(jnp.where(lane == 64 + k, summed, 0.0)) for k in range(number)]


def pick(ref, k):
    lane = iota((1, 128), 1)
    return jnp.sum(jnp.where(lane == k, ref[0:1, :], 0.0))


def constants(ref):
    kron = ref[0:256, :], ref[256:512, :]
    second = ref[512:576, 0:32], ref[576:640, 0:32]
    return kron, second, (ref[640:672, 0:64], ref[672:704, 0:64])


def row_tile(piece, j):
    place = 3 * piece + j
    first = 256 + 32 * (place // 2)
    return slice(first, first + 32), slice(128 * (place % 2), 128 * (place % 2) + 128)


def keep_rows(ref, piece, value):
    for j in range(3):
        ref[row_tile(piece, j)] = tile_of(value, j)


def kept_rows(ref, piece):
    return jnp.concatenate([ref[row_tile(piece, j)] for j in range(3)], axis=1)


def start_kernel(
    table_hbm, weight_hbm, start2_hbm, band2_hbm, start3_hbm, band3_hbm,
    send_ref, wide_ref, inner_ref,
    table_ref, weight_ref, start2_ref, band2_ref, start3_ref, band3_ref, sems,
    product_ref, packed_ref, field_ref, rows_ref, stack_ref,
):
    copies = [
        pltpu.make_async_copy(source, target, sems.at[k])
        for k, (source, target) in enumerate(
            (
                (start3_hbm, start3_ref),
                (band3_hbm, band3_ref),
                (start2_hbm, start2_ref),
                (band2_hbm, band2_ref),
                (weight_hbm, weight_ref),
                (table_hbm, table_ref),
            )
        )
    ]
    for copy in copies:
        copy.start()
    copies[0].wait()
    copies[1].wait()
    pick_bin = (iota((256, N3), 0) % N3 == iota((256, N3), 1)) & (iota((256, N3), 0) < 4 * N3)
    same = iota((256, 128), 0) // N3 == iota((256, 128), 1) // 32
    picker = jnp.where(pick_bin, 1.0, 0.0).astype(jnp.bfloat16)
    for k, term in enumerate(split(banded_t(start3_ref, band3_ref, 128, 32))):
        spread_out = lax.dot_general(
            picker, term, (((1,), (1,)), ((), ())), preferred_element_type=f32
        )
        inner_ref[256 * k : 256 * k + 256, :] = jnp.where(same, spread_out, 0.0).astype(jnp.bfloat16)
    copies[2].wait()
    copies[3].wait()
    order, other = iota((N2, N2), 1), iota((N2, N2), 0)
    permute = jnp.where((order % 16) * 4 + order // 16 == other, 1.0, 0.0).astype(jnp.bfloat16)
    back = jnp.where((other % 16) * 4 + other // 16 == order, 1.0, 0.0).astype(jnp.bfloat16)
    for k, term in enumerate(split(banded_t(start2_ref, band2_ref, 32, 32))):
        value = jnp.dot(term, permute, preferred_element_type=f32)
        inner_ref[640 + 32 * k : 672 + 32 * k, 0:64] = value.astype(jnp.bfloat16)
        value = lax.dot_general(back, term, (((1,), (1,)), ((), ())), preferred_element_type=f32)
        inner_ref[512 + 64 * k : 576 + 64 * k, 0:32] = value.astype(jnp.bfloat16)
    kron, _, turned = constants(inner_ref)
    copies[4].wait()
    copies[5].wait()
    packed_ref[8:16, :] = jnp.zeros((8, N2 * N3), f32)
    product_ref[8:16, :] = jnp.zeros((8, N2 * N3), f32)
    for b in range(L1):
        weight = weight_ref[b]
        packed_ref[L0 * b : L0 * b + L0, :] = weight
        product_ref[L0 * b : L0 * b + L0, :] = weight * table_ref[b]
    for p in range(16):
        for source, target in ((packed_ref, wide_ref), (product_ref, field_ref)):
            low, high = expand(source, p)
            target[16 * p : 16 * p + 16, 0:128] = low
            target[16 * p : 16 * p + 16, 128:256] = high
    mixed = table_to_mixed(field_ref[...], kron, turned, rows_ref, stack_ref)
    once = inner_penalty(mixed)
    keep_rows(wide_ref, 1, mixed)
    keep_rows(wide_ref, 2, once)
    for base, value in ((0, mixed), (3, once)):
        put(send_ref, base, 5, tile_of(value, 0))
        put(send_ref, base + 1, 5, tile_of(value, 1))
    lane = iota((32, 128), 1)
    put(send_ref, 2, 5, jnp.where(lane < 64, tile_of(mixed, 2), pltpu.roll(tile_of(once, 2), 64, 1)))


def pentadiagonal(n):
    gap = jnp.abs(iota((n, n), 0) - iota((n, n), 1))
    return jnp.where(gap == 0, 6.0, jnp.where(gap == 1, -4.0, jnp.where(gap == 2, 1.0, 0.0)))


def choose(pieces, selector):
    out = None
    for piece in pieces:
        term = jnp.dot(piece, selector, preferred_element_type=f32)
        out = term if out is None else out + term
    return out


def powers(basis_t, count):
    penalty_matrix = pentadiagonal(basis_t.shape[0])
    out = [basis_t]
    for _ in range(count - 1):
        out.append(mm(penalty_matrix, out[-1]))
    return out


def store_split(high_ref, low_ref, rows, value):
    high, low = split(value)
    high_ref[rows, :] = high
    low_ref[rows, :] = low


def gram_blocks(refs, count, small_ref, rows0_h, rows0_l, rows1_h, rows1_l):
    start0_ref, band0_ref, start1_ref, band1_ref = refs
    total = DEVICES * ROWS
    powers0 = powers(banded_t(start0_ref, band0_ref, K0, K0), count)
    powers1 = powers(banded_t(start1_ref, band1_ref, K1, K1), 4)
    small_ref[...] = jnp.zeros((48, 128), f32)
    first, second = powers0[0].T, powers1[0].T
    for k in range(count):
        small_ref[0:N0, 32 * k : 32 * k + N0] = mm(first, powers0[k])
        small_ref[N0 : N0 + N1, 32 * k : 32 * k + N1] = mm(second, powers1[k])
    row0 = iota((total, N0), 0)
    pick0 = L0 * (row0 % 32 // GRPS) + row0 // 32 // L1 == iota((total, N0), 1)
    row1 = iota((total, 16), 0)
    pick1 = L1 * (row1 % GRPS) + row1 // 32 % L1 == iota((total, 16), 1)
    for pick, rows, targets in (
        (pick0, slice(0, N0), (rows0_h, rows0_l)),
        (pick1, slice(N0, N0 + 16), (rows1_h, rows1_l)),
    ):
        chooser = jnp.where(pick, 1.0, 0.0).astype(jnp.bfloat16)
        for term, target in zip(split(small_ref[rows, :]), targets):
            spread_out = jnp.dot(chooser, term, preferred_element_type=f32)
            target[...] = spread_out.astype(jnp.bfloat16)
    line, column = iota((128, total), 0), iota((128, total), 1)
    match0 = line % 32 == L0 * (column % 32 // GRPS) + column // 32 // L1
    match1 = line % 32 == L1 * (column % GRPS) + column // 32 % L1
    select0, select1 = [
        [
            jnp.where(match & (line // 32 == k), 1.0, 0.0).astype(jnp.bfloat16)
            for k in range(count)
        ]
        for match in (match0, match1)
    ]

    def block(base):
        block0 = rows0_h[pl.ds(base, 64), :], rows0_l[pl.ds(base, 64), :]
        block1 = rows1_h[pl.ds(base, 64), :], rows1_l[pl.ds(base, 64), :]
        g = [choose(block0, selector) for selector in select0]
        h = [choose(block1, selector) for selector in select1]
        return g, h

    return powers0, powers1, select0[0][0:N0, :], block


def matrix_kernel(
    group_ref, start0_ref, band0_ref, start1_ref, band1_ref,
    gram_h_ref, gram_l_ref, lift_h_ref, lift_l_ref, side_ref, small_h_ref, small_l_ref, *scratch,
):
    total = DEVICES * ROWS
    refs = (start0_ref, band0_ref, start1_ref, band1_ref)
    powers0, powers1, chosen, block = gram_blocks(refs, 2, *scratch)

    @pl.loop(0, 5)
    def _(step):
        base = pl.multiple_of(step * 64, 64)
        g, h = block(base)
        store_split(gram_h_ref, gram_l_ref, pl.ds(base, 64), g[0] * h[0])
        store_split(
            gram_h_ref, gram_l_ref, pl.ds(base + total, 64), g[1] * h[0] + g[0] * h[1]
        )

    lifted = [
        jnp.dot(term, chosen, preferred_element_type=f32)
        for term in split(powers0[0])
    ]
    spot = iota((N0, N0), 1)
    order = jnp.where(L0 * (spot % 16) + spot // 16 == iota((N0, N0), 0), 1.0, 0.0).astype(jnp.bfloat16)
    for term, target in zip(split(powers0[0]), (small_h_ref, small_l_ref)):
        target[...] = jnp.dot(term, order, preferred_element_type=f32).astype(jnp.bfloat16)
    owner = L1 * (iota((K0, total), 1) % GRPS) + iota((K0, total), 1) // 32 % L1
    for n in range(N1):
        rows = slice(K0 * n, K0 * n + K0)
        for term, target in zip(lifted, (lift_h_ref, lift_l_ref)):
            target[rows, :] = jnp.where(owner == n, term, 0.0).astype(jnp.bfloat16)
    group = group_ref[0]
    coef = iota((128, K1), 0) % 32 + 32 * group
    pick_coef = jnp.where(coef == iota((128, K1), 1), 1.0, 0.0)
    half = iota((N1, N1), 1) // L1
    wanted = L1 * jnp.where(half == group, 0, 1) + iota((N1, N1), 1) % L1
    reorder = jnp.where(iota((N1, N1), 0) == wanted, 1.0, 0.0)
    side_ref[...] = jnp.zeros((192, 384), f32)
    across = powers1[0].T
    for k in range(4):
        side_ref[128 + 16 * k : 128 + 16 * k + N1, 0:N1] = mm(across, powers1[k])
    for k in range(3):
        own = mm(pick_coef, powers1[k])
        halves = mm(own, reorder)
        for alpha in range(4):
            rows = slice(32 * alpha, 32 * alpha + 32)
            if k == 0:
                side_ref[rows, 10 * alpha : 10 * alpha + 10] = own[rows, :]
            for h in range(2):
                piece = halves[rows, L1 * h : L1 * h + L1]
                place = 40 * k + 20 * h + L1 * alpha
                side_ref[rows, 256 + place : 256 + place + L1] = piece
                if k < 2:
                    side_ref[rows, 128 + place : 128 + place + L1] = piece


def unpack(ref, row, count, r, source, target):
    return move(ref[pl.ds(row, 32, stride=count), :], source, target)


def first_column_kernel(recv_ref, gram_h_ref, gram_l_ref, send_ref, fields_ref, images_ref):
    total = DEVICES * ROWS
    zero = jnp.zeros((32, 128), f32)
    for r in range(ROWS):
        j, q = r // 4, r % 4
        where0 = (j, q) if j < 2 else (2, q)
        where1 = (3 + j, q) if j < 2 else (2, q + 2)
        parts = [
            unpack(recv_ref, place[0], 5, r, place[1], k) for k, place in enumerate((where0, where1))
        ]
        fields_ref[32 * r : 32 * r + 32, :] = merge(parts + [zero])
    fields = fields_ref[...]
    applied = product(load((gram_h_ref, gram_l_ref)), split(fields))
    lane = iota((total, 128), 1)
    images = applied[:total] + jnp.where(
        (lane >= 32) & (lane < 64), pltpu.roll(applied[total:], 32, 1), 0.0
    )
    images_ref[...] = images
    norm = jnp.sum(jnp.where(lane < 32, fields * images, 0.0))
    bend = jnp.sum(jnp.where(lane < 32, fields * pltpu.roll(images, 96, 1), 0.0))
    send_rows(send_ref, images_ref, (norm, bend))


def send_rows(send_ref, value_ref, values=()):
    for j in range(3):
        parts = []
        for q in range(4):
            r = 4 * j + q
            if r < ROWS:
                parts.append(move(value_ref[32 * r : 32 * r + 32, :], 0, q))
            else:
                parts.append(jnp.zeros((32, 128), f32))
        tile = merge(parts)
        put(send_ref, j, PLAIN, with_scalars(tile, values) if j == 2 else tile)


def received_rows(recv_ref):
    tiles = [recv_ref[pl.ds(j, 32, stride=PLAIN), :] for j in range(3)]
    tiles[2] = jnp.where(iota((32, 128), 1) < 64, tiles[2], 0.0)
    return jnp.concatenate(tiles, axis=1)


def first_row_kernel(
    recv_ref, wide_ref, inner_ref, send_ref, scalar_ref, carried_ref, rows_ref, stack_ref,
):
    norm, bend = totals(recv_ref, PLAIN, 2)
    scalar_ref[...] = lanes((norm, bend))
    kron, second, turned = constants(inner_ref)
    field = mixed_to_table(received_rows(recv_ref), kron, second, rows_ref, stack_ref)
    weighted = wide_ref[0:256, :] * field
    energy = jnp.sum(field * weighted)
    mixed = table_to_mixed(weighted, kron, turned, rows_ref, stack_ref)
    carried_ref[...] = wide_ref[...]
    keep_rows(carried_ref, 0, mixed)
    for j in range(2):
        put(send_ref, j, PLAIN, tile_of(mixed, j))
    put(send_ref, 2, PLAIN, with_scalars(tile_of(mixed, 2), (energy,)))


def second_column_kernel(
    recv_ref, gram_h_ref, gram_l_ref, fields_ref, images_ref, scalar_ref,
    send_ref, blend_ref, out_scalar_ref, next_ref, image_ref,
):
    zero = jnp.zeros((32, 128), f32)
    for r in range(ROWS):
        part = unpack(recv_ref, r // 4, PLAIN, r, r % 4, 0)
        next_ref[32 * r : 32 * r + 32, :] = merge([part, zero])
    (energy,) = totals(recv_ref, PLAIN, 1)
    norm, bend = pick(scalar_ref, 0), pick(scalar_ref, 1)
    step = norm / (energy + 0.1 * bend)
    out_scalar_ref[...] = lanes((norm, step))
    fields, images, following = fields_ref[...], images_ref[...], next_ref[...]
    gram = gram_h_ref[0 : DEVICES * ROWS, :], gram_l_ref[0 : DEVICES * ROWS, :]
    image = product(gram, split(following))
    image_ref[...] = images - step * (image + 0.1 * pltpu.roll(images, 96, 1))
    send_rows(send_ref, image_ref)
    lane = iota(fields.shape, 1)
    reduced = fields - step * (following + 0.1 * pltpu.roll(fields, 96, 1))
    kept = jnp.where(lane < 64, 0.0, pltpu.roll(fields, 64, 1))
    blend_ref[...] = jnp.where(lane < 32, reduced, kept)


def coefficient_penalty(value):
    k = iota(value.shape, 0) % K0
    count = value.shape[0]
    total = 6.0 * value
    for d, weight in ((1, -4.0), (2, 1.0)):
        total = total + weight * (
            jnp.where(k >= d, pltpu.roll(value, d, 0), 0.0)
            + jnp.where(k < K0 - d, pltpu.roll(value, count - d, 0), 0.0)
        )
    return total


def send_blocks(send_ref, count, base, value_ref, block):
    for j in range(10):
        parts = []
        for q in range(4):
            m = 4 * j + q
            alpha, n = m // 10, m % 10
            parts.append(move(value_ref[pl.ds(K0 * n + alpha, 16, stride=4), :], block, q))
        merged = merge(parts)
        for g in range(GRPS):
            send_ref[pl.ds(g * count + base + j, 16, stride=2 * count), :] = merged


def send_halves(send_ref, count, base, value_ref, block):
    for g in range(GRPS):
        for j in range(5):
            parts = []
            for q in range(4):
                alpha, b = divmod(4 * j + q, L1)
                row = K0 * (L1 * g + b) + alpha
                parts.append(move(value_ref[pl.ds(row, 16, stride=4), :], block, q))
            send_ref[pl.ds(g * count + base + j, 16, stride=2 * count), :] = merge(parts)


def middle_kernel(
    blend_ref, lift_h_ref, lift_l_ref, scalar_ref, side_ref, send_ref, keep_ref, sums_ref, four_ref
):
    step = pick(scalar_ref, 1)
    small = 0.1 * step
    lifted = product(load((lift_h_ref, lift_l_ref)), split(blend_ref[...]))
    once = coefficient_penalty(lifted)
    twice = coefficient_penalty(once)
    h_a = lifted - small * pltpu.roll(once, 64, 1)
    y_1 = once + pltpu.roll(lifted, 96, 1)
    x_a = once - small * pltpu.roll(twice, 64, 1)
    h_0 = pltpu.roll(lifted, 64, 1)
    lane = iota(lifted.shape, 1)

    def blocks(first, second, third, fourth):
        return jnp.where(
            lane < 32, first, jnp.where(lane < 64, second, jnp.where(lane < 96, third, fourth))
        )

    keep_ref[...] = blocks(h_0, pltpu.roll(h_a, 32, 1), y_1, pltpu.roll(x_a, 96, 1))
    flat = x_a - small * pltpu.roll(once, 32, 1)
    slope = h_a - small * pltpu.roll(y_1, 64, 1)
    four_ref[...] = blocks(
        h_a, -small * pltpu.roll(h_0, 32, 1), pltpu.roll(flat, 64, 1), pltpu.roll(slope, 96, 1)
    )
    grams = split(side_ref[128:192, 0:N1])
    corner = iota((16, 128), 1) // 32
    norm, bend = jnp.zeros((16, 128), f32), jnp.zeros((16, 128), f32)
    filler = jnp.zeros((16 - N1, 128), f32)
    for chunk in range(8):
        tiles = [four_ref[pl.ds(8 * chunk + k, N1, stride=K0), :] for k in range(8)]
        applied = product(grams, split(jnp.concatenate(tiles, axis=1)))
        for k, tile in enumerate(tiles):
            x = jnp.concatenate([tile, filler], axis=0)
            r1, r2, r3 = [pltpu.roll(x, 32 * d, 1) for d in (1, 2, 3)]
            y0, y1, y2, y3 = [applied[16 * d : 16 * d + 16, 128 * k : 128 * k + 128] for d in range(4)]
            norm = norm + jnp.where(
                corner == 0, x * y0, jnp.where(corner == 1, 2.0 * r1 * y1 + x * y2, 0.0)
            )
            bend = bend + jnp.where(
                corner == 1,
                r1 * y2 + x * y3,
                jnp.where(
                    corner == 2, r2 * y0 + r1 * y1, jnp.where(corner == 3, r3 * y1 + r2 * y2, 0.0)
                ),
            )
    sums_ref[...] = lanes((jnp.sum(norm), jnp.sum(bend)))
    for block in range(3):
        send_halves(send_ref, JOINT, PLAIN + 5 * block, keep_ref, block)


def second_row_kernel(
    early_ref, recv_ref, sums_ref, scalar_ref, wide_ref, inner_ref,
    send_ref, rows_ref, stack_ref,
):
    kron, second, turned = constants(inner_ref)
    send_ref[...] = early_ref[...]
    image = received_rows(recv_ref)
    step = pick(scalar_ref, 1)
    reduced = kept_rows(wide_ref, 1) - step * (
        kept_rows(wide_ref, 0) + 0.1 * kept_rows(wide_ref, 2)
    )
    inner = jnp.sum(reduced * inner_penalty(image))
    field = mixed_to_table(image, kron, second, rows_ref, stack_ref)
    weighted = wide_ref[0:256, :] * field
    energy = jnp.sum(field * weighted)
    mixed = table_to_mixed(weighted, kron, turned, rows_ref, stack_ref)
    for j in range(2):
        put(send_ref, j, JOINT, tile_of(mixed, j))
    values = (energy, pick(sums_ref, 0), pick(sums_ref, 1) + inner)
    put(send_ref, 2, JOINT, with_scalars(tile_of(mixed, 2), values))


def third_column_kernel(
    recv_ref, small_h_ref, small_l_ref, keep_ref, scalar_ref,
    send_ref, out_scalar_ref, packed_ref, lifted_ref, mixed_ref,
):
    for a in range(L0):
        for t in range(3):
            parts = []
            for block in range(4):
                n = 4 * t + block
                if n < N1:
                    g, b = divmod(n, L1)
                    j, q = divmod(L1 * a + b, 4)
                    part = recv_ref[pl.ds(g * JOINT + j, 16, stride=2 * JOINT), :]
                    parts.append(move(part, q, block))
                else:
                    parts.append(jnp.zeros((16, 128), f32))
            packed_ref[16 * a : 16 * a + 16, 128 * t : 128 * t + 128] = merge(parts)
    packed = product(load((small_h_ref, small_l_ref)), split(packed_ref[...]))
    for n in range(N1):
        lifted_ref[K0 * n : K0 * n + K0, :] = move(tile_of(packed, n // 4), n % 4, 0)
    energy, norm_next, bend = totals(recv_ref, JOINT, 3)
    norm, step = pick(scalar_ref, 0), pick(scalar_ref, 1)
    ratio = norm_next / norm
    curve = energy + 0.1 * bend - ratio * norm_next / step
    step_next = norm_next / curve
    out_scalar_ref[...] = lanes((norm, step, ratio, step_next))
    lifted = lifted_ref[...]
    keep = keep_ref[...]
    h_a, x_a = pltpu.roll(keep, 96, 1), pltpu.roll(keep, 32, 1)
    mixed_ref[...] = (
        h_a - step_next * (lifted + 0.1 * x_a) - (step_next * ratio / step) * (keep - h_a)
    )
    send_blocks(send_ref, 10, 0, mixed_ref, 0)


def gather_blocks(ref, count, base, rows, out_ref, first):
    for j in range(rows):
        taken = [ref[pl.ds(rho * count + base + j, 8, stride=4 * count), :] for rho in range(4)]
        for q in range(4):
            m = first + 4 * j + q
            merged = merge([move(taken[rho], q, rho) for rho in range(4)])
            out_ref[pl.ds(m // 8 * 64 + m % 8, 8, stride=8), :] = merged


def take(ref, block, tile):
    return jnp.concatenate(
        [ref[pl.ds((5 * block + t) * 64 + 8 * tile, 8), :] for t in range(5)], axis=0
    )


def bent_rows(value):
    lane = iota(value.shape, 1)
    inside = lane % 32
    total = 12.0 * value
    for d, weight in ((1, -4.0), (2, 1.0)):
        total = total + weight * (
            jnp.where(lane >= 32 * d, pltpu.roll(value, 32 * d, 1), 0.0)
            + jnp.where(lane < 1024 - 32 * d, pltpu.roll(value, 1024 - 32 * d, 1), 0.0)
            + jnp.where(inside >= d, pltpu.roll(value, d, 1), 0.0)
            + jnp.where(inside < 32 - d, pltpu.roll(value, 1024 - d, 1), 0.0)
        )
    return total


def settle_kernel(own_ref, partner_ref, side_ref, scalar_ref, solution_ref, part_ref, early):
    for block in range(3):
        for h, ref in enumerate((own_ref, partner_ref)):
            gather_blocks(ref, JOINT, PLAIN + 5 * block, 5, early, 40 * block + 20 * h)
    step, ratio, step_next = pick(scalar_ref, 1), pick(scalar_ref, 2), pick(scalar_ref, 3)
    small = 0.1 * step
    value = split(side_ref[0:128, 128:208])
    slope = split(side_ref[0:128, 256:376])
    bent = bent_rows(jnp.concatenate([take(early, 1, tile) for tile in range(8)], axis=1))
    for tile in range(8):
        h_0, h_a, y_1 = take(early, 0, tile), take(early, 1, tile), take(early, 2, tile)
        right = jnp.concatenate(
            [(step + step_next * ratio) * h_0 + step_next * h_a, (-step_next * small) * h_0], axis=0
        )
        columns = slice(128 * tile, 128 * tile + 128)
        solution_ref[:, :, columns] = product(value, split(right)).reshape(4, 32, 128)
        right = jnp.concatenate(
            [
                (-0.1 * step_next) * bent[:, columns],
                (-small * (1.0 + step_next * ratio / step)) * h_0
                - (0.1 * step_next) * (h_a - small * y_1),
                (0.1 * step_next * small) * h_0,
            ],
            axis=0,
        )
        part_ref[:, columns] = product(slope, split(right))


def final_kernel(late_ref, side_ref, part_ref, residual_ref, late):
    gather_blocks(late_ref, 10, 0, 10, late, 0)
    value = split(side_ref[0:128, 0:40])
    for tile in range(8):
        columns = slice(128 * tile, 128 * tile + 128)
        whole = part_ref[:, columns] + product(value, split(take(late, 0, tile)))
        residual_ref[:, :, columns] = whole.reshape(4, 32, 128)


def call(kernel, outputs, scratch, *operands, aliases={}, left=(), scalars=(), limit=16):
    vmem = pl.BlockSpec(memory_space=pltpu.VMEM)
    specs = [vmem] * len(operands)
    for k in left:
        specs[k] = pl.BlockSpec(memory_space=pltpu.HBM)
    for k in scalars:
        specs[k] = pl.BlockSpec(memory_space=pltpu.SMEM)
    return pl.pallas_call(
        kernel,
        out_shape=[
            shape if isinstance(shape, jax.ShapeDtypeStruct) else jax.ShapeDtypeStruct(shape, f32)
            for shape in outputs
        ],
        in_specs=specs,
        out_specs=[vmem] * len(outputs),
        scratch_shapes=[
            pltpu.VMEM(shape, f32) if isinstance(shape, tuple) else shape for shape in scratch
        ],
        input_output_aliases=aliases,
        compiler_params=pltpu.CompilerParams(vmem_limit_bytes=limit * 2**20),
    )(*operands)


def pair_of(*shape):
    return [jax.ShapeDtypeStruct(shape, jnp.bfloat16)] * 2


def exchange(buffer):
    count = buffer.shape[0] // DEVICES
    tiled = count == 4 or count % 8 == 0
    shape = (DEVICES, count, 128) if tiled else (DEVICES, 1, count * 128)
    moved = lax.all_to_all(buffer.reshape(shape), ("slab", "grp"), 0, 0, tiled=True)
    return moved.reshape(buffer.shape)


def fast_program(
    photon_table,
    bin_weights,
    first_start,
    first_band,
    second_start,
    second_band,
    third_start,
    third_band,
    fourth_start,
    fourth_band,
):
    total = DEVICES * ROWS
    work = [(256, 128), (64, 384)]
    outer = (first_start, first_band.T, second_start, second_band.T)
    inputs = (
        photon_table.transpose(1, 0, 2),
        bin_weights.transpose(1, 0, 2),
        third_start,
        third_band.T,
        fourth_start,
        fourth_band.T,
    )
    send, wide, inner = call(
        start_kernel,
        [(160, 128), (416, 256), jax.ShapeDtypeStruct((704, 128), jnp.bfloat16)],
        [pltpu.VMEM(value.shape, value.dtype) for value in inputs]
        + [pltpu.SemaphoreType.DMA((len(inputs),))]
        + [(16, N2 * N3), (16, N2 * N3), (256, 256)]
        + work,
        *inputs,
        left=range(len(inputs)),
        limit=LARGE,
    )
    recv = exchange(send)
    grams = [(48, 128)] + [pltpu.VMEM((total, 128), jnp.bfloat16)] * 4
    group = lax.axis_index("grp").reshape(1)
    *matrices, side, small_h, small_l = call(
        matrix_kernel,
        pair_of(2 * total, total) + pair_of(K0 * N1, total) + [(192, 384)] + pair_of(K0, N0),
        grams,
        group, *outer,
        scalars=(0,),
    )
    gram, lift = matrices[0:2], matrices[2:4]
    send, fields, images = call(
        first_column_kernel, [(32 * PLAIN, 128), (total, 128), (total, 128)], [], recv, *gram
    )
    recv = exchange(send)
    send, scalars, wide = call(
        first_row_kernel,
        [(32 * PLAIN, 128), (8, 128), (416, 256)],
        work,
        recv, wide, inner,
        aliases={1: 2},
    )
    recv = exchange(send)
    send, blend, scalars = call(
        second_column_kernel,
        [(32 * PLAIN, 128), (total, 128), (8, 128)],
        [(total, 128), (total, 128)],
        recv, *gram, fields, images, scalars,
        aliases={3: 1},
    )
    recv = exchange(send)
    send, keep, sums = call(
        middle_kernel,
        [(DEVICES * JOINT, 128), (K0 * N1, 128), (8, 128)],
        [(K0 * N1, 128)],
        blend, *lift, scalars, side,
    )
    (send,) = call(
        second_row_kernel,
        [(DEVICES * JOINT, 128)],
        work,
        send, recv, sums, scalars, wide, inner,
        aliases={0: 0},
    )
    recv = exchange(send)
    partner = lax.ppermute(recv, "grp", [(0, 1), (1, 0)])
    send, scalars = call(
        third_column_kernel,
        [(DEVICES * 10, 128), (8, 128)],
        [(32, 384), (K0 * N1, 128), (K0 * N1, 128)],
        recv, small_h, small_l, keep, scalars,
    )
    late = exchange(send)
    solution_part, part = call(
        settle_kernel,
        [(4, 32, 1024), (128, 1024)],
        [(960, 128)],
        recv, partner, side, scalars,
    )
    (residual,) = call(final_kernel, [(4, 32, 1024)], [(320, 128)], late, side, part)
    return solution_part, residual


def fits(mesh):
    return (mesh.shape["slab"], mesh.shape["grp"]) == (SLABS, GRPS)


def solution(mesh):
    placed = (
        P("slab", "grp", None),
        P("slab", "grp", None),
        P(),
        P(),
        P(),
        P(),
        P(),
        P(),
        P(),
        P(),
    )
    return jax.shard_map(
        fast_program if fits(mesh) else per_device,
        mesh=mesh,
        in_specs=placed,
        out_specs=(P("slab", "grp", None), P("slab", "grp", None)),
        check_vma=False,
    )
```

```python
import jax
import jax.numpy as jnp
from jax import lax
from jax.experimental import pallas as pl
from jax.experimental.pallas import tpu as pltpu
from jax.sharding import PartitionSpec as P

K0 = 64
K1 = 64
K2 = 32
K3 = 32
ITERS = 2


highest = lax.Precision.HIGHEST
smoothing = 0.1
stencil_weights = (1.0, -4.0, 6.0, -4.0, 1.0)


def with_halo(value, sides, width):
    for axis, dim in sides:
        count, length = (lax.axis_size(axis), value.shape[dim])
        up = [(i, (i + 1) % count) for i in range(count - 1)]
        down = [(j, i) for i, j in up]
        last = lax.slice_in_dim(value, length - width, length, axis=dim)
        initial = lax.slice_in_dim(value, 0, width, axis=dim)
        before = lax.ppermute(last, axis, up)
        after = lax.ppermute(initial, axis, down)
        value = jnp.concatenate([before, value, after], axis=dim)
    return value


def dense_basis(starts, values, coef_count):
    relative = jnp.arange(coef_count, dtype=jnp.int32)[None, :] - starts[:, None]
    matrix = jnp.zeros((starts.shape[0], coef_count), jnp.float32)
    for offset in range(4):
        matrix = matrix + jnp.where(relative == offset, values[:, offset : offset + 1], 0.0)
    return matrix


def five_point(source, along, extent):
    running = stencil_weights[0] * lax.slice_in_dim(source, 0, extent, axis=along)
    for offset in range(1, 5):
        running = running + stencil_weights[offset] * lax.slice_in_dim(
            source, offset, offset + extent, axis=along
        )
    return running


def local_stencil(tensor, along):
    widths = [(0, 0)] * tensor.ndim
    widths[along] = (2, 2)
    return five_point(jnp.pad(tensor, widths), along, tensor.shape[along])


def inner_forward(tensor, third_basis, fourth_basis):
    leading, middle = (tensor.shape[0], tensor.shape[1])
    blocked = tensor.reshape(leading, middle, third_basis.shape[1], fourth_basis.shape[1])
    blocked = jnp.einsum("abcd,nd->abcn", blocked, fourth_basis, precision=highest)
    blocked = jnp.einsum("abcn,mc->abmn", blocked, third_basis, precision=highest)
    return blocked.reshape(leading, middle, third_basis.shape[0] * fourth_basis.shape[0])


def inner_adjoint(tensor, third_basis, fourth_basis):
    leading, middle = (tensor.shape[0], tensor.shape[1])
    blocked = tensor.reshape(leading, middle, third_basis.shape[0], fourth_basis.shape[0])
    blocked = jnp.einsum("abmn,mc->abcn", blocked, third_basis, precision=highest)
    blocked = jnp.einsum("abcn,nd->abcd", blocked, fourth_basis, precision=highest)
    return blocked.reshape(leading, middle, third_basis.shape[1] * fourth_basis.shape[1])


def lead_product(tensor, matrix):
    combined = jnp.einsum(
        "ka,ain->kin",
        matrix,
        lax.all_to_all(tensor, "slab", split_axis=2, concat_axis=0, tiled=True),
        precision=highest,
    )
    return lax.all_to_all(combined, "slab", split_axis=0, concat_axis=2, tiled=True)


def second_product(tensor, matrix):
    return jnp.einsum(
        "lp,apn->aln", matrix, lax.all_gather(tensor, "grp", axis=1, tiled=True), precision=highest
    )


def penalty(coeffs):
    leading, middle = (coeffs.shape[0], coeffs.shape[1])
    padded = with_halo(coeffs, (("slab", 0), ("grp", 1)), 2)
    along_lead = five_point(padded[:, 2 : 2 + middle], 0, leading)
    along_rows = five_point(padded[2 : 2 + leading, :], 1, middle)
    blocked = coeffs.reshape(leading, middle, K2, K3)
    inner_part = local_stencil(blocked, 2) + local_stencil(blocked, 3)
    return along_lead + along_rows + inner_part.reshape(leading, middle, K2 * K3)


def squared_total(vector):
    return lax.psum(jnp.sum(vector * vector), ("slab", "grp"))


def per_device(
    photon_table,
    bin_weights,
    first_start,
    first_band,
    second_start,
    second_band,
    third_start,
    third_band,
    fourth_start,
    fourth_band,
):
    first_basis = dense_basis(first_start, first_band, K0)
    second_basis = dense_basis(second_start, second_band, K1)
    third_basis = dense_basis(third_start, third_band, K2)
    fourth_basis = dense_basis(fourth_start, fourth_band, K3)
    first_back = first_basis.T
    group_index = lax.axis_index("grp")
    row_count = photon_table.shape[1]
    coef_rows = K1 // lax.axis_size("grp")
    near_rows = lax.dynamic_slice_in_dim(second_basis, group_index * row_count, row_count, 0)
    back_rows = lax.dynamic_slice_in_dim(second_basis.T, group_index * coef_rows, coef_rows, 0)

    def adjoint(table):
        tensor = lead_product(table, first_back)
        tensor = second_product(tensor, back_rows)
        return inner_adjoint(tensor, third_basis, fourth_basis)

    right_side = adjoint(bin_weights * photon_table)
    solution = jnp.zeros_like(right_side)
    residual = right_side
    direction = right_side
    norm_now = squared_total(residual)
    for sweep in range(ITERS):
        forward_tensor = inner_forward(direction, third_basis, fourth_basis)
        forward_tensor = second_product(forward_tensor, near_rows)
        mapped = adjoint(
            bin_weights * lead_product(forward_tensor, first_basis)
        ) + smoothing * penalty(direction)
        curve_total = lax.psum(jnp.sum(direction * mapped), ("slab", "grp"))
        step_size = norm_now / curve_total
        solution = solution + step_size * direction
        residual = residual - step_size * mapped
        norm_next = squared_total(residual)
        direction = residual + norm_next / norm_now * direction
        norm_now = norm_next
    return (solution, residual)


SLABS, GRPS = 16, 2
DEVICES = SLABS * GRPS
L0, L1 = 2, 5
ROWS = L0 * L1
N2, N3 = 64, 50
N0, N1 = 32, 10
HI = lax.Precision.HIGHEST
f32 = jnp.float32
JOINT = 18
PLAIN = 3
LARGE = 60


def iota(shape, dim):
    return lax.broadcasted_iota(jnp.int32, shape, dim)


def mm(a, b):
    return jnp.dot(a, b, precision=HI, preferred_element_type=f32)


def mm_t(a, b):
    return lax.dot_general(
        a, b, (((1,), (1,)), ((), ())), precision=HI, preferred_element_type=f32
    )


def split(value):
    high = value.astype(jnp.bfloat16)
    return high, (value - high.astype(f32)).astype(jnp.bfloat16)


def product(a, b, transposed=False):
    dims = (((1,), (1 if transposed else 0,)), ((), ()))

    def one(x, y):
        return lax.dot_general(x, y, dims, preferred_element_type=f32)

    return one(a[0], b[0]) + (one(a[0], b[1]) + one(a[1], b[0]))


def load(pair):
    return pair[0][...], pair[1][...]


def move(block, source, target):
    shift = (target - source) * 32 % 128
    return pltpu.roll(block, shift, 1) if shift else block


def merge(parts):
    lane = iota(parts[0].shape, 1)
    out = parts[-1]
    for q in range(len(parts) - 2, -1, -1):
        out = jnp.where(lane < 32 * (q + 1), parts[q], out)
    return out


def slot(r):
    return L0 * (r % L1) + r // L1


def banded_t(start_ref, band_ref, width, wrap):
    n = start_ref.shape[0]
    relative = (iota((width, n), 0) % wrap) - start_ref[...].reshape(1, n)
    out = jnp.zeros((width, n), f32)
    for offset in range(4):
        out = out + jnp.where(relative == offset, band_ref[offset : offset + 1, :], 0.0)
    return out


def expand(ref, p):
    first = 200 * p
    tile, off = first // 128, first % 128
    lane = iota((16, 128), 1)

    def window(t):
        low = ref[:, t * 128 : (t + 1) * 128]
        if off == 0:
            return low
        t1 = min(t + 1, 24)
        high = ref[:, t1 * 128 : (t1 + 1) * 128]
        return jnp.where(
            lane < 128 - off, pltpu.roll(low, 128 - off, 1), pltpu.roll(high, 128 - off, 1)
        )

    return window(tile), window(min(tile + 1, 24))


def table_to_mixed(field, kron_third, second_t, rows_ref, stack_ref):
    rows_ref[...] = product(split(field), kron_third)
    for c in range(4):
        for j in range(3):
            parts = []
            for q in range(4):
                r = 4 * j + q
                if r < ROWS:
                    part = rows_ref[pl.ds(slot(r), 16, stride=16), :]
                    parts.append(move(part, c, q))
                else:
                    parts.append(jnp.zeros((16, 128), f32))
            stack_ref[16 * c : 16 * c + 16, 128 * j : 128 * j + 128] = merge(parts)
    return product(second_t, split(stack_ref[...]))


def mixed_to_table(value, kron_third, second, rows_ref, stack_ref):
    stack_ref[...] = product(second, split(value))
    rows_ref[...] = jnp.zeros((256, 128), f32)
    for r in range(ROWS):
        j, q = r // 4, r % 4
        parts = [
            move(stack_ref[16 * c : 16 * c + 16, 128 * j : 128 * j + 128], q, c) for c in range(4)
        ]
        rows_ref[pl.ds(slot(r), 16, stride=16), :] = merge(parts)
    return product(split(rows_ref[...]), kron_third, True)


def inner_penalty(value):
    out = 12.0 * value
    row = iota((32, 128), 0)
    inside = iota((32, 128), 1) % 32
    tiles = []
    for j in range(3):
        tile = value[:, 128 * j : 128 * j + 128]
        total = 12.0 * tile
        for d, weight in ((1, -4.0), (2, 1.0)):
            total = total + weight * (
                jnp.where(row >= d, pltpu.roll(tile, d, 0), 0.0)
                + jnp.where(row < 32 - d, pltpu.roll(tile, 32 - d, 0), 0.0)
                + jnp.where(inside >= d, pltpu.roll(tile, d, 1), 0.0)
                + jnp.where(inside < 32 - d, pltpu.roll(tile, 128 - d, 1), 0.0)
            )
        tiles.append(total)
    return jnp.concatenate(tiles, axis=1)


def tile_of(value, j):
    return value[:, 128 * j : 128 * j + 128]


def put(ref, row, count, value):
    ref[pl.ds(row, 32, stride=count), :] = value


def lanes(values):
    lane = iota((8, 128), 1)
    out = jnp.zeros((8, 128), f32)
    for k, value in enumerate(values):
        out = jnp.where(lane == k, value, out)
    return out


def with_scalars(tile, values):
    one = pltpu.roll(lanes(values), 64, 1)
    return jnp.where(iota((32, 128), 1) < 64, tile, jnp.concatenate([one] * 4, axis=0))


def totals(ref, count, number):
    summed = jnp.sum(ref[pl.ds(2, 32, stride=count), :], axis=0, keepdims=True)
    lane = iota((1, 128), 1)
    return [jnp.sum(jnp.where(lane == 64 + k, summed, 0.0)) for k in range(number)]


def pick(ref, k):
    lane = iota((1, 128), 1)
    return jnp.sum(jnp.where(lane == k, ref[0:1, :], 0.0))


def constants(ref):
    kron = ref[0:256, :], ref[256:512, :]
    second = ref[512:576, 0:32], ref[576:640, 0:32]
    return kron, second, (ref[640:672, 0:64], ref[672:704, 0:64])


def row_tile(piece, j):
    place = 3 * piece + j
    first = 256 + 32 * (place // 2)
    return slice(first, first + 32), slice(128 * (place % 2), 128 * (place % 2) + 128)


def keep_rows(ref, piece, value):
    for j in range(3):
        ref[row_tile(piece, j)] = tile_of(value, j)


def kept_rows(ref, piece):
    return jnp.concatenate([ref[row_tile(piece, j)] for j in range(3)], axis=1)


def start_kernel(
    table_hbm, weight_hbm, start2_hbm, band2_hbm, start3_hbm, band3_hbm,
    send_ref, wide_ref, inner_ref,
    table_ref, weight_ref, start2_ref, band2_ref, start3_ref, band3_ref, sems,
    product_ref, packed_ref, field_ref, rows_ref, stack_ref,
):
    copies = [
        pltpu.make_async_copy(source, target, sems.at[k])
        for k, (source, target) in enumerate(
            (
                (start3_hbm, start3_ref),
                (band3_hbm, band3_ref),
                (start2_hbm, start2_ref),
                (band2_hbm, band2_ref),
                (weight_hbm, weight_ref),
                (table_hbm, table_ref),
            )
        )
    ]
    for copy in copies:
        copy.start()
    copies[0].wait()
    copies[1].wait()
    pick_bin = (iota((256, N3), 0) % N3 == iota((256, N3), 1)) & (iota((256, N3), 0) < 4 * N3)
    same = iota((256, 128), 0) // N3 == iota((256, 128), 1) // 32
    picker = jnp.where(pick_bin, 1.0, 0.0).astype(jnp.bfloat16)
    for k, term in enumerate(split(banded_t(start3_ref, band3_ref, 128, 32))):
        spread_out = lax.dot_general(
            picker, term, (((1,), (1,)), ((), ())), preferred_element_type=f32
        )
        inner_ref[256 * k : 256 * k + 256, :] = jnp.where(same, spread_out, 0.0).astype(jnp.bfloat16)
    copies[2].wait()
    copies[3].wait()
    order, other = iota((N2, N2), 1), iota((N2, N2), 0)
    permute = jnp.where((order % 16) * 4 + order // 16 == other, 1.0, 0.0).astype(jnp.bfloat16)
    back = jnp.where((other % 16) * 4 + other // 16 == order, 1.0, 0.0).astype(jnp.bfloat16)
    for k, term in enumerate(split(banded_t(start2_ref, band2_ref, 32, 32))):
        value = jnp.dot(term, permute, preferred_element_type=f32)
        inner_ref[640 + 32 * k : 672 + 32 * k, 0:64] = value.astype(jnp.bfloat16)
        value = lax.dot_general(back, term, (((1,), (1,)), ((), ())), preferred_element_type=f32)
        inner_ref[512 + 64 * k : 576 + 64 * k, 0:32] = value.astype(jnp.bfloat16)
    kron, _, turned = constants(inner_ref)
    copies[4].wait()
    copies[5].wait()
    packed_ref[8:16, :] = jnp.zeros((8, N2 * N3), f32)
    product_ref[8:16, :] = jnp.zeros((8, N2 * N3), f32)
    for b in range(L1):
        weight = weight_ref[b]
        packed_ref[L0 * b : L0 * b + L0, :] = weight
        product_ref[L0 * b : L0 * b + L0, :] = weight * table_ref[b]
    for p in range(16):
        for source, target in ((packed_ref, wide_ref), (product_ref, field_ref)):
            low, high = expand(source, p)
            target[16 * p : 16 * p + 16, 0:128] = low
            target[16 * p : 16 * p + 16, 128:256] = high
    mixed = table_to_mixed(field_ref[...], kron, turned, rows_ref, stack_ref)
    once = inner_penalty(mixed)
    keep_rows(wide_ref, 1, mixed)
    keep_rows(wide_ref, 2, once)
    for base, value in ((0, mixed), (3, once)):
        put(send_ref, base, 5, tile_of(value, 0))
        put(send_ref, base + 1, 5, tile_of(value, 1))
    lane = iota((32, 128), 1)
    put(send_ref, 2, 5, jnp.where(lane < 64, tile_of(mixed, 2), pltpu.roll(tile_of(once, 2), 64, 1)))


def pentadiagonal(n):
    gap = jnp.abs(iota((n, n), 0) - iota((n, n), 1))
    return jnp.where(gap == 0, 6.0, jnp.where(gap == 1, -4.0, jnp.where(gap == 2, 1.0, 0.0)))


def choose(pieces, selector):
    out = None
    for piece in pieces:
        term = jnp.dot(piece, selector, preferred_element_type=f32)
        out = term if out is None else out + term
    return out


def powers(basis_t, count):
    penalty_matrix = pentadiagonal(basis_t.shape[0])
    out = [basis_t]
    for _ in range(count - 1):
        out.append(mm(penalty_matrix, out[-1]))
    return out


def store_split(high_ref, low_ref, rows, value):
    high, low = split(value)
    high_ref[rows, :] = high
    low_ref[rows, :] = low


def gram_blocks(refs, count, small_ref, rows0_h, rows0_l, rows1_h, rows1_l):
    start0_ref, band0_ref, start1_ref, band1_ref = refs
    total = DEVICES * ROWS
    powers0 = powers(banded_t(start0_ref, band0_ref, K0, K0), count)
    powers1 = powers(banded_t(start1_ref, band1_ref, K1, K1), 4)
    small_ref[...] = jnp.zeros((48, 128), f32)
    first, second = powers0[0].T, powers1[0].T
    for k in range(count):
        small_ref[0:N0, 32 * k : 32 * k + N0] = mm(first, powers0[k])
        small_ref[N0 : N0 + N1, 32 * k : 32 * k + N1] = mm(second, powers1[k])
    row0 = iota((total, N0), 0)
    pick0 = L0 * (row0 % 32 // GRPS) + row0 // 32 // L1 == iota((total, N0), 1)
    row1 = iota((total, 16), 0)
    pick1 = L1 * (row1 % GRPS) + row1 // 32 % L1 == iota((total, 16), 1)
    for pick, rows, targets in (
        (pick0, slice(0, N0), (rows0_h, rows0_l)),
        (pick1, slice(N0, N0 + 16), (rows1_h, rows1_l)),
    ):
        chooser = jnp.where(pick, 1.0, 0.0).astype(jnp.bfloat16)
        for term, target in zip(split(small_ref[rows, :]), targets):
            spread_out = jnp.dot(chooser, term, preferred_element_type=f32)
            target[...] = spread_out.astype(jnp.bfloat16)
    line, column = iota((128, total), 0), iota((128, total), 1)
    match0 = line % 32 == L0 * (column % 32 // GRPS) + column // 32 // L1
    match1 = line % 32 == L1 * (column % GRPS) + column // 32 % L1
    select0, select1 = [
        [
            jnp.where(match & (line // 32 == k), 1.0, 0.0).astype(jnp.bfloat16)
            for k in range(count)
        ]
        for match in (match0, match1)
    ]

    def block(base):
        block0 = rows0_h[pl.ds(base, 64), :], rows0_l[pl.ds(base, 64), :]
        block1 = rows1_h[pl.ds(base, 64), :], rows1_l[pl.ds(base, 64), :]
        g = [choose(block0, selector) for selector in select0]
        h = [choose(block1, selector) for selector in select1]
        return g, h

    return powers0, powers1, select0[0][0:N0, :], block


def matrix_kernel(
    group_ref, start0_ref, band0_ref, start1_ref, band1_ref,
    gram_h_ref, gram_l_ref, lift_h_ref, lift_l_ref, side_ref, small_h_ref, small_l_ref, *scratch,
):
    total = DEVICES * ROWS
    refs = (start0_ref, band0_ref, start1_ref, band1_ref)
    powers0, powers1, chosen, block = gram_blocks(refs, 2, *scratch)

    @pl.loop(0, 5)
    def _(step):
        base = pl.multiple_of(step * 64, 64)
        g, h = block(base)
        store_split(gram_h_ref, gram_l_ref, pl.ds(base, 64), g[0] * h[0])
        store_split(
            gram_h_ref, gram_l_ref, pl.ds(base + total, 64), g[1] * h[0] + g[0] * h[1]
        )

    lifted = [
        jnp.dot(term, chosen, preferred_element_type=f32)
        for term in split(powers0[0])
    ]
    spot = iota((N0, N0), 1)
    order = jnp.where(L0 * (spot % 16) + spot // 16 == iota((N0, N0), 0), 1.0, 0.0).astype(jnp.bfloat16)
    for term, target in zip(split(powers0[0]), (small_h_ref, small_l_ref)):
        target[...] = jnp.dot(term, order, preferred_element_type=f32).astype(jnp.bfloat16)
    owner = L1 * (iota((K0, total), 1) % GRPS) + iota((K0, total), 1) // 32 % L1
    for n in range(N1):
        rows = slice(K0 * n, K0 * n + K0)
        for term, target in zip(lifted, (lift_h_ref, lift_l_ref)):
            target[rows, :] = jnp.where(owner == n, term, 0.0).astype(jnp.bfloat16)
    group = group_ref[0]
    coef = iota((128, K1), 0) % 32 + 32 * group
    pick_coef = jnp.where(coef == iota((128, K1), 1), 1.0, 0.0)
    half = iota((N1, N1), 1) // L1
    wanted = L1 * jnp.where(half == group, 0, 1) + iota((N1, N1), 1) % L1
    reorder = jnp.where(iota((N1, N1), 0) == wanted, 1.0, 0.0)
    side_ref[...] = jnp.zeros((192, 384), f32)
    across = powers1[0].T
    for k in range(4):
        side_ref[128 + 16 * k : 128 + 16 * k + N1, 0:N1] = mm(across, powers1[k])
    for k in range(3):
        own = mm(pick_coef, powers1[k])
        halves = mm(own, reorder)
        for alpha in range(4):
            rows = slice(32 * alpha, 32 * alpha + 32)
            if k == 0:
                side_ref[rows, 10 * alpha : 10 * alpha + 10] = own[rows, :]
            for h in range(2):
                piece = halves[rows, L1 * h : L1 * h + L1]
                place = 40 * k + 20 * h + L1 * alpha
                side_ref[rows, 256 + place : 256 + place + L1] = piece
                if k < 2:
                    side_ref[rows, 128 + place : 128 + place + L1] = piece


def unpack(ref, row, count, r, source, target):
    return move(ref[pl.ds(row, 32, stride=count), :], source, target)


def first_column_kernel(recv_ref, gram_h_ref, gram_l_ref, send_ref, fields_ref, images_ref):
    total = DEVICES * ROWS
    zero = jnp.zeros((32, 128), f32)
    for r in range(ROWS):
        j, q = r // 4, r % 4
        where0 = (j, q) if j < 2 else (2, q)
        where1 = (3 + j, q) if j < 2 else (2, q + 2)
        parts = [
            unpack(recv_ref, place[0], 5, r, place[1], k) for k, place in enumerate((where0, where1))
        ]
        fields_ref[32 * r : 32 * r + 32, :] = merge(parts + [zero])
    fields = fields_ref[...]
    applied = product(load((gram_h_ref, gram_l_ref)), split(fields))
    lane = iota((total, 128), 1)
    images = applied[:total] + jnp.where(
        (lane >= 32) & (lane < 64), pltpu.roll(applied[total:], 32, 1), 0.0
    )
    images_ref[...] = images
    norm = jnp.sum(jnp.where(lane < 32, fields * images, 0.0))
    bend = jnp.sum(jnp.where(lane < 32, fields * pltpu.roll(images, 96, 1), 0.0))
    send_rows(send_ref, images_ref, (norm, bend))


def send_rows(send_ref, value_ref, values=()):
    for j in range(3):
        parts = []
        for q in range(4):
            r = 4 * j + q
            if r < ROWS:
                parts.append(move(value_ref[32 * r : 32 * r + 32, :], 0, q))
            else:
                parts.append(jnp.zeros((32, 128), f32))
        tile = merge(parts)
        put(send_ref, j, PLAIN, with_scalars(tile, values) if j == 2 else tile)


def received_rows(recv_ref):
    tiles = [recv_ref[pl.ds(j, 32, stride=PLAIN), :] for j in range(3)]
    tiles[2] = jnp.where(iota((32, 128), 1) < 64, tiles[2], 0.0)
    return jnp.concatenate(tiles, axis=1)


def first_row_kernel(
    recv_ref, wide_ref, inner_ref, send_ref, scalar_ref, carried_ref, rows_ref, stack_ref,
):
    norm, bend = totals(recv_ref, PLAIN, 2)
    scalar_ref[...] = lanes((norm, bend))
    kron, second, turned = constants(inner_ref)
    field = mixed_to_table(received_rows(recv_ref), kron, second, rows_ref, stack_ref)
    weighted = wide_ref[0:256, :] * field
    energy = jnp.sum(field * weighted)
    mixed = table_to_mixed(weighted, kron, turned, rows_ref, stack_ref)
    keep_rows(carried_ref, 0, mixed)
    for j in range(2):
        put(send_ref, j, PLAIN, tile_of(mixed, j))
    put(send_ref, 2, PLAIN, with_scalars(tile_of(mixed, 2), (energy,)))


def second_column_kernel(
    recv_ref, gram_h_ref, gram_l_ref, fields_ref, images_ref, scalar_ref,
    send_ref, blend_ref, out_scalar_ref, next_ref, image_ref,
):
    zero = jnp.zeros((32, 128), f32)
    for r in range(ROWS):
        part = unpack(recv_ref, r // 4, PLAIN, r, r % 4, 0)
        next_ref[32 * r : 32 * r + 32, :] = merge([part, zero])
    (energy,) = totals(recv_ref, PLAIN, 1)
    norm, bend = pick(scalar_ref, 0), pick(scalar_ref, 1)
    step = norm / (energy + 0.1 * bend)
    out_scalar_ref[...] = lanes((norm, step))
    fields, images, following = fields_ref[...], images_ref[...], next_ref[...]
    gram = gram_h_ref[0 : DEVICES * ROWS, :], gram_l_ref[0 : DEVICES * ROWS, :]
    image = product(gram, split(following))
    image_ref[...] = images - step * (image + 0.1 * pltpu.roll(images, 96, 1))
    send_rows(send_ref, image_ref)
    lane = iota(fields.shape, 1)
    reduced = fields - step * (following + 0.1 * pltpu.roll(fields, 96, 1))
    kept = jnp.where(lane < 64, 0.0, pltpu.roll(fields, 64, 1))
    blend_ref[...] = jnp.where(lane < 32, reduced, kept)


def coefficient_penalty(value):
    k = iota(value.shape, 0) % K0
    count = value.shape[0]
    total = 6.0 * value
    for d, weight in ((1, -4.0), (2, 1.0)):
        total = total + weight * (
            jnp.where(k >= d, pltpu.roll(value, d, 0), 0.0)
            + jnp.where(k < K0 - d, pltpu.roll(value, count - d, 0), 0.0)
        )
    return total


def send_blocks(send_ref, count, base, value_ref, block):
    for j in range(10):
        parts = []
        for q in range(4):
            m = 4 * j + q
            alpha, n = m // 10, m % 10
            parts.append(move(value_ref[pl.ds(K0 * n + alpha, 16, stride=4), :], block, q))
        merged = merge(parts)
        for g in range(GRPS):
            send_ref[pl.ds(g * count + base + j, 16, stride=2 * count), :] = merged


def send_halves(send_ref, count, base, value_ref, block):
    for g in range(GRPS):
        for j in range(5):
            parts = []
            for q in range(4):
                alpha, b = divmod(4 * j + q, L1)
                row = K0 * (L1 * g + b) + alpha
                parts.append(move(value_ref[pl.ds(row, 16, stride=4), :], block, q))
            send_ref[pl.ds(g * count + base + j, 16, stride=2 * count), :] = merge(parts)


def middle_kernel(
    blend_ref, lift_h_ref, lift_l_ref, scalar_ref, side_ref, send_ref, keep_ref, sums_ref, four_ref
):
    step = pick(scalar_ref, 1)
    small = 0.1 * step
    lifted = product(load((lift_h_ref, lift_l_ref)), split(blend_ref[...]))
    once = coefficient_penalty(lifted)
    twice = coefficient_penalty(once)
    h_a = lifted - small * pltpu.roll(once, 64, 1)
    y_1 = once + pltpu.roll(lifted, 96, 1)
    x_a = once - small * pltpu.roll(twice, 64, 1)
    h_0 = pltpu.roll(lifted, 64, 1)
    lane = iota(lifted.shape, 1)

    def blocks(first, second, third, fourth):
        return jnp.where(
            lane < 32, first, jnp.where(lane < 64, second, jnp.where(lane < 96, third, fourth))
        )

    keep_ref[...] = blocks(h_0, pltpu.roll(h_a, 32, 1), y_1, pltpu.roll(x_a, 96, 1))
    flat = x_a - small * pltpu.roll(once, 32, 1)
    slope = h_a - small * pltpu.roll(y_1, 64, 1)
    four_ref[...] = blocks(
        h_a, -small * pltpu.roll(h_0, 32, 1), pltpu.roll(flat, 64, 1), pltpu.roll(slope, 96, 1)
    )
    grams = split(side_ref[128:192, 0:N1])
    corner = iota((16, 128), 1) // 32
    norm, bend = jnp.zeros((16, 128), f32), jnp.zeros((16, 128), f32)
    filler = jnp.zeros((16 - N1, 128), f32)
    for chunk in range(8):
        tiles = [four_ref[pl.ds(8 * chunk + k, N1, stride=K0), :] for k in range(8)]
        applied = product(grams, split(jnp.concatenate(tiles, axis=1)))
        for k, tile in enumerate(tiles):
            x = jnp.concatenate([tile, filler], axis=0)
            r1, r2, r3 = [pltpu.roll(x, 32 * d, 1) for d in (1, 2, 3)]
            y0, y1, y2, y3 = [applied[16 * d : 16 * d + 16, 128 * k : 128 * k + 128] for d in range(4)]
            norm = norm + jnp.where(
                corner == 0, x * y0, jnp.where(corner == 1, 2.0 * r1 * y1 + x * y2, 0.0)
            )
            bend = bend + jnp.where(
                corner == 1,
                r1 * y2 + x * y3,
                jnp.where(
                    corner == 2, r2 * y0 + r1 * y1, jnp.where(corner == 3, r3 * y1 + r2 * y2, 0.0)
                ),
            )
    sums_ref[...] = lanes((jnp.sum(norm), jnp.sum(bend)))
    for block in range(3):
        send_halves(send_ref, JOINT, PLAIN + 5 * block, keep_ref, block)


def second_row_kernel(
    early_ref, recv_ref, sums_ref, scalar_ref, wide_ref, inner_ref,
    send_ref, rows_ref, stack_ref,
):
    kron, second, turned = constants(inner_ref)
    image = received_rows(recv_ref)
    step = pick(scalar_ref, 1)
    reduced = kept_rows(wide_ref, 1) - step * (
        kept_rows(wide_ref, 0) + 0.1 * kept_rows(wide_ref, 2)
    )
    inner = jnp.sum(reduced * inner_penalty(image))
    field = mixed_to_table(image, kron, second, rows_ref, stack_ref)
    weighted = wide_ref[0:256, :] * field
    energy = jnp.sum(field * weighted)
    mixed = table_to_mixed(weighted, kron, turned, rows_ref, stack_ref)
    for j in range(2):
        put(send_ref, j, JOINT, tile_of(mixed, j))
    values = (energy, pick(sums_ref, 0), pick(sums_ref, 1) + inner)
    put(send_ref, 2, JOINT, with_scalars(tile_of(mixed, 2), values))


def third_column_kernel(
    recv_ref, small_h_ref, small_l_ref, keep_ref, scalar_ref,
    send_ref, out_scalar_ref, packed_ref, lifted_ref, mixed_ref,
):
    for a in range(L0):
        for t in range(3):
            parts = []
            for block in range(4):
                n = 4 * t + block
                if n < N1:
                    g, b = divmod(n, L1)
                    j, q = divmod(L1 * a + b, 4)
                    part = recv_ref[pl.ds(g * JOINT + j, 16, stride=2 * JOINT), :]
                    parts.append(move(part, q, block))
                else:
                    parts.append(jnp.zeros((16, 128), f32))
            packed_ref[16 * a : 16 * a + 16, 128 * t : 128 * t + 128] = merge(parts)
    packed = product(load((small_h_ref, small_l_ref)), split(packed_ref[...]))
    for n in range(N1):
        lifted_ref[K0 * n : K0 * n + K0, :] = move(tile_of(packed, n // 4), n % 4, 0)
    energy, norm_next, bend = totals(recv_ref, JOINT, 3)
    norm, step = pick(scalar_ref, 0), pick(scalar_ref, 1)
    ratio = norm_next / norm
    curve = energy + 0.1 * bend - ratio * norm_next / step
    step_next = norm_next / curve
    out_scalar_ref[...] = lanes((norm, step, ratio, step_next))
    lifted = lifted_ref[...]
    keep = keep_ref[...]
    h_a, x_a = pltpu.roll(keep, 96, 1), pltpu.roll(keep, 32, 1)
    mixed_ref[...] = (
        h_a - step_next * (lifted + 0.1 * x_a) - (step_next * ratio / step) * (keep - h_a)
    )
    send_blocks(send_ref, 10, 0, mixed_ref, 0)


def gather_blocks(ref, count, base, rows, out_ref, first):
    for j in range(rows):
        taken = [ref[pl.ds(rho * count + base + j, 8, stride=4 * count), :] for rho in range(4)]
        for q in range(4):
            m = first + 4 * j + q
            merged = merge([move(taken[rho], q, rho) for rho in range(4)])
            out_ref[pl.ds(m // 8 * 64 + m % 8, 8, stride=8), :] = merged


def take(ref, block, tile):
    return jnp.concatenate(
        [ref[pl.ds((5 * block + t) * 64 + 8 * tile, 8), :] for t in range(5)], axis=0
    )


def bent_rows(value):
    lane = iota(value.shape, 1)
    inside = lane % 32
    total = 12.0 * value
    for d, weight in ((1, -4.0), (2, 1.0)):
        total = total + weight * (
            jnp.where(lane >= 32 * d, pltpu.roll(value, 32 * d, 1), 0.0)
            + jnp.where(lane < 1024 - 32 * d, pltpu.roll(value, 1024 - 32 * d, 1), 0.0)
            + jnp.where(inside >= d, pltpu.roll(value, d, 1), 0.0)
            + jnp.where(inside < 32 - d, pltpu.roll(value, 1024 - d, 1), 0.0)
        )
    return total


def settle_kernel(own_ref, partner_ref, side_ref, scalar_ref, solution_ref, part_ref, early):
    for block in range(3):
        for h, ref in enumerate((own_ref, partner_ref)):
            gather_blocks(ref, JOINT, PLAIN + 5 * block, 5, early, 40 * block + 20 * h)
    step, ratio, step_next = pick(scalar_ref, 1), pick(scalar_ref, 2), pick(scalar_ref, 3)
    small = 0.1 * step
    value = split(side_ref[0:128, 128:208])
    slope = split(side_ref[0:128, 256:376])
    bent = bent_rows(jnp.concatenate([take(early, 1, tile) for tile in range(8)], axis=1))
    for tile in range(8):
        h_0, h_a, y_1 = take(early, 0, tile), take(early, 1, tile), take(early, 2, tile)
        right = jnp.concatenate(
            [(step + step_next * ratio) * h_0 + step_next * h_a, (-step_next * small) * h_0], axis=0
        )
        columns = slice(128 * tile, 128 * tile + 128)
        solution_ref[:, :, columns] = product(value, split(right)).reshape(4, 32, 128)
        right = jnp.concatenate(
            [
                (-0.1 * step_next) * bent[:, columns],
                (-small * (1.0 + step_next * ratio / step)) * h_0
                - (0.1 * step_next) * (h_a - small * y_1),
                (0.1 * step_next * small) * h_0,
            ],
            axis=0,
        )
        part_ref[:, columns] = product(slope, split(right))


def final_kernel(late_ref, side_ref, part_ref, residual_ref, late):
    gather_blocks(late_ref, 10, 0, 10, late, 0)
    value = split(side_ref[0:128, 0:40])
    for tile in range(8):
        columns = slice(128 * tile, 128 * tile + 128)
        whole = part_ref[:, columns] + product(value, split(take(late, 0, tile)))
        residual_ref[:, :, columns] = whole.reshape(4, 32, 128)


def call(kernel, outputs, scratch, *operands, aliases={}, left=(), scalars=(), limit=16):
    vmem = pl.BlockSpec(memory_space=pltpu.VMEM)
    specs = [vmem] * len(operands)
    for k in left:
        specs[k] = pl.BlockSpec(memory_space=pltpu.HBM)
    for k in scalars:
        specs[k] = pl.BlockSpec(memory_space=pltpu.SMEM)
    return pl.pallas_call(
        kernel,
        out_shape=[
            shape if isinstance(shape, jax.ShapeDtypeStruct) else jax.ShapeDtypeStruct(shape, f32)
            for shape in outputs
        ],
        in_specs=specs,
        out_specs=[vmem] * len(outputs),
        scratch_shapes=[
            pltpu.VMEM(shape, f32) if isinstance(shape, tuple) else shape for shape in scratch
        ],
        input_output_aliases=aliases,
        compiler_params=pltpu.CompilerParams(vmem_limit_bytes=limit * 2**20),
    )(*operands)


def pair_of(*shape):
    return [jax.ShapeDtypeStruct(shape, jnp.bfloat16)] * 2


def exchange(buffer):
    count = buffer.shape[0] // DEVICES
    tiled = count == 4 or count % 8 == 0
    shape = (DEVICES, count, 128) if tiled else (DEVICES, 1, count * 128)
    moved = lax.all_to_all(buffer.reshape(shape), ("slab", "grp"), 0, 0, tiled=True)
    return moved.reshape(buffer.shape)


def fast_program(
    photon_table,
    bin_weights,
    first_start,
    first_band,
    second_start,
    second_band,
    third_start,
    third_band,
    fourth_start,
    fourth_band,
):
    total = DEVICES * ROWS
    work = [(256, 128), (64, 384)]
    outer = (first_start, first_band.T, second_start, second_band.T)
    inputs = (
        photon_table.transpose(1, 0, 2),
        bin_weights.transpose(1, 0, 2),
        third_start,
        third_band.T,
        fourth_start,
        fourth_band.T,
    )
    send, wide, inner = call(
        start_kernel,
        [(160, 128), (416, 256), jax.ShapeDtypeStruct((704, 128), jnp.bfloat16)],
        [pltpu.VMEM(value.shape, value.dtype) for value in inputs]
        + [pltpu.SemaphoreType.DMA((len(inputs),))]
        + [(16, N2 * N3), (16, N2 * N3), (256, 256)]
        + work,
        *inputs,
        left=range(len(inputs)),
        limit=LARGE,
    )
    recv = exchange(send)
    grams = [(48, 128)] + [pltpu.VMEM((total, 128), jnp.bfloat16)] * 4
    group = lax.axis_index("grp").reshape(1)
    *matrices, side, small_h, small_l = call(
        matrix_kernel,
        pair_of(2 * total, total) + pair_of(K0 * N1, total) + [(192, 384)] + pair_of(K0, N0),
        grams,
        group, *outer,
        scalars=(0,),
    )
    gram, lift = matrices[0:2], matrices[2:4]
    send, fields, images = call(
        first_column_kernel, [(32 * PLAIN, 128), (total, 128), (total, 128)], [], recv, *gram
    )
    recv = exchange(send)
    send, scalars, wide = call(
        first_row_kernel,
        [(32 * PLAIN, 128), (8, 128), (416, 256)],
        work,
        recv, wide, inner,
        aliases={1: 2},
    )
    recv = exchange(send)
    send, blend, scalars = call(
        second_column_kernel,
        [(32 * PLAIN, 128), (total, 128), (8, 128)],
        [(total, 128), (total, 128)],
        recv, *gram, fields, images, scalars,
        aliases={3: 1},
    )
    recv = exchange(send)
    send, keep, sums = call(
        middle_kernel,
        [(DEVICES * JOINT, 128), (K0 * N1, 128), (8, 128)],
        [(K0 * N1, 128)],
        blend, *lift, scalars, side,
    )
    (send,) = call(
        second_row_kernel,
        [(DEVICES * JOINT, 128)],
        work,
        send, recv, sums, scalars, wide, inner,
        aliases={0: 0},
    )
    recv = exchange(send)
    partner = lax.ppermute(recv, "grp", [(0, 1), (1, 0)])
    send, scalars = call(
        third_column_kernel,
        [(DEVICES * 10, 128), (8, 128)],
        [(32, 384), (K0 * N1, 128), (K0 * N1, 128)],
        recv, small_h, small_l, keep, scalars,
    )
    late = exchange(send)
    solution_part, part = call(
        settle_kernel,
        [(4, 32, 1024), (128, 1024)],
        [(960, 128)],
        recv, partner, side, scalars,
    )
    (residual,) = call(final_kernel, [(4, 32, 1024)], [(320, 128)], late, side, part)
    return solution_part, residual


def fits(mesh):
    return (mesh.shape["slab"], mesh.shape["grp"]) == (SLABS, GRPS)


def solution(mesh):
    placed = (
        P("slab", "grp", None),
        P("slab", "grp", None),
        P(),
        P(),
        P(),
        P(),
        P(),
        P(),
        P(),
        P(),
    )
    return jax.shard_map(
        fast_program if fits(mesh) else per_device,
        mesh=mesh,
        in_specs=placed,
        out_specs=(P("slab", "grp", None), P("slab", "grp", None)),
        check_vma=False,
    )
```
